32 devices in a mesh: dp: 4 (over y, x), seq: 8 (over z, core).
Axes of the slice: x: 2, y: 2, z: 4, core: 2. Of those that a mesh axis runs over, the one named last changes fastest.
Arguments:
- tokens: bfloat16 [4, 1024, 1024], P('dp', 'seq'), may hold values from -6 to 6
- attn_gain: float32 [1024], replicated, may hold values from 0.1 to 1.9
- query_weight: float32 [1024, 1024], P('seq', 'dp'), may hold values from -0.1875 to 0.1875
- key_weight: float32 [1024, 1024], P('seq', 'dp'), may hold values from -0.1875 to 0.1875
- value_weight: float32 [1024, 1024], P('seq', 'dp'), may hold values from -0.1875 to 0.1875
- out_weight: float32 [1024, 1024], P('seq', 'dp'), may hold values from -2 to 2
- same_bias: float32 [16], replicated, may hold values from -1 to 1
- cross_bias: float32 [16], replicated, may hold values from -1 to 1
- ffn_gain: float32 [1024], replicated, may hold values from 0.1 to 1.9
- gate_weight: float32 [1024, 4096], P('seq', 'dp'), may hold values from -0.1875 to 0.1875
- up_weight: float32 [1024, 4096], P('seq', 'dp'), may hold values from -0.1875 to 0.1875
- down_weight: float32 [4096, 1024], P('seq', 'dp'), may hold values from -0.09375 to 0.09375
- segment_ids: int32 [4, 1024], P('dp', 'seq'), may hold values from 0 to 3, never falling along the last dimension, each value on 1 to 512 neighbouring positions
- variate_ids: int32 [4, 1024], P('dp', 'seq'), may hold values from 0 to 3
- time_ids: int32 [4, 1024], P('dp', 'seq'), may hold values from 0 to 511
- observed: int32 [4, 1024], P('dp', 'seq'), may hold values 0 or 1
- cotangent: bfloat16 [4, 1024, 1024], P('dp', 'seq'), may hold values from -6 to 6
Outputs:
- output: bfloat16 [4, 1024, 1024], P('dp', 'seq')
- tokens_grad: bfloat16 [4, 1024, 1024], P('dp', 'seq')
- attn_gain_grad: float32 [1024], replicated
- query_weight_grad: float32 [1024, 1024], P('seq', 'dp')
- key_weight_grad: float32 [1024, 1024], P('seq', 'dp')
- value_weight_grad: float32 [1024, 1024], P('seq', 'dp')
- out_weight_grad: float32 [1024, 1024], P('seq', 'dp')
- same_bias_grad: float32 [16], replicated
- cross_bias_grad: float32 [16], replicated
- ffn_gain_grad: float32 [1024], replicated
- gate_weight_grad: float32 [1024, 4096], P('seq', 'dp')
- up_weight_grad: float32 [1024, 4096], P('seq', 'dp')
- down_weight_grad: float32 [4096, 1024], P('seq', 'dp')
The draws below stay inside these ranges and needn't reach their ends.
Inputs may be any that keep to these rules, and one draw needn't show every extreme that they name: `segment_ids`: within each sequence segment numbers never fall; each of the 4 documents has 1 to 512 tokens, one exactly 512.
All inputs are finite; a program needn't handle non-finite values. No bound on the sum of `observed` on one device may be relied on, other than what follows from the above.
Results may differ from the reference program's by a relative error of at most 0.035.
Values may be sent and summed in bfloat16 or wider, within the bound.
A program may use at most 256 MiB of HBM per device.

```python
import math
import jax
import jax.numpy as jnp
import numpy as np
from jax import lax

D = 1024
HEADS = 16
FF = 4096
VARIATES = 4
TIME_SPAN = 512
SEG_COUNT = 4
LEN = 1024
SEG_MOST = 512
SEQS = 4


def set_ends(result, stream_key, low, largest):
    shape = result.shape
    index_at = [jax.random.randint(jax.random.fold_in(stream_key, axis), (), 0, shape[axis]) for axis in range(len(shape))]
    result = result.at[tuple(index_at)].set(low)
    longest = shape.index(max(shape))
    index_at[longest] = (index_at[longest] + 1) % shape[longest]
    return result.at[tuple(index_at)].set(largest)


def shard_levels(key, shape, split, least, top_value):
    gain = 1.0
    for dim, shards_of in split:
        draws = jax.random.uniform(jax.random.fold_in(jax.random.fold_in(key, 6), dim), (shards_of,), jnp.float32, least / len(split), top_value / len(split))
        gain = gain * jnp.repeat(jnp.exp(draws), shape[dim] // shards_of).reshape((-1,) + (1,) * (len(shape) - 1 - dim))
    return gain


def profile(number_of, total, most, lean):
    portions = [(1 << 20) // math.isqrt(grade ** lean) + 1 for grade in range(2, number_of + 1)]
    spare, given = total - most - (number_of - 1), [1] * (number_of - 1)
    while spare > 0:
        free = [i for i in range(number_of - 1) if given[i] < most]
        whole, budget = sum([portions[i] for i in free]), spare
        for i in free:
            extra = min(most - given[i], max(1, budget * portions[i] // whole), spare)
            given[i] = given[i] + extra
            spare = spare - extra
    return np.array([most] + given)


def ragged(own_key, count, total, reach, slope):
    if count == 2:
        one = jax.random.randint(own_key, (), max(1, total - reach), min(reach, total - 1) + 1)
        return jnp.stack([one, total - one])
    sizes = jnp.asarray(profile(count, total, reach, slope), jnp.int32)
    pairs = (count - 1) // 2
    source_of, sink = sizes[1:1 + 2 * pairs:2], sizes[2:2 + 2 * pairs:2]
    room = jnp.minimum(source_of - 1, reach - sink)
    shifted = jax.random.randint(jax.random.fold_in(own_key, 1), (pairs,), 0, 1 << 20) % (room + 1)
    sizes = sizes.at[1:1 + 2 * pairs:2].set(source_of - shifted).at[2:2 + 2 * pairs:2].set(sink + shifted)
    return sizes[jax.random.permutation(jax.random.fold_in(own_key, 2), count)]


def bell_draw(own_key, dims, width, reach, cuts=(), held_as=jnp.bfloat16):
    loudness = shard_levels(own_key, dims, cuts, -0.22, 0.18) if cuts else 1.0
    result = jax.random.normal(own_key, dims, jnp.float32) * width * loudness
    return jnp.minimum(jnp.maximum(result, -reach), reach).astype(held_as)


def setup_inputs(seed: int = 0) -> dict:
    streams_of = jax.random.split(jax.random.key(seed), 18)
    return {
        "tokens": bell_draw(streams_of[0], (SEQS, LEN, D), 1.0, 6.0, ((0, 4), (1, 8))),
        "attn_gain": jnp.clip(1.0 + 0.18 * jax.random.normal(streams_of[1], (D,), jnp.float32), 0.1, 1.9),
        "query_weight": bell_draw(streams_of[2], (D, D), D ** -0.5, 0.1875, ((0, 8), (1, 4)), jnp.float32),
        "key_weight": bell_draw(streams_of[3], (D, D), D ** -0.5, 0.1875, ((0, 8), (1, 4)), jnp.float32),
        "value_weight": bell_draw(streams_of[4], (D, D), D ** -0.5, 0.1875, ((0, 8), (1, 4)), jnp.float32),
        "out_weight": bell_draw(streams_of[5], (D, D), (D // 128) ** -0.5, 2.0, ((0, 8), (1, 4)), jnp.float32),
        "same_bias": jnp.clip(jax.random.uniform(streams_of[6], (HEADS,), jnp.float32, -1.0, 1.0), -1.0, 1.0),
        "cross_bias": jnp.clip(jax.random.uniform(streams_of[7], (HEADS,), jnp.float32, -1.0, 1.0), -1.0, 1.0),
        "ffn_gain": jnp.clip(1.0 + 0.18 * jax.random.normal(streams_of[8], (D,), jnp.float32), 0.1, 1.9),
        "gate_weight": bell_draw(streams_of[9], (D, FF), D ** -0.5, 0.1875, ((0, 8), (1, 4)), jnp.float32),
        "up_weight": bell_draw(streams_of[10], (D, FF), D ** -0.5, 0.1875, ((0, 8), (1, 4)), jnp.float32),
        "down_weight": bell_draw(streams_of[11], (FF, D), FF ** -0.5, 0.09375, ((0, 8), (1, 4)), jnp.float32),
        "segment_ids": jax.vmap(lambda own: jnp.searchsorted(jnp.cumsum(ragged(own, SEG_COUNT, LEN, SEG_MOST, 2)), jnp.arange(LEN), side="right"))(jax.random.split(streams_of[12], SEQS)).reshape((SEQS, LEN)).astype(jnp.int32),
        "variate_ids": set_ends(jax.random.randint(streams_of[13], (SEQS, LEN), 0, VARIATES), jax.random.fold_in(streams_of[13], 1), 0, VARIATES - 1).astype(jnp.int32),
        "time_ids": set_ends(jax.random.randint(streams_of[14], (SEQS, LEN), 0, TIME_SPAN), jax.random.fold_in(streams_of[14], 1), 0, TIME_SPAN - 1).astype(jnp.int32),
        "observed": set_ends((jax.random.randint(streams_of[15], (SEQS, LEN), 0, 8) < 7).astype(jnp.int32), jax.random.fold_in(streams_of[15], 1), 0, 1),
        "cotangent": bell_draw(streams_of[16], (SEQS, LEN, D), 1.0, 6.0, ((0, 4), (1, 8))),
    }


@jax.custom_vjp
def low(v):
    return lax.optimization_barrier(v.astype(jnp.bfloat16)).astype(jnp.float32)

@jax.custom_vjp
def low_back(v):
    return v

def low_keep(v):
    return (low(v), None)

def low_pass(kept, grad):
    return (grad,)

def back_keep(v):
    return (v, None)

def back_low(kept, grad):
    return (low(grad),)
low.defvjp(low_keep, low_pass)
low_back.defvjp(back_keep, back_low)
epsilon = 1e-06

def matmul(left_side, right_side):
    return jnp.dot(left_side, right_side, precision=lax.Precision.HIGHEST, preferred_element_type=jnp.float32)

def angles_of(moments, head_width):
    half_width = head_width // 2
    powers = jnp.arange(half_width).astype(jnp.float32) * (2.0 / head_width)
    return moments.astype(jnp.float32)[:, None] * (10000.0 ** (-powers))[None, :]

def rotate(shaped, angles):
    half_width = shaped.shape[-1] // 2
    first_half = shaped[..., :half_width]
    second = shaped[..., half_width:]
    cosine = jnp.cos(angles)[:, None, :]
    sine_part = jnp.sin(angles)[:, None, :]
    return jnp.concatenate([first_half * cosine - second * sine_part, second * cosine + first_half * sine_part], axis=-1)

def rms_scale(values, gain_row):
    return values * lax.rsqrt(lax.optimization_barrier(jnp.mean(values * values, axis=-1, keepdims=True)) + epsilon) * gain_row

def block_forward(tokens, attn_gain, query_weight, key_weight, value_weight, out_weight, same_bias, cross_bias, ffn_gain, gate_weight, up_weight, down_weight, segment, variate, moments, seen_row):
    length, model_width = tokens.shape
    head_count = same_bias.shape[0]
    head_width = model_width // head_count
    scaling = head_width ** (-0.5)
    places = jnp.arange(length)
    allowed = (segment[:, None] == segment[None, :]) & (seen_row[None, :] == 1) | (places[:, None] == places[None, :])
    same_kind = variate[:, None] == variate[None, :]
    angles = angles_of(moments, head_width)
    first_low = low(rms_scale(tokens, low(attn_gain)))
    query_pre = low_back(matmul(first_low, low(query_weight)))
    key_pre = low_back(matmul(first_low, low(key_weight)))
    value_low = low(low_back(matmul(first_low, low(value_weight))))
    queries = low(rotate(query_pre.reshape(length, head_count, head_width), angles))
    keys_all = low(rotate(key_pre.reshape(length, head_count, head_width), angles))
    values_all = value_low.reshape(length, head_count, head_width)

    def one_head(operands):
        query_head, key_head, value_head, same_value, cross_value = operands
        scores = low_back(matmul(query_head, key_head.T) * scaling + jnp.where(same_kind, same_value, cross_value))
        row_top = lax.optimization_barrier(jnp.max(jnp.where(allowed, scores, -jnp.inf), axis=-1, keepdims=True))
        exponent = jnp.exp(jnp.where(allowed, scores - row_top, -jnp.inf))
        probabilities = exponent / lax.optimization_barrier(jnp.sum(exponent, axis=-1, keepdims=True))
        return matmul(low(probabilities), value_head)
    head_outputs = lax.map(jax.checkpoint(one_head), (queries.transpose(1, 0, 2), keys_all.transpose(1, 0, 2), values_all.transpose(1, 0, 2), same_bias, cross_bias))
    mixed_low = low_back(low(head_outputs.transpose(1, 0, 2).reshape(length, model_width)))
    middle = tokens + low_back(matmul(mixed_low, low(out_weight)))
    second_low = low(rms_scale(middle, low(ffn_gain)))
    gate_pre = low_back(matmul(second_low, low(gate_weight)))
    up_pre = low_back(matmul(second_low, low(up_weight)))
    hidden = low(jax.nn.silu(gate_pre) * up_pre)
    return middle + matmul(hidden, low(down_weight))

def reference(tokens, attn_gain, query_weight, key_weight, value_weight, out_weight, same_bias, cross_bias, ffn_gain, gate_weight, up_weight, down_weight, segment_ids, variate_ids, time_ids, observed, cotangent):
    params = (attn_gain, query_weight, key_weight, value_weight, out_weight, same_bias, cross_bias, ffn_gain, gate_weight, up_weight, down_weight)

    def sequence_step(totals, operands):
        tokens_row, segment, variate, moments, seen_row, cotangent_row = operands

        def forward(tokens_in, *weights):
            return block_forward(tokens_in, *weights, segment, variate, moments, seen_row)
        output_row, pullback = jax.vjp(forward, tokens_row.astype(jnp.float32), *params)
        gradients = pullback(cotangent_row.astype(jnp.float32))
        totals = jax.tree.map(jnp.add, totals, tuple(gradients[1:]))
        return (totals, (output_row.astype(jnp.bfloat16), gradients[0].astype(jnp.bfloat16)))
    zero_totals = tuple((jnp.zeros_like(weight_item) for weight_item in params))
    totals, (outputs, input_grads) = lax.scan(sequence_step, zero_totals, (tokens, segment_ids, variate_ids, time_ids, observed, cotangent))
    return (outputs, input_grads, totals[0], totals[1], totals[2], totals[3], totals[4], totals[5], totals[6], totals[7], totals[8], totals[9], totals[10])
```

```python
import jax
import jax.numpy as jnp
from jax import lax
from jax.experimental import pallas as pl
from jax.experimental.pallas import tpu as pltpu
from jax.sharding import PartitionSpec as P

epsilon = 1e-06


def product(left_side, right_side):
    return jnp.dot(left_side, right_side, preferred_element_type=jnp.float32)


def contract_rows(left_side, right_side):
    return lax.dot_general(
        left_side, right_side, (((0,), (0,)), ((), ())), preferred_element_type=jnp.float32
    )


def contract_cols(left_side, right_side):
    return lax.dot_general(
        left_side, right_side, (((1,), (1,)), ((), ())), preferred_element_type=jnp.float32
    )


def angles_of(moments, head_width):
    half_width = head_width // 2
    powers = jnp.arange(half_width).astype(jnp.float32) * (2.0 / head_width)
    return moments.astype(jnp.float32)[:, None] * (10000.0 ** (-powers))[None, :]


def rotate(values, angles, head_count):
    row_count, model_width = values.shape
    shaped = values.reshape(row_count, head_count, model_width // head_count)
    half_width = model_width // head_count // 2
    first_half = shaped[..., :half_width]
    second = shaped[..., half_width:]
    cosine = jnp.cos(angles)[:, None, :]
    sine_part = jnp.sin(angles)[:, None, :]
    turned = jnp.concatenate(
        [first_half * cosine - second * sine_part, second * cosine + first_half * sine_part],
        axis=-1,
    )
    return turned.reshape(row_count, model_width)


def normalize(values, gain_row):
    factor = lax.rsqrt(jnp.mean(values * values, axis=-1, keepdims=True) + epsilon)
    normed = values * factor
    return (normed, factor, normed * gain_row)


def norm_back(incoming, normed, factor, gain_row):
    scaled = incoming * gain_row
    inner_sum = jnp.mean(scaled * normed, axis=-1, keepdims=True)
    return (factor * (scaled - normed * inner_sum), jnp.sum(incoming * normed, axis=0))


def make_tables(segment, variate, key_segment, key_variate, first_row):
    query_place = first_row + jnp.arange(segment.shape[0])
    key_place = jnp.arange(key_segment.shape[0])
    allowed = (segment.astype(jnp.float32)[:, None] == key_segment.astype(jnp.float32)[None, :]) | (
        query_place[:, None] == key_place[None, :]
    )
    same_kind = variate.astype(jnp.float32)[:, None] == key_variate.astype(jnp.float32)[None, :]
    return (allowed, same_kind)


def block_scores(
    block_index, query_low, keys_all, same_kind, same_bias, cross_bias, head_group, head_width
):
    block_width = head_group * head_width
    query_block = lax.dynamic_slice_in_dim(
        query_low, block_index * block_width, block_width, 1
    ).reshape(query_low.shape[0], head_group, head_width)
    key_block = lax.dynamic_slice_in_dim(
        keys_all, block_index * block_width, block_width, 1
    ).reshape(keys_all.shape[0], head_group, head_width)
    raw_scores = jnp.einsum(
        "thd,shd->hts", query_block, key_block, preferred_element_type=jnp.float32
    )
    same_part = lax.dynamic_slice_in_dim(same_bias, block_index * head_group, head_group)
    cross_part = lax.dynamic_slice_in_dim(cross_bias, block_index * head_group, head_group)
    offset = jnp.where(same_kind[None], same_part[:, None, None], cross_part[:, None, None])
    return (raw_scores * head_width ** (-0.5) + offset, query_block, key_block)


def body(
    tokens,
    attn_gain,
    query_weight,
    key_weight,
    value_weight,
    out_weight,
    same_bias,
    cross_bias,
    ffn_gain,
    gate_weight,
    up_weight,
    down_weight,
    segment_ids,
    variate_ids,
    time_ids,
    observed,
    cotangent,
):
    row_count = tokens.shape[1]
    model_width = tokens.shape[2]
    head_count = same_bias.shape[0]
    head_width = model_width // head_count
    head_group = max(1, 128 // head_width)
    block_width = head_group * head_width
    block_total = head_count // head_group
    scaling = head_width ** (-0.5)
    first_row = lax.axis_index("seq") * row_count
    gain_one = attn_gain.astype(jnp.bfloat16).astype(jnp.float32)
    gain_two = ffn_gain.astype(jnp.bfloat16).astype(jnp.float32)
    low_masters = (
        query_weight.astype(jnp.bfloat16),
        key_weight.astype(jnp.bfloat16),
        value_weight.astype(jnp.bfloat16),
        out_weight.astype(jnp.bfloat16),
        gate_weight.astype(jnp.bfloat16),
        up_weight.astype(jnp.bfloat16),
        down_weight.astype(jnp.bfloat16),
    )
    row_parts = (
        lax.all_gather(low_masters[0], "seq", axis=0, tiled=True),
        lax.all_gather(low_masters[1], "seq", axis=0, tiled=True),
        lax.all_gather(low_masters[2], "seq", axis=0, tiled=True),
        lax.all_gather(low_masters[3], "seq", axis=0, tiled=True),
        lax.all_gather(low_masters[4], "seq", axis=0, tiled=True),
        lax.all_gather(low_masters[5], "seq", axis=0, tiled=True),
        lax.all_gather(low_masters[6], "seq", axis=0, tiled=True),
    )
    gathered = (
        lax.all_gather(row_parts[0], "dp", axis=1, tiled=True),
        lax.all_gather(row_parts[1], "dp", axis=1, tiled=True),
        lax.all_gather(row_parts[2], "dp", axis=1, tiled=True),
        lax.all_gather(row_parts[3], "dp", axis=1, tiled=True),
        lax.all_gather(row_parts[4], "dp", axis=1, tiled=True),
        lax.all_gather(row_parts[5], "dp", axis=1, tiled=True),
        lax.all_gather(row_parts[6], "dp", axis=1, tiled=True),
    )
    w_query, w_key, w_value, w_out, w_gate, w_up, w_down = gathered
    inputs = tokens[0].astype(jnp.float32)
    segment = segment_ids[0]
    variate = variate_ids[0]
    seen_row = observed[0]
    angles = angles_of(time_ids[0], head_width)
    normed_one, factor_one, scaled_one = normalize(inputs, gain_one)
    first_low = scaled_one.astype(jnp.bfloat16)
    query_low = rotate(product(first_low, w_query), angles, head_count).astype(jnp.bfloat16)
    key_low = rotate(product(first_low, w_key), angles, head_count).astype(jnp.bfloat16)
    value_low = product(first_low, w_value).astype(jnp.bfloat16)
    key_segment = jnp.where(seen_row == 1, segment, -1).astype(jnp.bfloat16)
    key_variate = variate.astype(jnp.bfloat16)
    keys_all, values_all, segments_all, variates_all = (
        lax.all_gather(key_low, "seq", axis=0, tiled=True),
        lax.all_gather(value_low, "seq", axis=0, tiled=True),
        lax.all_gather(key_segment, "seq", axis=0, tiled=True),
        lax.all_gather(key_variate, "seq", axis=0, tiled=True),
    )
    length = keys_all.shape[0]
    allowed, same_kind = make_tables(segment, variate, segments_all, variates_all, first_row)

    def forward_block(block_index, state_now):
        mixed, summary = state_now
        scores, query_block, key_block = block_scores(
            block_index,
            query_low,
            keys_all,
            same_kind,
            same_bias,
            cross_bias,
            head_group,
            head_width,
        )
        row_top = jnp.max(jnp.where(allowed[None], scores, -jnp.inf), axis=-1, keepdims=True)
        exponent = jnp.exp(jnp.where(allowed[None], scores - row_top, -jnp.inf))
        row_total = jnp.sum(exponent, axis=-1, keepdims=True)
        prob_low = (exponent / row_total).astype(jnp.bfloat16)
        value_block = lax.dynamic_slice_in_dim(
            values_all, block_index * block_width, block_width, 1
        ).reshape(length, head_group, head_width)
        attended = jnp.einsum(
            "hts,shd->thd", prob_low, value_block, preferred_element_type=jnp.float32
        ).reshape(row_count, block_width)
        mixed = lax.dynamic_update_slice_in_dim(mixed, attended, block_index * block_width, 1)
        summary = lax.dynamic_update_slice_in_dim(
            summary, (row_top + jnp.log(row_total))[..., 0], block_index * head_group, 0
        )
        return (mixed, summary)

    mixed, summary = lax.fori_loop(
        0,
        block_total,
        forward_block,
        (
            jnp.zeros((row_count, model_width), jnp.float32),
            jnp.zeros((head_count, row_count), jnp.float32),
        ),
    )
    mixed_low = mixed.astype(jnp.bfloat16)
    middle = inputs + product(mixed_low, w_out)
    normed_two, factor_two, scaled_two = normalize(middle, gain_two)
    second_low = scaled_two.astype(jnp.bfloat16)
    gate_pre = product(second_low, w_gate)
    up_pre = product(second_low, w_up)
    sigma = jax.nn.sigmoid(gate_pre)
    activated = gate_pre * sigma
    hidden_low = (activated * up_pre).astype(jnp.bfloat16)
    result = middle + product(hidden_low, w_down)
    rows_again = (
        lax.all_gather(low_masters[0], "seq", axis=0, tiled=True),
        lax.all_gather(low_masters[1], "seq", axis=0, tiled=True),
        lax.all_gather(low_masters[2], "seq", axis=0, tiled=True),
        lax.all_gather(low_masters[3], "seq", axis=0, tiled=True),
        lax.all_gather(low_masters[4], "seq", axis=0, tiled=True),
        lax.all_gather(low_masters[5], "seq", axis=0, tiled=True),
        lax.all_gather(low_masters[6], "seq", axis=0, tiled=True),
    )
    regathered = (
        lax.all_gather(rows_again[0], "dp", axis=1, tiled=True),
        lax.all_gather(rows_again[1], "dp", axis=1, tiled=True),
        lax.all_gather(rows_again[2], "dp", axis=1, tiled=True),
        lax.all_gather(rows_again[3], "dp", axis=1, tiled=True),
        lax.all_gather(rows_again[4], "dp", axis=1, tiled=True),
        lax.all_gather(rows_again[5], "dp", axis=1, tiled=True),
        lax.all_gather(rows_again[6], "dp", axis=1, tiled=True),
    )
    w_query, w_key, w_value, w_out, w_gate, w_up, w_down = regathered
    cot_low = cotangent[0]
    hidden_grad = contract_cols(cot_low, w_down)
    down_grad = contract_rows(hidden_low, cot_low)
    gate_grad = (hidden_grad * up_pre * sigma * (1.0 + gate_pre * (1.0 - sigma))).astype(
        jnp.bfloat16
    )
    up_grad = (hidden_grad * activated).astype(jnp.bfloat16)
    gate_w_grad = contract_rows(second_low, gate_grad)
    up_w_grad = contract_rows(second_low, up_grad)
    second_grad = contract_cols(gate_grad, w_gate) + contract_cols(up_grad, w_up)
    middle_part, ffn_gain_grad = norm_back(second_grad, normed_two, factor_two, gain_two)
    middle_grad = cot_low.astype(jnp.float32) + middle_part
    middle_low = middle_grad.astype(jnp.bfloat16)
    out_w_grad = contract_rows(mixed_low, middle_low)
    mixed_grad = contract_cols(middle_low, w_out).astype(jnp.bfloat16)
    keys_back, values_back, segments_back, variates_back = (
        lax.all_gather(key_low, "seq", axis=0, tiled=True),
        lax.all_gather(value_low, "seq", axis=0, tiled=True),
        lax.all_gather(key_segment, "seq", axis=0, tiled=True),
        lax.all_gather(key_variate, "seq", axis=0, tiled=True),
    )
    allowed_back, same_back = make_tables(segment, variate, segments_back, variates_back, first_row)

    def query_side(block_index):
        scores, query_block, key_block = block_scores(
            block_index,
            query_low,
            keys_back,
            same_back,
            same_bias,
            cross_bias,
            head_group,
            head_width,
        )
        lse_block = lax.dynamic_slice_in_dim(summary, block_index * head_group, head_group, 0)
        probabilities = jnp.exp(
            jnp.where(allowed_back[None], scores - lse_block[:, :, None], -jnp.inf)
        )
        grad_block = lax.dynamic_slice_in_dim(
            mixed_grad, block_index * block_width, block_width, 1
        ).reshape(row_count, head_group, head_width)
        value_block = lax.dynamic_slice_in_dim(
            values_back, block_index * block_width, block_width, 1
        ).reshape(length, head_group, head_width)
        prob_grad = jnp.einsum(
            "thd,shd->hts", grad_block, value_block, preferred_element_type=jnp.float32
        )
        inner_sum = jnp.sum(probabilities * prob_grad, axis=-1, keepdims=True)
        score_low = (probabilities * (prob_grad - inner_sum)).astype(jnp.bfloat16)
        score_wide = score_low.astype(jnp.float32)
        same_part = jnp.sum(jnp.where(same_back[None], score_wide, 0.0), axis=(1, 2))
        cross_part = jnp.sum(jnp.where(same_back[None], 0.0, score_wide), axis=(1, 2))
        query_part = (
            jnp.einsum(
                "hts,shd->thd", score_low, key_block, preferred_element_type=jnp.float32
            ).reshape(row_count, block_width)
            * scaling
        )
        return (
            probabilities,
            score_low,
            query_block,
            grad_block,
            inner_sum[..., 0],
            same_part,
            cross_part,
            query_part,
        )

    def backward_block(block_index, state_now):
        query_grad, key_grad, value_grad, same_grad, cross_grad = state_now
        (
            probabilities,
            score_low,
            query_block,
            grad_block,
            inner_sum,
            same_part,
            cross_part,
            query_part,
        ) = query_side(block_index)
        key_part = (
            jnp.einsum(
                "hts,thd->shd", score_low, query_block, preferred_element_type=jnp.float32
            ).reshape(length, block_width)
            * scaling
        )
        value_part = jnp.einsum(
            "hts,thd->shd",
            probabilities.astype(jnp.bfloat16),
            grad_block,
            preferred_element_type=jnp.float32,
        ).reshape(length, block_width)
        query_grad = lax.dynamic_update_slice_in_dim(
            query_grad, query_part, block_index * block_width, 1
        )
        key_grad = lax.dynamic_update_slice_in_dim(key_grad, key_part, block_index * block_width, 1)
        value_grad = lax.dynamic_update_slice_in_dim(
            value_grad, value_part, block_index * block_width, 1
        )
        same_grad = lax.dynamic_update_slice_in_dim(
            same_grad, same_part, block_index * head_group, 0
        )
        cross_grad = lax.dynamic_update_slice_in_dim(
            cross_grad, cross_part, block_index * head_group, 0
        )
        return (query_grad, key_grad, value_grad, same_grad, cross_grad)

    start_state = (
        jnp.zeros((row_count, model_width), jnp.float32),
        jnp.zeros((length, model_width), jnp.float32),
        jnp.zeros((length, model_width), jnp.float32),
        jnp.zeros((head_count,), jnp.float32),
        jnp.zeros((head_count,), jnp.float32),
    )
    query_grad, key_grad, value_grad, same_grad, cross_grad = lax.fori_loop(
        0, block_total, backward_block, start_state
    )
    key_share, value_share = (
        lax.psum_scatter(
            key_grad.astype(jnp.bfloat16), "seq", scatter_dimension=0, tiled=True
        ).astype(jnp.float32),
        lax.psum_scatter(
            value_grad.astype(jnp.bfloat16), "seq", scatter_dimension=0, tiled=True
        ).astype(jnp.float32),
    )
    query_pre_grad = rotate(query_grad, -angles, head_count).astype(jnp.bfloat16)
    key_pre_grad = rotate(key_share, -angles, head_count).astype(jnp.bfloat16)
    value_pre_grad = value_share.astype(jnp.bfloat16)
    query_w_grad = contract_rows(first_low, query_pre_grad)
    key_w_grad = contract_rows(first_low, key_pre_grad)
    value_w_grad = contract_rows(first_low, value_pre_grad)
    first_grad = (
        contract_cols(query_pre_grad, w_query)
        + contract_cols(key_pre_grad, w_key)
        + contract_cols(value_pre_grad, w_value)
    )
    input_part, attn_gain_grad = norm_back(first_grad, normed_one, factor_one, gain_one)
    input_grad = (middle_grad + input_part).astype(jnp.bfloat16)
    col_shares = (
        lax.psum_scatter(
            query_w_grad.astype(jnp.bfloat16), "dp", scatter_dimension=1, tiled=True
        ).astype(jnp.float32),
        lax.psum_scatter(
            key_w_grad.astype(jnp.bfloat16), "dp", scatter_dimension=1, tiled=True
        ).astype(jnp.float32),
        lax.psum_scatter(
            value_w_grad.astype(jnp.bfloat16), "dp", scatter_dimension=1, tiled=True
        ).astype(jnp.float32),
        lax.psum_scatter(
            out_w_grad.astype(jnp.bfloat16), "dp", scatter_dimension=1, tiled=True
        ).astype(jnp.float32),
        lax.psum_scatter(
            gate_w_grad.astype(jnp.bfloat16), "dp", scatter_dimension=1, tiled=True
        ).astype(jnp.float32),
        lax.psum_scatter(
            up_w_grad.astype(jnp.bfloat16), "dp", scatter_dimension=1, tiled=True
        ).astype(jnp.float32),
        lax.psum_scatter(
            down_grad.astype(jnp.bfloat16), "dp", scatter_dimension=1, tiled=True
        ).astype(jnp.float32),
    )
    shares = (
        lax.psum_scatter(
            col_shares[0].astype(jnp.bfloat16), "seq", scatter_dimension=0, tiled=True
        ).astype(jnp.float32),
        lax.psum_scatter(
            col_shares[1].astype(jnp.bfloat16), "seq", scatter_dimension=0, tiled=True
        ).astype(jnp.float32),
        lax.psum_scatter(
            col_shares[2].astype(jnp.bfloat16), "seq", scatter_dimension=0, tiled=True
        ).astype(jnp.float32),
        lax.psum_scatter(
            col_shares[3].astype(jnp.bfloat16), "seq", scatter_dimension=0, tiled=True
        ).astype(jnp.float32),
        lax.psum_scatter(
            col_shares[4].astype(jnp.bfloat16), "seq", scatter_dimension=0, tiled=True
        ).astype(jnp.float32),
        lax.psum_scatter(
            col_shares[5].astype(jnp.bfloat16), "seq", scatter_dimension=0, tiled=True
        ).astype(jnp.float32),
        lax.psum_scatter(
            col_shares[6].astype(jnp.bfloat16), "seq", scatter_dimension=0, tiled=True
        ).astype(jnp.float32),
    )
    small_totals = lax.psum((same_grad, cross_grad, attn_gain_grad, ffn_gain_grad), ("dp", "seq"))
    return (
        result.astype(jnp.bfloat16)[None],
        input_grad[None],
        small_totals[2],
        shares[0],
        shares[1],
        shares[2],
        shares[3],
        small_totals[0],
        small_totals[1],
        small_totals[3],
        shares[4],
        shares[5],
        shares[6],
    )


MESH = pl.DeviceIdType.MESH
NEG = -1e30
low = jnp.bfloat16
wide = jnp.float32


def remote(src, dst, send_sem, recv_sem, d, s):
    return pltpu.make_async_remote_copy(
        src_ref=src,
        dst_ref=dst,
        send_sem=send_sem,
        recv_sem=recv_sem,
        device_id=(d, s),
        device_id_type=MESH,
    )


def arrived(dst, recv_sem, d, s):
    remote(dst, dst, recv_sem, recv_sem, d, s).wait_recv()


def sent(src, send_sem, d, s):
    remote(src, src, send_sem, send_sem, d, s).wait_send()


def greet(d, s):
    barrier = pltpu.get_barrier_semaphore()
    for k in range(1, 8):
        pl.semaphore_signal(barrier, inc=1, device_id=(d, lax.rem(s + k, 8)), device_id_type=MESH)
    for k in range(1, 4):
        pl.semaphore_signal(barrier, inc=1, device_id=(lax.rem(d + k, 4), s), device_id_type=MESH)
    pl.semaphore_wait(barrier, 10)


def pair_of(s):
    z = s // 2
    c = lax.rem(s, 2)
    return 2 * (2 * c + lax.rem(z, 2)) + z // 2


class Chain:
    def __init__(self, d, s, view, up_sem, recv_sem, side_sem, side_recv):
        self.d, self.s, self.z, self.c = d, s, s // 2, lax.rem(s, 2)
        self.view = view
        self.up_sem, self.recv_sem = up_sem, recv_sem
        self.side_sem, self.side_recv = side_sem, side_recv

    def block(self, z):
        return self.view(2 * z + self.c)

    def up(self, z):
        b = self.block(z)
        return remote(b, b, self.up_sem.at[self.z - z], self.recv_sem.at[z], self.d, self.s + 2)

    def down(self, z):
        b = self.block(z)
        return remote(b, b, self.up_sem.at[3 + z - self.z], self.recv_sem.at[z], self.d, self.s - 2)

    def side(self, z):
        b = self.block(z)
        return remote(b, b, self.side_sem.at[z], self.side_recv.at[z], self.d, self.s + 1 - 2 * self.c)

    def start(self):
        @pl.when(self.z < 3)
        def _():
            self.up(self.z).start()

        @pl.when(self.z > 0)
        def _():
            self.down(self.z).start()

        self.side(self.z).start()

    def step(self, k):
        lo, hi = self.z - k, self.z + k

        @pl.when(lo >= 0)
        def _():
            arrived(self.block(lo), self.recv_sem.at[lo], self.d, self.s)

            @pl.when(self.z < 3)
            def _():
                self.up(lo).start()

            self.side(lo).start()

        @pl.when(hi <= 3)
        def _():
            arrived(self.block(hi), self.recv_sem.at[hi], self.d, self.s)

            @pl.when(self.z > 0)
            def _():
                self.down(hi).start()

            self.side(hi).start()

    def wait_side(self, z):
        arrived(self.view(2 * z + 1 - self.c), self.side_recv.at[z], self.d, self.s)

    def finish(self):
        for z in range(4):
            self.wait_side(z)
        self.drain()

    def drain(self):
        own = self.block(self.z)
        for z in range(4):
            sent(own, self.side_sem.at[z], self.d, self.s)
        for k in range(3):

            @pl.when((self.z < 3) & (self.z - k >= 0))
            def _():
                sent(own, self.up_sem.at[k], self.d, self.s)

            @pl.when((self.z > 0) & (self.z + k <= 3))
            def _():
                sent(own, self.up_sem.at[3 + k], self.d, self.s)


class Plane:
    def __init__(self, d, s, whole, half, send_sem, recv_sem):
        self.d, self.s = d, s
        self.dx = d + 1 - 2 * lax.rem(d, 2)
        self.dy = lax.rem(d + 2, 4)
        self.far = 3 - d
        self.whole, self.half = whole, half
        self.send_sem, self.recv_sem = send_sem, recv_sem

    def start(self):
        w = self.whole(self.d)
        remote(w, w, self.send_sem.at[0], self.recv_sem.at[0], self.dx, self.s).start()
        remote(w, w, self.send_sem.at[1], self.recv_sem.at[1], self.dy, self.s).start()

    def step(self):
        arrived(self.whole(self.dx), self.recv_sem.at[0], self.d, self.s)
        h = self.half(self.dx, 0)
        remote(h, h, self.send_sem.at[2], self.recv_sem.at[2], self.dy, self.s).start()
        arrived(self.whole(self.dy), self.recv_sem.at[1], self.d, self.s)
        h = self.half(self.dy, 1)
        remote(h, h, self.send_sem.at[3], self.recv_sem.at[3], self.dx, self.s).start()

    def finish(self):
        arrived(self.half(self.far, 0), self.recv_sem.at[2], self.d, self.s)
        arrived(self.half(self.far, 1), self.recv_sem.at[3], self.d, self.s)
        w = self.whole(self.d)
        sent(w, self.send_sem.at[0], self.d, self.s)
        sent(w, self.send_sem.at[1], self.d, self.s)
        h = self.half(self.d, 0)
        sent(h, self.send_sem.at[2], self.d, self.s)
        h = self.half(self.d, 1)
        sent(h, self.send_sem.at[3], self.d, self.s)


def lanes(i):
    return pl.ds(pl.multiple_of(i * 128, 128), 128)


def rows(i, n=128):
    return pl.ds(pl.multiple_of(i * n, n), n)


def dot(a, b):
    return jnp.dot(a, b, preferred_element_type=wide)


def dot_nt(a, b):
    return lax.dot_general(a, b, (((1,), (1,)), ((), ())), preferred_element_type=wide)


def dot_tn(a, b):
    return lax.dot_general(a, b, (((0,), (0,)), ((), ())), preferred_element_type=wide)


def head_lanes(h):
    place = lax.broadcasted_iota(jnp.int32, (1, 128), 1)
    return (place // 64) == h


def partner(x):
    place = lax.broadcasted_iota(jnp.int32, x.shape, 1)
    return jnp.where(lax.rem(place, 64) < 32, pltpu.roll(x, 96, 1), pltpu.roll(x, 32, 1))


def front_kernel(
    tokens, gain, wq, wk, wv, wo_in, wg_in, wu_in, wd_in, bias, ids, freq, cot,
    xall, q_out, k_out, v_out, lse, wqkv, wo, wgu, wd, call, idr, idc, cosine, sine, mixed,
    qkv_src, gu_src, d_src_, head_out, keyrow,
    qs_s, qs_r, qp_s, qp_r, id_s, id_r, x_u, x_r, x_b, x_c, gu_s, gu_r, dn_s, dn_r,
    wo_u, wo_r, wo_b, wo_c, c_u, c_r, c_b, c_c, pl_s, pl_r, m_s, m_r,
):
    d = lax.axis_index("dp")
    s = lax.axis_index("seq")
    z = s // 2
    c = lax.rem(s, 2)
    dx = d + 1 - 2 * lax.rem(d, 2)
    dy = lax.rem(d + 2, 4)
    greet(d, s)

    for i in range(2):
        for n, w in enumerate((wq, wk, wv)):
            qkv_src[i, :, 128 * n : 128 * (n + 1)] = w[:, 128 * i : 128 * (i + 1)].astype(low)
    home = 2 * c + lax.rem(z, 2)
    is_home = d == home
    owner = [2 * (lax.rem(d, 2) + 2 * i) + d // 2 for i in range(2)]
    for i in range(2):

        @pl.when(owner[i] != s)
        def _():
            remote(qkv_src.at[i], wqkv.at[rows(s)], qs_s.at[i], qs_r.at[s], d, owner[i]).start()

        @pl.when(owner[i] == s)
        def _():
            wqkv[rows(s), :] = qkv_src[i]

    idr[s] = ids[...]
    for k in range(1, 8):
        t = lax.rem(s + k, 8)
        remote(ids, idr.at[s], id_s.at[k], id_r.at[s], d, t).start()

    value = tokens[...].astype(wide)
    factor = lax.rsqrt(jnp.mean(value * value, axis=-1, keepdims=True) + epsilon)
    xall[s] = (value * factor * gain[...]).astype(low)
    ring = Chain(d, s, lambda b: xall.at[b], x_u, x_r, x_b, x_c)
    ring.start()

    gu_src[0] = wg_in[...].astype(low)
    gu_src[1] = wu_in[...].astype(low)
    d_src_[...] = wd_in[...].astype(low)
    wo[s, :, pl.ds(pl.multiple_of(d * 256, 256), 256)] = wo_in[...].astype(low)
    call[s] = cot[...]

    for k in range(1, 8):
        t = lax.rem(s + k, 8)
        arrived(idr.at[t], id_r.at[t], d, s)
    for b in range(8):
        block = idr[b]
        for n in range(4):
            keyrow[n : n + 1, 128 * b : 128 * (b + 1)] = block[n : n + 1, :]
        full = jnp.concatenate([block] * 16, axis=0)
        idc[128 * b : 128 * (b + 1), :] = full.T

    ring.step(1)
    place = lax.broadcasted_iota(jnp.int32, (1, 128), 1)
    sign = jnp.where(lax.rem(place, 64) < 32, -1.0, 1.0)

    def trig(b, carry):
        angle = idc[rows(b), 3:4] * freq[...]
        cosine[rows(b), :] = jnp.cos(angle)
        sine[rows(b), :] = jnp.sin(angle) * sign
        return carry

    lax.fori_loop(0, 4, trig, 0)
    ring.step(2)
    lax.fori_loop(4, 8, trig, 0)

    half_qkv = lambda n: wqkv.at[pl.ds(512 * n, 512)]

    @pl.when(is_home)
    def _():
        for k in range(1, 8):
            t = lax.rem(s + k, 8)
            arrived(wqkv.at[rows(t)], qs_r.at[t], d, s)
        remote(wqkv, wqkv, qp_s.at[0], qp_r.at[0], dx, s).start()
        remote(wqkv, wqkv, qp_s.at[1], qp_r.at[0], dy, s).start()

    ring.step(3)

    cols_d = lanes(d)
    for k in range(1, 8):
        t = lax.rem(s + k, 8)
        remote(
            gu_src.at[:, :, lanes(t)], wgu.at[:, rows(s), cols_d], gu_s.at[k], gu_r.at[s], d, t
        ).start()
    wgu[:, rows(s), cols_d] = gu_src[:, :, lanes(s)]
    wide_d = pl.ds(pl.multiple_of(d * 256, 256), 256)
    for m in range(4):
        t = lax.rem(s, 2) * 4 + m

        @pl.when(t != s)
        def _():
            remote(
                d_src_.at[pl.ds(128 * m, 128)], wd.at[rows(s // 2), wide_d],
                dn_s.at[m], dn_r.at[s // 2], d, t,
            ).start()

        @pl.when(t == s)
        def _():
            wd[rows(s // 2), wide_d] = d_src_[pl.ds(128 * m, 128), :]

    wo_ring = Chain(d, s, lambda b: wo.at[b, :, wide_d], wo_u, wo_r, wo_b, wo_c)
    wo_ring.start()
    c_ring = Chain(d, s, lambda b: call.at[b], c_u, c_r, c_b, c_c)
    c_ring.start()

    for zz in range(4):
        ring.wait_side(zz)

    @pl.when(home == dx)
    def _():
        arrived(wqkv, qp_r.at[0], d, s)
        remote(half_qkv(0), half_qkv(0), qp_s.at[2], qp_r.at[1], dy, s).start()

    @pl.when(home == dy)
    def _():
        arrived(wqkv, qp_r.at[0], d, s)
        remote(half_qkv(1), half_qkv(1), qp_s.at[2], qp_r.at[2], dx, s).start()

    @pl.when(home == 3 - d)
    def _():
        arrived(half_qkv(0), qp_r.at[1], d, s)
        arrived(half_qkv(1), qp_r.at[2], d, s)

    def project(i, carry):
        block = xall[pl.ds(2 * i, 2)].reshape(256, 1024)
        pre = dot(block, wqkv[...])
        cs, sn = cosine[rows(i, 256), :], sine[rows(i, 256), :]
        qp, kp = pre[:, :128], pre[:, 128:256]
        q_out[rows(i, 256), :] = (qp * cs + partner(qp) * sn).astype(low)
        k_out[rows(i, 256), :] = (kp * cs + partner(kp) * sn).astype(low)
        v_out[rows(i, 256), :] = pre[:, 256:].astype(low)
        return carry

    lax.fori_loop(0, 4, project, 0)
    wo_ring.step(1)
    c_ring.step(1)

    def attend(b, carry):
        pick = rows(b)
        seg_col, var_col = idc[pick, 0:1], idc[pick, 2:3]
        q_place = b * 128 + lax.broadcasted_iota(jnp.int32, (128, 1), 0)
        k_place = lax.broadcasted_iota(jnp.int32, (1, 1024), 1)
        allowed = (seg_col == keyrow[1:2, :]) | (q_place == k_place)
        same = var_col == keyrow[2:3, :]
        q_block = q_out[pick, :]
        attended, total_lse = None, None
        for h in range(2):
            mine = head_lanes(h)
            qh = jnp.where(mine, q_block, jnp.zeros_like(q_block))
            scores = dot_nt(qh, k_out[...]) * 0.125
            scores = scores + jnp.where(same, bias[h : h + 1, 0:1], bias[h : h + 1, 1:2])
            scores = jnp.where(allowed, scores, NEG)
            top = jnp.max(scores, axis=-1, keepdims=True)
            e = jnp.exp(scores - top)
            total = jnp.sum(e, axis=-1, keepdims=True)
            part = dot((e * (1.0 / total)).astype(low), v_out[...])
            one = top + jnp.log(total)
            if h == 0:
                attended, total_lse = part, one
            else:
                attended = jnp.where(mine, part, attended)
                total_lse = jnp.where(mine, one, total_lse)
        head_out[b] = attended.astype(low)
        lse[pick, :] = jnp.broadcast_to(total_lse, (128, 128))
        return carry

    pair = pair_of(s)

    def send_mixed(t):
        @pl.when(t != s)
        def _():
            remote(head_out.at[t], mixed.at[pair], m_s.at[t], m_r.at[s], d, t).start()

        @pl.when(t == s)
        def _():
            mixed[pair] = head_out[t]

    gu_plane = Plane(
        d, s, lambda i: wgu.at[:, :, lanes(i)], lambda i, n: wgu.at[n, :, lanes(i)],
        pl_s.at[0], pl_r.at[0],
    )
    wide_of = lambda i: pl.ds(pl.multiple_of(i * 256, 256), 256)
    dn_plane = Plane(
        d, s, lambda i: wd.at[:, wide_of(i)], lambda i, n: wd.at[pl.ds(256 * n, 256), wide_of(i)],
        pl_s.at[1], pl_r.at[1],
    )
    wo_plane = Plane(
        d, s, lambda i: wo.at[:, :, wide_of(i)], lambda i, n: wo.at[pl.ds(4 * n, 4), :, wide_of(i)],
        pl_s.at[2], pl_r.at[2],
    )

    lax.fori_loop(0, 2, attend, 0)
    send_mixed(0)
    send_mixed(1)
    wo_ring.step(2)
    c_ring.step(2)
    for k in range(1, 8):
        t = lax.rem(s + k, 8)
        arrived(wgu.at[:, rows(t), cols_d], gu_r.at[t], d, s)
    gu_plane.start()
    lax.fori_loop(2, 4, attend, 0)
    send_mixed(2)
    send_mixed(3)
    wo_ring.step(3)
    c_ring.step(3)
    for j in range(4):

        @pl.when(2 * j + s // 4 != s)
        def _():
            arrived(wd.at[pl.ds(128 * j, 128), wide_d], dn_r.at[j], d, s)

    dn_plane.start()
    lax.fori_loop(4, 6, attend, 0)
    send_mixed(4)
    send_mixed(5)
    wo_ring.finish()
    wo_plane.start()
    gu_plane.step()
    lax.fori_loop(6, 8, attend, 0)
    send_mixed(6)
    send_mixed(7)
    dn_plane.step()
    wo_plane.step()
    c_ring.finish()
    gu_plane.finish()
    dn_plane.finish()
    wo_plane.finish()

    ring.drain()
    for i in range(2):

        @pl.when(owner[i] != s)
        def _():
            sent(qkv_src.at[i], qs_s.at[i], d, s)

    for k in range(1, 8):
        sent(ids, id_s.at[k], d, s)
        sent(gu_src.at[:, :, pl.ds(0, 128)], gu_s.at[k], d, s)

    @pl.when(is_home)
    def _():
        sent(wqkv, qp_s.at[0], d, s)
        sent(wqkv, qp_s.at[1], d, s)

    @pl.when((home == dx) | (home == dy))
    def _():
        sent(half_qkv(0), qp_s.at[2], d, s)

    for m in range(4):

        @pl.when(lax.rem(s, 2) * 4 + m != s)
        def _():
            sent(d_src_.at[pl.ds(128 * m, 128)], dn_s.at[m], d, s)

    for t in range(8):

        @pl.when(t != s)
        def _():
            arrived(mixed.at[pair_of(t)], m_r.at[t], d, s)
            sent(head_out.at[t], m_s.at[t], d, s)


def vmem():
    return pl.BlockSpec(memory_space=pltpu.VMEM)


def shape(*dims, kind=low):
    return jax.ShapeDtypeStruct(dims, kind)


def dma(*dims):
    return pltpu.SemaphoreType.DMA(dims)


def front(tokens, gain, wq, wk, wv, wo, wg, wu, wd, bias, ids, freq, cot):
    outs = (
        shape(8, 128, 1024),
        shape(1024, 128), shape(1024, 128), shape(1024, 128),
        shape(1024, 128, kind=wide),
        shape(1024, 384),
        shape(8, 128, 1024),
        shape(2, 1024, 512),
        shape(512, 1024),
        shape(8, 128, 1024),
        shape(8, 8, 128, kind=wide),
        shape(1024, 128, kind=wide),
        shape(1024, 128, kind=wide),
        shape(1024, 128, kind=wide),
        shape(8, 128, 128),
    )
    return pl.pallas_call(
        front_kernel,
        name="front",
        out_shape=outs,
        in_specs=[vmem()] * 13,
        out_specs=[vmem()] * len(outs),
        scratch_shapes=[
            pltpu.VMEM((2, 128, 384), low),
            pltpu.VMEM((2, 128, 1024), low),
            pltpu.VMEM((512, 256), low),
            pltpu.VMEM((8, 128, 128), low),
            pltpu.VMEM((8, 1024), wide),
            dma(2), dma(8), dma(3), dma(3), dma(8), dma(8), dma(6), dma(4), dma(4), dma(4),
            dma(8), dma(8), dma(4), dma(4),
            dma(6), dma(4), dma(4), dma(4), dma(6), dma(4), dma(4), dma(4),
            dma(3, 4), dma(3, 4), dma(8), dma(8),
        ],
        compiler_params=pltpu.CompilerParams(
            collective_id=0, has_side_effects=True, vmem_limit_bytes=60 << 20
        ),
    )(tokens, gain, wq, wk, wv, wo, wg, wu, wd, bias, ids, freq, cot)


def fast_body(
    tokens, attn_gain, query_weight, key_weight, value_weight, out_weight, same_bias, cross_bias,
    ffn_gain, gate_weight, up_weight, down_weight, segment_ids, variate_ids, time_ids, observed,
    cotangent,
):
    s = lax.axis_index("seq")
    d = lax.axis_index("dp")
    pair = pair_of(s)
    gain_one = attn_gain.astype(low).astype(wide)[None]
    gain_two = ffn_gain.astype(low).astype(wide)[None]
    both = jnp.stack([same_bias, cross_bias], axis=1)
    bias = jnp.pad(lax.dynamic_slice_in_dim(both, 2 * pair, 2, 0), ((0, 6), (0, 126)))
    segment = segment_ids[0]
    ids = jnp.stack(
        [segment, jnp.where(observed[0] == 1, segment, -1), variate_ids[0], time_ids[0]]
    ).astype(wide)
    ids = jnp.pad(ids, ((0, 4), (0, 0)))
    powers = jnp.arange(32).astype(wide) * (2.0 / 64)
    freq = jnp.tile(10000.0 ** (-powers), 4)[None]
    tok = tokens[0]
    (
        xall, q, k, v, lse, wqkv, wo, wgu, wd, call, idr, idc, cosine, sine, mixed
    ) = front(
        tok, gain_one, query_weight, key_weight, value_weight, out_weight, gate_weight, up_weight,
        down_weight, bias, ids, freq, cotangent[0],
    )
    out, mgrad_all, middle_grad, gu_grad, dn_grad, wo_grad, ffn_gain_grad = middle_stage(
        tok, mixed, wo, gain_two, wgu, wd, call
    )
    tokens_grad, qkv_grad, attn_gain_grad, same_grad, cross_grad = back_stage(
        tok, gain_one, xall, q, k, v, lse, wqkv, mgrad_all, middle_grad, bias, idr, idc, cosine, sine
    )
    return (out[None], tokens_grad[None]) + last_stage(
        pair, gu_grad, dn_grad, wo_grad, qkv_grad, attn_gain_grad, ffn_gain_grad, same_grad, cross_grad
    )


def place_of_pair():
    order = [0] * 8
    for sv in range(8):
        zz, cc = sv // 2, sv % 2
        order[2 * (2 * cc + zz % 2) + zz // 2] = sv
    return jnp.array(order)


def middle_stage(tok, mixed, wo, gain, wgu, wd, call):
    x = tok.astype(wide)
    m2 = mixed.transpose(1, 0, 2).reshape(128, 1024)
    wo2 = wo.reshape(1024, 1024)
    middle = x + dot(m2, wo2)
    normed, factor, scaled = normalize(middle, gain)
    second = lax.all_gather(scaled.astype(low), "seq", axis=0, tiled=True)
    gate_pre, up_pre = dot(second, wgu[0]), dot(second, wgu[1])
    sigma = jax.nn.sigmoid(gate_pre)
    act = gate_pre * sigma
    hidden = (act * up_pre).astype(low)
    out = middle + lax.psum_scatter(dot(hidden, wd).astype(low), "seq", scatter_dimension=0, tiled=True).astype(wide)
    cot = call.reshape(1024, 1024)
    hg = dot_nt(cot, wd)
    dn_grad = dot_tn(hidden, cot)
    gg = (hg * up_pre * sigma * (1.0 + gate_pre * (1.0 - sigma))).astype(low)
    ug = (hg * act).astype(low)
    gu_grad = jnp.stack([dot_tn(second, gg), dot_tn(second, ug)])
    sg = lax.psum_scatter((dot_nt(gg, wgu[0]) + dot_nt(ug, wgu[1])).astype(low), "seq", scatter_dimension=0, tiled=True).astype(wide)
    part, ffn_gain_grad = norm_back(sg, normed, factor, gain)
    s = lax.axis_index("seq")
    own = lax.dynamic_index_in_dim(call, s, 0, False)
    middle_grad = own.astype(wide) + part
    ml = middle_grad.astype(low)
    wo_grad = dot_tn(m2, ml)
    mg = dot_nt(ml, wo2).astype(low)
    mg_all = lax.all_gather(mg, "seq", axis=0, tiled=True)
    mg_all = lax.dynamic_slice_in_dim(mg_all, pair_of(s) * 128, 128, 1)
    return out.astype(low), mg_all, middle_grad, gu_grad.astype(low), dn_grad.astype(low), wo_grad.astype(low), ffn_gain_grad[None]


def back_stage(tok, gain, xall, q, k, v, lse, wqkv, mgrad, middle_grad, bias, idr, idc, cosine, sine):
    s = lax.axis_index("seq")
    kseg = idr[:, 1, :].reshape(1024)
    kvar = idr[:, 2, :].reshape(1024)
    allowed = (idc[:, 0:1] == kseg[None]) | (jnp.arange(1024)[:, None] == jnp.arange(1024)[None])
    same = idc[:, 2:3] == kvar[None]
    dq, dk, dv, sb, cb = [], [], [], [], []
    for h in range(2):
        cut = slice(64 * h, 64 * h + 64)
        sc = dot_nt(q[:, cut], k[:, cut]) * 0.125 + jnp.where(same, bias[h, 0], bias[h, 1])
        p = jnp.exp(jnp.where(allowed, sc - lse[:, 64 * h : 64 * h + 1], -jnp.inf))
        pg = dot_nt(mgrad[:, cut], v[:, cut])
        inner = jnp.sum(p * pg, axis=-1, keepdims=True)
        ds = (p * (pg - inner)).astype(low)
        sb.append(jnp.sum(jnp.where(same, ds.astype(wide), 0.0)))
        cb.append(jnp.sum(jnp.where(same, 0.0, ds.astype(wide))))
        dq.append(dot(ds, k[:, cut]) * 0.125)
        dk.append(dot_tn(ds, q[:, cut]) * 0.125)
        dv.append(dot_tn(p.astype(low), mgrad[:, cut]))
    dq, dk, dv = (jnp.concatenate(t, axis=1) for t in (dq, dk, dv))

    def back(x):
        place = jnp.arange(128) % 64 < 32
        other = jnp.where(place[None], jnp.roll(x, -32, 1), jnp.roll(x, 32, 1))
        return x * cosine - other * sine

    grads = jnp.concatenate([back(dq), back(dk), dv], axis=1).astype(low)
    xf = xall.reshape(1024, 1024)
    qkv_grad = dot_tn(xf, grads)
    fg = lax.psum_scatter(dot_nt(grads, wqkv).astype(low), "seq", scatter_dimension=0, tiled=True).astype(wide)
    normed, factor, _ = normalize(tok.astype(wide), gain)
    part, ag = norm_back(fg, normed, factor, gain)
    return (middle_grad + part).astype(low), qkv_grad.astype(low), ag[None], jnp.stack(sb), jnp.stack(cb)


def last_stage(pair, gu_grad, dn_grad, wo_grad, qkv_grad, ag, fg, sb, cb):
    s, d = lax.axis_index("seq"), lax.axis_index("dp")
    order = place_of_pair()
    g = lax.psum(gu_grad.astype(wide), "dp")
    g = lax.all_gather(g, "seq")
    g = lax.dynamic_slice(g, (0, 0, s * 128, d * 128), (8, 2, 128, 128)).transpose(1, 2, 0, 3).reshape(2, 128, 1024)
    dn = lax.all_gather(lax.psum(dn_grad.astype(wide), "dp"), "seq")
    dn = dn.reshape(8, 4, 128, 1024).transpose(1, 0, 2, 3).reshape(4096, 1024)
    dn = lax.dynamic_slice(dn, (s * 512, d * 256), (512, 256))
    w = lax.psum(wo_grad.astype(wide), ("dp", "seq"))
    w = lax.dynamic_slice(w, (s * 128, d * 256), (128, 256))
    qg = lax.all_gather(lax.psum(qkv_grad.astype(wide), "dp"), "seq")[order]
    qg = qg.reshape(8, 1024, 3, 128).transpose(2, 1, 0, 3).reshape(3, 1024, 1024)
    qg = lax.dynamic_slice(qg, (0, s * 128, d * 256), (3, 128, 256))
    ag, fg = lax.psum((ag[0], fg[0]), ("dp", "seq"))
    zero = jnp.zeros((16,), wide)
    sb = lax.psum(lax.dynamic_update_slice(zero, sb, (2 * pair,)), ("dp", "seq"))
    cb = lax.psum(lax.dynamic_update_slice(zero, cb, (2 * pair,)), ("dp", "seq"))
    return (ag, qg[0], qg[1], qg[2], w, sb, cb, fg, g[0], g[1], dn)


def fits(mesh):
    return mesh.shape["dp"] == 4 and mesh.shape["seq"] == 8


def solution(mesh):
    in_specs = (
        P("dp", "seq", None),
        P(),
        P("seq", "dp"),
        P("seq", "dp"),
        P("seq", "dp"),
        P("seq", "dp"),
        P(),
        P(),
        P(),
        P("seq", "dp"),
        P("seq", "dp"),
        P("seq", "dp"),
        P("dp", "seq"),
        P("dp", "seq"),
        P("dp", "seq"),
        P("dp", "seq"),
        P("dp", "seq", None),
    )
    out_specs = (
        P("dp", "seq", None),
        P("dp", "seq", None),
        P(),
        P("seq", "dp"),
        P("seq", "dp"),
        P("seq", "dp"),
        P("seq", "dp"),
        P(),
        P(),
        P(),
        P("seq", "dp"),
        P("seq", "dp"),
        P("seq", "dp"),
    )
    part = fast_body if fits(mesh) else body
    return jax.shard_map(part, mesh=mesh, in_specs=in_specs, out_specs=out_specs, check_vma=False)
```

```python
import jax
import jax.numpy as jnp
from jax import lax
from jax.experimental import pallas as pl
from jax.experimental.pallas import tpu as pltpu
from jax.sharding import PartitionSpec as P

epsilon = 1e-06


def product(left_side, right_side):
    return jnp.dot(left_side, right_side, preferred_element_type=jnp.float32)


def contract_rows(left_side, right_side):
    return lax.dot_general(
        left_side, right_side, (((0,), (0,)), ((), ())), preferred_element_type=jnp.float32
    )


def contract_cols(left_side, right_side):
    return lax.dot_general(
        left_side, right_side, (((1,), (1,)), ((), ())), preferred_element_type=jnp.float32
    )


def angles_of(moments, head_width):
    half_width = head_width // 2
    powers = jnp.arange(half_width).astype(jnp.float32) * (2.0 / head_width)
    return moments.astype(jnp.float32)[:, None] * (10000.0 ** (-powers))[None, :]


def rotate(values, angles, head_count):
    row_count, model_width = values.shape
    shaped = values.reshape(row_count, head_count, model_width // head_count)
    half_width = model_width // head_count // 2
    first_half = shaped[..., :half_width]
    second = shaped[..., half_width:]
    cosine = jnp.cos(angles)[:, None, :]
    sine_part = jnp.sin(angles)[:, None, :]
    turned = jnp.concatenate(
        [first_half * cosine - second * sine_part, second * cosine + first_half * sine_part],
        axis=-1,
    )
    return turned.reshape(row_count, model_width)


def normalize(values, gain_row):
    factor = lax.rsqrt(jnp.mean(values * values, axis=-1, keepdims=True) + epsilon)
    normed = values * factor
    return (normed, factor, normed * gain_row)


def norm_back(incoming, normed, factor, gain_row):
    scaled = incoming * gain_row
    inner_sum = jnp.mean(scaled * normed, axis=-1, keepdims=True)
    return (factor * (scaled - normed * inner_sum), jnp.sum(incoming * normed, axis=0))


def make_tables(segment, variate, key_segment, key_variate, first_row):
    query_place = first_row + jnp.arange(segment.shape[0])
    key_place = jnp.arange(key_segment.shape[0])
    allowed = (segment.astype(jnp.float32)[:, None] == key_segment.astype(jnp.float32)[None, :]) | (
        query_place[:, None] == key_place[None, :]
    )
    same_kind = variate.astype(jnp.float32)[:, None] == key_variate.astype(jnp.float32)[None, :]
    return (allowed, same_kind)


def block_scores(
    block_index, query_low, keys_all, same_kind, same_bias, cross_bias, head_group, head_width
):
    block_width = head_group * head_width
    query_block = lax.dynamic_slice_in_dim(
        query_low, block_index * block_width, block_width, 1
    ).reshape(query_low.shape[0], head_group, head_width)
    key_block = lax.dynamic_slice_in_dim(
        keys_all, block_index * block_width, block_width, 1
    ).reshape(keys_all.shape[0], head_group, head_width)
    raw_scores = jnp.einsum(
        "thd,shd->hts", query_block, key_block, preferred_element_type=jnp.float32
    )
    same_part = lax.dynamic_slice_in_dim(same_bias, block_index * head_group, head_group)
    cross_part = lax.dynamic_slice_in_dim(cross_bias, block_index * head_group, head_group)
    offset = jnp.where(same_kind[None], same_part[:, None, None], cross_part[:, None, None])
    return (raw_scores * head_width ** (-0.5) + offset, query_block, key_block)


def body(
    tokens,
    attn_gain,
    query_weight,
    key_weight,
    value_weight,
    out_weight,
    same_bias,
    cross_bias,
    ffn_gain,
    gate_weight,
    up_weight,
    down_weight,
    segment_ids,
    variate_ids,
    time_ids,
    observed,
    cotangent,
):
    row_count = tokens.shape[1]
    model_width = tokens.shape[2]
    head_count = same_bias.shape[0]
    head_width = model_width // head_count
    head_group = max(1, 128 // head_width)
    block_width = head_group * head_width
    block_total = head_count // head_group
    scaling = head_width ** (-0.5)
    first_row = lax.axis_index("seq") * row_count
    gain_one = attn_gain.astype(jnp.bfloat16).astype(jnp.float32)
    gain_two = ffn_gain.astype(jnp.bfloat16).astype(jnp.float32)
    low_masters = (
        query_weight.astype(jnp.bfloat16),
        key_weight.astype(jnp.bfloat16),
        value_weight.astype(jnp.bfloat16),
        out_weight.astype(jnp.bfloat16),
        gate_weight.astype(jnp.bfloat16),
        up_weight.astype(jnp.bfloat16),
        down_weight.astype(jnp.bfloat16),
    )
    row_parts = (
        lax.all_gather(low_masters[0], "seq", axis=0, tiled=True),
        lax.all_gather(low_masters[1], "seq", axis=0, tiled=True),
        lax.all_gather(low_masters[2], "seq", axis=0, tiled=True),
        lax.all_gather(low_masters[3], "seq", axis=0, tiled=True),
        lax.all_gather(low_masters[4], "seq", axis=0, tiled=True),
        lax.all_gather(low_masters[5], "seq", axis=0, tiled=True),
        lax.all_gather(low_masters[6], "seq", axis=0, tiled=True),
    )
    gathered = (
        lax.all_gather(row_parts[0], "dp", axis=1, tiled=True),
        lax.all_gather(row_parts[1], "dp", axis=1, tiled=True),
        lax.all_gather(row_parts[2], "dp", axis=1, tiled=True),
        lax.all_gather(row_parts[3], "dp", axis=1, tiled=True),
        lax.all_gather(row_parts[4], "dp", axis=1, tiled=True),
        lax.all_gather(row_parts[5], "dp", axis=1, tiled=True),
        lax.all_gather(row_parts[6], "dp", axis=1, tiled=True),
    )
    w_query, w_key, w_value, w_out, w_gate, w_up, w_down = gathered
    inputs = tokens[0].astype(jnp.float32)
    segment = segment_ids[0]
    variate = variate_ids[0]
    seen_row = observed[0]
    angles = angles_of(time_ids[0], head_width)
    normed_one, factor_one, scaled_one = normalize(inputs, gain_one)
    first_low = scaled_one.astype(jnp.bfloat16)
    query_low = rotate(product(first_low, w_query), angles, head_count).astype(jnp.bfloat16)
    key_low = rotate(product(first_low, w_key), angles, head_count).astype(jnp.bfloat16)
    value_low = product(first_low, w_value).astype(jnp.bfloat16)
    key_segment = jnp.where(seen_row == 1, segment, -1).astype(jnp.bfloat16)
    key_variate = variate.astype(jnp.bfloat16)
    keys_all, values_all, segments_all, variates_all = (
        lax.all_gather(key_low, "seq", axis=0, tiled=True),
        lax.all_gather(value_low, "seq", axis=0, tiled=True),
        lax.all_gather(key_segment, "seq", axis=0, tiled=True),
        lax.all_gather(key_variate, "seq", axis=0, tiled=True),
    )
    length = keys_all.shape[0]
    allowed, same_kind = make_tables(segment, variate, segments_all, variates_all, first_row)

    def forward_block(block_index, state_now):
        mixed, summary = state_now
        scores, query_block, key_block = block_scores(
            block_index,
            query_low,
            keys_all,
            same_kind,
            same_bias,
            cross_bias,
            head_group,
            head_width,
        )
        row_top = jnp.max(jnp.where(allowed[None], scores, -jnp.inf), axis=-1, keepdims=True)
        exponent = jnp.exp(jnp.where(allowed[None], scores - row_top, -jnp.inf))
        row_total = jnp.sum(exponent, axis=-1, keepdims=True)
        prob_low = (exponent / row_total).astype(jnp.bfloat16)
        value_block = lax.dynamic_slice_in_dim(
            values_all, block_index * block_width, block_width, 1
        ).reshape(length, head_group, head_width)
        attended = jnp.einsum(
            "hts,shd->thd", prob_low, value_block, preferred_element_type=jnp.float32
        ).reshape(row_count, block_width)
        mixed = lax.dynamic_update_slice_in_dim(mixed, attended, block_index * block_width, 1)
        summary = lax.dynamic_update_slice_in_dim(
            summary, (row_top + jnp.log(row_total))[..., 0], block_index * head_group, 0
        )
        return (mixed, summary)

    mixed, summary = lax.fori_loop(
        0,
        block_total,
        forward_block,
        (
            jnp.zeros((row_count, model_width), jnp.float32),
            jnp.zeros((head_count, row_count), jnp.float32),
        ),
    )
    mixed_low = mixed.astype(jnp.bfloat16)
    middle = inputs + product(mixed_low, w_out)
    normed_two, factor_two, scaled_two = normalize(middle, gain_two)
    second_low = scaled_two.astype(jnp.bfloat16)
    gate_pre = product(second_low, w_gate)
    up_pre = product(second_low, w_up)
    sigma = jax.nn.sigmoid(gate_pre)
    activated = gate_pre * sigma
    hidden_low = (activated * up_pre).astype(jnp.bfloat16)
    result = middle + product(hidden_low, w_down)
    rows_again = (
        lax.all_gather(low_masters[0], "seq", axis=0, tiled=True),
        lax.all_gather(low_masters[1], "seq", axis=0, tiled=True),
        lax.all_gather(low_masters[2], "seq", axis=0, tiled=True),
        lax.all_gather(low_masters[3], "seq", axis=0, tiled=True),
        lax.all_gather(low_masters[4], "seq", axis=0, tiled=True),
        lax.all_gather(low_masters[5], "seq", axis=0, tiled=True),
        lax.all_gather(low_masters[6], "seq", axis=0, tiled=True),
    )
    regathered = (
        lax.all_gather(rows_again[0], "dp", axis=1, tiled=True),
        lax.all_gather(rows_again[1], "dp", axis=1, tiled=True),
        lax.all_gather(rows_again[2], "dp", axis=1, tiled=True),
        lax.all_gather(rows_again[3], "dp", axis=1, tiled=True),
        lax.all_gather(rows_again[4], "dp", axis=1, tiled=True),
        lax.all_gather(rows_again[5], "dp", axis=1, tiled=True),
        lax.all_gather(rows_again[6], "dp", axis=1, tiled=True),
    )
    w_query, w_key, w_value, w_out, w_gate, w_up, w_down = regathered
    cot_low = cotangent[0]
    hidden_grad = contract_cols(cot_low, w_down)
    down_grad = contract_rows(hidden_low, cot_low)
    gate_grad = (hidden_grad * up_pre * sigma * (1.0 + gate_pre * (1.0 - sigma))).astype(
        jnp.bfloat16
    )
    up_grad = (hidden_grad * activated).astype(jnp.bfloat16)
    gate_w_grad = contract_rows(second_low, gate_grad)
    up_w_grad = contract_rows(second_low, up_grad)
    second_grad = contract_cols(gate_grad, w_gate) + contract_cols(up_grad, w_up)
    middle_part, ffn_gain_grad = norm_back(second_grad, normed_two, factor_two, gain_two)
    middle_grad = cot_low.astype(jnp.float32) + middle_part
    middle_low = middle_grad.astype(jnp.bfloat16)
    out_w_grad = contract_rows(mixed_low, middle_low)
    mixed_grad = contract_cols(middle_low, w_out).astype(jnp.bfloat16)
    keys_back, values_back, segments_back, variates_back = (
        lax.all_gather(key_low, "seq", axis=0, tiled=True),
        lax.all_gather(value_low, "seq", axis=0, tiled=True),
        lax.all_gather(key_segment, "seq", axis=0, tiled=True),
        lax.all_gather(key_variate, "seq", axis=0, tiled=True),
    )
    allowed_back, same_back = make_tables(segment, variate, segments_back, variates_back, first_row)

    def query_side(block_index):
        scores, query_block, key_block = block_scores(
            block_index,
            query_low,
            keys_back,
            same_back,
            same_bias,
            cross_bias,
            head_group,
            head_width,
        )
        lse_block = lax.dynamic_slice_in_dim(summary, block_index * head_group, head_group, 0)
        probabilities = jnp.exp(
            jnp.where(allowed_back[None], scores - lse_block[:, :, None], -jnp.inf)
        )
        grad_block = lax.dynamic_slice_in_dim(
            mixed_grad, block_index * block_width, block_width, 1
        ).reshape(row_count, head_group, head_width)
        value_block = lax.dynamic_slice_in_dim(
            values_back, block_index * block_width, block_width, 1
        ).reshape(length, head_group, head_width)
        prob_grad = jnp.einsum(
            "thd,shd->hts", grad_block, value_block, preferred_element_type=jnp.float32
        )
        inner_sum = jnp.sum(probabilities * prob_grad, axis=-1, keepdims=True)
        score_low = (probabilities * (prob_grad - inner_sum)).astype(jnp.bfloat16)
        score_wide = score_low.astype(jnp.float32)
        same_part = jnp.sum(jnp.where(same_back[None], score_wide, 0.0), axis=(1, 2))
        cross_part = jnp.sum(jnp.where(same_back[None], 0.0, score_wide), axis=(1, 2))
        query_part = (
            jnp.einsum(
                "hts,shd->thd", score_low, key_block, preferred_element_type=jnp.float32
            ).reshape(row_count, block_width)
            * scaling
        )
        return (
            probabilities,
            score_low,
            query_block,
            grad_block,
            inner_sum[..., 0],
            same_part,
            cross_part,
            query_part,
        )

    def backward_block(block_index, state_now):
        query_grad, key_grad, value_grad, same_grad, cross_grad = state_now
        (
            probabilities,
            score_low,
            query_block,
            grad_block,
            inner_sum,
            same_part,
            cross_part,
            query_part,
        ) = query_side(block_index)
        key_part = (
            jnp.einsum(
                "hts,thd->shd", score_low, query_block, preferred_element_type=jnp.float32
            ).reshape(length, block_width)
            * scaling
        )
        value_part = jnp.einsum(
            "hts,thd->shd",
            probabilities.astype(jnp.bfloat16),
            grad_block,
            preferred_element_type=jnp.float32,
        ).reshape(length, block_width)
        query_grad = lax.dynamic_update_slice_in_dim(
            query_grad, query_part, block_index * block_width, 1
        )
        key_grad = lax.dynamic_update_slice_in_dim(key_grad, key_part, block_index * block_width, 1)
        value_grad = lax.dynamic_update_slice_in_dim(
            value_grad, value_part, block_index * block_width, 1
        )
        same_grad = lax.dynamic_update_slice_in_dim(
            same_grad, same_part, block_index * head_group, 0
        )
        cross_grad = lax.dynamic_update_slice_in_dim(
            cross_grad, cross_part, block_index * head_group, 0
        )
        return (query_grad, key_grad, value_grad, same_grad, cross_grad)

    start_state = (
        jnp.zeros((row_count, model_width), jnp.float32),
        jnp.zeros((length, model_width), jnp.float32),
        jnp.zeros((length, model_width), jnp.float32),
        jnp.zeros((head_count,), jnp.float32),
        jnp.zeros((head_count,), jnp.float32),
    )
    query_grad, key_grad, value_grad, same_grad, cross_grad = lax.fori_loop(
        0, block_total, backward_block, start_state
    )
    key_share, value_share = (
        lax.psum_scatter(
            key_grad.astype(jnp.bfloat16), "seq", scatter_dimension=0, tiled=True
        ).astype(jnp.float32),
        lax.psum_scatter(
            value_grad.astype(jnp.bfloat16), "seq", scatter_dimension=0, tiled=True
        ).astype(jnp.float32),
    )
    query_pre_grad = rotate(query_grad, -angles, head_count).astype(jnp.bfloat16)
    key_pre_grad = rotate(key_share, -angles, head_count).astype(jnp.bfloat16)
    value_pre_grad = value_share.astype(jnp.bfloat16)
    query_w_grad = contract_rows(first_low, query_pre_grad)
    key_w_grad = contract_rows(first_low, key_pre_grad)
    value_w_grad = contract_rows(first_low, value_pre_grad)
    first_grad = (
        contract_cols(query_pre_grad, w_query)
        + contract_cols(key_pre_grad, w_key)
        + contract_cols(value_pre_grad, w_value)
    )
    input_part, attn_gain_grad = norm_back(first_grad, normed_one, factor_one, gain_one)
    input_grad = (middle_grad + input_part).astype(jnp.bfloat16)
    col_shares = (
        lax.psum_scatter(
            query_w_grad.astype(jnp.bfloat16), "dp", scatter_dimension=1, tiled=True
        ).astype(jnp.float32),
        lax.psum_scatter(
            key_w_grad.astype(jnp.bfloat16), "dp", scatter_dimension=1, tiled=True
        ).astype(jnp.float32),
        lax.psum_scatter(
            value_w_grad.astype(jnp.bfloat16), "dp", scatter_dimension=1, tiled=True
        ).astype(jnp.float32),
        lax.psum_scatter(
            out_w_grad.astype(jnp.bfloat16), "dp", scatter_dimension=1, tiled=True
        ).astype(jnp.float32),
        lax.psum_scatter(
            gate_w_grad.astype(jnp.bfloat16), "dp", scatter_dimension=1, tiled=True
        ).astype(jnp.float32),
        lax.psum_scatter(
            up_w_grad.astype(jnp.bfloat16), "dp", scatter_dimension=1, tiled=True
        ).astype(jnp.float32),
        lax.psum_scatter(
            down_grad.astype(jnp.bfloat16), "dp", scatter_dimension=1, tiled=True
        ).astype(jnp.float32),
    )
    shares = (
        lax.psum_scatter(
            col_shares[0].astype(jnp.bfloat16), "seq", scatter_dimension=0, tiled=True
        ).astype(jnp.float32),
        lax.psum_scatter(
            col_shares[1].astype(jnp.bfloat16), "seq", scatter_dimension=0, tiled=True
        ).astype(jnp.float32),
        lax.psum_scatter(
            col_shares[2].astype(jnp.bfloat16), "seq", scatter_dimension=0, tiled=True
        ).astype(jnp.float32),
        lax.psum_scatter(
            col_shares[3].astype(jnp.bfloat16), "seq", scatter_dimension=0, tiled=True
        ).astype(jnp.float32),
        lax.psum_scatter(
            col_shares[4].astype(jnp.bfloat16), "seq", scatter_dimension=0, tiled=True
        ).astype(jnp.float32),
        lax.psum_scatter(
            col_shares[5].astype(jnp.bfloat16), "seq", scatter_dimension=0, tiled=True
        ).astype(jnp.float32),
        lax.psum_scatter(
            col_shares[6].astype(jnp.bfloat16), "seq", scatter_dimension=0, tiled=True
        ).astype(jnp.float32),
    )
    small_totals = lax.psum((same_grad, cross_grad, attn_gain_grad, ffn_gain_grad), ("dp", "seq"))
    return (
        result.astype(jnp.bfloat16)[None],
        input_grad[None],
        small_totals[2],
        shares[0],
        shares[1],
        shares[2],
        shares[3],
        small_totals[0],
        small_totals[1],
        small_totals[3],
        shares[4],
        shares[5],
        shares[6],
    )


MESH = pl.DeviceIdType.MESH
NEG = -1e30
low = jnp.bfloat16
wide = jnp.float32


def remote(src, dst, send_sem, recv_sem, d, s):
    return pltpu.make_async_remote_copy(
        src_ref=src,
        dst_ref=dst,
        send_sem=send_sem,
        recv_sem=recv_sem,
        device_id=(d, s),
        device_id_type=MESH,
    )


def arrived(dst, recv_sem, d, s):
    remote(dst, dst, recv_sem, recv_sem, d, s).wait_recv()


def sent(src, send_sem, d, s):
    remote(src, src, send_sem, send_sem, d, s).wait_send()


def greet(d, s):
    barrier = pltpu.get_barrier_semaphore()
    for k in range(1, 8):
        pl.semaphore_signal(barrier, inc=1, device_id=(d, lax.rem(s + k, 8)), device_id_type=MESH)
    for k in range(1, 4):
        pl.semaphore_signal(barrier, inc=1, device_id=(lax.rem(d + k, 4), s), device_id_type=MESH)
    pl.semaphore_wait(barrier, 10)


def pair_of(s):
    z = s // 2
    c = lax.rem(s, 2)
    return 2 * (2 * c + lax.rem(z, 2)) + z // 2


class Chain:
    def __init__(self, d, s, view, up_sem, recv_sem, side_sem, side_recv):
        self.d, self.s, self.z, self.c = d, s, s // 2, lax.rem(s, 2)
        self.view = view
        self.up_sem, self.recv_sem = up_sem, recv_sem
        self.side_sem, self.side_recv = side_sem, side_recv

    def block(self, z):
        return self.view(2 * z + self.c)

    def up(self, z):
        b = self.block(z)
        return remote(b, b, self.up_sem.at[self.z - z], self.recv_sem.at[z], self.d, self.s + 2)

    def down(self, z):
        b = self.block(z)
        return remote(b, b, self.up_sem.at[3 + z - self.z], self.recv_sem.at[z], self.d, self.s - 2)

    def side(self, z):
        b = self.block(z)
        return remote(b, b, self.side_sem.at[z], self.side_recv.at[z], self.d, self.s + 1 - 2 * self.c)

    def start(self):
        @pl.when(self.z < 3)
        def _():
            self.up(self.z).start()

        @pl.when(self.z > 0)
        def _():
            self.down(self.z).start()

        self.side(self.z).start()

    def step(self, k):
        lo, hi = self.z - k, self.z + k

        @pl.when(lo >= 0)
        def _():
            arrived(self.block(lo), self.recv_sem.at[lo], self.d, self.s)

            @pl.when(self.z < 3)
            def _():
                self.up(lo).start()

            self.side(lo).start()

        @pl.when(hi <= 3)
        def _():
            arrived(self.block(hi), self.recv_sem.at[hi], self.d, self.s)

            @pl.when(self.z > 0)
            def _():
                self.down(hi).start()

            self.side(hi).start()

    def wait_side(self, z):
        arrived(self.view(2 * z + 1 - self.c), self.side_recv.at[z], self.d, self.s)

    def finish(self):
        for z in range(4):
            self.wait_side(z)
        self.drain()

    def drain(self):
        own = self.block(self.z)
        for z in range(4):
            sent(own, self.side_sem.at[z], self.d, self.s)
        for k in range(3):

            @pl.when((self.z < 3) & (self.z - k >= 0))
            def _():
                sent(own, self.up_sem.at[k], self.d, self.s)

            @pl.when((self.z > 0) & (self.z + k <= 3))
            def _():
                sent(own, self.up_sem.at[3 + k], self.d, self.s)


class Plane:
    def __init__(self, d, s, whole, half, send_sem, recv_sem):
        self.d, self.s = d, s
        self.dx = d + 1 - 2 * lax.rem(d, 2)
        self.dy = lax.rem(d + 2, 4)
        self.far = 3 - d
        self.whole, self.half = whole, half
        self.send_sem, self.recv_sem = send_sem, recv_sem

    def start(self):
        w = self.whole(self.d)
        remote(w, w, self.send_sem.at[0], self.recv_sem.at[0], self.dx, self.s).start()
        remote(w, w, self.send_sem.at[1], self.recv_sem.at[1], self.dy, self.s).start()

    def step(self):
        arrived(self.whole(self.dx), self.recv_sem.at[0], self.d, self.s)
        h = self.half(self.dx, 0)
        remote(h, h, self.send_sem.at[2], self.recv_sem.at[2], self.dy, self.s).start()
        arrived(self.whole(self.dy), self.recv_sem.at[1], self.d, self.s)
        h = self.half(self.dy, 1)
        remote(h, h, self.send_sem.at[3], self.recv_sem.at[3], self.dx, self.s).start()

    def finish(self):
        arrived(self.half(self.far, 0), self.recv_sem.at[2], self.d, self.s)
        arrived(self.half(self.far, 1), self.recv_sem.at[3], self.d, self.s)
        w = self.whole(self.d)
        sent(w, self.send_sem.at[0], self.d, self.s)
        sent(w, self.send_sem.at[1], self.d, self.s)
        h = self.half(self.d, 0)
        sent(h, self.send_sem.at[2], self.d, self.s)
        h = self.half(self.d, 1)
        sent(h, self.send_sem.at[3], self.d, self.s)


def lanes(i):
    return pl.ds(pl.multiple_of(i * 128, 128), 128)


def rows(i, n=128):
    return pl.ds(pl.multiple_of(i * n, n), n)


def dot(a, b):
    return jnp.dot(a, b, preferred_element_type=wide)


def dot_nt(a, b):
    return lax.dot_general(a, b, (((1,), (1,)), ((), ())), preferred_element_type=wide)


def dot_tn(a, b):
    return lax.dot_general(a, b, (((0,), (0,)), ((), ())), preferred_element_type=wide)


def head_lanes(h):
    place = lax.broadcasted_iota(jnp.int32, (1, 128), 1)
    return (place // 64) == h


def partner(x):
    place = lax.broadcasted_iota(jnp.int32, x.shape, 1)
    return jnp.where(lax.rem(place, 64) < 32, pltpu.roll(x, 96, 1), pltpu.roll(x, 32, 1))


def front_kernel(
    tokens, gain, wq, wk, wv, wo_in, wg_in, wu_in, wd_in, bias, ids, freq, cot,
    xall, q_out, k_out, v_out, lse, wqkv, wo, wgu, wd, call, idr, idc, cosine, sine, mixed,
    qkv_src, gu_src, d_src_, head_out, keyrow,
    qs_s, qs_r, qp_s, qp_r, id_s, id_r, x_u, x_r, x_b, x_c, gu_s, gu_r, dn_s, dn_r,
    wo_u, wo_r, wo_b, wo_c, c_u, c_r, c_b, c_c, pl_s, pl_r, m_s, m_r,
):
    d = lax.axis_index("dp")
    s = lax.axis_index("seq")
    z = s // 2
    c = lax.rem(s, 2)
    dx = d + 1 - 2 * lax.rem(d, 2)
    dy = lax.rem(d + 2, 4)
    greet(d, s)

    for i in range(2):
        for n, w in enumerate((wq, wk, wv)):
            qkv_src[i, :, 128 * n : 128 * (n + 1)] = w[:, 128 * i : 128 * (i + 1)].astype(low)
    home = 2 * c + lax.rem(z, 2)
    is_home = d == home
    owner = [2 * (lax.rem(d, 2) + 2 * i) + d // 2 for i in range(2)]
    for i in range(2):

        @pl.when(owner[i] != s)
        def _():
            remote(qkv_src.at[i], wqkv.at[rows(s)], qs_s.at[i], qs_r.at[s], d, owner[i]).start()

        @pl.when(owner[i] == s)
        def _():
            wqkv[rows(s), :] = qkv_src[i]

    idr[s] = ids[...]
    for k in range(1, 8):
        t = lax.rem(s + k, 8)
        remote(ids, idr.at[s], id_s.at[k], id_r.at[s], d, t).start()

    value = tokens[...].astype(wide)
    factor = lax.rsqrt(jnp.mean(value * value, axis=-1, keepdims=True) + epsilon)
    xall[s] = (value * factor * gain[...]).astype(low)
    ring = Chain(d, s, lambda b: xall.at[b], x_u, x_r, x_b, x_c)
    ring.start()

    gu_src[0] = wg_in[...].astype(low)
    gu_src[1] = wu_in[...].astype(low)
    d_src_[...] = wd_in[...].astype(low)
    wo[s, :, pl.ds(pl.multiple_of(d * 256, 256), 256)] = wo_in[...].astype(low)
    call[s] = cot[...]

    for k in range(1, 8):
        t = lax.rem(s + k, 8)
        arrived(idr.at[t], id_r.at[t], d, s)
    for b in range(8):
        block = idr[b]
        for n in range(4):
            keyrow[n : n + 1, 128 * b : 128 * (b + 1)] = block[n : n + 1, :]
        full = jnp.concatenate([block] * 16, axis=0)
        idc[128 * b : 128 * (b + 1), :] = full.T

    ring.step(1)
    place = lax.broadcasted_iota(jnp.int32, (1, 128), 1)
    sign = jnp.where(lax.rem(place, 64) < 32, -1.0, 1.0)

    def trig(b, carry):
        angle = idc[rows(b), 3:4] * freq[...]
        cosine[rows(b), :] = jnp.cos(angle)
        sine[rows(b), :] = jnp.sin(angle) * sign
        return carry

    lax.fori_loop(0, 4, trig, 0)
    ring.step(2)
    lax.fori_loop(4, 8, trig, 0)

    half_qkv = lambda n: wqkv.at[pl.ds(512 * n, 512)]

    @pl.when(is_home)
    def _():
        for k in range(1, 8):
            t = lax.rem(s + k, 8)
            arrived(wqkv.at[rows(t)], qs_r.at[t], d, s)
        remote(wqkv, wqkv, qp_s.at[0], qp_r.at[0], dx, s).start()
        remote(wqkv, wqkv, qp_s.at[1], qp_r.at[0], dy, s).start()

    ring.step(3)

    cols_d = lanes(d)
    for k in range(1, 8):
        t = lax.rem(s + k, 8)
        remote(
            gu_src.at[:, :, lanes(t)], wgu.at[:, rows(s), cols_d], gu_s.at[k], gu_r.at[s], d, t
        ).start()
    wgu[:, rows(s), cols_d] = gu_src[:, :, lanes(s)]
    wide_d = pl.ds(pl.multiple_of(d * 256, 256), 256)
    for m in range(4):
        t = lax.rem(s, 2) * 4 + m

        @pl.when(t != s)
        def _():
            remote(
                d_src_.at[pl.ds(128 * m, 128)], wd.at[rows(s // 2), wide_d],
                dn_s.at[m], dn_r.at[s // 2], d, t,
            ).start()

        @pl.when(t == s)
        def _():
            wd[rows(s // 2), wide_d] = d_src_[pl.ds(128 * m, 128), :]

    wo_ring = Chain(d, s, lambda b: wo.at[b, :, wide_d], wo_u, wo_r, wo_b, wo_c)
    wo_ring.start()
    c_ring = Chain(d, s, lambda b: call.at[b], c_u, c_r, c_b, c_c)
    c_ring.start()

    for zz in range(4):
        ring.wait_side(zz)

    @pl.when(home == dx)
    def _():
        arrived(wqkv, qp_r.at[0], d, s)
        remote(half_qkv(0), half_qkv(0), qp_s.at[2], qp_r.at[1], dy, s).start()

    @pl.when(home == dy)
    def _():
        arrived(wqkv, qp_r.at[0], d, s)
        remote(half_qkv(1), half_qkv(1), qp_s.at[2], qp_r.at[2], dx, s).start()

    @pl.when(home == 3 - d)
    def _():
        arrived(half_qkv(0), qp_r.at[1], d, s)
        arrived(half_qkv(1), qp_r.at[2], d, s)

    def project(i, carry):
        block = xall[pl.ds(2 * i, 2)].reshape(256, 1024)
        pre = dot(block, wqkv[...])
        cs, sn = cosine[rows(i, 256), :], sine[rows(i, 256), :]
        qp, kp = pre[:, :128], pre[:, 128:256]
        q_out[rows(i, 256), :] = (qp * cs + partner(qp) * sn).astype(low)
        k_out[rows(i, 256), :] = (kp * cs + partner(kp) * sn).astype(low)
        v_out[rows(i, 256), :] = pre[:, 256:].astype(low)
        return carry

    lax.fori_loop(0, 4, project, 0)
    wo_ring.step(1)
    c_ring.step(1)

    def attend(b, carry):
        pick = rows(b)
        seg_col, var_col = idc[pick, 0:1], idc[pick, 2:3]
        q_place = b * 128 + lax.broadcasted_iota(jnp.int32, (128, 1), 0)
        k_place = lax.broadcasted_iota(jnp.int32, (1, 1024), 1)
        allowed = (seg_col == keyrow[1:2, :]) | (q_place == k_place)
        same = var_col == keyrow[2:3, :]
        q_block = q_out[pick, :]
        attended, total_lse = None, None
        for h in range(2):
            mine = head_lanes(h)
            qh = jnp.where(mine, q_block, jnp.zeros_like(q_block))
            scores = dot_nt(qh, k_out[...]) * 0.125
            scores = scores + jnp.where(same, bias[h : h + 1, 0:1], bias[h : h + 1, 1:2])
            scores = jnp.where(allowed, scores, NEG)
            top = jnp.max(scores, axis=-1, keepdims=True)
            e = jnp.exp(scores - top)
            total = jnp.sum(e, axis=-1, keepdims=True)
            part = dot((e * (1.0 / total)).astype(low), v_out[...])
            one = top + jnp.log(total)
            if h == 0:
                attended, total_lse = part, one
            else:
                attended = jnp.where(mine, part, attended)
                total_lse = jnp.where(mine, one, total_lse)
        head_out[b] = attended.astype(low)
        lse[pick, :] = jnp.broadcast_to(total_lse, (128, 128))
        return carry

    pair = pair_of(s)

    def send_mixed(t):
        @pl.when(t != s)
        def _():
            remote(head_out.at[t], mixed.at[pair], m_s.at[t], m_r.at[s], d, t).start()

        @pl.when(t == s)
        def _():
            mixed[pair] = head_out[t]

    gu_plane = Plane(
        d, s, lambda i: wgu.at[:, :, lanes(i)], lambda i, n: wgu.at[n, :, lanes(i)],
        pl_s.at[0], pl_r.at[0],
    )
    wide_of = lambda i: pl.ds(pl.multiple_of(i * 256, 256), 256)
    dn_plane = Plane(
        d, s, lambda i: wd.at[:, wide_of(i)], lambda i, n: wd.at[pl.ds(256 * n, 256), wide_of(i)],
        pl_s.at[1], pl_r.at[1],
    )
    wo_plane = Plane(
        d, s, lambda i: wo.at[:, :, wide_of(i)], lambda i, n: wo.at[pl.ds(4 * n, 4), :, wide_of(i)],
        pl_s.at[2], pl_r.at[2],
    )

    lax.fori_loop(0, 2, attend, 0)
    send_mixed(0)
    send_mixed(1)
    wo_ring.step(2)
    c_ring.step(2)
    for k in range(1, 8):
        t = lax.rem(s + k, 8)
        arrived(wgu.at[:, rows(t), cols_d], gu_r.at[t], d, s)
    gu_plane.start()
    lax.fori_loop(2, 4, attend, 0)
    send_mixed(2)
    send_mixed(3)
    wo_ring.step(3)
    c_ring.step(3)
    for j in range(4):

        @pl.when(2 * j + s // 4 != s)
        def _():
            arrived(wd.at[pl.ds(128 * j, 128), wide_d], dn_r.at[j], d, s)

    dn_plane.start()
    lax.fori_loop(4, 6, attend, 0)
    send_mixed(4)
    send_mixed(5)
    wo_ring.finish()
    wo_plane.start()
    gu_plane.step()
    lax.fori_loop(6, 8, attend, 0)
    send_mixed(6)
    send_mixed(7)
    dn_plane.step()
    wo_plane.step()
    c_ring.finish()
    gu_plane.finish()
    dn_plane.finish()
    wo_plane.finish()

    ring.drain()
    for i in range(2):

        @pl.when(owner[i] != s)
        def _():
            sent(qkv_src.at[i], qs_s.at[i], d, s)

    for k in range(1, 8):
        sent(ids, id_s.at[k], d, s)
        sent(gu_src.at[:, :, pl.ds(0, 128)], gu_s.at[k], d, s)

    @pl.when(is_home)
    def _():
        sent(wqkv, qp_s.at[0], d, s)
        sent(wqkv, qp_s.at[1], d, s)

    @pl.when((home == dx) | (home == dy))
    def _():
        sent(half_qkv(0), qp_s.at[2], d, s)

    for m in range(4):

        @pl.when(lax.rem(s, 2) * 4 + m != s)
        def _():
            sent(d_src_.at[pl.ds(128 * m, 128)], dn_s.at[m], d, s)

    for t in range(8):

        @pl.when(t != s)
        def _():
            arrived(mixed.at[pair_of(t)], m_r.at[t], d, s)
            sent(head_out.at[t], m_s.at[t], d, s)


def vmem():
    return pl.BlockSpec(memory_space=pltpu.VMEM)


def shape(*dims, kind=low):
    return jax.ShapeDtypeStruct(dims, kind)


def dma(*dims):
    return pltpu.SemaphoreType.DMA(dims)


def front(tokens, gain, wq, wk, wv, wo, wg, wu, wd, bias, ids, freq, cot):
    outs = (
        shape(8, 128, 1024),
        shape(1024, 128), shape(1024, 128), shape(1024, 128),
        shape(1024, 128, kind=wide),
        shape(1024, 384),
        shape(8, 128, 1024),
        shape(2, 1024, 512),
        shape(512, 1024),
        shape(8, 128, 1024),
        shape(8, 8, 128, kind=wide),
        shape(1024, 128, kind=wide),
        shape(1024, 128, kind=wide),
        shape(1024, 128, kind=wide),
        shape(8, 128, 128),
    )
    return pl.pallas_call(
        front_kernel,
        name="front",
        out_shape=outs,
        in_specs=[vmem()] * 13,
        out_specs=[vmem()] * len(outs),
        scratch_shapes=[
            pltpu.VMEM((2, 128, 384), low),
            pltpu.VMEM((2, 128, 1024), low),
            pltpu.VMEM((512, 256), low),
            pltpu.VMEM((8, 128, 128), low),
            pltpu.VMEM((8, 1024), wide),
            dma(2), dma(8), dma(3), dma(3), dma(8), dma(8), dma(6), dma(4), dma(4), dma(4),
            dma(8), dma(8), dma(4), dma(4),
            dma(6), dma(4), dma(4), dma(4), dma(6), dma(4), dma(4), dma(4),
            dma(3, 4), dma(3, 4), dma(8), dma(8),
        ],
        compiler_params=pltpu.CompilerParams(
            collective_id=0, has_side_effects=True, vmem_limit_bytes=60 << 20
        ),
    )(tokens, gain, wq, wk, wv, wo, wg, wu, wd, bias, ids, freq, cot)


def fast_body(
    tokens, attn_gain, query_weight, key_weight, value_weight, out_weight, same_bias, cross_bias,
    ffn_gain, gate_weight, up_weight, down_weight, segment_ids, variate_ids, time_ids, observed,
    cotangent,
):
    s = lax.axis_index("seq")
    d = lax.axis_index("dp")
    pair = pair_of(s)
    gain_one = attn_gain.astype(low).astype(wide)[None]
    gain_two = ffn_gain.astype(low).astype(wide)[None]
    both = jnp.stack([same_bias, cross_bias], axis=1)
    bias = jnp.pad(lax.dynamic_slice_in_dim(both, 2 * pair, 2, 0), ((0, 6), (0, 126)))
    segment = segment_ids[0]
    ids = jnp.stack(
        [segment, jnp.where(observed[0] == 1, segment, -1), variate_ids[0], time_ids[0]]
    ).astype(wide)
    ids = jnp.pad(ids, ((0, 4), (0, 0)))
    powers = jnp.arange(32).astype(wide) * (2.0 / 64)
    freq = jnp.tile(10000.0 ** (-powers), 4)[None]
    tok = tokens[0]
    (
        xall, q, k, v, lse, wqkv, wo, wgu, wd, call, idr, idc, cosine, sine, mixed
    ) = front(
        tok, gain_one, query_weight, key_weight, value_weight, out_weight, gate_weight, up_weight,
        down_weight, bias, ids, freq, cotangent[0],
    )
    out, mgrad_all, middle_grad, gu_grad, dn_grad, wo_grad, ffn_gain_grad = middle_stage(
        tok, mixed, wo, gain_two, wgu, wd, call
    )
    tok_grad, g_gate, g_up, g_down, g_query, g_key, g_value, g_out, small = back_stage(
        tok, gain_one, xall, q, k, v, lse, wqkv, mgrad_all, middle_grad, bias, idr, idc, cosine, sine,
        gu_grad, dn_grad, wo_grad, ffn_gain_grad,
    )
    return (
        out[None], tok_grad[None], small[0], g_query, g_key, g_value, g_out,
        small[2, 0:16], small[2, 128:144], small[1], g_gate, g_up, g_down,
    )


def fits(mesh):
    return mesh.shape["dp"] == 4 and mesh.shape["seq"] == 8


class Scatter:
    def __init__(self, d, s, keep, side_out, side_in, out, got, sems):
        self.d, self.s, self.z, self.c = d, s, s // 2, lax.rem(s, 2)
        self.keep, self.side_out, self.side_in = keep, side_out, side_in
        self.out, self.got = out, got
        self.side_s, self.side_r, self.send_s, self.send_r = (sems.at[i] for i in range(4))

    def give(self, z, value):
        first, second = value[:128], value[128:]
        even = self.c == 0
        self.side_out[z] = jnp.where(even, second, first).astype(low)
        remote(
            self.side_out.at[z], self.side_in.at[z], self.side_s.at[z], self.side_r.at[z],
            self.d, self.s + 1 - 2 * self.c,
        ).start()
        self.keep[z] = jnp.where(even, first, second)

    def pass_on(self, z):
        arrived(self.side_in.at[z], self.side_r.at[z], self.d, self.s)
        total = self.keep[z] + self.side_in[z].astype(wide)

        @pl.when(z == self.z)
        def _():
            self.keep[z] = total

        @pl.when(z != self.z)
        def _():
            self.out[z] = total.astype(low)
            remote(
                self.out.at[z], self.got.at[self.z], self.send_s.at[z], self.send_r.at[self.z],
                self.d, 2 * z + self.c,
            ).start()

    def total(self):
        value = self.keep[self.z]
        for k in range(1, 4):
            t = lax.rem(self.z + k, 4)
            arrived(self.got.at[t], self.send_r.at[t], self.d, self.s)
            value = value + self.got[t].astype(wide)
        return value

    def drain(self):
        for z in range(4):
            sent(self.side_out.at[z], self.side_s.at[z], self.d, self.s)

            @pl.when(z != self.z)
            def _():
                sent(self.out.at[z], self.send_s.at[z], self.d, self.s)


def scatter_scratch():
    return [
        pltpu.VMEM((4, 128, 1024), wide),
        pltpu.VMEM((4, 128, 1024), low),
        pltpu.VMEM((4, 128, 1024), low),
        pltpu.VMEM((4, 128, 1024), low),
        pltpu.VMEM((4, 128, 1024), low),
        dma(4, 4),
    ]


def chip_order(z, j):
    table = ((0, 1, 2, 3), (1, 0, 2, 3), (2, 1, 3, 0), (3, 2, 1, 0))
    value = z * 0 + table[0][j]
    for n in range(1, 4):
        value = jnp.where(z == n, table[n][j], value)
    return value


def pair_owner(p):
    dd, i = p // 2, p % 2
    return 2 * (dd % 2 + 2 * i) + dd // 2


def middle_kernel(
    tokens, mixed, wo, gain, wgu, wd, call,
    out, mgrad, mid_grad, gu_grad, dn_grad, wo_grad, gain_grad,
    sall, gg, ug, hid, hgrad, mid, mg_src,
    g_keep, g_so, g_si, g_out, g_got, g_sem, o_keep, o_so, o_si, o_out, o_got, o_sem,
    x_u, x_r, x_b, x_c, m_s, m_r,
):
    d = lax.axis_index("dp")
    s = lax.axis_index("seq")
    z = s // 2
    c = lax.rem(s, 2)
    greet(d, s)
    joined = jnp.concatenate([mixed[p] for p in range(8)], axis=1)
    middle = tokens[...].astype(wide) + dot(joined, wo[...].reshape(1024, 1024))
    factor = lax.rsqrt(jnp.mean(middle * middle, axis=-1, keepdims=True) + epsilon)
    sall[s] = (middle * factor * gain[...]).astype(low)
    ring = Chain(d, s, lambda b: sall.at[b], x_u, x_r, x_b, x_c)
    ring.start()
    mid[...] = middle

    def early(i, carry):
        hgrad[rows(i, 256), :] = dot_nt(call[pl.ds(2 * i, 2)].reshape(256, 1024), wd[...])
        return carry

    lax.fori_loop(0, 4, early, 0)
    grads = Scatter(d, s, g_keep, g_so, g_si, g_out, g_got, g_sem)
    outs = Scatter(d, s, o_keep, o_so, o_si, o_out, o_got, o_sem)

    for j in range(4):
        zj = chip_order(z, j)
        if j > 0:
            arrived(ring.block(zj), x_r.at[zj], d, s)

            @pl.when((zj < z) & (z < 3))
            def _():
                ring.up(zj).start()

            @pl.when((zj > z) & (z > 0))
            def _():
                ring.down(zj).start()

            ring.side(zj).start()
        ring.wait_side(zj)
        pick = rows(zj, 256)
        block = sall[pl.ds(2 * zj, 2)].reshape(256, 1024)
        gate_pre = dot(block, wgu[0])
        up_pre = dot(block, wgu[1])
        sigma = jax.nn.sigmoid(gate_pre)
        act = gate_pre * sigma
        hidden = (act * up_pre).astype(low)
        hid[pick, :] = hidden
        hg = hgrad[pick, :]
        g_low = (hg * up_pre * sigma * (1.0 + gate_pre * (1.0 - sigma))).astype(low)
        u_low = (hg * act).astype(low)
        gg[pick, :] = g_low
        ug[pick, :] = u_low
        grads.give(zj, dot_nt(g_low, wgu[0]) + dot_nt(u_low, wgu[1]))
        outs.give(zj, dot(hidden, wd[...]))
        if j > 0:
            last = chip_order(z, j - 1)
            grads.pass_on(last)
            outs.pass_on(last)
    last = chip_order(z, 3)
    grads.pass_on(last)
    outs.pass_on(last)

    def weigh(i, carry):
        block = sall[:, :, pl.ds(pl.multiple_of(i * 256, 256), 256)].reshape(1024, 256)
        gu_grad[0, rows(i, 256), :] = dot_tn(block, gg[...]).astype(low)
        gu_grad[1, rows(i, 256), :] = dot_tn(block, ug[...]).astype(low)
        cols = pl.ds(pl.multiple_of(i * 256, 256), 256)
        dn_grad[:, cols] = dot_tn(hid[...], call[:, :, cols].reshape(1024, 256)).astype(low)
        return carry

    lax.fori_loop(0, 4, weigh, 0)

    middle = mid[...]
    factor = lax.rsqrt(jnp.mean(middle * middle, axis=-1, keepdims=True) + epsilon)
    normed = middle * factor
    second_grad = grads.total()
    scaled = second_grad * gain[...]
    inner = jnp.mean(scaled * normed, axis=-1, keepdims=True)
    gain_grad[...] = jnp.sum(second_grad * normed, axis=0, keepdims=True)
    value = call[s].astype(wide) + factor * (scaled - normed * inner)
    mid_grad[...] = value
    v_low = value.astype(low)
    mg = dot_nt(v_low, wo[...].reshape(1024, 1024)).astype(low)
    for p in range(8):
        mg_src[p] = mg[:, 128 * p : 128 * (p + 1)]
        t = pair_owner(p)

        @pl.when(s != t)
        def _():
            remote(mg_src.at[p], mgrad.at[s], m_s.at[p], m_r.at[s], d, t).start()

        @pl.when(s == t)
        def _():
            mgrad[s] = mg_src[p]

    def weigh_out(i, carry):
        cols = pl.ds(pl.multiple_of(i * 256, 256), 256)
        left = jnp.concatenate([mixed[2 * i], mixed[2 * i + 1]], axis=1)
        wo_grad[rows(i, 256), :] = dot_tn(left, v_low).astype(low)
        return carry

    lax.fori_loop(0, 4, weigh_out, 0)
    out[...] = (mid[...] + outs.total()).astype(low)
    for k in range(1, 8):
        t = lax.rem(s + k, 8)
        arrived(mgrad.at[t], m_r.at[t], d, s)
    for p in range(8):

        @pl.when(s != pair_owner(p))
        def _():
            sent(mg_src.at[p], m_s.at[p], d, s)

    ring.drain()
    grads.drain()
    outs.drain()


def middle_stage(tok, mixed, wo, gain, wgu, wd, call):
    outs = (
        shape(128, 1024),
        shape(8, 128, 128),
        shape(128, 1024, kind=wide),
        shape(2, 1024, 512),
        shape(512, 1024),
        shape(1024, 1024),
        shape(1, 1024, kind=wide),
    )
    out, mgrad, mid_grad, gu_grad, dn_grad, wo_grad, gain_grad = pl.pallas_call(
        middle_kernel,
        name="middle",
        out_shape=outs,
        in_specs=[vmem()] * 7,
        out_specs=[vmem()] * len(outs),
        scratch_shapes=[
            pltpu.VMEM((8, 128, 1024), low),
            pltpu.VMEM((1024, 512), low),
            pltpu.VMEM((1024, 512), low),
            pltpu.VMEM((1024, 512), low),
            pltpu.VMEM((1024, 512), wide),
            pltpu.VMEM((128, 1024), wide),
            pltpu.VMEM((8, 128, 128), low),
            *scatter_scratch(),
            *scatter_scratch(),
            dma(6), dma(4), dma(4), dma(4), dma(8), dma(8),
        ],
        compiler_params=pltpu.CompilerParams(
            collective_id=1, has_side_effects=True, vmem_limit_bytes=60 << 20
        ),
    )(tok, mixed, wo, gain, wgu, wd, call)
    return out, mgrad.reshape(1024, 128), mid_grad, gu_grad, dn_grad, wo_grad, gain_grad


class PlaneScatter:
    def __init__(self, d, s, part, first_a, first_b, middle_out, second, send_sem, recv_sem):
        self.d, self.s = d, s
        self.dx = d + 1 - 2 * lax.rem(d, 2)
        self.dy = lax.rem(d + 2, 4)
        self.far = 3 - d
        self.part = part
        self.first = (first_a, first_b)
        self.middle_out, self.second = middle_out, second
        self.send_sem, self.recv_sem = send_sem, recv_sem

    def start(self):
        for n, near in enumerate((self.dx, self.dy)):
            for m, block in enumerate((self.far, near)):
                k = 2 * n + m
                remote(
                    self.part(block, n), self.first[n].at[m], self.send_sem.at[k], self.recv_sem.at[k],
                    near, self.s,
                ).start()

    def step(self):
        for n, other in enumerate((self.dy, self.dx)):
            arrived(self.first[n].at[0], self.recv_sem.at[2 * n], self.d, self.s)
            total = self.part(other, n)[...].astype(wide) + self.first[n][0].astype(wide)
            self.middle_out[n] = total.astype(low)
            remote(
                self.middle_out.at[n], self.second.at[n], self.send_sem.at[4 + n],
                self.recv_sem.at[4 + n], other, self.s,
            ).start()

    def total(self, n):
        arrived(self.first[n].at[1], self.recv_sem.at[2 * n + 1], self.d, self.s)
        arrived(self.second.at[n], self.recv_sem.at[4 + n], self.d, self.s)
        value = self.part(self.d, n)[...].astype(wide) + self.first[n][1].astype(wide)
        return value + self.second[n].astype(wide)

    def drain(self):
        for k in range(4):
            sent(self.first[0].at[0], self.send_sem.at[k], self.d, self.s)
        for k in range(2):
            sent(self.middle_out.at[0], self.send_sem.at[4 + k], self.d, self.s)


def plane_scatter_scratch(*dims):
    return [
        pltpu.VMEM((2, *dims), low),
        pltpu.VMEM((2, *dims), low),
        pltpu.VMEM((2, *dims), low),
        pltpu.VMEM((2, *dims), low),
        dma(6),
        dma(6),
    ]


def owner_of(dd, i):
    return 2 * (lax.rem(dd, 2) + 2 * i) + dd // 2


def back_kernel(
    tokens, gain, xall, q_all, k_all, v_all, lse, wqkv, mgrad, mid_grad, bias, keyrow, idc, cosine, sine,
    gu_grad, dn_grad, wo_grad, ffn_gain_grad,
    tok_grad, gate_out, up_out, dn_out, q_out, k_out, v_out, wo_out, small_out,
    dk, dv, gr, bsum, qkv_grad,
    g_keep, g_so, g_si, g_out, g_got, g_sem,
    gu_a, gu_b, gu_m, gu_2, gu_ss, gu_rs,
    dn_a, dn_b, dn_m, dn_2, dn_ss, dn_rs,
    wo_a, wo_b, wo_m, wo_2, wo_ss, wo_rs,
    wo_side, wo_sum, gu_sum, dn_sum, wo_fin, gu_rx, dn_rx, wo_rx, q_in, q_sum, q_rx,
    small, small_p, small_q, small_z,
    side_s, side_r, guz_s, guz_r, dnz_s, dnz_r, woz_s, woz_r, qp_s, qp_r, qz_s, qz_r,
    sp_s, sp_r, sz_s, sz_r,
):
    d = lax.axis_index("dp")
    s = lax.axis_index("seq")
    z = s // 2
    c = lax.rem(s, 2)
    home = 2 * c + lax.rem(z, 2)
    own_is_target = (home == d) & (lax.rem(s, 4) == d)

    barrier = pltpu.get_barrier_semaphore()
    for k in range(1, 8):
        pl.semaphore_signal(barrier, inc=1, device_id=(d, lax.rem(s + k, 8)), device_id_type=MESH)
    for k in range(1, 4):
        pl.semaphore_signal(barrier, inc=1, device_id=(lax.rem(d + k, 4), s), device_id_type=MESH)
    for i in range(2):
        giver = owner_of(d, i)

        @pl.when((giver != s) | (lax.rem(s, 4) != d))
        def _():
            pl.semaphore_signal(
                barrier, inc=1, device_id=(lax.rem(s, 4), giver), device_id_type=MESH
            )

    @pl.when(own_is_target)
    def _():
        pl.semaphore_wait(barrier, 11)

    @pl.when(jnp.logical_not(own_is_target))
    def _():
        pl.semaphore_wait(barrier, 12)

    wide_of = lambda i: pl.ds(pl.multiple_of(i * 256, 256), 256)
    gu = PlaneScatter(
        d, s, lambda i, n: gu_grad.at[n, :, lanes(i)], gu_a, gu_b, gu_m, gu_2, gu_ss, gu_rs
    )
    dn = PlaneScatter(
        d, s, lambda i, n: dn_grad.at[pl.ds(256 * n, 256), wide_of(i)],
        dn_a, dn_b, dn_m, dn_2, dn_ss, dn_rs,
    )
    wo = PlaneScatter(
        d, s, lambda i, n: wo_sum.at[pl.ds(2 * n, 2), :, wide_of(i)],
        wo_a, wo_b, wo_m, wo_2, wo_ss, wo_rs,
    )
    side = remote(wo_grad.at[:, 1 - c], wo_side, side_s, side_r, d, s + 1 - 2 * c)
    side.start()
    gu.start()
    dn.start()
    dk[...] = jnp.zeros_like(dk)
    dv[...] = jnp.zeros_like(dv)
    bsum[...] = jnp.zeros_like(bsum)

    def unturn(x, pick):
        return x * cosine[pick, :] - partner(x) * sine[pick, :]

    def attend(b):
        pick = rows(b, 256)
        seg_col, var_col = idc[pick, 0:1], idc[pick, 2:3]
        q_place = b * 256 + lax.broadcasted_iota(jnp.int32, (256, 1), 0)
        k_place = lax.broadcasted_iota(jnp.int32, (1, 1024), 1)
        allowed = (seg_col == keyrow[1:2, :]) | (q_place == k_place)
        same = var_col == keyrow[2:3, :]
        q_block, m_block = q_all[pick, :], mgrad[pick, :]
        dq = None
        for h in range(2):
            mine = head_lanes(h)
            qh = jnp.where(mine, q_block, jnp.zeros_like(q_block))
            mh = jnp.where(mine, m_block, jnp.zeros_like(m_block))
            scores = dot_nt(qh, k_all[...]) * 0.125
            scores = scores + jnp.where(same, bias[h : h + 1, 0:1], bias[h : h + 1, 1:2])
            p = jnp.exp(jnp.where(allowed, scores - lse[pick, 64 * h : 64 * h + 1], NEG))
            pg = dot_nt(mh, v_all[...])
            inner = jnp.sum(p * pg, axis=-1, keepdims=True)
            ds = (p * (pg - inner)).astype(low)
            ds_wide = ds.astype(wide)
            bsum[2 * h : 2 * h + 1, :] += jnp.sum(jnp.where(same, ds_wide, 0.0), axis=0, keepdims=True)
            bsum[2 * h + 1 : 2 * h + 2, :] += jnp.sum(jnp.where(same, 0.0, ds_wide), axis=0, keepdims=True)
            one = dot(ds, k_all[...]) * 0.125
            dq = one if h == 0 else jnp.where(mine, one, dq)
            dk[...] += dot_tn(ds, qh)
            dv[...] += dot_tn(p.astype(low), mh)
        gr[pick, 0:128] = unturn(dq, pick).astype(low)

    def send_gu(n):
        gu_sum[n] = gu.total(n).astype(low)
        for k in range(1, 8):
            t = lax.rem(s + k, 8)
            remote(
                gu_sum.at[n, rows(t)], gu_rx.at[n, s], guz_s.at[n, k], guz_r.at[n, s], d, t
            ).start()
        gu_rx[n, s] = gu_sum[n, rows(s), :]

    def send_dn():
        for j in range(4):
            t = 2 * j + s // 4

            @pl.when(t != s)
            def _():
                remote(
                    dn_sum.at[pl.ds(128 * j, 128)], dn_rx.at[lax.rem(s, 4)], dnz_s.at[j],
                    dnz_r.at[lax.rem(s, 4)], d, t,
                ).start()

            @pl.when(t == s)
            def _():
                dn_rx[lax.rem(s, 4)] = dn_sum[pl.ds(128 * j, 128), :]

    attend(0)
    side.wait_recv()
    for b in range(4):
        wo_sum[b] = (wo_grad[b, c].astype(wide) + wo_side[b].astype(wide)).astype(low)
    wo.start()
    gu.step()
    attend(1)
    dn.step()
    send_gu(0)
    send_gu(1)
    attend(2)
    wo.step()
    for n in range(2):
        dn_sum[pl.ds(256 * n, 256), :] = dn.total(n).astype(low)
    send_dn()
    attend(3)

    for n in range(2):
        wo_fin[pl.ds(2 * n, 2)] = wo.total(n).astype(low)
    for k in range(1, 4):
        t = lax.rem(z + k, 4)
        remote(wo_fin.at[t], wo_rx.at[z], woz_s.at[t], woz_r.at[z], d, 2 * t + c).start()

    def turn(b, carry):
        pick = rows(b, 256)
        gr[pick, 128:256] = unturn(dk[pick, :] * 0.125, pick).astype(low)
        gr[pick, 256:384] = dv[pick, :].astype(low)
        return carry

    lax.fori_loop(0, 4, turn, 0)
    grads = Scatter(d, s, g_keep, g_so, g_si, g_out, g_got, g_sem)
    for j in range(4):
        zj = lax.rem(z + 3 - j, 4)
        grads.give(zj, dot_nt(gr[rows(zj, 256), :], wqkv[...]))
        if j > 0:
            grads.pass_on(lax.rem(z + 4 - j, 4))
    grads.pass_on(z)

    def weigh(i, carry):
        block = xall[:, :, wide_of(i)].reshape(1024, 256)
        value = dot_tn(block, gr[...]).astype(low)
        qkv_grad[2 * i] = value[:128]
        qkv_grad[2 * i + 1] = value[128:]
        return carry

    lax.fori_loop(0, 4, weigh, 0)
    for k in range(1, 4):
        t = lax.rem(d + k, 4)
        for m in range(2):
            remote(
                qkv_grad.at[t + 4 * m], q_in.at[d, m], qp_s.at[t, m], qp_r.at[d, m], t, s
            ).start()

    for k in range(1, 8):
        t = lax.rem(s + k, 8)
        for n in range(2):
            arrived(gu_rx.at[n, t], guz_r.at[n, t], d, s)
    for t in range(8):
        gate_out[:, 128 * t : 128 * (t + 1)] = gu_rx[0, t].astype(wide)
        up_out[:, 128 * t : 128 * (t + 1)] = gu_rx[1, t].astype(wide)
    for m in range(4):

        @pl.when(4 * lax.rem(s, 2) + m != s)
        def _():
            arrived(dn_rx.at[m], dnz_r.at[m], d, s)

        dn_out[128 * m : 128 * (m + 1), :] = dn_rx[m].astype(wide)
    total = wo_fin[z].astype(wide)
    for k in range(1, 4):
        t = lax.rem(z + k, 4)
        arrived(wo_rx.at[t], woz_r.at[t], d, s)
        total = total + wo_rx[t].astype(wide)
    wo_out[...] = total

    for m in range(2):
        value = qkv_grad[d + 4 * m].astype(wide)
        for k in range(1, 4):
            t = lax.rem(d + k, 4)
            arrived(q_in.at[t, m], qp_r.at[t, m], d, s)
            value = value + q_in[t, m].astype(wide)
        q_sum[m] = value.astype(low)
        target = d + 4 * m
        mine = (target == s) & (home == d)

        @pl.when(jnp.logical_not(mine))
        def _():
            remote(q_sum.at[m], q_rx.at[z // 2], qz_s.at[m], qz_r.at[z // 2], home, target).start()

        @pl.when(mine)
        def _():
            q_rx[z // 2] = q_sum[m]

    value = tokens[...].astype(wide)
    factor = lax.rsqrt(jnp.mean(value * value, axis=-1, keepdims=True) + epsilon)
    normed = value * factor
    first_grad = grads.total()
    scaled = first_grad * gain[...]
    inner = jnp.mean(scaled * normed, axis=-1, keepdims=True)
    tok_grad[...] = (mid_grad[...] + factor * (scaled - normed * inner)).astype(low)

    small[...] = jnp.zeros_like(small)
    small[0:1, :] = jnp.sum(first_grad * normed, axis=0, keepdims=True)
    small[1:2, :] = ffn_gain_grad[...]
    pair = pair_of(s)
    place = lax.broadcasted_iota(jnp.int32, (1, 1024), 1)
    line = jnp.zeros((1, 1024), wide)
    for h in range(2):
        for n in range(2):
            k = 2 * h + n
            one = jnp.sum(bsum[k : k + 1, :], axis=1, keepdims=True)
            line = line + jnp.where(place == 128 * n + 2 * pair + h, one, 0.0)
    small[2:3, :] = line
    for k in range(1, 4):
        t = lax.rem(d + k, 4)
        remote(small, small_p.at[d], sp_s.at[k], sp_r.at[d], t, s).start()
    value = small[...]
    for k in range(1, 4):
        t = lax.rem(d + k, 4)
        arrived(small_p.at[t], sp_r.at[t], d, s)
    small_p[d] = value
    small_q[...] = small_p[0] + small_p[1] + small_p[2] + small_p[3]
    for k in range(1, 8):
        t = lax.rem(s + k, 8)
        remote(small_q, small_z.at[s], sz_s.at[k], sz_r.at[s], d, t).start()
    small_z[s] = small_q[...]

    for i in range(2):
        giver = owner_of(d, i)

        @pl.when((giver != s) | (lax.rem(s, 4) != d))
        def _():
            arrived(q_rx.at[i], qz_r.at[i], d, s)

        cols = slice(128 * i, 128 * (i + 1))
        q_out[:, cols] = q_rx[i, :, 0:128].astype(wide)
        k_out[:, cols] = q_rx[i, :, 128:256].astype(wide)
        v_out[:, cols] = q_rx[i, :, 256:384].astype(wide)

    for k in range(1, 8):
        t = lax.rem(s + k, 8)
        arrived(small_z.at[t], sz_r.at[t], d, s)
    total = small_z[0]
    for t in range(1, 8):
        total = total + small_z[t]
    small_out[...] = total

    side.wait_send()
    gu.drain()
    dn.drain()
    wo.drain()
    grads.drain()
    for k in range(1, 8):
        for n in range(2):
            sent(gu_sum.at[n, rows(0)], guz_s.at[n, k], d, s)
        sent(small_q, sz_s.at[k], d, s)
    for j in range(4):

        @pl.when(2 * j + s // 4 != s)
        def _():
            sent(dn_sum.at[pl.ds(0, 128)], dnz_s.at[j], d, s)

    for k in range(1, 4):
        t = lax.rem(z + k, 4)
        sent(wo_fin.at[t], woz_s.at[t], d, s)
        t = lax.rem(d + k, 4)
        for m in range(2):
            sent(q_sum.at[m], qp_s.at[t, m], d, s)
        sent(small, sp_s.at[k], d, s)
    for m in range(2):

        @pl.when(jnp.logical_not((d + 4 * m == s) & (home == d)))
        def _():
            sent(q_sum.at[m], qz_s.at[m], d, s)


def back_stage(
    tok, gain, xall, q, k, v, lse, wqkv, mgrad, mid_grad, bias, idr, idc, cosine, sine,
    gu_grad, dn_grad, wo_grad, ffn_gain_grad,
):
    keyrow = idr.transpose(1, 0, 2).reshape(8, 1024)
    outs = (
        shape(128, 1024),
        shape(128, 1024, kind=wide),
        shape(128, 1024, kind=wide),
        shape(512, 256, kind=wide),
        shape(128, 256, kind=wide),
        shape(128, 256, kind=wide),
        shape(128, 256, kind=wide),
        shape(128, 256, kind=wide),
        shape(8, 1024, kind=wide),
    )
    return pl.pallas_call(
        back_kernel,
        name="back",
        out_shape=outs,
        in_specs=[vmem()] * 19,
        out_specs=[vmem()] * len(outs),
        scratch_shapes=[
            pltpu.VMEM((1024, 128), wide),
            pltpu.VMEM((1024, 128), wide),
            pltpu.VMEM((1024, 384), low),
            pltpu.VMEM((8, 1024), wide),
            pltpu.VMEM((8, 128, 384), low),
            *scatter_scratch(),
            *plane_scatter_scratch(1024, 128),
            *plane_scatter_scratch(256, 256),
            *plane_scatter_scratch(2, 128, 256),
            pltpu.VMEM((4, 128, 1024), low),
            pltpu.VMEM((4, 128, 1024), low),
            pltpu.VMEM((2, 1024, 128), low),
            pltpu.VMEM((512, 256), low),
            pltpu.VMEM((4, 128, 256), low),
            pltpu.VMEM((2, 8, 128, 128), low),
            pltpu.VMEM((4, 128, 256), low),
            pltpu.VMEM((4, 128, 256), low),
            pltpu.VMEM((4, 2, 128, 384), low),
            pltpu.VMEM((2, 128, 384), low),
            pltpu.VMEM((2, 128, 384), low),
            pltpu.VMEM((8, 1024), wide),
            pltpu.VMEM((4, 8, 1024), wide),
            pltpu.VMEM((8, 1024), wide),
            pltpu.VMEM((8, 8, 1024), wide),
            dma(), dma(), dma(2, 8), dma(2, 8), dma(4), dma(4), dma(4), dma(4),
            dma(4, 2), dma(4, 2), dma(2), dma(2), dma(8), dma(4), dma(8), dma(8),
        ],
        compiler_params=pltpu.CompilerParams(
            collective_id=2, has_side_effects=True, vmem_limit_bytes=60 << 20
        ),
    )(
        tok, gain, xall, q, k, v, lse, wqkv, mgrad, mid_grad, bias, keyrow, idc, cosine, sine,
        gu_grad, dn_grad, wo_grad.reshape(4, 2, 128, 1024), ffn_gain_grad,
    )


def solution(mesh):
    in_specs = (
        P("dp", "seq", None),
        P(),
        P("seq", "dp"),
        P("seq", "dp"),
        P("seq", "dp"),
        P("seq", "dp"),
        P(),
        P(),
        P(),
        P("seq", "dp"),
        P("seq", "dp"),
        P("seq", "dp"),
        P("dp", "seq"),
        P("dp", "seq"),
        P("dp", "seq"),
        P("dp", "seq"),
        P("dp", "seq", None),
    )
    out_specs = (
        P("dp", "seq", None),
        P("dp", "seq", None),
        P(),
        P("seq", "dp"),
        P("seq", "dp"),
        P("seq", "dp"),
        P("seq", "dp"),
        P(),
        P(),
        P(),
        P("seq", "dp"),
        P("seq", "dp"),
        P("seq", "dp"),
    )
    part = fast_body if fits(mesh) else body
    return jax.shard_map(part, mesh=mesh, in_specs=in_specs, out_specs=out_specs, check_vma=False)
```

```python
import functools
import types

import jax
import jax.numpy as jnp
import numpy as np
from jax import lax
from jax.experimental import pallas as pl
from jax.experimental.pallas import tpu as pltpu
from jax.sharding import PartitionSpec as P

epsilon = 1e-06


def product(left_side, right_side):
    return jnp.dot(left_side, right_side, preferred_element_type=jnp.float32)


def contract_rows(left_side, right_side):
    return lax.dot_general(
        left_side, right_side, (((0,), (0,)), ((), ())), preferred_element_type=jnp.float32
    )


def contract_cols(left_side, right_side):
    return lax.dot_general(
        left_side, right_side, (((1,), (1,)), ((), ())), preferred_element_type=jnp.float32
    )


def angles_of(moments, head_width):
    half_width = head_width // 2
    powers = jnp.arange(half_width).astype(jnp.float32) * (2.0 / head_width)
    return moments.astype(jnp.float32)[:, None] * (10000.0 ** (-powers))[None, :]


def rotate(values, angles, head_count):
    row_count, model_width = values.shape
    shaped = values.reshape(row_count, head_count, model_width // head_count)
    half_width = model_width // head_count // 2
    first_half = shaped[..., :half_width]
    second = shaped[..., half_width:]
    cosine = jnp.cos(angles)[:, None, :]
    sine_part = jnp.sin(angles)[:, None, :]
    turned = jnp.concatenate(
        [first_half * cosine - second * sine_part, second * cosine + first_half * sine_part],
        axis=-1,
    )
    return turned.reshape(row_count, model_width)


def normalize(values, gain_row):
    factor = lax.rsqrt(jnp.mean(values * values, axis=-1, keepdims=True) + epsilon)
    normed = values * factor
    return (normed, factor, normed * gain_row)


def norm_back(incoming, normed, factor, gain_row):
    scaled = incoming * gain_row
    inner_sum = jnp.mean(scaled * normed, axis=-1, keepdims=True)
    return (factor * (scaled - normed * inner_sum), jnp.sum(incoming * normed, axis=0))


def make_tables(segment, variate, key_segment, key_variate, first_row):
    query_place = first_row + jnp.arange(segment.shape[0])
    key_place = jnp.arange(key_segment.shape[0])
    allowed = (segment.astype(jnp.float32)[:, None] == key_segment.astype(jnp.float32)[None, :]) | (
        query_place[:, None] == key_place[None, :]
    )
    same_kind = variate.astype(jnp.float32)[:, None] == key_variate.astype(jnp.float32)[None, :]
    return (allowed, same_kind)


def block_scores(
    block_index, query_low, keys_all, same_kind, same_bias, cross_bias, head_group, head_width
):
    block_width = head_group * head_width
    query_block = lax.dynamic_slice_in_dim(
        query_low, block_index * block_width, block_width, 1
    ).reshape(query_low.shape[0], head_group, head_width)
    key_block = lax.dynamic_slice_in_dim(
        keys_all, block_index * block_width, block_width, 1
    ).reshape(keys_all.shape[0], head_group, head_width)
    raw_scores = jnp.einsum(
        "thd,shd->hts", query_block, key_block, preferred_element_type=jnp.float32
    )
    same_part = lax.dynamic_slice_in_dim(same_bias, block_index * head_group, head_group)
    cross_part = lax.dynamic_slice_in_dim(cross_bias, block_index * head_group, head_group)
    offset = jnp.where(same_kind[None], same_part[:, None, None], cross_part[:, None, None])
    return (raw_scores * head_width ** (-0.5) + offset, query_block, key_block)


def body(
    tokens,
    attn_gain,
    query_weight,
    key_weight,
    value_weight,
    out_weight,
    same_bias,
    cross_bias,
    ffn_gain,
    gate_weight,
    up_weight,
    down_weight,
    segment_ids,
    variate_ids,
    time_ids,
    observed,
    cotangent,
):
    row_count = tokens.shape[1]
    model_width = tokens.shape[2]
    head_count = same_bias.shape[0]
    head_width = model_width // head_count
    head_group = max(1, 128 // head_width)
    block_width = head_group * head_width
    block_total = head_count // head_group
    scaling = head_width ** (-0.5)
    first_row = lax.axis_index("seq") * row_count
    gain_one = attn_gain.astype(jnp.bfloat16).astype(jnp.float32)
    gain_two = ffn_gain.astype(jnp.bfloat16).astype(jnp.float32)
    low_masters = (
        query_weight.astype(jnp.bfloat16),
        key_weight.astype(jnp.bfloat16),
        value_weight.astype(jnp.bfloat16),
        out_weight.astype(jnp.bfloat16),
        gate_weight.astype(jnp.bfloat16),
        up_weight.astype(jnp.bfloat16),
        down_weight.astype(jnp.bfloat16),
    )
    row_parts = (
        lax.all_gather(low_masters[0], "seq", axis=0, tiled=True),
        lax.all_gather(low_masters[1], "seq", axis=0, tiled=True),
        lax.all_gather(low_masters[2], "seq", axis=0, tiled=True),
        lax.all_gather(low_masters[3], "seq", axis=0, tiled=True),
        lax.all_gather(low_masters[4], "seq", axis=0, tiled=True),
        lax.all_gather(low_masters[5], "seq", axis=0, tiled=True),
        lax.all_gather(low_masters[6], "seq", axis=0, tiled=True),
    )
    gathered = (
        lax.all_gather(row_parts[0], "dp", axis=1, tiled=True),
        lax.all_gather(row_parts[1], "dp", axis=1, tiled=True),
        lax.all_gather(row_parts[2], "dp", axis=1, tiled=True),
        lax.all_gather(row_parts[3], "dp", axis=1, tiled=True),
        lax.all_gather(row_parts[4], "dp", axis=1, tiled=True),
        lax.all_gather(row_parts[5], "dp", axis=1, tiled=True),
        lax.all_gather(row_parts[6], "dp", axis=1, tiled=True),
    )
    w_query, w_key, w_value, w_out, w_gate, w_up, w_down = gathered
    inputs = tokens[0].astype(jnp.float32)
    segment = segment_ids[0]
    variate = variate_ids[0]
    seen_row = observed[0]
    angles = angles_of(time_ids[0], head_width)
    normed_one, factor_one, scaled_one = normalize(inputs, gain_one)
    first_low = scaled_one.astype(jnp.bfloat16)
    query_low = rotate(product(first_low, w_query), angles, head_count).astype(jnp.bfloat16)
    key_low = rotate(product(first_low, w_key), angles, head_count).astype(jnp.bfloat16)
    value_low = product(first_low, w_value).astype(jnp.bfloat16)
    key_segment = jnp.where(seen_row == 1, segment, -1).astype(jnp.bfloat16)
    key_variate = variate.astype(jnp.bfloat16)
    keys_all, values_all, segments_all, variates_all = (
        lax.all_gather(key_low, "seq", axis=0, tiled=True),
        lax.all_gather(value_low, "seq", axis=0, tiled=True),
        lax.all_gather(key_segment, "seq", axis=0, tiled=True),
        lax.all_gather(key_variate, "seq", axis=0, tiled=True),
    )
    length = keys_all.shape[0]
    allowed, same_kind = make_tables(segment, variate, segments_all, variates_all, first_row)

    def forward_block(block_index, state_now):
        mixed, summary = state_now
        scores, query_block, key_block = block_scores(
            block_index,
            query_low,
            keys_all,
            same_kind,
            same_bias,
            cross_bias,
            head_group,
            head_width,
        )
        row_top = jnp.max(jnp.where(allowed[None], scores, -jnp.inf), axis=-1, keepdims=True)
        exponent = jnp.exp(jnp.where(allowed[None], scores - row_top, -jnp.inf))
        row_total = jnp.sum(exponent, axis=-1, keepdims=True)
        prob_low = (exponent / row_total).astype(jnp.bfloat16)
        value_block = lax.dynamic_slice_in_dim(
            values_all, block_index * block_width, block_width, 1
        ).reshape(length, head_group, head_width)
        attended = jnp.einsum(
            "hts,shd->thd", prob_low, value_block, preferred_element_type=jnp.float32
        ).reshape(row_count, block_width)
        mixed = lax.dynamic_update_slice_in_dim(mixed, attended, block_index * block_width, 1)
        summary = lax.dynamic_update_slice_in_dim(
            summary, (row_top + jnp.log(row_total))[..., 0], block_index * head_group, 0
        )
        return (mixed, summary)

    mixed, summary = lax.fori_loop(
        0,
        block_total,
        forward_block,
        (
            jnp.zeros((row_count, model_width), jnp.float32),
            jnp.zeros((head_count, row_count), jnp.float32),
        ),
    )
    mixed_low = mixed.astype(jnp.bfloat16)
    middle = inputs + product(mixed_low, w_out)
    normed_two, factor_two, scaled_two = normalize(middle, gain_two)
    second_low = scaled_two.astype(jnp.bfloat16)
    gate_pre = product(second_low, w_gate)
    up_pre = product(second_low, w_up)
    sigma = jax.nn.sigmoid(gate_pre)
    activated = gate_pre * sigma
    hidden_low = (activated * up_pre).astype(jnp.bfloat16)
    result = middle + product(hidden_low, w_down)
    rows_again = (
        lax.all_gather(low_masters[0], "seq", axis=0, tiled=True),
        lax.all_gather(low_masters[1], "seq", axis=0, tiled=True),
        lax.all_gather(low_masters[2], "seq", axis=0, tiled=True),
        lax.all_gather(low_masters[3], "seq", axis=0, tiled=True),
        lax.all_gather(low_masters[4], "seq", axis=0, tiled=True),
        lax.all_gather(low_masters[5], "seq", axis=0, tiled=True),
        lax.all_gather(low_masters[6], "seq", axis=0, tiled=True),
    )
    regathered = (
        lax.all_gather(rows_again[0], "dp", axis=1, tiled=True),
        lax.all_gather(rows_again[1], "dp", axis=1, tiled=True),
        lax.all_gather(rows_again[2], "dp", axis=1, tiled=True),
        lax.all_gather(rows_again[3], "dp", axis=1, tiled=True),
        lax.all_gather(rows_again[4], "dp", axis=1, tiled=True),
        lax.all_gather(rows_again[5], "dp", axis=1, tiled=True),
        lax.all_gather(rows_again[6], "dp", axis=1, tiled=True),
    )
    w_query, w_key, w_value, w_out, w_gate, w_up, w_down = regathered
    cot_low = cotangent[0]
    hidden_grad = contract_cols(cot_low, w_down)
    down_grad = contract_rows(hidden_low, cot_low)
    gate_grad = (hidden_grad * up_pre * sigma * (1.0 + gate_pre * (1.0 - sigma))).astype(
        jnp.bfloat16
    )
    up_grad = (hidden_grad * activated).astype(jnp.bfloat16)
    gate_w_grad = contract_rows(second_low, gate_grad)
    up_w_grad = contract_rows(second_low, up_grad)
    second_grad = contract_cols(gate_grad, w_gate) + contract_cols(up_grad, w_up)
    middle_part, ffn_gain_grad = norm_back(second_grad, normed_two, factor_two, gain_two)
    middle_grad = cot_low.astype(jnp.float32) + middle_part
    middle_low = middle_grad.astype(jnp.bfloat16)
    out_w_grad = contract_rows(mixed_low, middle_low)
    mixed_grad = contract_cols(middle_low, w_out).astype(jnp.bfloat16)
    keys_back, values_back, segments_back, variates_back = (
        lax.all_gather(key_low, "seq", axis=0, tiled=True),
        lax.all_gather(value_low, "seq", axis=0, tiled=True),
        lax.all_gather(key_segment, "seq", axis=0, tiled=True),
        lax.all_gather(key_variate, "seq", axis=0, tiled=True),
    )
    allowed_back, same_back = make_tables(segment, variate, segments_back, variates_back, first_row)

    def query_side(block_index):
        scores, query_block, key_block = block_scores(
            block_index,
            query_low,
            keys_back,
            same_back,
            same_bias,
            cross_bias,
            head_group,
            head_width,
        )
        lse_block = lax.dynamic_slice_in_dim(summary, block_index * head_group, head_group, 0)
        probabilities = jnp.exp(
            jnp.where(allowed_back[None], scores - lse_block[:, :, None], -jnp.inf)
        )
        grad_block = lax.dynamic_slice_in_dim(
            mixed_grad, block_index * block_width, block_width, 1
        ).reshape(row_count, head_group, head_width)
        value_block = lax.dynamic_slice_in_dim(
            values_back, block_index * block_width, block_width, 1
        ).reshape(length, head_group, head_width)
        prob_grad = jnp.einsum(
            "thd,shd->hts", grad_block, value_block, preferred_element_type=jnp.float32
        )
        inner_sum = jnp.sum(probabilities * prob_grad, axis=-1, keepdims=True)
        score_low = (probabilities * (prob_grad - inner_sum)).astype(jnp.bfloat16)
        score_wide = score_low.astype(jnp.float32)
        same_part = jnp.sum(jnp.where(same_back[None], score_wide, 0.0), axis=(1, 2))
        cross_part = jnp.sum(jnp.where(same_back[None], 0.0, score_wide), axis=(1, 2))
        query_part = (
            jnp.einsum(
                "hts,shd->thd", score_low, key_block, preferred_element_type=jnp.float32
            ).reshape(row_count, block_width)
            * scaling
        )
        return (
            probabilities,
            score_low,
            query_block,
            grad_block,
            inner_sum[..., 0],
            same_part,
            cross_part,
            query_part,
        )

    def backward_block(block_index, state_now):
        query_grad, key_grad, value_grad, same_grad, cross_grad = state_now
        (
            probabilities,
            score_low,
            query_block,
            grad_block,
            inner_sum,
            same_part,
            cross_part,
            query_part,
        ) = query_side(block_index)
        key_part = (
            jnp.einsum(
                "hts,thd->shd", score_low, query_block, preferred_element_type=jnp.float32
            ).reshape(length, block_width)
            * scaling
        )
        value_part = jnp.einsum(
            "hts,thd->shd",
            probabilities.astype(jnp.bfloat16),
            grad_block,
            preferred_element_type=jnp.float32,
        ).reshape(length, block_width)
        query_grad = lax.dynamic_update_slice_in_dim(
            query_grad, query_part, block_index * block_width, 1
        )
        key_grad = lax.dynamic_update_slice_in_dim(key_grad, key_part, block_index * block_width, 1)
        value_grad = lax.dynamic_update_slice_in_dim(
            value_grad, value_part, block_index * block_width, 1
        )
        same_grad = lax.dynamic_update_slice_in_dim(
            same_grad, same_part, block_index * head_group, 0
        )
        cross_grad = lax.dynamic_update_slice_in_dim(
            cross_grad, cross_part, block_index * head_group, 0
        )
        return (query_grad, key_grad, value_grad, same_grad, cross_grad)

    start_state = (
        jnp.zeros((row_count, model_width), jnp.float32),
        jnp.zeros((length, model_width), jnp.float32),
        jnp.zeros((length, model_width), jnp.float32),
        jnp.zeros((head_count,), jnp.float32),
        jnp.zeros((head_count,), jnp.float32),
    )
    query_grad, key_grad, value_grad, same_grad, cross_grad = lax.fori_loop(
        0, block_total, backward_block, start_state
    )
    key_share, value_share = (
        lax.psum_scatter(
            key_grad.astype(jnp.bfloat16), "seq", scatter_dimension=0, tiled=True
        ).astype(jnp.float32),
        lax.psum_scatter(
            value_grad.astype(jnp.bfloat16), "seq", scatter_dimension=0, tiled=True
        ).astype(jnp.float32),
    )
    query_pre_grad = rotate(query_grad, -angles, head_count).astype(jnp.bfloat16)
    key_pre_grad = rotate(key_share, -angles, head_count).astype(jnp.bfloat16)
    value_pre_grad = value_share.astype(jnp.bfloat16)
    query_w_grad = contract_rows(first_low, query_pre_grad)
    key_w_grad = contract_rows(first_low, key_pre_grad)
    value_w_grad = contract_rows(first_low, value_pre_grad)
    first_grad = (
        contract_cols(query_pre_grad, w_query)
        + contract_cols(key_pre_grad, w_key)
        + contract_cols(value_pre_grad, w_value)
    )
    input_part, attn_gain_grad = norm_back(first_grad, normed_one, factor_one, gain_one)
    input_grad = (middle_grad + input_part).astype(jnp.bfloat16)
    col_shares = (
        lax.psum_scatter(
            query_w_grad.astype(jnp.bfloat16), "dp", scatter_dimension=1, tiled=True
        ).astype(jnp.float32),
        lax.psum_scatter(
            key_w_grad.astype(jnp.bfloat16), "dp", scatter_dimension=1, tiled=True
        ).astype(jnp.float32),
        lax.psum_scatter(
            value_w_grad.astype(jnp.bfloat16), "dp", scatter_dimension=1, tiled=True
        ).astype(jnp.float32),
        lax.psum_scatter(
            out_w_grad.astype(jnp.bfloat16), "dp", scatter_dimension=1, tiled=True
        ).astype(jnp.float32),
        lax.psum_scatter(
            gate_w_grad.astype(jnp.bfloat16), "dp", scatter_dimension=1, tiled=True
        ).astype(jnp.float32),
        lax.psum_scatter(
            up_w_grad.astype(jnp.bfloat16), "dp", scatter_dimension=1, tiled=True
        ).astype(jnp.float32),
        lax.psum_scatter(
            down_grad.astype(jnp.bfloat16), "dp", scatter_dimension=1, tiled=True
        ).astype(jnp.float32),
    )
    shares = (
        lax.psum_scatter(
            col_shares[0].astype(jnp.bfloat16), "seq", scatter_dimension=0, tiled=True
        ).astype(jnp.float32),
        lax.psum_scatter(
            col_shares[1].astype(jnp.bfloat16), "seq", scatter_dimension=0, tiled=True
        ).astype(jnp.float32),
        lax.psum_scatter(
            col_shares[2].astype(jnp.bfloat16), "seq", scatter_dimension=0, tiled=True
        ).astype(jnp.float32),
        lax.psum_scatter(
            col_shares[3].astype(jnp.bfloat16), "seq", scatter_dimension=0, tiled=True
        ).astype(jnp.float32),
        lax.psum_scatter(
            col_shares[4].astype(jnp.bfloat16), "seq", scatter_dimension=0, tiled=True
        ).astype(jnp.float32),
        lax.psum_scatter(
            col_shares[5].astype(jnp.bfloat16), "seq", scatter_dimension=0, tiled=True
        ).astype(jnp.float32),
        lax.psum_scatter(
            col_shares[6].astype(jnp.bfloat16), "seq", scatter_dimension=0, tiled=True
        ).astype(jnp.float32),
    )
    small_totals = lax.psum((same_grad, cross_grad, attn_gain_grad, ffn_gain_grad), ("dp", "seq"))
    return (
        result.astype(jnp.bfloat16)[None],
        input_grad[None],
        small_totals[2],
        shares[0],
        shares[1],
        shares[2],
        shares[3],
        small_totals[0],
        small_totals[1],
        small_totals[3],
        shares[4],
        shares[5],
        shares[6],
    )


MESH = pl.DeviceIdType.MESH
NEG = -1e30
low = jnp.bfloat16
wide = jnp.float32

def remote(src, dst, send_sem, recv_sem, d, s):
    return pltpu.make_async_remote_copy(
        src_ref=src,
        dst_ref=dst,
        send_sem=send_sem,
        recv_sem=recv_sem,
        device_id=(d, s),
        device_id_type=MESH,
    )


def arrived(dst, recv_sem, d, s):
    remote(dst, dst, recv_sem, recv_sem, d, s).wait_recv()


def sent(src, send_sem, d, s):
    remote(src, src, send_sem, send_sem, d, s).wait_send()


def pair_of(s):
    z = s // 2
    c = lax.rem(s, 2)
    return 2 * (2 * c + lax.rem(z, 2)) + z // 2


class Chain:
    def __init__(self, d, s, view, up_sem, recv_sem, side_sem, side_recv):
        self.d, self.s, self.z, self.c = d, s, s // 2, lax.rem(s, 2)
        self.view = view
        self.up_sem, self.recv_sem = up_sem, recv_sem
        self.side_sem, self.side_recv = side_sem, side_recv

    def block(self, z):
        return self.view(2 * z + self.c)

    def up(self, z):
        b = self.block(z)
        return remote(b, b, self.up_sem.at[self.z - z], self.recv_sem.at[z], self.d, self.s + 2)

    def down(self, z):
        b = self.block(z)
        return remote(b, b, self.up_sem.at[3 + z - self.z], self.recv_sem.at[z], self.d, self.s - 2)

    def side(self, z):
        b = self.block(z)
        return remote(b, b, self.side_sem.at[z], self.side_recv.at[z], self.d, self.s + 1 - 2 * self.c)

    def start(self):
        @pl.when(self.z < 3)
        def _():
            self.up(self.z).start()

        @pl.when(self.z > 0)
        def _():
            self.down(self.z).start()

        self.side(self.z).start()

    def step(self, k):
        lo, hi = self.z - k, self.z + k

        @pl.when(lo >= 0)
        def _():
            arrived(self.block(lo), self.recv_sem.at[lo], self.d, self.s)

            @pl.when(self.z < 3)
            def _():
                self.up(lo).start()

            self.side(lo).start()

        @pl.when(hi <= 3)
        def _():
            arrived(self.block(hi), self.recv_sem.at[hi], self.d, self.s)

            @pl.when(self.z > 0)
            def _():
                self.down(hi).start()

            self.side(hi).start()

    def start_lane(self):
        @pl.when(self.z < 3)
        def _():
            self.up(self.z).start()

        @pl.when(self.z > 0)
        def _():
            self.down(self.z).start()

    def lane_step(self, k):
        lo, hi = self.z - k, self.z + k

        @pl.when(lo >= 0)
        def _():
            arrived(self.block(lo), self.recv_sem.at[lo], self.d, self.s)

            @pl.when(self.z < 3)
            def _():
                self.up(lo).start()

        @pl.when(hi <= 3)
        def _():
            arrived(self.block(hi), self.recv_sem.at[hi], self.d, self.s)

            @pl.when(self.z > 0)
            def _():
                self.down(hi).start()

    def wait_side(self, z):
        arrived(self.view(2 * z + 1 - self.c), self.side_recv.at[z], self.d, self.s)

    def finish(self):
        for z in range(4):
            self.wait_side(z)
        self.drain()

    def drain(self):
        own = self.block(self.z)
        for z in range(4):
            sent(own, self.side_sem.at[z], self.d, self.s)
        self.lane_drain()

    def lane_drain(self):
        own = self.block(self.z)
        for k in range(3):

            @pl.when((self.z < 3) & (self.z - k >= 0))
            def _():
                sent(own, self.up_sem.at[k], self.d, self.s)

            @pl.when((self.z > 0) & (self.z + k <= 3))
            def _():
                sent(own, self.up_sem.at[3 + k], self.d, self.s)


class Plane:
    def __init__(self, d, s, whole, half, send_sem, recv_sem):
        self.d, self.s = d, s
        self.dx = d + 1 - 2 * lax.rem(d, 2)
        self.dy = lax.rem(d + 2, 4)
        self.far = 3 - d
        self.whole, self.half = whole, half
        self.send_sem, self.recv_sem = send_sem, recv_sem

    def start(self):
        w = self.whole(self.d)
        remote(w, w, self.send_sem.at[0], self.recv_sem.at[0], self.dx, self.s).start()
        remote(w, w, self.send_sem.at[1], self.recv_sem.at[1], self.dy, self.s).start()

    def step(self):
        arrived(self.whole(self.dx), self.recv_sem.at[0], self.d, self.s)
        h = self.half(self.dx, 0)
        remote(h, h, self.send_sem.at[2], self.recv_sem.at[2], self.dy, self.s).start()
        arrived(self.whole(self.dy), self.recv_sem.at[1], self.d, self.s)
        h = self.half(self.dy, 1)
        remote(h, h, self.send_sem.at[3], self.recv_sem.at[3], self.dx, self.s).start()

    def finish(self):
        arrived(self.half(self.far, 0), self.recv_sem.at[2], self.d, self.s)
        arrived(self.half(self.far, 1), self.recv_sem.at[3], self.d, self.s)
        w = self.whole(self.d)
        sent(w, self.send_sem.at[0], self.d, self.s)
        sent(w, self.send_sem.at[1], self.d, self.s)
        h = self.half(self.d, 0)
        sent(h, self.send_sem.at[2], self.d, self.s)
        h = self.half(self.d, 1)
        sent(h, self.send_sem.at[3], self.d, self.s)


def lanes(i):
    return pl.ds(pl.multiple_of(i * 128, 128), 128)


def rows(i, n=128):
    return pl.ds(pl.multiple_of(i * n, n), n)


def dot(a, b):
    return jnp.dot(a, b, preferred_element_type=wide)


def dot_nt(a, b):
    return lax.dot_general(a, b, (((1,), (1,)), ((), ())), preferred_element_type=wide)


def dot_tn(a, b):
    return lax.dot_general(a, b, (((0,), (0,)), ((), ())), preferred_element_type=wide)


def head_lanes(h):
    place = lax.broadcasted_iota(jnp.int32, (1, 128), 1)
    return (place // 64) == h


def partner(x):
    place = lax.broadcasted_iota(jnp.int32, x.shape, 1)
    return jnp.where(lax.rem(place, 64) < 32, pltpu.roll(x, 96, 1), pltpu.roll(x, 32, 1))


class Scatter:
    def __init__(self, d, s, keep, own, side_out, side_in, out, got, sems):
        self.d, self.s, self.z, self.c = d, s, s // 2, lax.rem(s, 2)
        self.keep, self.own, self.side_out, self.side_in = keep, own, side_out, side_in
        self.out, self.got = out, got
        self.side_s, self.side_r, self.send_s, self.send_r = (sems.at[i] for i in range(4))

    def give(self, j, z, value):
        first, second = value[:128], value[128:]
        even = self.c == 0
        self.side_out[z] = jnp.where(even, second, first).astype(low)
        remote(
            self.side_out.at[z], self.side_in.at[z], self.side_s.at[z], self.side_r.at[z],
            self.d, self.s + 1 - 2 * self.c,
        ).start()
        self.keep[j % 2] = jnp.where(even, first, second)

    def pass_on(self, j, z):
        arrived(self.side_in.at[z], self.side_r.at[z], self.d, self.s)
        total = self.keep[j % 2] + self.side_in[z].astype(wide)

        @pl.when(z == self.z)
        def _():
            self.own[...] = total

        @pl.when(z != self.z)
        def _():
            self.out[z] = total.astype(low)
            remote(
                self.out.at[z], self.got.at[self.z], self.send_s.at[z], self.send_r.at[self.z],
                self.d, 2 * z + self.c,
            ).start()

    def total(self):
        value = self.own[...]
        for k in range(1, 4):
            t = lax.rem(self.z + k, 4)
            arrived(self.got.at[t], self.send_r.at[t], self.d, self.s)
            value = value + self.got[t].astype(wide)
        return value

    def drain(self):
        for z in range(4):
            sent(self.side_out.at[z], self.side_s.at[z], self.d, self.s)

            @pl.when(z != self.z)
            def _():
                sent(self.out.at[z], self.send_s.at[z], self.d, self.s)


def scatter_scratch(name):
    return {
        name + "keep": pltpu.VMEM((2, 128, 1024), wide),
        name + "own": pltpu.VMEM((128, 1024), wide),
        name + "side_out": pltpu.VMEM((4, 128, 1024), low),
        name + "side_in": pltpu.VMEM((4, 128, 1024), low),
        name + "out": pltpu.VMEM((4, 128, 1024), low),
        name + "got": pltpu.VMEM((4, 128, 1024), low),
        name + "sem": dma(4, 4),
    }


def scatter_of(r, name, d, s):
    parts = ("keep", "own", "side_out", "side_in", "out", "got", "sem")
    return Scatter(d, s, *(getattr(r, name + p) for p in parts))


def ring_scratch(name):
    return {name + "u": dma(6), name + "r": dma(4), name + "b": dma(4), name + "c": dma(4)}


def ring_of(r, name, d, s, view):
    return Chain(d, s, view, *(getattr(r, name + p) for p in "urbc"))


class PlaneScatter:
    def __init__(self, d, s, part, first_a, first_b, middle_out, second, send_sem, recv_sem):
        self.d, self.s = d, s
        self.dx = d + 1 - 2 * lax.rem(d, 2)
        self.dy = lax.rem(d + 2, 4)
        self.far = 3 - d
        self.part = part
        self.first = (first_a, first_b)
        self.middle_out, self.second = middle_out, second
        self.send_sem, self.recv_sem = send_sem, recv_sem

    def start(self):
        for n, near in enumerate((self.dx, self.dy)):
            for m, block in enumerate((self.far, near)):
                k = 2 * n + m
                remote(
                    self.part(block, n), self.first[n].at[m], self.send_sem.at[k], self.recv_sem.at[k],
                    near, self.s,
                ).start()

    def step(self):
        for n, other in enumerate((self.dy, self.dx)):
            arrived(self.first[n].at[0], self.recv_sem.at[2 * n], self.d, self.s)
            total = self.part(other, n)[...].astype(wide) + self.first[n][0].astype(wide)
            self.middle_out[n] = total.astype(low)
            remote(
                self.middle_out.at[n], self.second.at[n], self.send_sem.at[4 + n],
                self.recv_sem.at[4 + n], other, self.s,
            ).start()

    def total(self, n):
        arrived(self.first[n].at[1], self.recv_sem.at[2 * n + 1], self.d, self.s)
        arrived(self.second.at[n], self.recv_sem.at[4 + n], self.d, self.s)
        value = self.part(self.d, n)[...].astype(wide) + self.first[n][1].astype(wide)
        return value + self.second[n].astype(wide)

    def drain(self):
        for k in range(4):
            sent(self.first[0].at[0], self.send_sem.at[k], self.d, self.s)
        for k in range(2):
            sent(self.middle_out.at[0], self.send_sem.at[4 + k], self.d, self.s)


def plane_scratch(name, *dims):
    return {
        name + "a": pltpu.VMEM((2, *dims), low),
        name + "b": pltpu.VMEM((2, *dims), low),
        name + "m": pltpu.VMEM((2, *dims), low),
        name + "2": pltpu.VMEM((2, *dims), low),
        name + "ss": dma(6),
        name + "rs": dma(6),
    }


def plane_scatter_of(r, name, d, s, part):
    return PlaneScatter(d, s, part, *(getattr(r, name + p) for p in ("a", "b", "m", "2", "ss", "rs")))


def owner_of(dd, i):
    return 2 * (lax.rem(dd, 2) + 2 * i) + dd // 2


def chip_order(z, j):
    table = ((0, 1, 2, 3), (1, 0, 2, 3), (2, 1, 3, 0), (3, 2, 1, 0))
    value = z * 0 + table[0][j]
    for n in range(1, 4):
        value = jnp.where(z == n, table[n][j], value)
    return value


def pair_owner(p):
    dd, i = p // 2, p % 2
    return 2 * (dd % 2 + 2 * i) + dd // 2


def row_norm(value):
    return lax.rsqrt(jnp.mean(value * value, axis=-1, keepdims=True) + epsilon)


def layer_kernel(names, *refs):
    r = types.SimpleNamespace(**dict(zip(names, refs)))
    d = lax.axis_index("dp")
    s = lax.axis_index("seq")
    z = s // 2
    c = lax.rem(s, 2)
    dx = d + 1 - 2 * lax.rem(d, 2)
    dy = lax.rem(d + 2, 4)
    sibling = s + 1 - 2 * c
    home = 2 * c + lax.rem(z, 2)
    is_home = d == home
    pair = pair_of(s)
    cols_d = lanes(d)
    wide_of = lambda i: pl.ds(pl.multiple_of(i * 256, 256), 256)
    wide_d = wide_of(d)

    own_is_target = is_home & (lax.rem(s, 4) == d)
    barrier = pltpu.get_barrier_semaphore()
    for k in range(1, 8):
        pl.semaphore_signal(barrier, inc=1, device_id=(d, lax.rem(s + k, 8)), device_id_type=MESH)
    for k in range(1, 4):
        pl.semaphore_signal(barrier, inc=1, device_id=(lax.rem(d + k, 4), s), device_id_type=MESH)
    for i in range(2):
        giver = owner_of(d, i)

        @pl.when((giver != s) | (lax.rem(s, 4) != d))
        def _():
            pl.semaphore_signal(
                barrier, inc=1, device_id=(lax.rem(s, 4), giver), device_id_type=MESH
            )

    for i in range(2):
        for n, w in enumerate((r.wq, r.wk, r.wv)):
            r.qkv_src[i, :, 128 * n : 128 * (n + 1)] = w[:, 128 * i : 128 * (i + 1)].astype(low)
    segment = r.segment[...]
    r.ids[0:1, :] = segment.astype(wide)
    r.ids[1:2, :] = jnp.where(r.observed[...] == 1, segment, -1).astype(wide)
    r.ids[2:3, :] = r.variate[...].astype(wide)
    r.ids[3:4, :] = r.moment[...].astype(wide)
    r.ids[4:8, :] = jnp.zeros((4, 128), wide)
    r.idr[s] = r.ids[...]
    gain_one = r.attn_gain[...].reshape(1, 1024).astype(low).astype(wide)
    gain_two = r.ffn_gain[...].reshape(1, 1024).astype(low).astype(wide)
    value = r.tokens[0].astype(wide)
    r.xall[s] = (value * row_norm(value) * gain_one).astype(low)

    @pl.when(own_is_target)
    def _():
        pl.semaphore_wait(barrier, 11)

    @pl.when(jnp.logical_not(own_is_target))
    def _():
        pl.semaphore_wait(barrier, 12)

    owner = [owner_of(d, i) for i in range(2)]
    for i in range(2):

        @pl.when(owner[i] != s)
        def _():
            remote(r.qkv_src.at[i], r.wqkv.at[rows(s)], r.qs_s.at[i], r.qs_r.at[s], d, owner[i]).start()

        @pl.when(owner[i] == s)
        def _():
            r.wqkv[rows(s), :] = r.qkv_src[i]

    for k in range(1, 8):
        remote(r.ids, r.idr.at[s], r.id_s.at[k], r.id_r.at[s], d, lax.rem(s + k, 8)).start()
    ring = ring_of(r, "x_", d, s, lambda b: r.xall.at[b])
    ring.start()

    r.gu_src[0] = r.wg_in[...].astype(low)
    r.gu_src[1] = r.wu_in[...].astype(low)
    r.dn_src[...] = r.wd_in[...].astype(low)
    r.wo[s, :, wide_d] = r.wo_in[...].astype(low)
    r.call[s] = r.cot[0]

    for k in range(1, 8):
        t = lax.rem(s + k, 8)
        arrived(r.idr.at[t], r.id_r.at[t], d, s)
    for b in range(8):
        block = r.idr[b]
        for n in range(4):
            r.keyrow[n : n + 1, 128 * b : 128 * (b + 1)] = block[n : n + 1, :]
        r.idc[128 * b : 128 * (b + 1), :] = jnp.concatenate([block] * 16, axis=0).T

    ring.step(1)
    place = lax.broadcasted_iota(jnp.int32, (1, 128), 1)
    sign = jnp.where(lax.rem(place, 64) < 32, -1.0, 1.0)
    freq = r.freq[...]

    def trig(b, carry):
        angle = r.idc[rows(b), 3:4] * freq
        r.cosine[rows(b), :] = jnp.cos(angle)
        r.sine[rows(b), :] = jnp.sin(angle) * sign
        return carry

    lax.fori_loop(0, 4, trig, 0)
    ring.step(2)
    lax.fori_loop(4, 8, trig, 0)

    half_qkv = lambda n: r.wqkv.at[pl.ds(512 * n, 512)]

    @pl.when(is_home)
    def _():
        for k in range(1, 8):
            t = lax.rem(s + k, 8)
            arrived(r.wqkv.at[rows(t)], r.qs_r.at[t], d, s)
        remote(r.wqkv, r.wqkv, r.qp_s.at[0], r.qp_r.at[0], dx, s).start()
        remote(r.wqkv, r.wqkv, r.qp_s.at[1], r.qp_r.at[0], dy, s).start()

    ring.step(3)

    wo_ring = ring_of(r, "wo_", d, s, lambda b: r.wo.at[b, :, wide_d])
    wo_ring.start_lane()
    for k in range(1, 8):
        t = lax.rem(s + k, 8)
        remote(
            r.gu_src.at[:, :, lanes(t)], r.wgu.at[:, rows(s), cols_d], r.gu_s.at[k], r.gu_r.at[s], d, t
        ).start()
    r.wgu[:, rows(s), cols_d] = r.gu_src[:, :, lanes(s)]
    for m in range(4):
        t = c * 4 + m

        @pl.when(t != s)
        def _():
            remote(
                r.dn_src.at[pl.ds(128 * m, 128)], r.wd.at[rows(z), wide_d],
                r.dn_s.at[m], r.dn_r.at[z], d, t,
            ).start()

        @pl.when(t == s)
        def _():
            r.wd[rows(z), wide_d] = r.dn_src[pl.ds(128 * m, 128), :]

    c_ring = ring_of(r, "c_", d, s, lambda b: r.call.at[b])

    for zz in range(4):
        ring.wait_side(zz)

    @pl.when(home == dx)
    def _():
        arrived(r.wqkv, r.qp_r.at[0], d, s)
        remote(half_qkv(0), half_qkv(0), r.qp_s.at[2], r.qp_r.at[1], dy, s).start()

    @pl.when(home == dy)
    def _():
        arrived(r.wqkv, r.qp_r.at[0], d, s)
        remote(half_qkv(1), half_qkv(1), r.qp_s.at[2], r.qp_r.at[2], dx, s).start()

    @pl.when(home == 3 - d)
    def _():
        arrived(half_qkv(0), r.qp_r.at[1], d, s)
        arrived(half_qkv(1), r.qp_r.at[2], d, s)

    def project(i, carry):
        pick = rows(i, 256)
        pre = dot(r.xall[pl.ds(2 * i, 2)].reshape(256, 1024), r.wqkv[...])
        cs, sn = r.cosine[pick, :], r.sine[pick, :]
        qp, kp = pre[:, :128], pre[:, 128:256]
        r.q_all[pick, :] = (qp * cs + partner(qp) * sn).astype(low)
        r.k_all[pick, :] = (kp * cs + partner(kp) * sn).astype(low)
        r.v_all[pick, :] = pre[:, 256:].astype(low)
        return carry

    lax.fori_loop(0, 4, project, 0)
    wo_ring.lane_step(1)

    def tables(pick, first, count):
        seg_col, var_col = r.idc[pick, 0:1], r.idc[pick, 2:3]
        q_place = first + lax.broadcasted_iota(jnp.int32, (count, 1), 0)
        k_place = lax.broadcasted_iota(jnp.int32, (1, 1024), 1)
        allowed = (seg_col == r.keyrow[1:2, :]) | (q_place == k_place)
        return allowed, var_col == r.keyrow[2:3, :]

    def scores_of(qh, h, same):
        scores = dot_nt(qh, r.k_all[...]) * 0.125
        return scores + jnp.where(same, r.same_bias[2 * pair + h], r.cross_bias[2 * pair + h])

    def attend(b, carry):
        pick = rows(b)
        allowed, same = tables(pick, b * 128, 128)
        q_block = r.q_all[pick, :]
        attended, total_lse = None, None
        for h in range(2):
            mine = head_lanes(h)
            qh = jnp.where(mine, q_block, jnp.zeros_like(q_block))
            scores = jnp.where(allowed, scores_of(qh, h, same), NEG)
            top = jnp.max(scores, axis=-1, keepdims=True)
            e = jnp.exp(scores - top)
            total = jnp.sum(e, axis=-1, keepdims=True)
            part = dot((e * (1.0 / total)).astype(low), r.v_all[...])
            one = top + jnp.log(total)
            attended = part if h == 0 else jnp.where(mine, part, attended)
            total_lse = one if h == 0 else jnp.where(mine, one, total_lse)
        r.head_out[b] = attended.astype(low)
        r.lse[pick, :] = jnp.broadcast_to(total_lse, (128, 128))
        return carry

    def send_mixed(t):
        @pl.when(t != s)
        def _():
            remote(r.head_out.at[t], r.mixed.at[pair], r.m_s.at[t], r.m_r.at[s], d, t).start()

        @pl.when(t == s)
        def _():
            r.mixed[pair] = r.head_out[t]

    gu_plane = Plane(
        d, s, lambda i: r.wgu.at[:, :, lanes(i)], lambda i, n: r.wgu.at[n, :, lanes(i)],
        r.pl_s.at[0], r.pl_r.at[0],
    )
    dn_plane = Plane(
        d, s, lambda i: r.wd.at[:, wide_of(i)], lambda i, n: r.wd.at[pl.ds(256 * n, 256), wide_of(i)],
        r.pl_s.at[1], r.pl_r.at[1],
    )
    wo_lane = r.wo.reshape(4, 2, 128, 1024)
    wo_plane = Plane(
        d, s, lambda i: wo_lane.at[:, c, :, wide_of(i)],
        lambda i, n: wo_lane.at[pl.ds(2 * n, 2), c, :, wide_of(i)],
        r.pl_s.at[2], r.pl_r.at[2],
    )
    wo_side = lambda: remote(
        wo_lane.at[:, c], wo_lane.at[:, c], r.wos_s, r.wos_r, d, sibling
    )

    lax.fori_loop(0, 2, attend, 0)
    send_mixed(0)
    send_mixed(1)
    wo_ring.lane_step(2)
    lax.fori_loop(2, 4, attend, 0)
    send_mixed(2)
    send_mixed(3)
    wo_ring.lane_step(3)
    wo_plane.start()
    c_ring.start()
    lax.fori_loop(4, 6, attend, 0)
    send_mixed(4)
    send_mixed(5)
    lax.fori_loop(6, 8, attend, 0)
    send_mixed(6)
    send_mixed(7)
    wo_plane.step()
    for k in range(1, 8):
        t = lax.rem(s + k, 8)
        arrived(r.wgu.at[:, rows(t), cols_d], r.gu_r.at[t], d, s)
    gu_plane.start()
    c_ring.step(1)
    for j in range(4):

        @pl.when(2 * j + s // 4 != s)
        def _():
            arrived(r.wd.at[pl.ds(128 * j, 128), wide_d], r.dn_r.at[j], d, s)

    dn_plane.start()
    wo_plane.finish()
    wo_side().start()
    c_ring.step(2)
    for t in range(8):

        @pl.when(t != s)
        def _():
            arrived(r.mixed.at[pair_of(t)], r.m_r.at[t], d, s)

    arrived(wo_lane.at[:, 1 - c], r.wos_r, d, s)

    joined = jnp.concatenate([r.mixed[p] for p in range(8)], axis=1)
    middle = r.tokens[0].astype(wide) + dot(joined, r.wo[...].reshape(1024, 1024))
    r.sall[s] = (middle * row_norm(middle) * gain_two).astype(low)
    ring = ring_of(r, "y_", d, s, lambda b: r.sall.at[b])
    ring.start()
    r.mid[...] = middle
    gu_plane.step()
    c_ring.step(3)
    dn_plane.step()
    c_ring.finish()
    gu_plane.finish()
    dn_plane.finish()

    grads = scatter_of(r, "g_", d, s)
    outs = scatter_of(r, "o_", d, s)
    for j in range(4):
        zj = chip_order(z, j)
        if j > 0:
            arrived(ring.block(zj), r.y_r.at[zj], d, s)

            @pl.when((zj < z) & (z < 3))
            def _():
                ring.up(zj).start()

            @pl.when((zj > z) & (z > 0))
            def _():
                ring.down(zj).start()

            ring.side(zj).start()
        ring.wait_side(zj)
        pick = rows(zj, 256)
        block = r.sall[pl.ds(2 * zj, 2)].reshape(256, 1024)
        gate_pre = dot(block, r.wgu[0])
        up_pre = dot(block, r.wgu[1])
        sigma = jax.nn.sigmoid(gate_pre)
        act = gate_pre * sigma
        hidden = (act * up_pre).astype(low)
        r.hid[pick, :] = hidden
        hg = dot_nt(r.call[pl.ds(2 * zj, 2)].reshape(256, 1024), r.wd[...])
        g_low = (hg * up_pre * sigma * (1.0 + gate_pre * (1.0 - sigma))).astype(low)
        u_low = (hg * act).astype(low)
        r.gg[pick, :] = g_low
        r.ug[pick, :] = u_low
        grads.give(j, zj, dot_nt(g_low, r.wgu[0]) + dot_nt(u_low, r.wgu[1]))
        outs.give(j, zj, dot(hidden, r.wd[...]))
        if j > 0:
            last = chip_order(z, j - 1)
            grads.pass_on(j - 1, last)
            outs.pass_on(j - 1, last)
    last = chip_order(z, 3)
    grads.pass_on(3, last)
    outs.pass_on(3, last)

    def weigh(i, carry):
        block = r.sall[:, :, wide_of(i)].reshape(1024, 256)
        r.gu_grad[0, rows(i, 256), :] = dot_tn(block, r.gg[...]).astype(low)
        r.gu_grad[1, rows(i, 256), :] = dot_tn(block, r.ug[...]).astype(low)
        return carry

    lax.fori_loop(0, 4, weigh, 0)
    gu = plane_scatter_of(r, "gu_", d, s, lambda i, n: r.gu_grad.at[n, :, lanes(i)])
    dn = plane_scatter_of(r, "dn_", d, s, lambda i, n: r.dn_grad.at[pl.ds(256 * n, 256), wide_of(i)])
    wo = plane_scatter_of(r, "wp_", d, s, lambda i, n: r.wo_sum.at[pl.ds(2 * n, 2), :, wide_of(i)])
    gu.start()

    def weigh_down(i, carry):
        cols = wide_of(i)
        r.dn_grad[:, cols] = dot_tn(r.hid[...], r.call[:, :, cols].reshape(1024, 256)).astype(low)
        return carry

    lax.fori_loop(0, 4, weigh_down, 0)
    dn.start()

    middle = r.mid[...]
    factor = row_norm(middle)
    normed = middle * factor
    second_grad = grads.total()
    scaled = second_grad * gain_two
    inner = jnp.mean(scaled * normed, axis=-1, keepdims=True)
    r.small[...] = jnp.zeros_like(r.small)
    r.small[1:2, :] = jnp.sum(second_grad * normed, axis=0, keepdims=True)
    value = r.call[s].astype(wide) + factor * (scaled - normed * inner)
    r.mid_grad[...] = value
    v_low = value.astype(low)
    mg = dot_nt(v_low, r.wo[...].reshape(1024, 1024)).astype(low)
    for p in range(8):
        r.mg_src[p] = mg[:, 128 * p : 128 * (p + 1)]
        t = pair_owner(p)

        @pl.when(s != t)
        def _():
            remote(r.mg_src.at[p], r.mgrad.at[s], r.mg_s.at[p], r.mg_r.at[s], d, t).start()

        @pl.when(s == t)
        def _():
            r.mgrad[s] = r.mg_src[p]

    def weigh_out(i, carry):
        left = jnp.concatenate([r.mixed[2 * i], r.mixed[2 * i + 1]], axis=1)
        part = dot_tn(left, v_low).astype(low)
        r.wo_grad[i, 0] = part[:128]
        r.wo_grad[i, 1] = part[128:]
        return carry

    lax.fori_loop(0, 4, weigh_out, 0)
    side = remote(r.wo_grad.at[:, 1 - c], r.wo_in2, r.side_s, r.side_r, d, sibling)
    side.start()
    r.dk[...] = jnp.zeros_like(r.dk)
    r.dv[...] = jnp.zeros_like(r.dv)
    r.bsum[...] = jnp.zeros_like(r.bsum)
    gu.step()
    for k in range(1, 8):
        t = lax.rem(s + k, 8)
        arrived(r.mgrad.at[t], r.mg_r.at[t], d, s)

    def unturn(x, pick):
        return x * r.cosine[pick, :] - partner(x) * r.sine[pick, :]

    def attend_back(b):
        pick = rows(b, 256)
        allowed, same = tables(pick, b * 256, 256)
        q_block = r.q_all[pick, :]
        m_block = r.mgrad[pl.ds(2 * b, 2)].reshape(256, 128)
        dq = None
        for h in range(2):
            mine = head_lanes(h)
            qh = jnp.where(mine, q_block, jnp.zeros_like(q_block))
            mh = jnp.where(mine, m_block, jnp.zeros_like(m_block))
            scores = scores_of(qh, h, same) - r.lse[pick, 64 * h : 64 * h + 1]
            p = jnp.exp(jnp.where(allowed, scores, NEG))
            pg = dot_nt(mh, r.v_all[...])
            inner = jnp.sum(p * pg, axis=-1, keepdims=True)
            ds = (p * (pg - inner)).astype(low)
            ds_wide = ds.astype(wide)
            r.bsum[2 * h : 2 * h + 1, :] += jnp.sum(jnp.where(same, ds_wide, 0.0), axis=0, keepdims=True)
            r.bsum[2 * h + 1 : 2 * h + 2, :] += jnp.sum(jnp.where(same, 0.0, ds_wide), axis=0, keepdims=True)
            one = dot(ds, r.k_all[...]) * 0.125
            dq = one if h == 0 else jnp.where(mine, one, dq)
            r.dk[...] += dot_tn(ds, qh)
            r.dv[...] += dot_tn(p.astype(low), mh)
        r.gr[pick, 0:128] = unturn(dq, pick).astype(low)

    def send_gu(n):
        r.gu_sum[n] = gu.total(n).astype(low)
        for k in range(1, 8):
            t = lax.rem(s + k, 8)
            remote(
                r.gu_sum.at[n, rows(t)], r.gu_rx.at[n, s], r.guz_s.at[n, k], r.guz_r.at[n, s], d, t
            ).start()
        r.gu_rx[n, s] = r.gu_sum[n, rows(s), :]

    def send_dn():
        for j in range(4):
            t = 2 * j + s // 4

            @pl.when(t != s)
            def _():
                remote(
                    r.dn_sum.at[pl.ds(128 * j, 128)], r.dn_rx.at[lax.rem(s, 4)], r.dnz_s.at[j],
                    r.dnz_r.at[lax.rem(s, 4)], d, t,
                ).start()

            @pl.when(t == s)
            def _():
                r.dn_rx[lax.rem(s, 4)] = r.dn_sum[pl.ds(128 * j, 128), :]

    attend_back(0)
    side.wait_recv()
    for b in range(4):
        r.wo_sum[b] = (r.wo_grad[b, c].astype(wide) + r.wo_in2[b].astype(wide)).astype(low)
    wo.start()
    dn.step()
    send_gu(0)
    send_gu(1)
    attend_back(1)
    for n in range(2):
        r.dn_sum[pl.ds(256 * n, 256), :] = dn.total(n).astype(low)
    send_dn()
    attend_back(2)
    wo.step()
    attend_back(3)
    for n in range(2):
        r.wo_fin[pl.ds(2 * n, 2)] = wo.total(n).astype(low)
    for k in range(1, 4):
        t = lax.rem(z + k, 4)
        remote(r.wo_fin.at[t], r.wo_rx.at[z], r.woz_s.at[t], r.woz_r.at[z], d, 2 * t + c).start()

    def turn(b, carry):
        pick = rows(b, 256)
        r.gr[pick, 128:256] = unturn(r.dk[pick, :] * 0.125, pick).astype(low)
        r.gr[pick, 256:384] = r.dv[pick, :].astype(low)
        return carry

    lax.fori_loop(0, 4, turn, 0)
    grads.drain()
    for j in range(4):
        zj = lax.rem(z + 3 - j, 4)
        grads.give(j, zj, dot_nt(r.gr[rows(zj, 256), :], r.wqkv[...]))
        if j > 0:
            grads.pass_on(j - 1, lax.rem(z + 4 - j, 4))
    grads.pass_on(3, z)

    def weigh_qkv(i, carry):
        block = r.xall[:, :, wide_of(i)].reshape(1024, 256)
        value = dot_tn(block, r.gr[...]).astype(low)
        r.qkv_grad[2 * i] = value[:128]
        r.qkv_grad[2 * i + 1] = value[128:]
        return carry

    lax.fori_loop(0, 4, weigh_qkv, 0)
    for k in range(1, 4):
        t = lax.rem(d + k, 4)
        for m in range(2):
            remote(
                r.qkv_grad.at[t + 4 * m], r.q_in.at[d, m], r.qg_s.at[t, m], r.qg_r.at[d, m], t, s
            ).start()
    r.out[0] = (r.mid[...] + outs.total()).astype(low)

    for m in range(2):
        value = r.qkv_grad[d + 4 * m].astype(wide)
        for k in range(1, 4):
            t = lax.rem(d + k, 4)
            arrived(r.q_in.at[t, m], r.qg_r.at[t, m], d, s)
            value = value + r.q_in[t, m].astype(wide)
        r.q_sum[m] = value.astype(low)
        target = d + 4 * m
        mine = (target == s) & is_home

        @pl.when(jnp.logical_not(mine))
        def _():
            remote(
                r.q_sum.at[m], r.q_rx.at[z // 2], r.qz_s.at[m], r.qz_r.at[z // 2], home, target
            ).start()

        @pl.when(mine)
        def _():
            r.q_rx[z // 2] = r.q_sum[m]

    value = r.tokens[0].astype(wide)
    factor = row_norm(value)
    normed = value * factor
    first_grad = grads.total()
    scaled = first_grad * gain_one
    inner = jnp.mean(scaled * normed, axis=-1, keepdims=True)

    r.small[0:1, :] = jnp.sum(first_grad * normed, axis=0, keepdims=True)
    place = lax.broadcasted_iota(jnp.int32, (1, 1024), 1)
    line = jnp.zeros((1, 1024), wide)
    for h in range(2):
        for n in range(2):
            k = 2 * h + n
            one = jnp.sum(r.bsum[k : k + 1, :], axis=1, keepdims=True)
            line = line + jnp.where(place == 128 * n + 2 * pair + h, one, 0.0)
    r.small[2:3, :] = line
    for k in range(1, 4):
        t = lax.rem(d + k, 4)
        remote(r.small, r.small_p.at[d], r.sp_s.at[k], r.sp_r.at[d], t, s).start()
    r.tok_grad[0] = (r.mid_grad[...] + factor * (scaled - normed * inner)).astype(low)
    for k in range(1, 4):
        t = lax.rem(d + k, 4)
        arrived(r.small_p.at[t], r.sp_r.at[t], d, s)
    r.small_p[d] = r.small[...]
    r.small_q[...] = r.small_p[0] + r.small_p[1] + r.small_p[2] + r.small_p[3]
    for k in range(1, 8):
        t = lax.rem(s + k, 8)
        remote(r.small_q, r.small_z.at[s], r.sz_s.at[k], r.sz_r.at[s], d, t).start()
    r.small_z[s] = r.small_q[...]

    for k in range(1, 8):
        t = lax.rem(s + k, 8)
        for n in range(2):
            arrived(r.gu_rx.at[n, t], r.guz_r.at[n, t], d, s)
    for m in range(4):

        @pl.when(4 * c + m != s)
        def _():
            arrived(r.dn_rx.at[m], r.dnz_r.at[m], d, s)

    r.wo_rx[z] = r.wo_fin[z]
    for k in range(1, 4):
        t = lax.rem(z + k, 4)
        arrived(r.wo_rx.at[t], r.woz_r.at[t], d, s)
    for i in range(2):

        @pl.when((owner[i] != s) | (lax.rem(s, 4) != d))
        def _():
            arrived(r.q_rx.at[i], r.qz_r.at[i], d, s)

    for k in range(1, 8):
        t = lax.rem(s + k, 8)
        arrived(r.small_z.at[t], r.sz_r.at[t], d, s)

    ring_of(r, "x_", d, s, lambda b: r.xall.at[b]).drain()
    ring.drain()
    wo_ring.lane_drain()
    wo_side().wait_send()
    for i in range(2):

        @pl.when(owner[i] != s)
        def _():
            sent(r.qkv_src.at[i], r.qs_s.at[i], d, s)

    for k in range(1, 8):
        sent(r.ids, r.id_s.at[k], d, s)
        sent(r.gu_src.at[:, :, pl.ds(0, 128)], r.gu_s.at[k], d, s)

    @pl.when(is_home)
    def _():
        sent(r.wqkv, r.qp_s.at[0], d, s)
        sent(r.wqkv, r.qp_s.at[1], d, s)

    @pl.when((home == dx) | (home == dy))
    def _():
        sent(half_qkv(0), r.qp_s.at[2], d, s)

    for m in range(4):

        @pl.when(c * 4 + m != s)
        def _():
            sent(r.dn_src.at[pl.ds(128 * m, 128)], r.dn_s.at[m], d, s)

    for t in range(8):

        @pl.when(t != s)
        def _():
            sent(r.head_out.at[t], r.m_s.at[t], d, s)

        @pl.when(s != pair_owner(t))
        def _():
            sent(r.mg_src.at[t], r.mg_s.at[t], d, s)

    side.wait_send()
    gu.drain()
    dn.drain()
    wo.drain()
    grads.drain()
    outs.drain()
    for k in range(1, 8):
        for n in range(2):
            sent(r.gu_sum.at[n, rows(0)], r.guz_s.at[n, k], d, s)
        sent(r.small_q, r.sz_s.at[k], d, s)
    for j in range(4):

        @pl.when(2 * j + s // 4 != s)
        def _():
            sent(r.dn_sum.at[pl.ds(0, 128)], r.dnz_s.at[j], d, s)

    for k in range(1, 4):
        t = lax.rem(z + k, 4)
        sent(r.wo_fin.at[t], r.woz_s.at[t], d, s)
        t = lax.rem(d + k, 4)
        for m in range(2):
            sent(r.q_sum.at[m], r.qg_s.at[t, m], d, s)
        sent(r.small, r.sp_s.at[k], d, s)
    for m in range(2):

        @pl.when(jnp.logical_not((d + 4 * m == s) & is_home))
        def _():
            sent(r.q_sum.at[m], r.qz_s.at[m], d, s)


def vmem():
    return pl.BlockSpec(memory_space=pltpu.VMEM)


def smem():
    return pl.BlockSpec(memory_space=pltpu.SMEM)


def shape(*dims, kind=low):
    return jax.ShapeDtypeStruct(dims, kind)


def dma(*dims):
    return pltpu.SemaphoreType.DMA(dims)


def layer(ins):
    outs = {
        "out": shape(1, 128, 1024),
        "tok_grad": shape(1, 128, 1024),
        "gu_rx": shape(2, 8, 128, 128),
        "dn_rx": shape(4, 128, 256),
        "wo_rx": shape(4, 128, 256),
        "q_rx": shape(2, 128, 384),
        "small_z": shape(8, 8, 1024, kind=wide),
    }
    scratch = {
        "xall": pltpu.VMEM((8, 128, 1024), low),
        "q_all": pltpu.VMEM((1024, 128), low),
        "k_all": pltpu.VMEM((1024, 128), low),
        "v_all": pltpu.VMEM((1024, 128), low),
        "lse": pltpu.VMEM((1024, 128), wide),
        "wqkv": pltpu.VMEM((1024, 384), low),
        "wo": pltpu.VMEM((8, 128, 1024), low),
        "wgu": pltpu.VMEM((2, 1024, 512), low),
        "wd": pltpu.VMEM((512, 1024), low),
        "call": pltpu.VMEM((8, 128, 1024), low),
        "ids": pltpu.VMEM((8, 128), wide),
        "idr": pltpu.VMEM((8, 8, 128), wide),
        "idc": pltpu.VMEM((1024, 128), wide),
        "keyrow": pltpu.VMEM((8, 1024), wide),
        "cosine": pltpu.VMEM((1024, 128), wide),
        "sine": pltpu.VMEM((1024, 128), wide),
        "mixed": pltpu.VMEM((8, 128, 128), low),
        "qkv_src": pltpu.VMEM((2, 128, 384), low),
        "gu_src": pltpu.VMEM((2, 128, 1024), low),
        "dn_src": pltpu.VMEM((512, 256), low),
        "head_out": pltpu.VMEM((8, 128, 128), low),
        "sall": pltpu.VMEM((8, 128, 1024), low),
        "gg": pltpu.VMEM((1024, 512), low),
        "ug": pltpu.VMEM((1024, 512), low),
        "hid": pltpu.VMEM((1024, 512), low),
        "mid": pltpu.VMEM((128, 1024), wide),
        "mid_grad": pltpu.VMEM((128, 1024), wide),
        "mg_src": pltpu.VMEM((8, 128, 128), low),
        "mgrad": pltpu.VMEM((8, 128, 128), low),
        "gu_grad": pltpu.VMEM((2, 1024, 512), low),
        "dn_grad": pltpu.VMEM((512, 1024), low),
        "wo_grad": pltpu.VMEM((4, 2, 128, 1024), low),
        "dk": pltpu.VMEM((1024, 128), wide),
        "dv": pltpu.VMEM((1024, 128), wide),
        "gr": pltpu.VMEM((1024, 384), low),
        "bsum": pltpu.VMEM((8, 1024), wide),
        "qkv_grad": pltpu.VMEM((8, 128, 384), low),
        "wo_in2": pltpu.VMEM((4, 128, 1024), low),
        "wo_sum": pltpu.VMEM((4, 128, 1024), low),
        "gu_sum": pltpu.VMEM((2, 1024, 128), low),
        "dn_sum": pltpu.VMEM((512, 256), low),
        "wo_fin": pltpu.VMEM((4, 128, 256), low),
        "q_in": pltpu.VMEM((4, 2, 128, 384), low),
        "q_sum": pltpu.VMEM((2, 128, 384), low),
        "small": pltpu.VMEM((8, 1024), wide),
        "small_p": pltpu.VMEM((4, 8, 1024), wide),
        "small_q": pltpu.VMEM((8, 1024), wide),
        **scatter_scratch("g_"),
        **scatter_scratch("o_"),
        **plane_scratch("gu_", 1024, 128),
        **plane_scratch("dn_", 256, 256),
        **plane_scratch("wp_", 2, 128, 256),
        **ring_scratch("x_"),
        **ring_scratch("y_"),
        **ring_scratch("c_"),
        **ring_scratch("wo_"),
        "qs_s": dma(2), "qs_r": dma(8), "qp_s": dma(3), "qp_r": dma(3),
        "id_s": dma(8), "id_r": dma(8), "gu_s": dma(8), "gu_r": dma(8),
        "dn_s": dma(4), "dn_r": dma(4), "pl_s": dma(3, 4), "pl_r": dma(3, 4),
        "wos_s": dma(), "wos_r": dma(), "m_s": dma(8), "m_r": dma(8),
        "mg_s": dma(8), "mg_r": dma(8), "side_s": dma(), "side_r": dma(),
        "guz_s": dma(2, 8), "guz_r": dma(2, 8), "dnz_s": dma(4), "dnz_r": dma(4),
        "woz_s": dma(4), "woz_r": dma(4), "qg_s": dma(4, 2), "qg_r": dma(4, 2),
        "qz_s": dma(2), "qz_r": dma(2), "sp_s": dma(8), "sp_r": dma(4),
        "sz_s": dma(8), "sz_r": dma(8),
    }
    names = (*ins, *outs, *scratch)
    got = pl.pallas_call(
        functools.partial(layer_kernel, names),
        name="whole",
        out_shape=tuple(outs.values()),
        in_specs=[smem() if n in ("same_bias", "cross_bias") else vmem() for n in ins],
        out_specs=[vmem()] * len(outs),
        scratch_shapes=list(scratch.values()),
        compiler_params=pltpu.CompilerParams(
            collective_id=0, has_side_effects=True, vmem_limit_bytes=64 << 20
        ),
    )(*ins.values())
    return dict(zip(outs, got))


def finish_kernel(
    out, tok_grad, gu, dn, wo, qkv, small,
    out2, tok2, gate2, up2, dn2, wo2, q2, k2, v2, g1, g2, same, cross,
):
    out2[...] = out[...]
    tok2[...] = tok_grad[...]
    for t in range(8):
        gate2[:, 128 * t : 128 * (t + 1)] = gu[0, t].astype(wide)
        up2[:, 128 * t : 128 * (t + 1)] = gu[1, t].astype(wide)
    for m in range(4):
        dn2[128 * m : 128 * (m + 1), :] = dn[m].astype(wide)
    total = wo[0].astype(wide)
    for m in range(1, 4):
        total = total + wo[m].astype(wide)
    wo2[...] = total
    for n, ref in enumerate((q2, k2, v2)):
        for i in range(2):
            ref[:, 128 * i : 128 * (i + 1)] = qkv[i, :, 128 * n : 128 * (n + 1)].astype(wide)
    total = small[0]
    for t in range(1, 8):
        total = total + small[t]
    g1[...] = total[0:1]
    g2[...] = total[1:2]
    same[...] = total[2:3, 0:128]
    cross[...] = total[2:3, 128:256]


def finish(got):
    order = ("out", "tok_grad", "gu_rx", "dn_rx", "wo_rx", "q_rx", "small_z")
    outs = (
        shape(1, 128, 1024), shape(1, 128, 1024),
        shape(128, 1024, kind=wide), shape(128, 1024, kind=wide), shape(512, 256, kind=wide),
        shape(128, 256, kind=wide), shape(128, 256, kind=wide), shape(128, 256, kind=wide),
        shape(128, 256, kind=wide), shape(1, 1024, kind=wide), shape(1, 1024, kind=wide),
        shape(1, 128, kind=wide), shape(1, 128, kind=wide),
    )
    return pl.pallas_call(
        finish_kernel,
        name="finish",
        out_shape=outs,
        in_specs=[vmem()] * 7,
        out_specs=[vmem()] * len(outs),
    )(*(got[n] for n in order))


def rope_rates():
    rates = np.float32(10000.0) ** (-np.arange(32, dtype=np.float32) * np.float32(2.0 / 64))
    return np.tile(rates.astype(np.float32), 4)[None]


def fast_body(
    tokens, attn_gain, query_weight, key_weight, value_weight, out_weight, same_bias, cross_bias,
    ffn_gain, gate_weight, up_weight, down_weight, segment_ids, variate_ids, time_ids, observed,
    cotangent,
):
    got = layer({
        "tokens": tokens, "attn_gain": attn_gain, "ffn_gain": ffn_gain,
        "wq": query_weight, "wk": key_weight, "wv": value_weight, "wo_in": out_weight,
        "wg_in": gate_weight, "wu_in": up_weight, "wd_in": down_weight,
        "same_bias": same_bias, "cross_bias": cross_bias, "segment": segment_ids,
        "freq": rope_rates(), "variate": variate_ids, "moment": time_ids, "observed": observed, "cot": cotangent,
    })
    out, tok, gate, up, dn, wo, q, k, v, g1, g2, same, cross = finish(got)
    return (
        out, tok, g1[0], q, k, v, wo, same[0, 0:16], cross[0, 0:16], g2[0], gate, up, dn,
    )


def fits(mesh):
    return mesh.shape["dp"] == 4 and mesh.shape["seq"] == 8


def solution(mesh):
    in_specs = (
        P("dp", "seq", None),
        P(),
        P("seq", "dp"),
        P("seq", "dp"),
        P("seq", "dp"),
        P("seq", "dp"),
        P(),
        P(),
        P(),
        P("seq", "dp"),
        P("seq", "dp"),
        P("seq", "dp"),
        P("dp", "seq"),
        P("dp", "seq"),
        P("dp", "seq"),
        P("dp", "seq"),
        P("dp", "seq", None),
    )
    out_specs = (
        P("dp", "seq", None),
        P("dp", "seq", None),
        P(),
        P("seq", "dp"),
        P("seq", "dp"),
        P("seq", "dp"),
        P("seq", "dp"),
        P(),
        P(),
        P(),
        P("seq", "dp"),
        P("seq", "dp"),
        P("seq", "dp"),
    )
    part = fast_body if fits(mesh) else body
    return jax.shard_map(part, mesh=mesh, in_specs=in_specs, out_specs=out_specs, check_vma=False)
```

```python
import functools
import types

import jax
import jax.numpy as jnp
import numpy as np
from jax import lax
from jax.experimental import pallas as pl
from jax.experimental.pallas import tpu as pltpu
from jax.sharding import PartitionSpec as P

epsilon = 1e-06


def product(left_side, right_side):
    return jnp.dot(left_side, right_side, preferred_element_type=jnp.float32)


def contract_rows(left_side, right_side):
    return lax.dot_general(
        left_side, right_side, (((0,), (0,)), ((), ())), preferred_element_type=jnp.float32
    )


def contract_cols(left_side, right_side):
    return lax.dot_general(
        left_side, right_side, (((1,), (1,)), ((), ())), preferred_element_type=jnp.float32
    )


def angles_of(moments, head_width):
    half_width = head_width // 2
    powers = jnp.arange(half_width).astype(jnp.float32) * (2.0 / head_width)
    return moments.astype(jnp.float32)[:, None] * (10000.0 ** (-powers))[None, :]


def rotate(values, angles, head_count):
    row_count, model_width = values.shape
    shaped = values.reshape(row_count, head_count, model_width // head_count)
    half_width = model_width // head_count // 2
    first_half = shaped[..., :half_width]
    second = shaped[..., half_width:]
    cosine = jnp.cos(angles)[:, None, :]
    sine_part = jnp.sin(angles)[:, None, :]
    turned = jnp.concatenate(
        [first_half * cosine - second * sine_part, second * cosine + first_half * sine_part],
        axis=-1,
    )
    return turned.reshape(row_count, model_width)


def normalize(values, gain_row):
    factor = lax.rsqrt(jnp.mean(values * values, axis=-1, keepdims=True) + epsilon)
    normed = values * factor
    return (normed, factor, normed * gain_row)


def norm_back(incoming, normed, factor, gain_row):
    scaled = incoming * gain_row
    inner_sum = jnp.mean(scaled * normed, axis=-1, keepdims=True)
    return (factor * (scaled - normed * inner_sum), jnp.sum(incoming * normed, axis=0))


def make_tables(segment, variate, key_segment, key_variate, first_row):
    query_place = first_row + jnp.arange(segment.shape[0])
    key_place = jnp.arange(key_segment.shape[0])
    allowed = (segment.astype(jnp.float32)[:, None] == key_segment.astype(jnp.float32)[None, :]) | (
        query_place[:, None] == key_place[None, :]
    )
    same_kind = variate.astype(jnp.float32)[:, None] == key_variate.astype(jnp.float32)[None, :]
    return (allowed, same_kind)


def block_scores(
    block_index, query_low, keys_all, same_kind, same_bias, cross_bias, head_group, head_width
):
    block_width = head_group * head_width
    query_block = lax.dynamic_slice_in_dim(
        query_low, block_index * block_width, block_width, 1
    ).reshape(query_low.shape[0], head_group, head_width)
    key_block = lax.dynamic_slice_in_dim(
        keys_all, block_index * block_width, block_width, 1
    ).reshape(keys_all.shape[0], head_group, head_width)
    raw_scores = jnp.einsum(
        "thd,shd->hts", query_block, key_block, preferred_element_type=jnp.float32
    )
    same_part = lax.dynamic_slice_in_dim(same_bias, block_index * head_group, head_group)
    cross_part = lax.dynamic_slice_in_dim(cross_bias, block_index * head_group, head_group)
    offset = jnp.where(same_kind[None], same_part[:, None, None], cross_part[:, None, None])
    return (raw_scores * head_width ** (-0.5) + offset, query_block, key_block)


def body(
    tokens,
    attn_gain,
    query_weight,
    key_weight,
    value_weight,
    out_weight,
    same_bias,
    cross_bias,
    ffn_gain,
    gate_weight,
    up_weight,
    down_weight,
    segment_ids,
    variate_ids,
    time_ids,
    observed,
    cotangent,
):
    row_count = tokens.shape[1]
    model_width = tokens.shape[2]
    head_count = same_bias.shape[0]
    head_width = model_width // head_count
    head_group = max(1, 128 // head_width)
    block_width = head_group * head_width
    block_total = head_count // head_group
    scaling = head_width ** (-0.5)
    first_row = lax.axis_index("seq") * row_count
    gain_one = attn_gain.astype(jnp.bfloat16).astype(jnp.float32)
    gain_two = ffn_gain.astype(jnp.bfloat16).astype(jnp.float32)
    low_masters = (
        query_weight.astype(jnp.bfloat16),
        key_weight.astype(jnp.bfloat16),
        value_weight.astype(jnp.bfloat16),
        out_weight.astype(jnp.bfloat16),
        gate_weight.astype(jnp.bfloat16),
        up_weight.astype(jnp.bfloat16),
        down_weight.astype(jnp.bfloat16),
    )
    row_parts = (
        lax.all_gather(low_masters[0], "seq", axis=0, tiled=True),
        lax.all_gather(low_masters[1], "seq", axis=0, tiled=True),
        lax.all_gather(low_masters[2], "seq", axis=0, tiled=True),
        lax.all_gather(low_masters[3], "seq", axis=0, tiled=True),
        lax.all_gather(low_masters[4], "seq", axis=0, tiled=True),
        lax.all_gather(low_masters[5], "seq", axis=0, tiled=True),
        lax.all_gather(low_masters[6], "seq", axis=0, tiled=True),
    )
    gathered = (
        lax.all_gather(row_parts[0], "dp", axis=1, tiled=True),
        lax.all_gather(row_parts[1], "dp", axis=1, tiled=True),
        lax.all_gather(row_parts[2], "dp", axis=1, tiled=True),
        lax.all_gather(row_parts[3], "dp", axis=1, tiled=True),
        lax.all_gather(row_parts[4], "dp", axis=1, tiled=True),
        lax.all_gather(row_parts[5], "dp", axis=1, tiled=True),
        lax.all_gather(row_parts[6], "dp", axis=1, tiled=True),
    )
    w_query, w_key, w_value, w_out, w_gate, w_up, w_down = gathered
    inputs = tokens[0].astype(jnp.float32)
    segment = segment_ids[0]
    variate = variate_ids[0]
    seen_row = observed[0]
    angles = angles_of(time_ids[0], head_width)
    normed_one, factor_one, scaled_one = normalize(inputs, gain_one)
    first_low = scaled_one.astype(jnp.bfloat16)
    query_low = rotate(product(first_low, w_query), angles, head_count).astype(jnp.bfloat16)
    key_low = rotate(product(first_low, w_key), angles, head_count).astype(jnp.bfloat16)
    value_low = product(first_low, w_value).astype(jnp.bfloat16)
    key_segment = jnp.where(seen_row == 1, segment, -1).astype(jnp.bfloat16)
    key_variate = variate.astype(jnp.bfloat16)
    keys_all, values_all, segments_all, variates_all = (
        lax.all_gather(key_low, "seq", axis=0, tiled=True),
        lax.all_gather(value_low, "seq", axis=0, tiled=True),
        lax.all_gather(key_segment, "seq", axis=0, tiled=True),
        lax.all_gather(key_variate, "seq", axis=0, tiled=True),
    )
    length = keys_all.shape[0]
    allowed, same_kind = make_tables(segment, variate, segments_all, variates_all, first_row)

    def forward_block(block_index, state_now):
        mixed, summary = state_now
        scores, query_block, key_block = block_scores(
            block_index,
            query_low,
            keys_all,
            same_kind,
            same_bias,
            cross_bias,
            head_group,
            head_width,
        )
        row_top = jnp.max(jnp.where(allowed[None], scores, -jnp.inf), axis=-1, keepdims=True)
        exponent = jnp.exp(jnp.where(allowed[None], scores - row_top, -jnp.inf))
        row_total = jnp.sum(exponent, axis=-1, keepdims=True)
        prob_low = (exponent / row_total).astype(jnp.bfloat16)
        value_block = lax.dynamic_slice_in_dim(
            values_all, block_index * block_width, block_width, 1
        ).reshape(length, head_group, head_width)
        attended = jnp.einsum(
            "hts,shd->thd", prob_low, value_block, preferred_element_type=jnp.float32
        ).reshape(row_count, block_width)
        mixed = lax.dynamic_update_slice_in_dim(mixed, attended, block_index * block_width, 1)
        summary = lax.dynamic_update_slice_in_dim(
            summary, (row_top + jnp.log(row_total))[..., 0], block_index * head_group, 0
        )
        return (mixed, summary)

    mixed, summary = lax.fori_loop(
        0,
        block_total,
        forward_block,
        (
            jnp.zeros((row_count, model_width), jnp.float32),
            jnp.zeros((head_count, row_count), jnp.float32),
        ),
    )
    mixed_low = mixed.astype(jnp.bfloat16)
    middle = inputs + product(mixed_low, w_out)
    normed_two, factor_two, scaled_two = normalize(middle, gain_two)
    second_low = scaled_two.astype(jnp.bfloat16)
    gate_pre = product(second_low, w_gate)
    up_pre = product(second_low, w_up)
    sigma = jax.nn.sigmoid(gate_pre)
    activated = gate_pre * sigma
    hidden_low = (activated * up_pre).astype(jnp.bfloat16)
    result = middle + product(hidden_low, w_down)
    rows_again = (
        lax.all_gather(low_masters[0], "seq", axis=0, tiled=True),
        lax.all_gather(low_masters[1], "seq", axis=0, tiled=True),
        lax.all_gather(low_masters[2], "seq", axis=0, tiled=True),
        lax.all_gather(low_masters[3], "seq", axis=0, tiled=True),
        lax.all_gather(low_masters[4], "seq", axis=0, tiled=True),
        lax.all_gather(low_masters[5], "seq", axis=0, tiled=True),
        lax.all_gather(low_masters[6], "seq", axis=0, tiled=True),
    )
    regathered = (
        lax.all_gather(rows_again[0], "dp", axis=1, tiled=True),
        lax.all_gather(rows_again[1], "dp", axis=1, tiled=True),
        lax.all_gather(rows_again[2], "dp", axis=1, tiled=True),
        lax.all_gather(rows_again[3], "dp", axis=1, tiled=True),
        lax.all_gather(rows_again[4], "dp", axis=1, tiled=True),
        lax.all_gather(rows_again[5], "dp", axis=1, tiled=True),
        lax.all_gather(rows_again[6], "dp", axis=1, tiled=True),
    )
    w_query, w_key, w_value, w_out, w_gate, w_up, w_down = regathered
    cot_low = cotangent[0]
    hidden_grad = contract_cols(cot_low, w_down)
    down_grad = contract_rows(hidden_low, cot_low)
    gate_grad = (hidden_grad * up_pre * sigma * (1.0 + gate_pre * (1.0 - sigma))).astype(
        jnp.bfloat16
    )
    up_grad = (hidden_grad * activated).astype(jnp.bfloat16)
    gate_w_grad = contract_rows(second_low, gate_grad)
    up_w_grad = contract_rows(second_low, up_grad)
    second_grad = contract_cols(gate_grad, w_gate) + contract_cols(up_grad, w_up)
    middle_part, ffn_gain_grad = norm_back(second_grad, normed_two, factor_two, gain_two)
    middle_grad = cot_low.astype(jnp.float32) + middle_part
    middle_low = middle_grad.astype(jnp.bfloat16)
    out_w_grad = contract_rows(mixed_low, middle_low)
    mixed_grad = contract_cols(middle_low, w_out).astype(jnp.bfloat16)
    keys_back, values_back, segments_back, variates_back = (
        lax.all_gather(key_low, "seq", axis=0, tiled=True),
        lax.all_gather(value_low, "seq", axis=0, tiled=True),
        lax.all_gather(key_segment, "seq", axis=0, tiled=True),
        lax.all_gather(key_variate, "seq", axis=0, tiled=True),
    )
    allowed_back, same_back = make_tables(segment, variate, segments_back, variates_back, first_row)

    def query_side(block_index):
        scores, query_block, key_block = block_scores(
            block_index,
            query_low,
            keys_back,
            same_back,
            same_bias,
            cross_bias,
            head_group,
            head_width,
        )
        lse_block = lax.dynamic_slice_in_dim(summary, block_index * head_group, head_group, 0)
        probabilities = jnp.exp(
            jnp.where(allowed_back[None], scores - lse_block[:, :, None], -jnp.inf)
        )
        grad_block = lax.dynamic_slice_in_dim(
            mixed_grad, block_index * block_width, block_width, 1
        ).reshape(row_count, head_group, head_width)
        value_block = lax.dynamic_slice_in_dim(
            values_back, block_index * block_width, block_width, 1
        ).reshape(length, head_group, head_width)
        prob_grad = jnp.einsum(
            "thd,shd->hts", grad_block, value_block, preferred_element_type=jnp.float32
        )
        inner_sum = jnp.sum(probabilities * prob_grad, axis=-1, keepdims=True)
        score_low = (probabilities * (prob_grad - inner_sum)).astype(jnp.bfloat16)
        score_wide = score_low.astype(jnp.float32)
        same_part = jnp.sum(jnp.where(same_back[None], score_wide, 0.0), axis=(1, 2))
        cross_part = jnp.sum(jnp.where(same_back[None], 0.0, score_wide), axis=(1, 2))
        query_part = (
            jnp.einsum(
                "hts,shd->thd", score_low, key_block, preferred_element_type=jnp.float32
            ).reshape(row_count, block_width)
            * scaling
        )
        return (
            probabilities,
            score_low,
            query_block,
            grad_block,
            inner_sum[..., 0],
            same_part,
            cross_part,
            query_part,
        )

    def backward_block(block_index, state_now):
        query_grad, key_grad, value_grad, same_grad, cross_grad = state_now
        (
            probabilities,
            score_low,
            query_block,
            grad_block,
            inner_sum,
            same_part,
            cross_part,
            query_part,
        ) = query_side(block_index)
        key_part = (
            jnp.einsum(
                "hts,thd->shd", score_low, query_block, preferred_element_type=jnp.float32
            ).reshape(length, block_width)
            * scaling
        )
        value_part = jnp.einsum(
            "hts,thd->shd",
            probabilities.astype(jnp.bfloat16),
            grad_block,
            preferred_element_type=jnp.float32,
        ).reshape(length, block_width)
        query_grad = lax.dynamic_update_slice_in_dim(
            query_grad, query_part, block_index * block_width, 1
        )
        key_grad = lax.dynamic_update_slice_in_dim(key_grad, key_part, block_index * block_width, 1)
        value_grad = lax.dynamic_update_slice_in_dim(
            value_grad, value_part, block_index * block_width, 1
        )
        same_grad = lax.dynamic_update_slice_in_dim(
            same_grad, same_part, block_index * head_group, 0
        )
        cross_grad = lax.dynamic_update_slice_in_dim(
            cross_grad, cross_part, block_index * head_group, 0
        )
        return (query_grad, key_grad, value_grad, same_grad, cross_grad)

    start_state = (
        jnp.zeros((row_count, model_width), jnp.float32),
        jnp.zeros((length, model_width), jnp.float32),
        jnp.zeros((length, model_width), jnp.float32),
        jnp.zeros((head_count,), jnp.float32),
        jnp.zeros((head_count,), jnp.float32),
    )
    query_grad, key_grad, value_grad, same_grad, cross_grad = lax.fori_loop(
        0, block_total, backward_block, start_state
    )
    key_share, value_share = (
        lax.psum_scatter(
            key_grad.astype(jnp.bfloat16), "seq", scatter_dimension=0, tiled=True
        ).astype(jnp.float32),
        lax.psum_scatter(
            value_grad.astype(jnp.bfloat16), "seq", scatter_dimension=0, tiled=True
        ).astype(jnp.float32),
    )
    query_pre_grad = rotate(query_grad, -angles, head_count).astype(jnp.bfloat16)
    key_pre_grad = rotate(key_share, -angles, head_count).astype(jnp.bfloat16)
    value_pre_grad = value_share.astype(jnp.bfloat16)
    query_w_grad = contract_rows(first_low, query_pre_grad)
    key_w_grad = contract_rows(first_low, key_pre_grad)
    value_w_grad = contract_rows(first_low, value_pre_grad)
    first_grad = (
        contract_cols(query_pre_grad, w_query)
        + contract_cols(key_pre_grad, w_key)
        + contract_cols(value_pre_grad, w_value)
    )
    input_part, attn_gain_grad = norm_back(first_grad, normed_one, factor_one, gain_one)
    input_grad = (middle_grad + input_part).astype(jnp.bfloat16)
    col_shares = (
        lax.psum_scatter(
            query_w_grad.astype(jnp.bfloat16), "dp", scatter_dimension=1, tiled=True
        ).astype(jnp.float32),
        lax.psum_scatter(
            key_w_grad.astype(jnp.bfloat16), "dp", scatter_dimension=1, tiled=True
        ).astype(jnp.float32),
        lax.psum_scatter(
            value_w_grad.astype(jnp.bfloat16), "dp", scatter_dimension=1, tiled=True
        ).astype(jnp.float32),
        lax.psum_scatter(
            out_w_grad.astype(jnp.bfloat16), "dp", scatter_dimension=1, tiled=True
        ).astype(jnp.float32),
        lax.psum_scatter(
            gate_w_grad.astype(jnp.bfloat16), "dp", scatter_dimension=1, tiled=True
        ).astype(jnp.float32),
        lax.psum_scatter(
            up_w_grad.astype(jnp.bfloat16), "dp", scatter_dimension=1, tiled=True
        ).astype(jnp.float32),
        lax.psum_scatter(
            down_grad.astype(jnp.bfloat16), "dp", scatter_dimension=1, tiled=True
        ).astype(jnp.float32),
    )
    shares = (
        lax.psum_scatter(
            col_shares[0].astype(jnp.bfloat16), "seq", scatter_dimension=0, tiled=True
        ).astype(jnp.float32),
        lax.psum_scatter(
            col_shares[1].astype(jnp.bfloat16), "seq", scatter_dimension=0, tiled=True
        ).astype(jnp.float32),
        lax.psum_scatter(
            col_shares[2].astype(jnp.bfloat16), "seq", scatter_dimension=0, tiled=True
        ).astype(jnp.float32),
        lax.psum_scatter(
            col_shares[3].astype(jnp.bfloat16), "seq", scatter_dimension=0, tiled=True
        ).astype(jnp.float32),
        lax.psum_scatter(
            col_shares[4].astype(jnp.bfloat16), "seq", scatter_dimension=0, tiled=True
        ).astype(jnp.float32),
        lax.psum_scatter(
            col_shares[5].astype(jnp.bfloat16), "seq", scatter_dimension=0, tiled=True
        ).astype(jnp.float32),
        lax.psum_scatter(
            col_shares[6].astype(jnp.bfloat16), "seq", scatter_dimension=0, tiled=True
        ).astype(jnp.float32),
    )
    small_totals = lax.psum((same_grad, cross_grad, attn_gain_grad, ffn_gain_grad), ("dp", "seq"))
    return (
        result.astype(jnp.bfloat16)[None],
        input_grad[None],
        small_totals[2],
        shares[0],
        shares[1],
        shares[2],
        shares[3],
        small_totals[0],
        small_totals[1],
        small_totals[3],
        shares[4],
        shares[5],
        shares[6],
    )


MESH = pl.DeviceIdType.MESH
NEG = -1e30
low = jnp.bfloat16
wide = jnp.float32

def remote(src, dst, send_sem, recv_sem, d, s):
    return pltpu.make_async_remote_copy(
        src_ref=src,
        dst_ref=dst,
        send_sem=send_sem,
        recv_sem=recv_sem,
        device_id=(d, s),
        device_id_type=MESH,
    )


def arrived(dst, recv_sem, d, s):
    remote(dst, dst, recv_sem, recv_sem, d, s).wait_recv()


def sent(src, send_sem, d, s):
    remote(src, src, send_sem, send_sem, d, s).wait_send()


def pair_of(s):
    z = s // 2
    c = lax.rem(s, 2)
    return 2 * (2 * c + lax.rem(z, 2)) + z // 2


class Chain:
    def __init__(self, d, s, view, up_sem, recv_sem, side_sem, side_recv):
        self.d, self.s, self.z, self.c = d, s, s // 2, lax.rem(s, 2)
        self.view = view
        self.up_sem, self.recv_sem = up_sem, recv_sem
        self.side_sem, self.side_recv = side_sem, side_recv

    def block(self, z):
        return self.view(2 * z + self.c)

    def up(self, z):
        b = self.block(z)
        return remote(b, b, self.up_sem.at[self.z - z], self.recv_sem.at[z], self.d, self.s + 2)

    def down(self, z):
        b = self.block(z)
        return remote(b, b, self.up_sem.at[3 + z - self.z], self.recv_sem.at[z], self.d, self.s - 2)

    def side(self, z):
        b = self.block(z)
        return remote(b, b, self.side_sem.at[z], self.side_recv.at[z], self.d, self.s + 1 - 2 * self.c)

    def start(self):
        @pl.when(self.z < 3)
        def _():
            self.up(self.z).start()

        @pl.when(self.z > 0)
        def _():
            self.down(self.z).start()

        self.side(self.z).start()

    def step(self, k):
        lo, hi = self.z - k, self.z + k

        @pl.when(lo >= 0)
        def _():
            arrived(self.block(lo), self.recv_sem.at[lo], self.d, self.s)

            @pl.when(self.z < 3)
            def _():
                self.up(lo).start()

            self.side(lo).start()

        @pl.when(hi <= 3)
        def _():
            arrived(self.block(hi), self.recv_sem.at[hi], self.d, self.s)

            @pl.when(self.z > 0)
            def _():
                self.down(hi).start()

            self.side(hi).start()

    def start_lane(self):
        @pl.when(self.z < 3)
        def _():
            self.up(self.z).start()

        @pl.when(self.z > 0)
        def _():
            self.down(self.z).start()

    def lane_step(self, k):
        lo, hi = self.z - k, self.z + k

        @pl.when(lo >= 0)
        def _():
            arrived(self.block(lo), self.recv_sem.at[lo], self.d, self.s)

            @pl.when(self.z < 3)
            def _():
                self.up(lo).start()

        @pl.when(hi <= 3)
        def _():
            arrived(self.block(hi), self.recv_sem.at[hi], self.d, self.s)

            @pl.when(self.z > 0)
            def _():
                self.down(hi).start()

    def wait_side(self, z):
        arrived(self.view(2 * z + 1 - self.c), self.side_recv.at[z], self.d, self.s)

    def finish(self):
        for z in range(4):
            self.wait_side(z)
        self.drain()

    def drain(self):
        own = self.block(self.z)
        for z in range(4):
            sent(own, self.side_sem.at[z], self.d, self.s)
        self.lane_drain()

    def lane_drain(self):
        own = self.block(self.z)
        for k in range(3):

            @pl.when((self.z < 3) & (self.z - k >= 0))
            def _():
                sent(own, self.up_sem.at[k], self.d, self.s)

            @pl.when((self.z > 0) & (self.z + k <= 3))
            def _():
                sent(own, self.up_sem.at[3 + k], self.d, self.s)


class Plane:
    def __init__(self, d, s, whole, half, send_sem, recv_sem):
        self.d, self.s = d, s
        self.dx = d + 1 - 2 * lax.rem(d, 2)
        self.dy = lax.rem(d + 2, 4)
        self.far = 3 - d
        self.whole, self.half = whole, half
        self.send_sem, self.recv_sem = send_sem, recv_sem

    def start(self):
        w = self.whole(self.d)
        remote(w, w, self.send_sem.at[0], self.recv_sem.at[0], self.dx, self.s).start()
        remote(w, w, self.send_sem.at[1], self.recv_sem.at[1], self.dy, self.s).start()

    def step(self):
        arrived(self.whole(self.dx), self.recv_sem.at[0], self.d, self.s)
        h = self.half(self.dx, 0)
        remote(h, h, self.send_sem.at[2], self.recv_sem.at[2], self.dy, self.s).start()
        arrived(self.whole(self.dy), self.recv_sem.at[1], self.d, self.s)
        h = self.half(self.dy, 1)
        remote(h, h, self.send_sem.at[3], self.recv_sem.at[3], self.dx, self.s).start()

    def finish(self):
        arrived(self.half(self.far, 0), self.recv_sem.at[2], self.d, self.s)
        arrived(self.half(self.far, 1), self.recv_sem.at[3], self.d, self.s)
        w = self.whole(self.d)
        sent(w, self.send_sem.at[0], self.d, self.s)
        sent(w, self.send_sem.at[1], self.d, self.s)
        h = self.half(self.d, 0)
        sent(h, self.send_sem.at[2], self.d, self.s)
        h = self.half(self.d, 1)
        sent(h, self.send_sem.at[3], self.d, self.s)


def lanes(i):
    return pl.ds(pl.multiple_of(i * 128, 128), 128)


def rows(i, n=128):
    return pl.ds(pl.multiple_of(i * n, n), n)


def dot(a, b):
    return jnp.dot(a, b, preferred_element_type=wide)


def dot_nt(a, b):
    return lax.dot_general(a, b, (((1,), (1,)), ((), ())), preferred_element_type=wide)


def dot_tn(a, b):
    return lax.dot_general(a, b, (((0,), (0,)), ((), ())), preferred_element_type=wide)


def head_lanes(h):
    place = lax.broadcasted_iota(jnp.int32, (1, 128), 1)
    return (place // 64) == h


def partner(x):
    place = lax.broadcasted_iota(jnp.int32, x.shape, 1)
    return jnp.where(lax.rem(place, 64) < 32, pltpu.roll(x, 96, 1), pltpu.roll(x, 32, 1))


class Scatter:
    def __init__(self, d, s, keep, own, side_out, side_in, out, got, relay, sems):
        self.d, self.s, self.z, self.c = d, s, s // 2, lax.rem(s, 2)
        self.keep, self.own, self.side_out, self.side_in = keep, own, side_out, side_in
        self.out, self.got, self.relay = out, got, relay
        self.side_s, self.side_r, self.send_s, self.recv = (sems.at[i] for i in range(4))

    def passes(self, z):
        return ((self.z == 1) & (z >= 2)) | ((self.z == 2) & (z <= 1))

    def give(self, j, z, value):
        first, second = value[:128], value[128:]
        even = self.c == 0
        self.side_out[z] = jnp.where(even, second, first).astype(low)
        remote(
            self.side_out.at[z], self.side_in.at[z], self.side_s.at[z], self.side_r.at[z],
            self.d, self.s + 1 - 2 * self.c,
        ).start()
        self.keep[j % 2] = jnp.where(even, first, second)

    def send(self, z, place, slot, chip):
        remote(
            self.out.at[z], place.at[slot], self.send_s.at[z],
            self.recv.at[slot if place is self.got else 2 + slot], self.d, 2 * chip + self.c,
        ).start()

    def pass_on(self, j, z):
        arrived(self.side_in.at[z], self.side_r.at[z], self.d, self.s)
        total = self.keep[j % 2] + self.side_in[z].astype(wide)
        end = (self.z == 0) | (self.z == 3)
        near = (z - self.z == 1) | (self.z - z == 1)

        @pl.when(z == self.z)
        def _():
            self.own[...] = total

        @pl.when(z != self.z)
        def _():
            self.out[z] = total.astype(low)

            @pl.when(near & jnp.logical_not(self.passes(z)))
            def _():
                self.send(z, self.got, 0, z)

            @pl.when(end & jnp.logical_not(near))
            def _():
                self.send(z, self.relay, lax.rem(z, 2), 1 + self.z // 3)

    def add_relay(self, z):
        @pl.when(self.passes(z))
        def _():
            slot = lax.rem(z, 2)
            arrived(self.relay.at[slot], self.recv.at[2 + slot], self.d, self.s)
            self.out[z] = (self.out[z].astype(wide) + self.relay[slot].astype(wide)).astype(low)
            self.send(z, self.got, 1, z)

    def total(self):
        value = self.own[...]
        for slot in range(2):
            arrived(self.got.at[slot], self.recv.at[slot], self.d, self.s)
            value = value + self.got[slot].astype(wide)
        return value

    def drain(self):
        for z in range(4):
            sent(self.side_out.at[z], self.side_s.at[z], self.d, self.s)

            @pl.when(z != self.z)
            def _():
                sent(self.out.at[z], self.send_s.at[z], self.d, self.s)


def scatter_scratch():
    blocks = pltpu.VMEM((4, 128, 1024), low)
    return dict(
        keep=pltpu.VMEM((2, 128, 1024), wide),
        own=pltpu.VMEM((128, 1024), wide),
        side_out=blocks,
        side_in=blocks,
        out=blocks,
        got=pltpu.VMEM((2, 128, 1024), low),
        relay=pltpu.VMEM((2, 128, 1024), low),
        sems=dma(4, 4),
    )


def ring_scratch():
    return dict(up_sem=dma(6), recv_sem=dma(4), side_sem=dma(4), side_recv=dma(4))


class PlaneScatter:
    def __init__(self, d, s, part, first_a, first_b, middle_out, second, send_sem, recv_sem):
        self.d, self.s = d, s
        self.dx = d + 1 - 2 * lax.rem(d, 2)
        self.dy = lax.rem(d + 2, 4)
        self.far = 3 - d
        self.part = part
        self.first = (first_a, first_b)
        self.middle_out, self.second = middle_out, second
        self.send_sem, self.recv_sem = send_sem, recv_sem

    def start(self):
        for n, near in enumerate((self.dx, self.dy)):
            for m, block in enumerate((self.far, near)):
                k = 2 * n + m
                remote(
                    self.part(block, n), self.first[n].at[m], self.send_sem.at[k], self.recv_sem.at[k],
                    near, self.s,
                ).start()

    def step(self):
        for n, other in enumerate((self.dy, self.dx)):
            arrived(self.first[n].at[0], self.recv_sem.at[2 * n], self.d, self.s)
            total = self.part(other, n)[...].astype(wide) + self.first[n][0].astype(wide)
            self.middle_out[n] = total.astype(low)
            remote(
                self.middle_out.at[n], self.second.at[n], self.send_sem.at[4 + n],
                self.recv_sem.at[4 + n], other, self.s,
            ).start()

    def total(self, n):
        arrived(self.first[n].at[1], self.recv_sem.at[2 * n + 1], self.d, self.s)
        arrived(self.second.at[n], self.recv_sem.at[4 + n], self.d, self.s)
        value = self.part(self.d, n)[...].astype(wide) + self.first[n][1].astype(wide)
        return value + self.second[n].astype(wide)

    def drain(self):
        for k in range(4):
            sent(self.first[0].at[0], self.send_sem.at[k], self.d, self.s)
        for k in range(2):
            sent(self.middle_out.at[0], self.send_sem.at[4 + k], self.d, self.s)


def plane_scratch(*dims):
    blocks = pltpu.VMEM((2, *dims), low)
    return dict(
        first_a=blocks, first_b=blocks, middle_out=blocks, second=blocks,
        send_sem=dma(6), recv_sem=dma(6),
    )


def owner_of(dd, i):
    return 2 * (lax.rem(dd, 2) + 2 * i) + dd // 2


def chip_order(z, j):
    table = ((0, 1, 2, 3), (1, 0, 2, 3), (2, 1, 3, 0), (3, 2, 1, 0))
    value = z * 0 + table[0][j]
    for n in range(1, 4):
        value = jnp.where(z == n, table[n][j], value)
    return value


def far_order(z, j):
    table = ((3, 2, 1, 0), (3, 2, 0, 1), (0, 1, 3, 2), (0, 1, 2, 3))
    value = z * 0 + table[0][j]
    for n in range(1, 4):
        value = jnp.where(z == n, table[n][j], value)
    return value


def pair_owner(p):
    dd, i = p // 2, p % 2
    return 2 * (dd % 2 + 2 * i) + dd // 2


def row_norm(value):
    return lax.rsqrt(jnp.mean(value * value, axis=-1, keepdims=True) + epsilon)


def layer_kernel(given, made, form, *refs):
    names = (*given, *made)
    held = jax.tree.unflatten(form, refs[len(names) :])
    r = types.SimpleNamespace(**dict(zip(names, refs)), **held)
    d = lax.axis_index("dp")
    s = lax.axis_index("seq")
    z = s // 2
    c = lax.rem(s, 2)
    dx = d + 1 - 2 * lax.rem(d, 2)
    dy = lax.rem(d + 2, 4)
    sibling = s + 1 - 2 * c
    home = 2 * c + lax.rem(z, 2)
    is_home = d == home
    pair = pair_of(s)
    cols_d = lanes(d)
    wide_of = lambda i: pl.ds(pl.multiple_of(i * 256, 256), 256)
    wide_d = wide_of(d)

    own_is_target = is_home & (lax.rem(s, 4) == d)
    barrier = pltpu.get_barrier_semaphore()
    for k in range(1, 8):
        pl.semaphore_signal(barrier, inc=1, device_id=(d, lax.rem(s + k, 8)), device_id_type=MESH)
    for k in range(1, 4):
        pl.semaphore_signal(barrier, inc=1, device_id=(lax.rem(d + k, 4), s), device_id_type=MESH)
    for i in range(2):
        giver = owner_of(d, i)

        @pl.when((giver != s) | (lax.rem(s, 4) != d))
        def _():
            pl.semaphore_signal(
                barrier, inc=1, device_id=(lax.rem(s, 4), giver), device_id_type=MESH
            )

    for i in range(2):
        for n, w in enumerate((r.wq, r.wk, r.wv)):
            r.qkv_src[i, :, 128 * n : 128 * (n + 1)] = w[:, 128 * i : 128 * (i + 1)].astype(low)
    segment = r.segment[...]
    r.ids[0:1, :] = segment.astype(wide)
    r.ids[1:2, :] = jnp.where(r.observed[...] == 1, segment, -1).astype(wide)
    r.ids[2:3, :] = r.variate[...].astype(wide)
    r.ids[3:4, :] = r.moment[...].astype(wide)
    r.ids[4:8, :] = jnp.zeros((4, 128), wide)
    r.idr[s] = r.ids[...]
    gain_one = r.attn_gain[...].reshape(1, 1024).astype(low).astype(wide)
    gain_two = r.ffn_gain[...].reshape(1, 1024).astype(low).astype(wide)
    value = r.tokens[0].astype(wide)
    r.xall[s] = (value * row_norm(value) * gain_one).astype(low)

    @pl.when(own_is_target)
    def _():
        pl.semaphore_wait(barrier, 11)

    @pl.when(jnp.logical_not(own_is_target))
    def _():
        pl.semaphore_wait(barrier, 12)

    owner = [owner_of(d, i) for i in range(2)]
    for i in range(2):

        @pl.when(owner[i] != s)
        def _():
            remote(r.qkv_src.at[i], r.wqkv.at[rows(s)], r.qs_s.at[i], r.qs_r.at[s], d, owner[i]).start()

        @pl.when(owner[i] == s)
        def _():
            r.wqkv[rows(s), :] = r.qkv_src[i]

    for k in range(1, 8):
        remote(r.ids, r.idr.at[s], r.id_s.at[k], r.id_r.at[s], d, lax.rem(s + k, 8)).start()
    r.wo[s, :, wide_d] = r.wo_in[...].astype(low)
    wo_ring = Chain(d, s, lambda b: r.wo.at[b, :, wide_d], **r.wo_sems)
    wo_ring.start_lane()
    x_ring = ring = Chain(d, s, lambda b: r.xall.at[b], **r.x_sems)
    ring.start()

    r.gu_src[0] = r.wg_in[...].astype(low)
    r.gu_src[1] = r.wu_in[...].astype(low)
    r.dn_src[...] = r.wd_in[...].astype(low)
    r.call[s] = r.cot[0]
    c_ring = Chain(d, s, lambda b: r.call.at[b], **r.c_sems)

    for k in range(1, 8):
        t = lax.rem(s + k, 8)
        arrived(r.idr.at[t], r.id_r.at[t], d, s)
    for b in range(8):
        block = r.idr[b]
        for n in range(4):
            r.keyrow[n : n + 1, 128 * b : 128 * (b + 1)] = block[n : n + 1, :]
        r.idc[128 * b : 128 * (b + 1), :] = jnp.concatenate([block] * 16, axis=0).T
    wo_ring.lane_step(1)

    half_qkv = lambda n: r.wqkv.at[pl.ds(512 * n, 512)]

    @pl.when(is_home)
    def _():
        for k in range(1, 8):
            t = lax.rem(s + k, 8)
            arrived(r.wqkv.at[rows(t)], r.qs_r.at[t], d, s)
        remote(r.wqkv, r.wqkv, r.qp_s.at[0], r.qp_r.at[0], dx, s).start()
        remote(r.wqkv, r.wqkv, r.qp_s.at[1], r.qp_r.at[0], dy, s).start()

    wo_ring.lane_step(2)
    ring.step(1)
    wo_ring.lane_step(3)
    place = lax.broadcasted_iota(jnp.int32, (1, 128), 1)
    sign = jnp.where(lax.rem(place, 64) < 32, -1.0, 1.0)
    freq = r.freq[...]

    def trig(b, carry):
        angle = r.idc[rows(b), 3:4] * freq
        r.cosine[rows(b), :] = jnp.cos(angle)
        r.sine[rows(b), :] = jnp.sin(angle) * sign
        return carry

    lax.fori_loop(0, 8, trig, 0)
    ring.step(2)

    for k in range(1, 8):
        t = lax.rem(s + k, 8)
        remote(
            r.gu_src.at[:, :, lanes(t)], r.wgu.at[:, rows(s), cols_d], r.gu_s.at[k], r.gu_r.at[s], d, t
        ).start()
    r.wgu[:, rows(s), cols_d] = r.gu_src[:, :, lanes(s)]
    for m in range(4):
        t = c * 4 + m

        @pl.when(t != s)
        def _():
            remote(
                r.dn_src.at[pl.ds(128 * m, 128)], r.wd.at[rows(z), wide_d],
                r.dn_s.at[m], r.dn_r.at[z], d, t,
            ).start()

        @pl.when(t == s)
        def _():
            r.wd[rows(z), wide_d] = r.dn_src[pl.ds(128 * m, 128), :]

    @pl.when(home == dx)
    def _():
        arrived(r.wqkv, r.qp_r.at[0], d, s)
        remote(half_qkv(0), half_qkv(0), r.qp_s.at[2], r.qp_r.at[1], dy, s).start()

    @pl.when(home == dy)
    def _():
        arrived(r.wqkv, r.qp_r.at[0], d, s)
        remote(half_qkv(1), half_qkv(1), r.qp_s.at[2], r.qp_r.at[2], dx, s).start()

    def group(i):
        zs = chip_order(z, i)
        part = rows(zs, 256)
        gu_part = Plane(
            d, s, lambda i: r.wgu.at[:, part, lanes(i)], lambda i, n: r.wgu.at[n, part, lanes(i)],
            r.gup_s.at[zs], r.gup_r.at[zs],
        )
        dn_part = Plane(
            d, s, lambda i: r.wd.at[rows(zs), wide_of(i)],
            lambda i, n: r.wd.at[rows(2 * zs + n, 64), wide_of(i)],
            r.dnp_s.at[zs], r.dnp_r.at[zs],
        )
        return zs, gu_part, dn_part

    def group_start(i):
        zs, gu_part, dn_part = group(i)
        for m in range(2):
            t = 2 * zs + m

            @pl.when(t != s)
            def _():
                arrived(r.wgu.at[:, rows(t), cols_d], r.gu_r.at[t], d, s)

        gu_part.start()

        @pl.when(2 * zs + s // 4 != s)
        def _():
            arrived(r.wd.at[rows(zs), wide_d], r.dn_r.at[zs], d, s)

        dn_part.start()

    def group_step(i):
        zs, gu_part, dn_part = group(i)
        gu_part.step()
        dn_part.step()

    def group_finish(i):
        zs, gu_part, dn_part = group(i)
        gu_part.finish()
        dn_part.finish()

    wo_lane = r.wo.reshape(4, 2, 128, 1024)
    wo_plane = Plane(
        d, s, lambda i: wo_lane.at[:, c, :, wide_of(i)],
        lambda i, n: wo_lane.at[pl.ds(2 * n, 2), c, :, wide_of(i)],
        r.pl_s, r.pl_r,
    )
    wo_side = lambda: remote(
        wo_lane.at[:, c], wo_lane.at[:, c], r.wos_s, r.wos_r, d, sibling
    )
    wo_plane.start()
    ring.step(3)
    group_start(0)
    for zz in range(4):
        ring.wait_side(zz)

    @pl.when(home == 3 - d)
    def _():
        arrived(half_qkv(0), r.qp_r.at[1], d, s)
        arrived(half_qkv(1), r.qp_r.at[2], d, s)

    def project(i, carry):
        pick = rows(i, 256)
        pre = dot(r.xall[pl.ds(2 * i, 2)].reshape(256, 1024), r.wqkv[...])
        cs, sn = r.cosine[pick, :], r.sine[pick, :]
        qp, kp = pre[:, :128], pre[:, 128:256]
        r.q_all[pick, :] = (qp * cs + partner(qp) * sn).astype(low)
        r.k_all[pick, :] = (kp * cs + partner(kp) * sn).astype(low)
        r.v_all[pick, :] = pre[:, 256:].astype(low)
        return carry

    lax.fori_loop(0, 4, project, 0)

    def tables(pick, first, count):
        seg_col, var_col = r.idc[pick, 0:1], r.idc[pick, 2:3]
        q_place = first + lax.broadcasted_iota(jnp.int32, (count, 1), 0)
        k_place = lax.broadcasted_iota(jnp.int32, (1, 1024), 1)
        allowed = (seg_col == r.keyrow[1:2, :]) | (q_place == k_place)
        return allowed, var_col == r.keyrow[2:3, :]

    def scores_of(qh, h, same):
        scores = dot_nt(qh, r.k_all[...]) * 0.125
        return scores + jnp.where(same, r.same_bias[2 * pair + h], r.cross_bias[2 * pair + h])

    def attend(b, carry):
        pick = rows(b)
        allowed, same = tables(pick, b * 128, 128)
        q_block = r.q_all[pick, :]
        attended, total_lse = None, None
        for h in range(2):
            mine = head_lanes(h)
            qh = jnp.where(mine, q_block, jnp.zeros_like(q_block))
            scores = jnp.where(allowed, scores_of(qh, h, same), NEG)
            top = jnp.max(scores, axis=-1, keepdims=True)
            e = jnp.exp(scores - top)
            total = jnp.sum(e, axis=-1, keepdims=True)
            part = dot((e * (1.0 / total)).astype(low), r.v_all[...])
            one = top + jnp.log(total)
            attended = part if h == 0 else jnp.where(mine, part, attended)
            total_lse = one if h == 0 else jnp.where(mine, one, total_lse)
        r.head_out[b] = attended.astype(low)
        r.lse[pick, :] = jnp.broadcast_to(total_lse, (128, 128))
        return carry

    def send_mixed(t):
        @pl.when(t != s)
        def _():
            remote(r.head_out.at[t], r.mixed.at[pair], r.m_s.at[t], r.m_r.at[s], d, t).start()

        @pl.when(t == s)
        def _():
            r.mixed[pair] = r.head_out[t]

    lax.fori_loop(0, 2, attend, 0)
    send_mixed(0)
    send_mixed(1)
    wo_plane.step()
    group_start(1)
    lax.fori_loop(2, 4, attend, 0)
    send_mixed(2)
    send_mixed(3)
    group_step(0)
    lax.fori_loop(4, 6, attend, 0)
    send_mixed(4)
    send_mixed(5)
    group_start(2)
    lax.fori_loop(6, 8, attend, 0)
    send_mixed(6)
    send_mixed(7)
    wo_plane.finish()
    wo_side().start()
    c_ring.start()
    group_step(1)
    group_start(3)
    for t in range(8):

        @pl.when(t != s)
        def _():
            arrived(r.mixed.at[pair_of(t)], r.m_r.at[t], d, s)

    arrived(wo_lane.at[:, 1 - c], r.wos_r, d, s)

    joined = jnp.concatenate([r.mixed[p] for p in range(8)], axis=1)
    middle = r.tokens[0].astype(wide) + dot(joined, r.wo[...].reshape(1024, 1024))
    r.sall[s] = (middle * row_norm(middle) * gain_two).astype(low)
    ring = Chain(d, s, lambda b: r.sall.at[b], **r.y_sems)
    ring.start()
    r.mid[...] = middle
    group_step(2)
    c_ring.step(1)
    group_step(3)
    c_ring.step(2)
    for i in range(4):
        group_finish(i)

    grads = Scatter(d, s, **r.g_parts)
    outs = Scatter(d, s, **r.o_parts)
    for j in range(4):
        zj = chip_order(z, j)
        if j > 0:
            arrived(ring.block(zj), ring.recv_sem.at[zj], d, s)

            @pl.when((zj < z) & (z < 3))
            def _():
                ring.up(zj).start()

            @pl.when((zj > z) & (z > 0))
            def _():
                ring.down(zj).start()

            ring.side(zj).start()
        ring.wait_side(zj)
        if j == 1:
            c_ring.step(3)
        c_ring.wait_side(zj)
        pick = rows(zj, 256)
        block = r.sall[pl.ds(2 * zj, 2)].reshape(256, 1024)
        gate_pre = dot(block, r.wgu[0])
        up_pre = dot(block, r.wgu[1])
        sigma = jax.nn.sigmoid(gate_pre)
        act = gate_pre * sigma
        hidden = (act * up_pre).astype(low)
        r.hid[pick, :] = hidden
        hg = dot_nt(r.call[pl.ds(2 * zj, 2)].reshape(256, 1024), r.wd[...])
        g_low = (hg * up_pre * sigma * (1.0 + gate_pre * (1.0 - sigma))).astype(low)
        u_low = (hg * act).astype(low)
        r.gg[pick, :] = g_low
        r.ug[pick, :] = u_low
        grads.give(j, zj, dot_nt(g_low, r.wgu[0]) + dot_nt(u_low, r.wgu[1]))
        if j > 0:
            grads.pass_on(j - 1, chip_order(z, j - 1))
        if j > 1:
            grads.add_relay(chip_order(z, j - 2))
    grads.pass_on(3, chip_order(z, 3))
    grads.add_relay(chip_order(z, 2))

    def weigh(i, carry):
        block = r.sall[:, :, wide_of(i)].reshape(1024, 256)
        r.gu_grad[0, rows(i, 256), :] = dot_tn(block, r.gg[...]).astype(low)
        r.gu_grad[1, rows(i, 256), :] = dot_tn(block, r.ug[...]).astype(low)
        return carry

    lax.fori_loop(0, 4, weigh, 0)
    grads.add_relay(chip_order(z, 3))
    gu = PlaneScatter(d, s, lambda i, n: r.gu_grad.at[n, :, lanes(i)], **r.gu_parts)
    dn = PlaneScatter(
        d, s, lambda i, n: r.dn_grad.at[pl.ds(256 * n, 256), wide_of(i)], **r.dn_parts
    )
    wo = PlaneScatter(
        d, s, lambda i, n: r.wo_sum.at[pl.ds(2 * n, 2), :, wide_of(i)], **r.wo_parts
    )
    gu.start()

    def weigh_down(i, carry):
        cols = wide_of(i)
        r.dn_grad[:, cols] = dot_tn(r.hid[...], r.call[:, :, cols].reshape(1024, 256)).astype(low)
        return carry

    lax.fori_loop(0, 4, weigh_down, 0)
    dn.start()

    middle = r.mid[...]
    factor = row_norm(middle)
    normed = middle * factor
    second_grad = grads.total()
    scaled = second_grad * gain_two
    inner = jnp.mean(scaled * normed, axis=-1, keepdims=True)
    r.small[...] = jnp.zeros_like(r.small)
    r.small[1:2, :] = jnp.sum(second_grad * normed, axis=0, keepdims=True)
    value = r.call[s].astype(wide) + factor * (scaled - normed * inner)
    r.mid_grad[...] = value
    v_low = value.astype(low)
    mg = dot_nt(v_low, r.wo[...].reshape(1024, 1024)).astype(low)
    for p in range(8):
        r.mg_src[p] = mg[:, 128 * p : 128 * (p + 1)]
        t = pair_owner(p)

        @pl.when(s != t)
        def _():
            remote(r.mg_src.at[p], r.mgrad.at[s], r.mg_s.at[p], r.mg_r.at[s], d, t).start()

        @pl.when(s == t)
        def _():
            r.mgrad[s] = r.mg_src[p]

    def weigh_out(i, carry):
        left = jnp.concatenate([r.mixed[2 * i], r.mixed[2 * i + 1]], axis=1)
        part = dot_tn(left, v_low).astype(low)
        r.wo_grad[i, 0] = part[:128]
        r.wo_grad[i, 1] = part[128:]
        return carry

    lax.fori_loop(0, 4, weigh_out, 0)
    side = remote(r.wo_grad.at[:, 1 - c], r.wo_in2, r.side_s, r.side_r, d, sibling)
    side.start()
    for j in range(4):
        zj = far_order(z, j)
        outs.give(j, zj, dot(r.hid[rows(zj, 256), :], r.wd[...]))
        if j > 0:
            outs.pass_on(j - 1, far_order(z, j - 1))
    outs.pass_on(3, z)
    r.dk[...] = jnp.zeros_like(r.dk)
    r.dv[...] = jnp.zeros_like(r.dv)
    r.bsum[...] = jnp.zeros_like(r.bsum)
    gu.step()
    for k in range(1, 8):
        t = lax.rem(s + k, 8)
        arrived(r.mgrad.at[t], r.mg_r.at[t], d, s)

    def unturn(x, pick):
        return x * r.cosine[pick, :] - partner(x) * r.sine[pick, :]

    def attend_back(b):
        pick = rows(b, 256)
        allowed, same = tables(pick, b * 256, 256)
        q_block = r.q_all[pick, :]
        m_block = r.mgrad[pl.ds(2 * b, 2)].reshape(256, 128)
        dq = None
        for h in range(2):
            mine = head_lanes(h)
            qh = jnp.where(mine, q_block, jnp.zeros_like(q_block))
            mh = jnp.where(mine, m_block, jnp.zeros_like(m_block))
            scores = scores_of(qh, h, same) - r.lse[pick, 64 * h : 64 * h + 1]
            p = jnp.exp(jnp.where(allowed, scores, NEG))
            pg = dot_nt(mh, r.v_all[...])
            inner = jnp.sum(p * pg, axis=-1, keepdims=True)
            ds = (p * (pg - inner)).astype(low)
            ds_wide = ds.astype(wide)
            r.bsum[2 * h : 2 * h + 1, :] += jnp.sum(jnp.where(same, ds_wide, 0.0), axis=0, keepdims=True)
            r.bsum[2 * h + 1 : 2 * h + 2, :] += jnp.sum(jnp.where(same, 0.0, ds_wide), axis=0, keepdims=True)
            one = dot(ds, r.k_all[...]) * 0.125
            dq = one if h == 0 else jnp.where(mine, one, dq)
            r.dk[...] += dot_tn(ds, qh)
            r.dv[...] += dot_tn(p.astype(low), mh)
        r.gr[pick, 0:128] = unturn(dq, pick).astype(low)

    def send_gu(n):
        r.gu_sum[n] = gu.total(n).astype(low)
        for k in range(1, 8):
            t = lax.rem(s + k, 8)
            remote(
                r.gu_sum.at[n, rows(t)], r.gu_rx.at[n, s], r.guz_s.at[n, k], r.guz_r.at[n, s], d, t
            ).start()
        r.gu_rx[n, s] = r.gu_sum[n, rows(s), :]

    def send_dn():
        for j in range(4):
            t = 2 * j + s // 4

            @pl.when(t != s)
            def _():
                remote(
                    r.dn_sum.at[pl.ds(128 * j, 128)], r.dn_rx.at[lax.rem(s, 4)], r.dnz_s.at[j],
                    r.dnz_r.at[lax.rem(s, 4)], d, t,
                ).start()

            @pl.when(t == s)
            def _():
                r.dn_rx[lax.rem(s, 4)] = r.dn_sum[pl.ds(128 * j, 128), :]

    attend_back(0)
    for j in range(4):
        outs.add_relay(far_order(z, j))
    side.wait_recv()
    for b in range(4):
        r.wo_sum[b] = (r.wo_grad[b, c].astype(wide) + r.wo_in2[b].astype(wide)).astype(low)
    wo.start()
    dn.step()
    send_gu(0)
    send_gu(1)
    attend_back(1)
    for n in range(2):
        r.dn_sum[pl.ds(256 * n, 256), :] = dn.total(n).astype(low)
    send_dn()
    attend_back(2)
    wo.step()
    attend_back(3)
    for n in range(2):
        r.wo_fin[pl.ds(2 * n, 2)] = wo.total(n).astype(low)
    for k in range(1, 4):
        t = lax.rem(z + k, 4)
        remote(r.wo_fin.at[t], r.wo_rx.at[z], r.woz_s.at[t], r.woz_r.at[z], d, 2 * t + c).start()

    def turn(b, carry):
        pick = rows(b, 256)
        r.gr[pick, 128:256] = unturn(r.dk[pick, :] * 0.125, pick).astype(low)
        r.gr[pick, 256:384] = r.dv[pick, :].astype(low)
        return carry

    lax.fori_loop(0, 4, turn, 0)
    grads.drain()
    for j in range(4):
        zj = far_order(z, j)
        grads.give(j, zj, dot_nt(r.gr[rows(zj, 256), :], r.wqkv[...]))
        if j > 0:
            grads.pass_on(j - 1, far_order(z, j - 1))
    grads.pass_on(3, z)

    def weigh_qkv(i, carry):
        block = r.xall[:, :, wide_of(i)].reshape(1024, 256)
        value = dot_tn(block, r.gr[...]).astype(low)
        r.qkv_grad[2 * i] = value[:128]
        r.qkv_grad[2 * i + 1] = value[128:]
        return carry

    lax.fori_loop(0, 4, weigh_qkv, 0)
    for j in range(2):
        grads.add_relay(far_order(z, j))
    for k in range(1, 4):
        t = lax.rem(d + k, 4)
        for m in range(2):
            remote(
                r.qkv_grad.at[t + 4 * m], r.q_in.at[d, m], r.qg_s.at[t, m], r.qg_r.at[d, m], t, s
            ).start()
    r.out[0] = (r.mid[...] + outs.total()).astype(low)

    for m in range(2):
        value = r.qkv_grad[d + 4 * m].astype(wide)
        for k in range(1, 4):
            t = lax.rem(d + k, 4)
            arrived(r.q_in.at[t, m], r.qg_r.at[t, m], d, s)
            value = value + r.q_in[t, m].astype(wide)
        r.q_sum[m] = value.astype(low)
        target = d + 4 * m
        mine = (target == s) & is_home

        @pl.when(jnp.logical_not(mine))
        def _():
            remote(
                r.q_sum.at[m], r.q_rx.at[z // 2], r.qz_s.at[m], r.qz_r.at[z // 2], home, target
            ).start()

        @pl.when(mine)
        def _():
            r.q_rx[z // 2] = r.q_sum[m]

    value = r.tokens[0].astype(wide)
    factor = row_norm(value)
    normed = value * factor
    first_grad = grads.total()
    scaled = first_grad * gain_one
    inner = jnp.mean(scaled * normed, axis=-1, keepdims=True)

    r.small[0:1, :] = jnp.sum(first_grad * normed, axis=0, keepdims=True)
    place = lax.broadcasted_iota(jnp.int32, (1, 1024), 1)
    line = jnp.zeros((1, 1024), wide)
    for h in range(2):
        for n in range(2):
            k = 2 * h + n
            one = jnp.sum(r.bsum[k : k + 1, :], axis=1, keepdims=True)
            line = line + jnp.where(place == 128 * n + 2 * pair + h, one, 0.0)
    r.small[2:3, :] = line
    for k in range(1, 4):
        t = lax.rem(d + k, 4)
        remote(r.small, r.small_p.at[d], r.sp_s.at[k], r.sp_r.at[d], t, s).start()
    r.tok_grad[0] = (r.mid_grad[...] + factor * (scaled - normed * inner)).astype(low)
    for k in range(1, 4):
        t = lax.rem(d + k, 4)
        arrived(r.small_p.at[t], r.sp_r.at[t], d, s)
    r.small_p[d] = r.small[...]
    r.small_q[...] = r.small_p[0] + r.small_p[1] + r.small_p[2] + r.small_p[3]
    for k in range(1, 8):
        t = lax.rem(s + k, 8)
        remote(r.small_q, r.small_z.at[s], r.sz_s.at[k], r.sz_r.at[s], d, t).start()
    r.small_z[s] = r.small_q[...]

    for k in range(1, 8):
        t = lax.rem(s + k, 8)
        for n in range(2):
            arrived(r.gu_rx.at[n, t], r.guz_r.at[n, t], d, s)
    for m in range(4):

        @pl.when(4 * c + m != s)
        def _():
            arrived(r.dn_rx.at[m], r.dnz_r.at[m], d, s)

    r.wo_rx[z] = r.wo_fin[z]
    for k in range(1, 4):
        t = lax.rem(z + k, 4)
        arrived(r.wo_rx.at[t], r.woz_r.at[t], d, s)
    for i in range(2):

        @pl.when((owner[i] != s) | (lax.rem(s, 4) != d))
        def _():
            arrived(r.q_rx.at[i], r.qz_r.at[i], d, s)

    for k in range(1, 8):
        t = lax.rem(s + k, 8)
        arrived(r.small_z.at[t], r.sz_r.at[t], d, s)

    x_ring.drain()
    c_ring.drain()
    ring.drain()
    wo_ring.lane_drain()
    wo_side().wait_send()
    for i in range(2):

        @pl.when(owner[i] != s)
        def _():
            sent(r.qkv_src.at[i], r.qs_s.at[i], d, s)

    for k in range(1, 8):
        sent(r.ids, r.id_s.at[k], d, s)
        sent(r.gu_src.at[:, :, pl.ds(0, 128)], r.gu_s.at[k], d, s)

    @pl.when(is_home)
    def _():
        sent(r.wqkv, r.qp_s.at[0], d, s)
        sent(r.wqkv, r.qp_s.at[1], d, s)

    @pl.when((home == dx) | (home == dy))
    def _():
        sent(half_qkv(0), r.qp_s.at[2], d, s)

    for m in range(4):

        @pl.when(c * 4 + m != s)
        def _():
            sent(r.dn_src.at[pl.ds(128 * m, 128)], r.dn_s.at[m], d, s)

    for t in range(8):

        @pl.when(t != s)
        def _():
            sent(r.head_out.at[t], r.m_s.at[t], d, s)

        @pl.when(s != pair_owner(t))
        def _():
            sent(r.mg_src.at[t], r.mg_s.at[t], d, s)

    side.wait_send()
    gu.drain()
    dn.drain()
    wo.drain()
    grads.drain()
    outs.drain()
    for k in range(1, 8):
        for n in range(2):
            sent(r.gu_sum.at[n, rows(0)], r.guz_s.at[n, k], d, s)
        sent(r.small_q, r.sz_s.at[k], d, s)
    for j in range(4):

        @pl.when(2 * j + s // 4 != s)
        def _():
            sent(r.dn_sum.at[pl.ds(0, 128)], r.dnz_s.at[j], d, s)

    for k in range(1, 4):
        t = lax.rem(z + k, 4)
        sent(r.wo_fin.at[t], r.woz_s.at[t], d, s)
        t = lax.rem(d + k, 4)
        for m in range(2):
            sent(r.q_sum.at[m], r.qg_s.at[t, m], d, s)
        sent(r.small, r.sp_s.at[k], d, s)
    for m in range(2):

        @pl.when(jnp.logical_not((d + 4 * m == s) & is_home))
        def _():
            sent(r.q_sum.at[m], r.qz_s.at[m], d, s)


def vmem():
    return pl.BlockSpec(memory_space=pltpu.VMEM)


def smem():
    return pl.BlockSpec(memory_space=pltpu.SMEM)


def shape(*dims, kind=low):
    return jax.ShapeDtypeStruct(dims, kind)


def dma(*dims):
    return pltpu.SemaphoreType.DMA(dims)


def layer(ins):
    outs = dict(
        out=shape(1, 128, 1024),
        tok_grad=shape(1, 128, 1024),
        gu_rx=shape(2, 8, 128, 128),
        dn_rx=shape(4, 128, 256),
        wo_rx=shape(4, 128, 256),
        q_rx=shape(2, 128, 384),
        small_z=shape(8, 8, 1024, kind=wide),
    )
    scratch = dict(
        xall=pltpu.VMEM((8, 128, 1024), low),
        q_all=pltpu.VMEM((1024, 128), low),
        k_all=pltpu.VMEM((1024, 128), low),
        v_all=pltpu.VMEM((1024, 128), low),
        lse=pltpu.VMEM((1024, 128), wide),
        wqkv=pltpu.VMEM((1024, 384), low),
        wo=pltpu.VMEM((8, 128, 1024), low),
        wgu=pltpu.VMEM((2, 1024, 512), low),
        wd=pltpu.VMEM((512, 1024), low),
        call=pltpu.VMEM((8, 128, 1024), low),
        ids=pltpu.VMEM((8, 128), wide),
        idr=pltpu.VMEM((8, 8, 128), wide),
        idc=pltpu.VMEM((1024, 128), wide),
        keyrow=pltpu.VMEM((8, 1024), wide),
        cosine=pltpu.VMEM((1024, 128), wide),
        sine=pltpu.VMEM((1024, 128), wide),
        mixed=pltpu.VMEM((8, 128, 128), low),
        qkv_src=pltpu.VMEM((2, 128, 384), low),
        gu_src=pltpu.VMEM((2, 128, 1024), low),
        dn_src=pltpu.VMEM((512, 256), low),
        head_out=pltpu.VMEM((8, 128, 128), low),
        sall=pltpu.VMEM((8, 128, 1024), low),
        gg=pltpu.VMEM((1024, 512), low),
        ug=pltpu.VMEM((1024, 512), low),
        hid=pltpu.VMEM((1024, 512), low),
        mid=pltpu.VMEM((128, 1024), wide),
        mid_grad=pltpu.VMEM((128, 1024), wide),
        mg_src=pltpu.VMEM((8, 128, 128), low),
        mgrad=pltpu.VMEM((8, 128, 128), low),
        gu_grad=pltpu.VMEM((2, 1024, 512), low),
        dn_grad=pltpu.VMEM((512, 1024), low),
        wo_grad=pltpu.VMEM((4, 2, 128, 1024), low),
        dk=pltpu.VMEM((1024, 128), wide),
        dv=pltpu.VMEM((1024, 128), wide),
        gr=pltpu.VMEM((1024, 384), low),
        bsum=pltpu.VMEM((8, 1024), wide),
        qkv_grad=pltpu.VMEM((8, 128, 384), low),
        wo_in2=pltpu.VMEM((4, 128, 1024), low),
        wo_sum=pltpu.VMEM((4, 128, 1024), low),
        gu_sum=pltpu.VMEM((2, 1024, 128), low),
        dn_sum=pltpu.VMEM((512, 256), low),
        wo_fin=pltpu.VMEM((4, 128, 256), low),
        q_in=pltpu.VMEM((4, 2, 128, 384), low),
        q_sum=pltpu.VMEM((2, 128, 384), low),
        small=pltpu.VMEM((8, 1024), wide),
        small_p=pltpu.VMEM((4, 8, 1024), wide),
        small_q=pltpu.VMEM((8, 1024), wide),
        g_parts=scatter_scratch(),
        o_parts=scatter_scratch(),
        gu_parts=plane_scratch(1024, 128),
        dn_parts=plane_scratch(256, 256),
        wo_parts=plane_scratch(2, 128, 256),
        x_sems=ring_scratch(),
        y_sems=ring_scratch(),
        c_sems=ring_scratch(),
        wo_sems=ring_scratch(),
        qs_s=dma(2), qs_r=dma(8), qp_s=dma(3), qp_r=dma(3),
        id_s=dma(8), id_r=dma(8), gu_s=dma(8), gu_r=dma(8), gup_s=dma(4, 4), gup_r=dma(4, 4), dnp_s=dma(4, 4), dnp_r=dma(4, 4),
        dn_s=dma(4), dn_r=dma(4), pl_s=dma(4), pl_r=dma(4),
        wos_s=dma(), wos_r=dma(), m_s=dma(8), m_r=dma(8),
        mg_s=dma(8), mg_r=dma(8), side_s=dma(), side_r=dma(),
        guz_s=dma(2, 8), guz_r=dma(2, 8), dnz_s=dma(4), dnz_r=dma(4),
        woz_s=dma(4), woz_r=dma(4), qg_s=dma(4, 2), qg_r=dma(4, 2),
        qz_s=dma(2), qz_r=dma(2), sp_s=dma(8), sp_r=dma(4),
        sz_s=dma(8), sz_r=dma(8),
    )
    flat, inner = jax.tree.flatten(scratch)
    got = pl.pallas_call(
        functools.partial(layer_kernel, tuple(ins), tuple(outs), inner),
        name="whole",
        out_shape=tuple(outs.values()),
        in_specs=[smem() if a.shape == (16,) else vmem() for a in ins.values()],
        out_specs=[vmem()] * len(outs),
        scratch_shapes=flat,
        compiler_params=pltpu.CompilerParams(
            collective_id=0, has_side_effects=True, vmem_limit_bytes=64 << 20
        ),
    )(*ins.values())
    return types.SimpleNamespace(**dict(zip(outs, got)))


def finish_kernel(
    out, tok_grad, gu, dn, wo, qkv, small,
    out2, tok2, gate2, up2, dn2, wo2, q2, k2, v2, g1, g2, same, cross,
):
    out2[...] = out[...]
    tok2[...] = tok_grad[...]
    for t in range(8):
        gate2[:, 128 * t : 128 * (t + 1)] = gu[0, t].astype(wide)
        up2[:, 128 * t : 128 * (t + 1)] = gu[1, t].astype(wide)
    for m in range(4):
        dn2[128 * m : 128 * (m + 1), :] = dn[m].astype(wide)
    total = wo[0].astype(wide)
    for m in range(1, 4):
        total = total + wo[m].astype(wide)
    wo2[...] = total
    for n, ref in enumerate((q2, k2, v2)):
        for i in range(2):
            ref[:, 128 * i : 128 * (i + 1)] = qkv[i, :, 128 * n : 128 * (n + 1)].astype(wide)
    total = small[0]
    for t in range(1, 8):
        total = total + small[t]
    g1[...] = total[0:1]
    g2[...] = total[1:2]
    same[...] = total[2:3, 0:128]
    cross[...] = total[2:3, 128:256]


def finish(got):
    outs = (
        shape(1, 128, 1024), shape(1, 128, 1024),
        shape(128, 1024, kind=wide), shape(128, 1024, kind=wide), shape(512, 256, kind=wide),
        shape(128, 256, kind=wide), shape(128, 256, kind=wide), shape(128, 256, kind=wide),
        shape(128, 256, kind=wide), shape(1, 1024, kind=wide), shape(1, 1024, kind=wide),
        shape(1, 128, kind=wide), shape(1, 128, kind=wide),
    )
    return pl.pallas_call(
        finish_kernel,
        name="finish",
        out_shape=outs,
        in_specs=[vmem()] * 7,
        out_specs=[vmem()] * len(outs),
    )(got.out, got.tok_grad, got.gu_rx, got.dn_rx, got.wo_rx, got.q_rx, got.small_z)


def rope_rates():
    rates = np.float32(10000.0) ** (-np.arange(32, dtype=np.float32) * np.float32(2.0 / 64))
    return np.tile(rates.astype(np.float32), 4)[None]


def fast_body(
    tokens, attn_gain, query_weight, key_weight, value_weight, out_weight, same_bias, cross_bias,
    ffn_gain, gate_weight, up_weight, down_weight, segment_ids, variate_ids, time_ids, observed,
    cotangent,
):
    got = layer(dict(
        tokens=tokens, attn_gain=attn_gain, ffn_gain=ffn_gain,
        wq=query_weight, wk=key_weight, wv=value_weight, wo_in=out_weight,
        wg_in=gate_weight, wu_in=up_weight, wd_in=down_weight,
        same_bias=same_bias, cross_bias=cross_bias, segment=segment_ids, freq=rope_rates(),
        variate=variate_ids, moment=time_ids, observed=observed, cot=cotangent,
    ))
    out, tok, gate, up, dn, wo, q, k, v, g1, g2, same, cross = finish(got)
    return (
        out, tok, g1[0], q, k, v, wo, same[0, 0:16], cross[0, 0:16], g2[0], gate, up, dn,
    )


def fits(mesh):
    return mesh.shape["dp"] == 4 and mesh.shape["seq"] == 8


def solution(mesh):
    in_specs = (
        P("dp", "seq", None),
        P(),
        P("seq", "dp"),
        P("seq", "dp"),
        P("seq", "dp"),
        P("seq", "dp"),
        P(),
        P(),
        P(),
        P("seq", "dp"),
        P("seq", "dp"),
        P("seq", "dp"),
        P("dp", "seq"),
        P("dp", "seq"),
        P("dp", "seq"),
        P("dp", "seq"),
        P("dp", "seq", None),
    )
    out_specs = (
        P("dp", "seq", None),
        P("dp", "seq", None),
        P(),
        P("seq", "dp"),
        P("seq", "dp"),
        P("seq", "dp"),
        P("seq", "dp"),
        P(),
        P(),
        P(),
        P("seq", "dp"),
        P("seq", "dp"),
        P("seq", "dp"),
    )
    part = fast_body if fits(mesh) else body
    return jax.shard_map(part, mesh=mesh, in_specs=in_specs, out_specs=out_specs, check_vma=False)
```

```python
import functools
import types

import jax
import jax.numpy as jnp
import numpy as np
from jax import lax
from jax.experimental import pallas as pl
from jax.experimental.pallas import tpu as pltpu
from jax.sharding import PartitionSpec as P

epsilon = 1e-06


def product(left_side, right_side):
    return jnp.dot(left_side, right_side, preferred_element_type=jnp.float32)


def contract_rows(left_side, right_side):
    return lax.dot_general(
        left_side, right_side, (((0,), (0,)), ((), ())), preferred_element_type=jnp.float32
    )


def contract_cols(left_side, right_side):
    return lax.dot_general(
        left_side, right_side, (((1,), (1,)), ((), ())), preferred_element_type=jnp.float32
    )


def angles_of(moments, head_width):
    half_width = head_width // 2
    powers = jnp.arange(half_width).astype(jnp.float32) * (2.0 / head_width)
    return moments.astype(jnp.float32)[:, None] * (10000.0 ** (-powers))[None, :]


def rotate(values, angles, head_count):
    row_count, model_width = values.shape
    shaped = values.reshape(row_count, head_count, model_width // head_count)
    half_width = model_width // head_count // 2
    first_half = shaped[..., :half_width]
    second = shaped[..., half_width:]
    cosine = jnp.cos(angles)[:, None, :]
    sine_part = jnp.sin(angles)[:, None, :]
    turned = jnp.concatenate(
        [first_half * cosine - second * sine_part, second * cosine + first_half * sine_part],
        axis=-1,
    )
    return turned.reshape(row_count, model_width)


def normalize(values, gain_row):
    factor = lax.rsqrt(jnp.mean(values * values, axis=-1, keepdims=True) + epsilon)
    normed = values * factor
    return (normed, factor, normed * gain_row)


def norm_back(incoming, normed, factor, gain_row):
    scaled = incoming * gain_row
    inner_sum = jnp.mean(scaled * normed, axis=-1, keepdims=True)
    return (factor * (scaled - normed * inner_sum), jnp.sum(incoming * normed, axis=0))


def make_tables(segment, variate, key_segment, key_variate, first_row):
    query_place = first_row + jnp.arange(segment.shape[0])
    key_place = jnp.arange(key_segment.shape[0])
    allowed = (segment.astype(jnp.float32)[:, None] == key_segment.astype(jnp.float32)[None, :]) | (
        query_place[:, None] == key_place[None, :]
    )
    same_kind = variate.astype(jnp.float32)[:, None] == key_variate.astype(jnp.float32)[None, :]
    return (allowed, same_kind)


def block_scores(
    block_index, query_low, keys_all, same_kind, same_bias, cross_bias, head_group, head_width
):
    block_width = head_group * head_width
    query_block = lax.dynamic_slice_in_dim(
        query_low, block_index * block_width, block_width, 1
    ).reshape(query_low.shape[0], head_group, head_width)
    key_block = lax.dynamic_slice_in_dim(
        keys_all, block_index * block_width, block_width, 1
    ).reshape(keys_all.shape[0], head_group, head_width)
    raw_scores = jnp.einsum(
        "thd,shd->hts", query_block, key_block, preferred_element_type=jnp.float32
    )
    same_part = lax.dynamic_slice_in_dim(same_bias, block_index * head_group, head_group)
    cross_part = lax.dynamic_slice_in_dim(cross_bias, block_index * head_group, head_group)
    offset = jnp.where(same_kind[None], same_part[:, None, None], cross_part[:, None, None])
    return (raw_scores * head_width ** (-0.5) + offset, query_block, key_block)


def body(
    tokens,
    attn_gain,
    query_weight,
    key_weight,
    value_weight,
    out_weight,
    same_bias,
    cross_bias,
    ffn_gain,
    gate_weight,
    up_weight,
    down_weight,
    segment_ids,
    variate_ids,
    time_ids,
    observed,
    cotangent,
):
    row_count = tokens.shape[1]
    model_width = tokens.shape[2]
    head_count = same_bias.shape[0]
    head_width = model_width // head_count
    head_group = max(1, 128 // head_width)
    block_width = head_group * head_width
    block_total = head_count // head_group
    scaling = head_width ** (-0.5)
    first_row = lax.axis_index("seq") * row_count
    gain_one = attn_gain.astype(jnp.bfloat16).astype(jnp.float32)
    gain_two = ffn_gain.astype(jnp.bfloat16).astype(jnp.float32)
    low_masters = (
        query_weight.astype(jnp.bfloat16),
        key_weight.astype(jnp.bfloat16),
        value_weight.astype(jnp.bfloat16),
        out_weight.astype(jnp.bfloat16),
        gate_weight.astype(jnp.bfloat16),
        up_weight.astype(jnp.bfloat16),
        down_weight.astype(jnp.bfloat16),
    )
    row_parts = (
        lax.all_gather(low_masters[0], "seq", axis=0, tiled=True),
        lax.all_gather(low_masters[1], "seq", axis=0, tiled=True),
        lax.all_gather(low_masters[2], "seq", axis=0, tiled=True),
        lax.all_gather(low_masters[3], "seq", axis=0, tiled=True),
        lax.all_gather(low_masters[4], "seq", axis=0, tiled=True),
        lax.all_gather(low_masters[5], "seq", axis=0, tiled=True),
        lax.all_gather(low_masters[6], "seq", axis=0, tiled=True),
    )
    gathered = (
        lax.all_gather(row_parts[0], "dp", axis=1, tiled=True),
        lax.all_gather(row_parts[1], "dp", axis=1, tiled=True),
        lax.all_gather(row_parts[2], "dp", axis=1, tiled=True),
        lax.all_gather(row_parts[3], "dp", axis=1, tiled=True),
        lax.all_gather(row_parts[4], "dp", axis=1, tiled=True),
        lax.all_gather(row_parts[5], "dp", axis=1, tiled=True),
        lax.all_gather(row_parts[6], "dp", axis=1, tiled=True),
    )
    w_query, w_key, w_value, w_out, w_gate, w_up, w_down = gathered
    inputs = tokens[0].astype(jnp.float32)
    segment = segment_ids[0]
    variate = variate_ids[0]
    seen_row = observed[0]
    angles = angles_of(time_ids[0], head_width)
    normed_one, factor_one, scaled_one = normalize(inputs, gain_one)
    first_low = scaled_one.astype(jnp.bfloat16)
    query_low = rotate(product(first_low, w_query), angles, head_count).astype(jnp.bfloat16)
    key_low = rotate(product(first_low, w_key), angles, head_count).astype(jnp.bfloat16)
    value_low = product(first_low, w_value).astype(jnp.bfloat16)
    key_segment = jnp.where(seen_row == 1, segment, -1).astype(jnp.bfloat16)
    key_variate = variate.astype(jnp.bfloat16)
    keys_all, values_all, segments_all, variates_all = (
        lax.all_gather(key_low, "seq", axis=0, tiled=True),
        lax.all_gather(value_low, "seq", axis=0, tiled=True),
        lax.all_gather(key_segment, "seq", axis=0, tiled=True),
        lax.all_gather(key_variate, "seq", axis=0, tiled=True),
    )
    length = keys_all.shape[0]
    allowed, same_kind = make_tables(segment, variate, segments_all, variates_all, first_row)

    def forward_block(block_index, state_now):
        mixed, summary = state_now
        scores, query_block, key_block = block_scores(
            block_index,
            query_low,
            keys_all,
            same_kind,
            same_bias,
            cross_bias,
            head_group,
            head_width,
        )
        row_top = jnp.max(jnp.where(allowed[None], scores, -jnp.inf), axis=-1, keepdims=True)
        exponent = jnp.exp(jnp.where(allowed[None], scores - row_top, -jnp.inf))
        row_total = jnp.sum(exponent, axis=-1, keepdims=True)
        prob_low = (exponent / row_total).astype(jnp.bfloat16)
        value_block = lax.dynamic_slice_in_dim(
            values_all, block_index * block_width, block_width, 1
        ).reshape(length, head_group, head_width)
        attended = jnp.einsum(
            "hts,shd->thd", prob_low, value_block, preferred_element_type=jnp.float32
        ).reshape(row_count, block_width)
        mixed = lax.dynamic_update_slice_in_dim(mixed, attended, block_index * block_width, 1)
        summary = lax.dynamic_update_slice_in_dim(
            summary, (row_top + jnp.log(row_total))[..., 0], block_index * head_group, 0
        )
        return (mixed, summary)

    mixed, summary = lax.fori_loop(
        0,
        block_total,
        forward_block,
        (
            jnp.zeros((row_count, model_width), jnp.float32),
            jnp.zeros((head_count, row_count), jnp.float32),
        ),
    )
    mixed_low = mixed.astype(jnp.bfloat16)
    middle = inputs + product(mixed_low, w_out)
    normed_two, factor_two, scaled_two = normalize(middle, gain_two)
    second_low = scaled_two.astype(jnp.bfloat16)
    gate_pre = product(second_low, w_gate)
    up_pre = product(second_low, w_up)
    sigma = jax.nn.sigmoid(gate_pre)
    activated = gate_pre * sigma
    hidden_low = (activated * up_pre).astype(jnp.bfloat16)
    result = middle + product(hidden_low, w_down)
    rows_again = (
        lax.all_gather(low_masters[0], "seq", axis=0, tiled=True),
        lax.all_gather(low_masters[1], "seq", axis=0, tiled=True),
        lax.all_gather(low_masters[2], "seq", axis=0, tiled=True),
        lax.all_gather(low_masters[3], "seq", axis=0, tiled=True),
        lax.all_gather(low_masters[4], "seq", axis=0, tiled=True),
        lax.all_gather(low_masters[5], "seq", axis=0, tiled=True),
        lax.all_gather(low_masters[6], "seq", axis=0, tiled=True),
    )
    regathered = (
        lax.all_gather(rows_again[0], "dp", axis=1, tiled=True),
        lax.all_gather(rows_again[1], "dp", axis=1, tiled=True),
        lax.all_gather(rows_again[2], "dp", axis=1, tiled=True),
        lax.all_gather(rows_again[3], "dp", axis=1, tiled=True),
        lax.all_gather(rows_again[4], "dp", axis=1, tiled=True),
        lax.all_gather(rows_again[5], "dp", axis=1, tiled=True),
        lax.all_gather(rows_again[6], "dp", axis=1, tiled=True),
    )
    w_query, w_key, w_value, w_out, w_gate, w_up, w_down = regathered
    cot_low = cotangent[0]
    hidden_grad = contract_cols(cot_low, w_down)
    down_grad = contract_rows(hidden_low, cot_low)
    gate_grad = (hidden_grad * up_pre * sigma * (1.0 + gate_pre * (1.0 - sigma))).astype(
        jnp.bfloat16
    )
    up_grad = (hidden_grad * activated).astype(jnp.bfloat16)
    gate_w_grad = contract_rows(second_low, gate_grad)
    up_w_grad = contract_rows(second_low, up_grad)
    second_grad = contract_cols(gate_grad, w_gate) + contract_cols(up_grad, w_up)
    middle_part, ffn_gain_grad = norm_back(second_grad, normed_two, factor_two, gain_two)
    middle_grad = cot_low.astype(jnp.float32) + middle_part
    middle_low = middle_grad.astype(jnp.bfloat16)
    out_w_grad = contract_rows(mixed_low, middle_low)
    mixed_grad = contract_cols(middle_low, w_out).astype(jnp.bfloat16)
    keys_back, values_back, segments_back, variates_back = (
        lax.all_gather(key_low, "seq", axis=0, tiled=True),
        lax.all_gather(value_low, "seq", axis=0, tiled=True),
        lax.all_gather(key_segment, "seq", axis=0, tiled=True),
        lax.all_gather(key_variate, "seq", axis=0, tiled=True),
    )
    allowed_back, same_back = make_tables(segment, variate, segments_back, variates_back, first_row)

    def query_side(block_index):
        scores, query_block, key_block = block_scores(
            block_index,
            query_low,
            keys_back,
            same_back,
            same_bias,
            cross_bias,
            head_group,
            head_width,
        )
        lse_block = lax.dynamic_slice_in_dim(summary, block_index * head_group, head_group, 0)
        probabilities = jnp.exp(
            jnp.where(allowed_back[None], scores - lse_block[:, :, None], -jnp.inf)
        )
        grad_block = lax.dynamic_slice_in_dim(
            mixed_grad, block_index * block_width, block_width, 1
        ).reshape(row_count, head_group, head_width)
        value_block = lax.dynamic_slice_in_dim(
            values_back, block_index * block_width, block_width, 1
        ).reshape(length, head_group, head_width)
        prob_grad = jnp.einsum(
            "thd,shd->hts", grad_block, value_block, preferred_element_type=jnp.float32
        )
        inner_sum = jnp.sum(probabilities * prob_grad, axis=-1, keepdims=True)
        score_low = (probabilities * (prob_grad - inner_sum)).astype(jnp.bfloat16)
        score_wide = score_low.astype(jnp.float32)
        same_part = jnp.sum(jnp.where(same_back[None], score_wide, 0.0), axis=(1, 2))
        cross_part = jnp.sum(jnp.where(same_back[None], 0.0, score_wide), axis=(1, 2))
        query_part = (
            jnp.einsum(
                "hts,shd->thd", score_low, key_block, preferred_element_type=jnp.float32
            ).reshape(row_count, block_width)
            * scaling
        )
        return (
            probabilities,
            score_low,
            query_block,
            grad_block,
            inner_sum[..., 0],
            same_part,
            cross_part,
            query_part,
        )

    def backward_block(block_index, state_now):
        query_grad, key_grad, value_grad, same_grad, cross_grad = state_now
        (
            probabilities,
            score_low,
            query_block,
            grad_block,
            inner_sum,
            same_part,
            cross_part,
            query_part,
        ) = query_side(block_index)
        key_part = (
            jnp.einsum(
                "hts,thd->shd", score_low, query_block, preferred_element_type=jnp.float32
            ).reshape(length, block_width)
            * scaling
        )
        value_part = jnp.einsum(
            "hts,thd->shd",
            probabilities.astype(jnp.bfloat16),
            grad_block,
            preferred_element_type=jnp.float32,
        ).reshape(length, block_width)
        query_grad = lax.dynamic_update_slice_in_dim(
            query_grad, query_part, block_index * block_width, 1
        )
        key_grad = lax.dynamic_update_slice_in_dim(key_grad, key_part, block_index * block_width, 1)
        value_grad = lax.dynamic_update_slice_in_dim(
            value_grad, value_part, block_index * block_width, 1
        )
        same_grad = lax.dynamic_update_slice_in_dim(
            same_grad, same_part, block_index * head_group, 0
        )
        cross_grad = lax.dynamic_update_slice_in_dim(
            cross_grad, cross_part, block_index * head_group, 0
        )
        return (query_grad, key_grad, value_grad, same_grad, cross_grad)

    start_state = (
        jnp.zeros((row_count, model_width), jnp.float32),
        jnp.zeros((length, model_width), jnp.float32),
        jnp.zeros((length, model_width), jnp.float32),
        jnp.zeros((head_count,), jnp.float32),
        jnp.zeros((head_count,), jnp.float32),
    )
    query_grad, key_grad, value_grad, same_grad, cross_grad = lax.fori_loop(
        0, block_total, backward_block, start_state
    )
    key_share, value_share = (
        lax.psum_scatter(
            key_grad.astype(jnp.bfloat16), "seq", scatter_dimension=0, tiled=True
        ).astype(jnp.float32),
        lax.psum_scatter(
            value_grad.astype(jnp.bfloat16), "seq", scatter_dimension=0, tiled=True
        ).astype(jnp.float32),
    )
    query_pre_grad = rotate(query_grad, -angles, head_count).astype(jnp.bfloat16)
    key_pre_grad = rotate(key_share, -angles, head_count).astype(jnp.bfloat16)
    value_pre_grad = value_share.astype(jnp.bfloat16)
    query_w_grad = contract_rows(first_low, query_pre_grad)
    key_w_grad = contract_rows(first_low, key_pre_grad)
    value_w_grad = contract_rows(first_low, value_pre_grad)
    first_grad = (
        contract_cols(query_pre_grad, w_query)
        + contract_cols(key_pre_grad, w_key)
        + contract_cols(value_pre_grad, w_value)
    )
    input_part, attn_gain_grad = norm_back(first_grad, normed_one, factor_one, gain_one)
    input_grad = (middle_grad + input_part).astype(jnp.bfloat16)
    col_shares = (
        lax.psum_scatter(
            query_w_grad.astype(jnp.bfloat16), "dp", scatter_dimension=1, tiled=True
        ).astype(jnp.float32),
        lax.psum_scatter(
            key_w_grad.astype(jnp.bfloat16), "dp", scatter_dimension=1, tiled=True
        ).astype(jnp.float32),
        lax.psum_scatter(
            value_w_grad.astype(jnp.bfloat16), "dp", scatter_dimension=1, tiled=True
        ).astype(jnp.float32),
        lax.psum_scatter(
            out_w_grad.astype(jnp.bfloat16), "dp", scatter_dimension=1, tiled=True
        ).astype(jnp.float32),
        lax.psum_scatter(
            gate_w_grad.astype(jnp.bfloat16), "dp", scatter_dimension=1, tiled=True
        ).astype(jnp.float32),
        lax.psum_scatter(
            up_w_grad.astype(jnp.bfloat16), "dp", scatter_dimension=1, tiled=True
        ).astype(jnp.float32),
        lax.psum_scatter(
            down_grad.astype(jnp.bfloat16), "dp", scatter_dimension=1, tiled=True
        ).astype(jnp.float32),
    )
    shares = (
        lax.psum_scatter(
            col_shares[0].astype(jnp.bfloat16), "seq", scatter_dimension=0, tiled=True
        ).astype(jnp.float32),
        lax.psum_scatter(
            col_shares[1].astype(jnp.bfloat16), "seq", scatter_dimension=0, tiled=True
        ).astype(jnp.float32),
        lax.psum_scatter(
            col_shares[2].astype(jnp.bfloat16), "seq", scatter_dimension=0, tiled=True
        ).astype(jnp.float32),
        lax.psum_scatter(
            col_shares[3].astype(jnp.bfloat16), "seq", scatter_dimension=0, tiled=True
        ).astype(jnp.float32),
        lax.psum_scatter(
            col_shares[4].astype(jnp.bfloat16), "seq", scatter_dimension=0, tiled=True
        ).astype(jnp.float32),
        lax.psum_scatter(
            col_shares[5].astype(jnp.bfloat16), "seq", scatter_dimension=0, tiled=True
        ).astype(jnp.float32),
        lax.psum_scatter(
            col_shares[6].astype(jnp.bfloat16), "seq", scatter_dimension=0, tiled=True
        ).astype(jnp.float32),
    )
    small_totals = lax.psum((same_grad, cross_grad, attn_gain_grad, ffn_gain_grad), ("dp", "seq"))
    return (
        result.astype(jnp.bfloat16)[None],
        input_grad[None],
        small_totals[2],
        shares[0],
        shares[1],
        shares[2],
        shares[3],
        small_totals[0],
        small_totals[1],
        small_totals[3],
        shares[4],
        shares[5],
        shares[6],
    )


MESH = pl.DeviceIdType.MESH
NEG = -1e30
low = jnp.bfloat16
wide = jnp.float32

def remote(src, dst, send_sem, recv_sem, d, s):
    return pltpu.make_async_remote_copy(
        src_ref=src,
        dst_ref=dst,
        send_sem=send_sem,
        recv_sem=recv_sem,
        device_id=(d, s),
        device_id_type=MESH,
    )


def arrived(dst, recv_sem, d, s):
    remote(dst, dst, recv_sem, recv_sem, d, s).wait_recv()


def sent(src, send_sem, d, s):
    remote(src, src, send_sem, send_sem, d, s).wait_send()


def pair_of(s):
    z = s // 2
    c = lax.rem(s, 2)
    return 2 * (2 * c + lax.rem(z, 2)) + z // 2


class Chain:
    def __init__(self, d, s, view, parts, up_sem, recv_sem, side_sem, side_recv):
        self.d, self.s, self.z, self.c = d, s, s // 2, lax.rem(s, 2)
        self.view, self.parts = view, parts
        self.up_sem, self.recv_sem = up_sem, recv_sem
        self.side_sem, self.side_recv = side_sem, side_recv

    def block(self, z):
        return self.view(2 * z + self.c)

    def part(self, z, h):
        n = 128 // self.parts
        return self.block(z).at[pl.ds(n * h, n)]

    def up(self, z, h):
        b = self.part(z, h)
        return remote(
            b, b, self.up_sem.at[(self.z - z) * self.parts + h],
            self.recv_sem.at[z * self.parts + h], self.d, self.s + 2,
        )

    def down(self, z, h):
        b = self.part(z, h)
        return remote(
            b, b, self.up_sem.at[(3 + z - self.z) * self.parts + h],
            self.recv_sem.at[z * self.parts + h], self.d, self.s - 2,
        )

    def side(self, z):
        b = self.block(z)
        return remote(b, b, self.side_sem.at[z], self.side_recv.at[z], self.d, self.s + 1 - 2 * self.c)

    def start_lane(self):
        for h in range(self.parts):

            @pl.when(self.z < 3)
            def _():
                self.up(self.z, h).start()

            @pl.when(self.z > 0)
            def _():
                self.down(self.z, h).start()

    def start(self):
        self.start_lane()
        self.side(self.z).start()

    def lane_step(self, k, share=False):
        lo, hi = self.z - k, self.z + k
        for h in range(self.parts):
            last = share and h == self.parts - 1

            @pl.when(lo >= 0)
            def _():
                arrived(self.part(lo, h), self.recv_sem.at[lo * self.parts + h], self.d, self.s)

                @pl.when(self.z < 3)
                def _():
                    self.up(lo, h).start()

                if last:
                    self.side(lo).start()

            @pl.when(hi <= 3)
            def _():
                arrived(self.part(hi, h), self.recv_sem.at[hi * self.parts + h], self.d, self.s)

                @pl.when(self.z > 0)
                def _():
                    self.down(hi, h).start()

                if last:
                    self.side(hi).start()

    def step(self, k):
        self.lane_step(k, True)

    def wait_side(self, z):
        arrived(self.view(2 * z + 1 - self.c), self.side_recv.at[z], self.d, self.s)

    def drain(self):
        own = self.block(self.z)
        for z in range(4):
            sent(own, self.side_sem.at[z], self.d, self.s)
        self.lane_drain()

    def lane_drain(self):
        for h in range(self.parts):
            own = self.part(self.z, h)
            for k in range(3):

                @pl.when((self.z < 3) & (self.z - k >= 0))
                def _():
                    sent(own, self.up_sem.at[k * self.parts + h], self.d, self.s)

                @pl.when((self.z > 0) & (self.z + k <= 3))
                def _():
                    sent(own, self.up_sem.at[(3 + k) * self.parts + h], self.d, self.s)

    def start_direct(self):
        own = self.block(self.z)
        for k in range(1, 4):
            t = lax.rem(self.z + k, 4)
            remote(
                own, own, self.up_sem.at[k], self.recv_sem.at[self.z], self.d, 2 * t + self.c
            ).start()
        self.side(self.z).start()

    def collect(self, z):
        arrived(self.block(z), self.recv_sem.at[z], self.d, self.s)
        self.side(z).start()

    def drain_direct(self):
        own = self.block(self.z)
        for z in range(4):
            sent(own, self.side_sem.at[z], self.d, self.s)
        for k in range(1, 4):
            sent(own, self.up_sem.at[k], self.d, self.s)


class Plane:
    def __init__(self, d, s, whole, half, send_sem, recv_sem):
        self.d, self.s = d, s
        self.dx = d + 1 - 2 * lax.rem(d, 2)
        self.dy = lax.rem(d + 2, 4)
        self.far = 3 - d
        self.whole, self.half = whole, half
        self.send_sem, self.recv_sem = send_sem, recv_sem

    def start(self):
        w = self.whole(self.d)
        remote(w, w, self.send_sem.at[0], self.recv_sem.at[0], self.dx, self.s).start()
        remote(w, w, self.send_sem.at[1], self.recv_sem.at[1], self.dy, self.s).start()

    def step(self):
        arrived(self.whole(self.dx), self.recv_sem.at[0], self.d, self.s)
        h = self.half(self.dx, 0)
        remote(h, h, self.send_sem.at[2], self.recv_sem.at[2], self.dy, self.s).start()
        arrived(self.whole(self.dy), self.recv_sem.at[1], self.d, self.s)
        h = self.half(self.dy, 1)
        remote(h, h, self.send_sem.at[3], self.recv_sem.at[3], self.dx, self.s).start()

    def finish(self):
        arrived(self.half(self.far, 0), self.recv_sem.at[2], self.d, self.s)
        arrived(self.half(self.far, 1), self.recv_sem.at[3], self.d, self.s)
        w = self.whole(self.d)
        sent(w, self.send_sem.at[0], self.d, self.s)
        sent(w, self.send_sem.at[1], self.d, self.s)
        h = self.half(self.d, 0)
        sent(h, self.send_sem.at[2], self.d, self.s)
        h = self.half(self.d, 1)
        sent(h, self.send_sem.at[3], self.d, self.s)


def lanes(i):
    return pl.ds(pl.multiple_of(i * 128, 128), 128)


def rows(i, n=128):
    return pl.ds(pl.multiple_of(i * n, n), n)


def dot(a, b):
    return jnp.dot(a, b, preferred_element_type=wide)


def dot_nt(a, b):
    return lax.dot_general(a, b, (((1,), (1,)), ((), ())), preferred_element_type=wide)


def dot_tn(a, b):
    return lax.dot_general(a, b, (((0,), (0,)), ((), ())), preferred_element_type=wide)


def head_lanes(h):
    place = lax.broadcasted_iota(jnp.int32, (1, 128), 1)
    return (place // 64) == h


def partner(x):
    place = lax.broadcasted_iota(jnp.int32, x.shape, 1)
    return jnp.where(lax.rem(place, 64) < 32, pltpu.roll(x, 96, 1), pltpu.roll(x, 32, 1))


class Scatter:
    def __init__(self, d, s, keep, own, side_out, side_in, out, got, relay, sems):
        self.d, self.s, self.z, self.c = d, s, s // 2, lax.rem(s, 2)
        self.keep, self.own, self.side_out, self.side_in = keep, own, side_out, side_in
        self.out, self.got, self.relay = out, got, relay
        self.side_s, self.side_r, self.send_s, self.recv = (sems.at[i] for i in range(4))

    def passes(self, z):
        return ((self.z == 1) & (z >= 2)) | ((self.z == 2) & (z <= 1))

    def give(self, j, z, value):
        first, second = value[:128], value[128:]
        even = self.c == 0
        self.side_out[z] = jnp.where(even, second, first).astype(low)
        remote(
            self.side_out.at[z], self.side_in.at[z], self.side_s.at[z], self.side_r.at[z],
            self.d, self.s + 1 - 2 * self.c,
        ).start()
        self.keep[j % 2] = jnp.where(even, first, second)

    def send(self, z, place, slot, chip):
        remote(
            self.out.at[z], place.at[slot], self.send_s.at[z],
            self.recv.at[slot if place is self.got else 2 + slot], self.d, 2 * chip + self.c,
        ).start()

    def pass_on(self, j, z):
        arrived(self.side_in.at[z], self.side_r.at[z], self.d, self.s)
        total = self.keep[j % 2] + self.side_in[z].astype(wide)
        end = (self.z == 0) | (self.z == 3)
        near = (z - self.z == 1) | (self.z - z == 1)

        @pl.when(z == self.z)
        def _():
            self.own[...] = total

        @pl.when(z != self.z)
        def _():
            self.out[z] = total.astype(low)

            @pl.when(near & jnp.logical_not(self.passes(z)))
            def _():
                self.send(z, self.got, 0, z)

            @pl.when(end & jnp.logical_not(near))
            def _():
                self.send(z, self.relay, lax.rem(z, 2), 1 + self.z // 3)

    def add_relay(self, z):
        @pl.when(self.passes(z))
        def _():
            slot = lax.rem(z, 2)
            arrived(self.relay.at[slot], self.recv.at[2 + slot], self.d, self.s)
            self.out[z] = (self.out[z].astype(wide) + self.relay[slot].astype(wide)).astype(low)
            self.send(z, self.got, 1, z)

    def total(self):
        value = self.own[...]
        for slot in range(2):
            arrived(self.got.at[slot], self.recv.at[slot], self.d, self.s)
            value = value + self.got[slot].astype(wide)
        return value

    def drain(self):
        for z in range(4):
            sent(self.side_out.at[z], self.side_s.at[z], self.d, self.s)

            @pl.when(z != self.z)
            def _():
                sent(self.out.at[z], self.send_s.at[z], self.d, self.s)


def scatter_scratch():
    blocks = pltpu.VMEM((4, 128, 1024), low)
    return dict(
        keep=pltpu.VMEM((2, 128, 1024), wide),
        own=pltpu.VMEM((128, 1024), wide),
        side_out=blocks,
        side_in=blocks,
        out=blocks,
        got=pltpu.VMEM((2, 128, 1024), low),
        relay=pltpu.VMEM((2, 128, 1024), low),
        sems=dma(4, 4),
    )


def ring_scratch(parts):
    return dict(
        up_sem=dma(6 * parts), recv_sem=dma(4 * parts), side_sem=dma(4), side_recv=dma(4)
    )


class PlaneScatter:
    def __init__(self, d, s, part, first_a, first_b, middle_out, second, send_sem, recv_sem):
        self.d, self.s = d, s
        self.dx = d + 1 - 2 * lax.rem(d, 2)
        self.dy = lax.rem(d + 2, 4)
        self.far = 3 - d
        self.part = part
        self.first = (first_a, first_b)
        self.middle_out, self.second = middle_out, second
        self.send_sem, self.recv_sem = send_sem, recv_sem

    def start(self):
        for n, near in enumerate((self.dx, self.dy)):
            for m, block in enumerate((self.far, near)):
                k = 2 * n + m
                remote(
                    self.part(block, n), self.first[n].at[m], self.send_sem.at[k], self.recv_sem.at[k],
                    near, self.s,
                ).start()

    def step(self):
        for n, other in enumerate((self.dy, self.dx)):
            arrived(self.first[n].at[0], self.recv_sem.at[2 * n], self.d, self.s)
            total = self.part(other, n)[...].astype(wide) + self.first[n][0].astype(wide)
            self.middle_out[n] = total.astype(low)
            remote(
                self.middle_out.at[n], self.second.at[n], self.send_sem.at[4 + n],
                self.recv_sem.at[4 + n], other, self.s,
            ).start()

    def total(self, n):
        arrived(self.first[n].at[1], self.recv_sem.at[2 * n + 1], self.d, self.s)
        arrived(self.second.at[n], self.recv_sem.at[4 + n], self.d, self.s)
        value = self.part(self.d, n)[...].astype(wide) + self.first[n][1].astype(wide)
        return value + self.second[n].astype(wide)

    def drain(self):
        for k in range(4):
            sent(self.first[0].at[0], self.send_sem.at[k], self.d, self.s)
        for k in range(2):
            sent(self.middle_out.at[0], self.send_sem.at[4 + k], self.d, self.s)


def plane_scratch(*dims):
    blocks = pltpu.VMEM((2, *dims), low)
    return dict(
        first_a=blocks, first_b=blocks, middle_out=blocks, second=blocks,
        send_sem=dma(6), recv_sem=dma(6),
    )


def owner_of(dd, i):
    return 2 * (lax.rem(dd, 2) + 2 * i) + dd // 2


def chip_order(z, j):
    table = ((0, 1, 2, 3), (1, 0, 2, 3), (2, 1, 3, 0), (3, 2, 1, 0))
    value = z * 0 + table[0][j]
    for n in range(1, 4):
        value = jnp.where(z == n, table[n][j], value)
    return value


def far_order(z, j):
    table = ((3, 2, 1, 0), (3, 2, 0, 1), (0, 1, 3, 2), (0, 1, 2, 3))
    value = z * 0 + table[0][j]
    for n in range(1, 4):
        value = jnp.where(z == n, table[n][j], value)
    return value


def pair_owner(p):
    dd, i = p // 2, p % 2
    return 2 * (dd % 2 + 2 * i) + dd // 2


def row_norm(value):
    return lax.rsqrt(jnp.mean(value * value, axis=-1, keepdims=True) + epsilon)


def layer_kernel(given, made, form, *refs):
    names = (*given, *made)
    held = jax.tree.unflatten(form, refs[len(names) :])
    r = types.SimpleNamespace(**dict(zip(names, refs)), **held)
    d = lax.axis_index("dp")
    s = lax.axis_index("seq")
    z = s // 2
    c = lax.rem(s, 2)
    dx = d + 1 - 2 * lax.rem(d, 2)
    dy = lax.rem(d + 2, 4)
    sibling = s + 1 - 2 * c
    home = 2 * c + lax.rem(z, 2)
    is_home = d == home
    pair = pair_of(s)
    cols_d = lanes(d)
    wide_of = lambda i: pl.ds(pl.multiple_of(i * 256, 256), 256)
    wide_d = wide_of(d)

    own_is_target = is_home & (lax.rem(s, 4) == d)
    barrier = pltpu.get_barrier_semaphore()
    for k in range(1, 8):
        pl.semaphore_signal(barrier, inc=1, device_id=(d, lax.rem(s + k, 8)), device_id_type=MESH)
    for k in range(1, 4):
        pl.semaphore_signal(barrier, inc=1, device_id=(lax.rem(d + k, 4), s), device_id_type=MESH)
    for i in range(2):
        giver = owner_of(d, i)

        @pl.when((giver != s) | (lax.rem(s, 4) != d))
        def _():
            pl.semaphore_signal(
                barrier, inc=1, device_id=(lax.rem(s, 4), giver), device_id_type=MESH
            )

    loads = [
        pltpu.make_async_copy(src, dst, r.load_s.at[n])
        for n, (src, dst) in enumerate((
            (r.wo_in, r.wo_f), (r.wg_in, r.gu_f.at[0]), (r.wu_in, r.gu_f.at[1]), (r.wd_in, r.dn_f),
            (r.cot.at[0], r.call.at[s]),
        ))
    ]
    for load in loads:
        load.start()

    for i in range(2):
        for n, w in enumerate((r.wq, r.wk, r.wv)):
            r.qkv_src[i, :, 128 * n : 128 * (n + 1)] = w[:, 128 * i : 128 * (i + 1)].astype(low)
    segment = r.segment[...]
    r.ids[0:1, :] = segment.astype(wide)
    r.ids[1:2, :] = jnp.where(r.observed[...] == 1, segment, -1).astype(wide)
    r.ids[2:3, :] = r.variate[...].astype(wide)
    r.ids[3:4, :] = r.moment[...].astype(wide)
    r.ids[4:8, :] = jnp.zeros((4, 128), wide)
    r.idr[s] = r.ids[...]
    gain_one = r.attn_gain[...].reshape(1, 1024).astype(low).astype(wide)
    gain_two = r.ffn_gain[...].reshape(1, 1024).astype(low).astype(wide)
    value = r.tokens[0].astype(wide)
    r.xall[s] = (value * row_norm(value) * gain_one).astype(low)

    @pl.when(own_is_target)
    def _():
        pl.semaphore_wait(barrier, 11)

    @pl.when(jnp.logical_not(own_is_target))
    def _():
        pl.semaphore_wait(barrier, 12)

    owner = [owner_of(d, i) for i in range(2)]
    for i in range(2):

        @pl.when(owner[i] != s)
        def _():
            remote(r.qkv_src.at[i], r.wqkv.at[rows(s)], r.qs_s.at[i], r.qs_r.at[s], d, owner[i]).start()

        @pl.when(owner[i] == s)
        def _():
            r.wqkv[rows(s), :] = r.qkv_src[i]

    for k in range(1, 8):
        remote(r.ids, r.idr.at[s], r.id_s.at[k], r.id_r.at[s], d, lax.rem(s + k, 8)).start()
    loads[0].wait()
    r.wo[s, :, wide_d] = r.wo_f[...].astype(low)
    wo_ring = Chain(d, s, lambda b: r.wo.at[b, :, wide_d], 1, **r.wo_sems)
    wo_ring.start_lane()
    x_ring = ring = Chain(d, s, lambda b: r.xall.at[b], 2, **r.x_sems)
    ring.start()

    for load in loads[1:]:
        load.wait()
    r.gu_src[...] = r.gu_f[...].astype(low)
    r.dn_src[...] = r.dn_f[...].astype(low)
    c_ring = Chain(d, s, lambda b: r.call.at[b], 2, **r.c_sems)

    for k in range(1, 8):
        t = lax.rem(s + k, 8)
        arrived(r.idr.at[t], r.id_r.at[t], d, s)
    for b in range(8):
        block = r.idr[b]
        for n in range(4):
            r.keyrow[n : n + 1, 128 * b : 128 * (b + 1)] = block[n : n + 1, :]
        r.idc[128 * b : 128 * (b + 1), :] = jnp.concatenate([block] * 16, axis=0).T
    wo_ring.lane_step(1)

    half_qkv = lambda n: r.wqkv.at[pl.ds(512 * n, 512)]

    @pl.when(is_home)
    def _():
        for k in range(1, 8):
            t = lax.rem(s + k, 8)
            arrived(r.wqkv.at[rows(t)], r.qs_r.at[t], d, s)
        remote(r.wqkv, r.wqkv, r.qp_s.at[0], r.qp_r.at[0], dx, s).start()
        remote(r.wqkv, r.wqkv, r.qp_s.at[1], r.qp_r.at[0], dy, s).start()

    wo_ring.lane_step(2)
    ring.step(1)
    wo_ring.lane_step(3)
    place = lax.broadcasted_iota(jnp.int32, (1, 128), 1)
    sign = jnp.where(lax.rem(place, 64) < 32, -1.0, 1.0)
    freq = r.freq[...]

    def trig(b, carry):
        angle = r.idc[rows(b), 3:4] * freq
        r.cosine[rows(b), :] = jnp.cos(angle)
        r.sine[rows(b), :] = jnp.sin(angle) * sign
        return carry

    lax.fori_loop(0, 8, trig, 0)
    ring.step(2)

    for k in range(1, 8):
        t = lax.rem(s + k, 8)
        remote(
            r.gu_src.at[:, :, lanes(t)], r.wgu.at[:, rows(s), cols_d], r.gu_s.at[k], r.gu_r.at[s], d, t
        ).start()
    r.wgu[:, rows(s), cols_d] = r.gu_src[:, :, lanes(s)]
    for m in range(4):
        t = c * 4 + m

        @pl.when(t != s)
        def _():
            remote(
                r.dn_src.at[pl.ds(128 * m, 128)], r.wd.at[rows(z), wide_d],
                r.dn_s.at[m], r.dn_r.at[z], d, t,
            ).start()

        @pl.when(t == s)
        def _():
            r.wd[rows(z), wide_d] = r.dn_src[pl.ds(128 * m, 128), :]

    @pl.when(home == dx)
    def _():
        arrived(r.wqkv, r.qp_r.at[0], d, s)
        remote(half_qkv(0), half_qkv(0), r.qp_s.at[2], r.qp_r.at[1], dy, s).start()

    @pl.when(home == dy)
    def _():
        arrived(r.wqkv, r.qp_r.at[0], d, s)
        remote(half_qkv(1), half_qkv(1), r.qp_s.at[2], r.qp_r.at[2], dx, s).start()

    def group(i):
        zs = chip_order(z, i)
        part = rows(zs, 256)
        gu_part = Plane(
            d, s, lambda i: r.wgu.at[:, part, lanes(i)], lambda i, n: r.wgu.at[n, part, lanes(i)],
            r.gup_s.at[zs], r.gup_r.at[zs],
        )
        dn_part = Plane(
            d, s, lambda i: r.wd.at[rows(zs), wide_of(i)],
            lambda i, n: r.wd.at[rows(2 * zs + n, 64), wide_of(i)],
            r.dnp_s.at[zs], r.dnp_r.at[zs],
        )
        return zs, gu_part, dn_part

    def group_start(i):
        zs, gu_part, dn_part = group(i)
        for m in range(2):
            t = 2 * zs + m

            @pl.when(t != s)
            def _():
                arrived(r.wgu.at[:, rows(t), cols_d], r.gu_r.at[t], d, s)

        gu_part.start()

        @pl.when(2 * zs + s // 4 != s)
        def _():
            arrived(r.wd.at[rows(zs), wide_d], r.dn_r.at[zs], d, s)

        dn_part.start()

    def group_step(i):
        zs, gu_part, dn_part = group(i)
        gu_part.step()
        dn_part.step()

    def group_finish(i):
        zs, gu_part, dn_part = group(i)
        gu_part.finish()
        dn_part.finish()

    wo_lane = r.wo.reshape(4, 2, 128, 1024)
    wo_plane = Plane(
        d, s, lambda i: wo_lane.at[:, c, :, wide_of(i)],
        lambda i, n: wo_lane.at[pl.ds(2 * n, 2), c, :, wide_of(i)],
        r.pl_s, r.pl_r,
    )
    wo_side = lambda: remote(
        wo_lane.at[:, c], wo_lane.at[:, c], r.wos_s, r.wos_r, d, sibling
    )
    wo_plane.start()
    ring.step(3)
    group_start(0)
    for zz in range(4):
        ring.wait_side(zz)

    @pl.when(home == 3 - d)
    def _():
        arrived(half_qkv(0), r.qp_r.at[1], d, s)
        arrived(half_qkv(1), r.qp_r.at[2], d, s)

    def project(i, carry):
        pick = rows(i, 256)
        pre = dot(r.xall[pl.ds(2 * i, 2)].reshape(256, 1024), r.wqkv[...])
        cs, sn = r.cosine[pick, :], r.sine[pick, :]
        qp, kp = pre[:, :128], pre[:, 128:256]
        r.q_all[pick, :] = (qp * cs + partner(qp) * sn).astype(low)
        r.k_all[pick, :] = (kp * cs + partner(kp) * sn).astype(low)
        r.v_all[pick, :] = pre[:, 256:].astype(low)
        return carry

    c_ring.start()
    lax.fori_loop(0, 4, project, 0)

    def tables(pick, first, count):
        seg_col, var_col = r.idc[pick, 0:1], r.idc[pick, 2:3]
        q_place = first + lax.broadcasted_iota(jnp.int32, (count, 1), 0)
        k_place = lax.broadcasted_iota(jnp.int32, (1, 1024), 1)
        allowed = (seg_col == r.keyrow[1:2, :]) | (q_place == k_place)
        return allowed, var_col == r.keyrow[2:3, :]

    def scores_of(qh, h, same):
        scores = dot_nt(qh, r.k_all[...]) * 0.125
        return scores + jnp.where(same, r.same_bias[2 * pair + h], r.cross_bias[2 * pair + h])

    def attend(b, carry):
        pick = rows(b)
        allowed, same = tables(pick, b * 128, 128)
        q_block = r.q_all[pick, :]
        attended, total_lse = None, None
        for h in range(2):
            mine = head_lanes(h)
            qh = jnp.where(mine, q_block, jnp.zeros_like(q_block))
            scores = jnp.where(allowed, scores_of(qh, h, same), NEG)
            top = jnp.max(scores, axis=-1, keepdims=True)
            e = jnp.exp(scores - top)
            total = jnp.sum(e, axis=-1, keepdims=True)
            part = dot((e * (1.0 / total)).astype(low), r.v_all[...])
            one = top + jnp.log(total)
            attended = part if h == 0 else jnp.where(mine, part, attended)
            total_lse = one if h == 0 else jnp.where(mine, one, total_lse)
        r.head_out[b] = attended.astype(low)
        r.lse[pick, :] = jnp.broadcast_to(total_lse, (128, 128))
        return carry

    def send_mixed(t):
        @pl.when(t != s)
        def _():
            remote(r.head_out.at[t], r.mixed.at[pair], r.m_s.at[t], r.m_r.at[s], d, t).start()

        @pl.when(t == s)
        def _():
            r.mixed[pair] = r.head_out[t]

    lax.fori_loop(0, 2, attend, 0)
    send_mixed(0)
    send_mixed(1)
    wo_plane.step()
    group_start(1)
    lax.fori_loop(2, 4, attend, 0)
    send_mixed(2)
    send_mixed(3)
    group_step(0)
    lax.fori_loop(4, 6, attend, 0)
    send_mixed(4)
    send_mixed(5)
    group_start(2)
    lax.fori_loop(6, 8, attend, 0)
    send_mixed(6)
    send_mixed(7)
    wo_plane.finish()
    wo_side().start()
    c_ring.step(1)
    group_step(1)
    group_start(3)
    for t in range(8):

        @pl.when(t != s)
        def _():
            arrived(r.mixed.at[pair_of(t)], r.m_r.at[t], d, s)

    arrived(wo_lane.at[:, 1 - c], r.wos_r, d, s)

    joined = jnp.concatenate([r.mixed[p] for p in range(8)], axis=1)
    middle = r.tokens[0].astype(wide) + dot(joined, r.wo[...].reshape(1024, 1024))
    r.sall[s] = (middle * row_norm(middle) * gain_two).astype(low)
    ring = Chain(d, s, lambda b: r.sall.at[b], 2, **r.y_sems)
    ring.start()
    r.mid[...] = middle
    group_step(2)
    ring.step(1)
    group_step(3)
    ring.step(2)
    for i in range(4):
        group_finish(i)

    grads = Scatter(d, s, **r.g_parts)
    outs = Scatter(d, s, **r.o_parts)
    for j in range(4):
        zj = chip_order(z, j)
        if j == 3:
            ring.step(3)
        ring.wait_side(zj)
        pick = rows(zj, 256)
        block = r.sall[pl.ds(2 * zj, 2)].reshape(256, 1024)
        gate_pre = dot(block, r.wgu[0])
        up_pre = dot(block, r.wgu[1])
        r.pre[0, pick, :] = gate_pre
        r.pre[1, pick, :] = up_pre
        hidden = (gate_pre * jax.nn.sigmoid(gate_pre) * up_pre).astype(low)
        r.hid[pick, :] = hidden
    for j in range(4):
        zj = chip_order(z, j)
        if j > 1:
            c_ring.step(j)
        c_ring.wait_side(zj)
        pick = rows(zj, 256)
        hg = dot_nt(r.call[pl.ds(2 * zj, 2)].reshape(256, 1024), r.wd[...])
        gate_pre, up_pre = r.pre[0, pick, :], r.pre[1, pick, :]
        sigma = jax.nn.sigmoid(gate_pre)
        g_low = (hg * up_pre * sigma * (1.0 + gate_pre * (1.0 - sigma))).astype(low)
        u_low = (hg * (gate_pre * sigma)).astype(low)
        r.gg[pick, :] = g_low
        r.ug[pick, :] = u_low
        grads.give(j, zj, dot_nt(g_low, r.wgu[0]) + dot_nt(u_low, r.wgu[1]))
        if j > 0:
            grads.pass_on(j - 1, chip_order(z, j - 1))
        if j > 1:
            grads.add_relay(chip_order(z, j - 2))
    grads.pass_on(3, chip_order(z, 3))
    grads.add_relay(chip_order(z, 2))

    def weigh(i, carry):
        block = r.sall[:, :, wide_of(i)].reshape(1024, 256)
        r.gu_grad[0, rows(i, 256), :] = dot_tn(block, r.gg[...]).astype(low)
        r.gu_grad[1, rows(i, 256), :] = dot_tn(block, r.ug[...]).astype(low)
        return carry

    lax.fori_loop(0, 4, weigh, 0)
    grads.add_relay(chip_order(z, 3))
    gu = PlaneScatter(d, s, lambda i, n: r.gu_grad.at[n, :, lanes(i)], **r.gu_parts)
    dn = PlaneScatter(
        d, s, lambda i, n: r.dn_grad.at[pl.ds(256 * n, 256), wide_of(i)], **r.dn_parts
    )
    wo = PlaneScatter(
        d, s, lambda i, n: r.wo_sum.at[pl.ds(2 * n, 2), :, wide_of(i)], **r.wo_parts
    )
    gu.start()

    def weigh_down(i, carry):
        cols = wide_of(i)
        r.dn_grad[:, cols] = dot_tn(r.hid[...], r.call[:, :, cols].reshape(1024, 256)).astype(low)
        return carry

    lax.fori_loop(0, 4, weigh_down, 0)
    dn.start()

    middle = r.mid[...]
    factor = row_norm(middle)
    normed = middle * factor
    second_grad = grads.total()
    scaled = second_grad * gain_two
    inner = jnp.mean(scaled * normed, axis=-1, keepdims=True)
    r.small[...] = jnp.zeros_like(r.small)
    r.small[1:2, :] = jnp.sum(second_grad * normed, axis=0, keepdims=True)
    value = r.call[s].astype(wide) + factor * (scaled - normed * inner)
    r.mid_grad[...] = value
    v_low = value.astype(low)
    mg = dot_nt(v_low, r.wo[...].reshape(1024, 1024)).astype(low)
    for p in range(8):
        r.mg_src[p] = mg[:, 128 * p : 128 * (p + 1)]
        t = pair_owner(p)

        @pl.when(s != t)
        def _():
            remote(r.mg_src.at[p], r.mgrad.at[s], r.mg_s.at[p], r.mg_r.at[s], d, t).start()

        @pl.when(s == t)
        def _():
            r.mgrad[s] = r.mg_src[p]

    def weigh_out(i, carry):
        left = jnp.concatenate([r.mixed[2 * i], r.mixed[2 * i + 1]], axis=1)
        part = dot_tn(left, v_low).astype(low)
        r.wo_grad[i, 0] = part[:128]
        r.wo_grad[i, 1] = part[128:]
        return carry

    lax.fori_loop(0, 4, weigh_out, 0)
    side = remote(r.wo_grad.at[:, 1 - c], r.wo_in2, r.side_s, r.side_r, d, sibling)
    side.start()
    for j in range(4):
        zj = far_order(z, j)
        outs.give(j, zj, dot(r.hid[rows(zj, 256), :], r.wd[...]))
        if j > 0:
            outs.pass_on(j - 1, far_order(z, j - 1))
    outs.pass_on(3, z)
    r.dk[...] = jnp.zeros_like(r.dk)
    r.dv[...] = jnp.zeros_like(r.dv)
    r.bsum[...] = jnp.zeros_like(r.bsum)
    gu.step()
    side.wait_recv()
    for b in range(4):
        r.wo_sum[b] = (r.wo_grad[b, c].astype(wide) + r.wo_in2[b].astype(wide)).astype(low)
    wo.start()
    for k in range(1, 8):
        t = lax.rem(s + k, 8)
        arrived(r.mgrad.at[t], r.mg_r.at[t], d, s)

    def unturn(x, pick):
        return x * r.cosine[pick, :] - partner(x) * r.sine[pick, :]

    def attend_back(b):
        pick = rows(b, 256)
        allowed, same = tables(pick, b * 256, 256)
        q_block = r.q_all[pick, :]
        m_block = r.mgrad[pl.ds(2 * b, 2)].reshape(256, 128)
        dq = None
        for h in range(2):
            mine = head_lanes(h)
            qh = jnp.where(mine, q_block, jnp.zeros_like(q_block))
            mh = jnp.where(mine, m_block, jnp.zeros_like(m_block))
            scores = scores_of(qh, h, same) - r.lse[pick, 64 * h : 64 * h + 1]
            p = jnp.exp(jnp.where(allowed, scores, NEG))
            pg = dot_nt(mh, r.v_all[...])
            inner = jnp.sum(p * pg, axis=-1, keepdims=True)
            ds = (p * (pg - inner)).astype(low)
            ds_wide = ds.astype(wide)
            r.bsum[2 * h : 2 * h + 1, :] += jnp.sum(jnp.where(same, ds_wide, 0.0), axis=0, keepdims=True)
            r.bsum[2 * h + 1 : 2 * h + 2, :] += jnp.sum(jnp.where(same, 0.0, ds_wide), axis=0, keepdims=True)
            one = dot(ds, r.k_all[...]) * 0.125
            dq = one if h == 0 else jnp.where(mine, one, dq)
            r.dk[...] += dot_tn(ds, qh)
            r.dv[...] += dot_tn(p.astype(low), mh)
        r.gr[pick, 0:128] = unturn(dq, pick).astype(low)

    def keep(n, src, dst):
        return pltpu.make_async_copy(src, dst, r.own_s.at[n])

    def send_gu(n):
        r.gu_sum[n] = gu.total(n).astype(low)
        for k in range(1, 8):
            t = lax.rem(s + k, 8)
            remote(
                r.gu_sum.at[n, rows(t)], r.gu_rx.at[n, s], r.guz_s.at[n, k], r.guz_r.at[n, s], d, t
            ).start()
        keep(n, r.gu_sum.at[n, rows(s)], r.gu_rx.at[n, s]).start()

    def send_dn():
        for j in range(4):
            t = 2 * j + s // 4

            @pl.when(t != s)
            def _():
                remote(
                    r.dn_sum.at[pl.ds(128 * j, 128)], r.dn_rx.at[lax.rem(s, 4)], r.dnz_s.at[j],
                    r.dnz_r.at[lax.rem(s, 4)], d, t,
                ).start()

            @pl.when(t == s)
            def _():
                keep(2, r.dn_sum.at[pl.ds(128 * j, 128)], r.dn_rx.at[lax.rem(s, 4)]).start()

    attend_back(0)
    attend_back(1)
    dn.step()
    outs.add_relay(far_order(z, 0))
    attend_back(2)
    send_gu(0)
    send_gu(1)
    attend_back(3)
    outs.add_relay(far_order(z, 1))

    def turn(b, carry):
        pick = rows(b, 256)
        r.gr[pick, 128:256] = unturn(r.dk[pick, :] * 0.125, pick).astype(low)
        r.gr[pick, 256:384] = r.dv[pick, :].astype(low)
        return carry

    lax.fori_loop(0, 4, turn, 0)
    grads.drain()
    for j in range(4):
        zj = far_order(z, j)
        grads.give(j, zj, dot_nt(r.gr[rows(zj, 256), :], r.wqkv[...]))
        if j > 0:
            grads.pass_on(j - 1, far_order(z, j - 1))
    grads.pass_on(3, z)

    def weigh_qkv(i, carry):
        block = r.xall[:, :, wide_of(i)].reshape(1024, 256)
        value = dot_tn(block, r.gr[...])
        along = jnp.sum(value * r.wqkv[rows(i, 256), :].astype(wide), axis=1, keepdims=True)
        r.small[0:1, wide_of(i)] = jnp.broadcast_to(along, (256, 128)).T[0:1]
        value = value.astype(low)
        r.qkv_grad[2 * i] = value[:128]
        r.qkv_grad[2 * i + 1] = value[128:]
        return carry

    for n in range(2):
        r.dn_sum[pl.ds(256 * n, 256), :] = dn.total(n).astype(low)
    send_dn()
    lax.fori_loop(0, 4, weigh_qkv, 0)
    grads.add_relay(far_order(z, 0))
    r.small[0:1, :] = r.small[0:1, :] / gain_one
    place = lax.broadcasted_iota(jnp.int32, (1, 1024), 1)
    line = jnp.zeros((1, 1024), wide)
    for h in range(2):
        for n in range(2):
            k = 2 * h + n
            one = jnp.sum(r.bsum[k : k + 1, :], axis=1, keepdims=True)
            line = line + jnp.where(place == 128 * n + 2 * pair + h, one, 0.0)
    r.small[2:3, :] = line
    for k in range(1, 4):
        t = lax.rem(d + k, 4)
        remote(r.small, r.small_p.at[d], r.sp_s.at[k], r.sp_r.at[d], t, s).start()
    for k in range(1, 4):
        t = lax.rem(d + k, 4)
        for m in range(2):
            remote(
                r.qkv_grad.at[t + 4 * m], r.q_in.at[d, m], r.qg_s.at[t, m], r.qg_r.at[d, m], t, s
            ).start()
    wo.step()
    grads.add_relay(far_order(z, 1))
    for k in range(1, 4):
        t = lax.rem(d + k, 4)
        arrived(r.small_p.at[t], r.sp_r.at[t], d, s)
    r.small_p[d] = r.small[...]
    r.small_q[...] = r.small_p[0] + r.small_p[1] + r.small_p[2] + r.small_p[3]
    for k in range(1, 8):
        t = lax.rem(s + k, 8)
        remote(r.small_q, r.small_z.at[s], r.sz_s.at[k], r.sz_r.at[s], d, t).start()
    keep(5, r.small_q, r.small_z.at[s]).start()

    r.out_v[...] = (r.mid[...] + outs.total()).astype(low)
    keep(4, r.out_v, r.out.at[0]).start()
    for n in range(2):
        r.wo_fin[pl.ds(2 * n, 2)] = wo.total(n).astype(low)
    keep(6, r.wo_fin.at[z], r.wo_rx.at[z]).start()
    for k in range(1, 4):
        t = lax.rem(z + k, 4)
        remote(r.wo_fin.at[t], r.wo_rx.at[z], r.woz_s.at[t], r.woz_r.at[z], d, 2 * t + c).start()

    for m in range(2):
        value = r.qkv_grad[d + 4 * m].astype(wide)
        for k in range(1, 4):
            t = lax.rem(d + k, 4)
            arrived(r.q_in.at[t, m], r.qg_r.at[t, m], d, s)
            value = value + r.q_in[t, m].astype(wide)
        r.q_sum[m] = value.astype(low)
        target = d + 4 * m
        mine = (target == s) & is_home

        @pl.when(jnp.logical_not(mine))
        def _():
            remote(
                r.q_sum.at[m], r.q_rx.at[z // 2], r.qz_s.at[m], r.qz_r.at[z // 2], home, target
            ).start()

        @pl.when(mine)
        def _():
            keep(3, r.q_sum.at[m], r.q_rx.at[z // 2]).start()

    value = r.tokens[0].astype(wide)
    factor = row_norm(value)
    normed = value * factor
    first_grad = grads.total()
    scaled = first_grad * gain_one
    inner = jnp.mean(scaled * normed, axis=-1, keepdims=True)

    r.tok_grad[0] = (r.mid_grad[...] + factor * (scaled - normed * inner)).astype(low)

    for k in range(1, 8):
        t = lax.rem(s + k, 8)
        for n in range(2):
            arrived(r.gu_rx.at[n, t], r.guz_r.at[n, t], d, s)
    for m in range(4):

        @pl.when(4 * c + m != s)
        def _():
            arrived(r.dn_rx.at[m], r.dnz_r.at[m], d, s)

    for k in range(1, 4):
        t = lax.rem(z + k, 4)
        arrived(r.wo_rx.at[t], r.woz_r.at[t], d, s)
    for i in range(2):

        @pl.when((owner[i] != s) | (lax.rem(s, 4) != d))
        def _():
            arrived(r.q_rx.at[i], r.qz_r.at[i], d, s)

    for k in range(1, 8):
        t = lax.rem(s + k, 8)
        arrived(r.small_z.at[t], r.sz_r.at[t], d, s)

    keep(0, r.gu_sum.at[0, rows(0)], r.gu_rx.at[0, 0]).wait()
    keep(1, r.gu_sum.at[0, rows(0)], r.gu_rx.at[0, 0]).wait()
    keep(4, r.out_v, r.out.at[0]).wait()
    keep(5, r.small_q, r.small_z.at[0]).wait()
    keep(6, r.wo_fin.at[0], r.wo_rx.at[0]).wait()

    @pl.when(s // 4 == lax.rem(s, 2))
    def _():
        keep(2, r.dn_sum.at[pl.ds(0, 128)], r.dn_rx.at[0]).wait()

    @pl.when(own_is_target)
    def _():
        keep(3, r.q_sum.at[0], r.q_rx.at[0]).wait()

    x_ring.drain()
    c_ring.drain()
    ring.drain()
    wo_ring.lane_drain()
    wo_side().wait_send()
    for i in range(2):

        @pl.when(owner[i] != s)
        def _():
            sent(r.qkv_src.at[i], r.qs_s.at[i], d, s)

    for k in range(1, 8):
        sent(r.ids, r.id_s.at[k], d, s)
        sent(r.gu_src.at[:, :, pl.ds(0, 128)], r.gu_s.at[k], d, s)

    @pl.when(is_home)
    def _():
        sent(r.wqkv, r.qp_s.at[0], d, s)
        sent(r.wqkv, r.qp_s.at[1], d, s)

    @pl.when((home == dx) | (home == dy))
    def _():
        sent(half_qkv(0), r.qp_s.at[2], d, s)

    for m in range(4):

        @pl.when(c * 4 + m != s)
        def _():
            sent(r.dn_src.at[pl.ds(128 * m, 128)], r.dn_s.at[m], d, s)

    for t in range(8):

        @pl.when(t != s)
        def _():
            sent(r.head_out.at[t], r.m_s.at[t], d, s)

        @pl.when(s != pair_owner(t))
        def _():
            sent(r.mg_src.at[t], r.mg_s.at[t], d, s)

    side.wait_send()
    gu.drain()
    dn.drain()
    wo.drain()
    grads.drain()
    outs.drain()
    for k in range(1, 8):
        for n in range(2):
            sent(r.gu_sum.at[n, rows(0)], r.guz_s.at[n, k], d, s)
        sent(r.small_q, r.sz_s.at[k], d, s)
    for j in range(4):

        @pl.when(2 * j + s // 4 != s)
        def _():
            sent(r.dn_sum.at[pl.ds(0, 128)], r.dnz_s.at[j], d, s)

    for k in range(1, 4):
        t = lax.rem(z + k, 4)
        sent(r.wo_fin.at[t], r.woz_s.at[t], d, s)
        t = lax.rem(d + k, 4)
        for m in range(2):
            sent(r.q_sum.at[m], r.qg_s.at[t, m], d, s)
        sent(r.small, r.sp_s.at[k], d, s)
    for m in range(2):

        @pl.when(jnp.logical_not((d + 4 * m == s) & is_home))
        def _():
            sent(r.q_sum.at[m], r.qz_s.at[m], d, s)


def vmem():
    return pl.BlockSpec(memory_space=pltpu.VMEM)


def hbm():
    return pl.BlockSpec(memory_space=pl.ANY)


def smem():
    return pl.BlockSpec(memory_space=pltpu.SMEM)


def shape(*dims, kind=low):
    return jax.ShapeDtypeStruct(dims, kind)


def dma(*dims):
    return pltpu.SemaphoreType.DMA(dims)


def layer(ins):
    outs = dict(
        tok_grad=shape(1, 128, 1024),
        out=shape(1, 128, 1024),
        gu_rx=shape(2, 8, 128, 128),
        dn_rx=shape(4, 128, 256),
        wo_rx=shape(4, 128, 256),
        q_rx=shape(2, 128, 384),
        small_z=shape(8, 8, 1024, kind=wide),
    )
    scratch = dict(
        xall=pltpu.VMEM((8, 128, 1024), low),
        q_all=pltpu.VMEM((1024, 128), low),
        k_all=pltpu.VMEM((1024, 128), low),
        v_all=pltpu.VMEM((1024, 128), low),
        lse=pltpu.VMEM((1024, 128), wide),
        wqkv=pltpu.VMEM((1024, 384), low),
        wo=pltpu.VMEM((8, 128, 1024), low),
        wgu=pltpu.VMEM((2, 1024, 512), low),
        wd=pltpu.VMEM((512, 1024), low),
        call=pltpu.VMEM((8, 128, 1024), low),
        ids=pltpu.VMEM((8, 128), wide),
        idr=pltpu.VMEM((8, 8, 128), wide),
        idc=pltpu.VMEM((1024, 128), wide),
        keyrow=pltpu.VMEM((8, 1024), wide),
        cosine=pltpu.VMEM((1024, 128), wide),
        sine=pltpu.VMEM((1024, 128), wide),
        mixed=pltpu.VMEM((8, 128, 128), low),
        wo_f=pltpu.VMEM((128, 256), wide),
        gu_f=pltpu.VMEM((2, 128, 1024), wide),
        dn_f=pltpu.VMEM((512, 256), wide),
        load_s=dma(5),
        own_s=dma(11),
        out_v=pltpu.VMEM((128, 1024), low),
        qkv_src=pltpu.VMEM((2, 128, 384), low),
        gu_src=pltpu.VMEM((2, 128, 1024), low),
        dn_src=pltpu.VMEM((512, 256), low),
        head_out=pltpu.VMEM((8, 128, 128), low),
        sall=pltpu.VMEM((8, 128, 1024), low),
        pre=pltpu.VMEM((2, 1024, 512), wide),
        gg=pltpu.VMEM((1024, 512), low),
        ug=pltpu.VMEM((1024, 512), low),
        hid=pltpu.VMEM((1024, 512), low),
        mid=pltpu.VMEM((128, 1024), wide),
        mid_grad=pltpu.VMEM((128, 1024), wide),
        mg_src=pltpu.VMEM((8, 128, 128), low),
        mgrad=pltpu.VMEM((8, 128, 128), low),
        gu_grad=pltpu.VMEM((2, 1024, 512), low),
        dn_grad=pltpu.VMEM((512, 1024), low),
        wo_grad=pltpu.VMEM((4, 2, 128, 1024), low),
        dk=pltpu.VMEM((1024, 128), wide),
        dv=pltpu.VMEM((1024, 128), wide),
        gr=pltpu.VMEM((1024, 384), low),
        bsum=pltpu.VMEM((8, 1024), wide),
        qkv_grad=pltpu.VMEM((8, 128, 384), low),
        wo_in2=pltpu.VMEM((4, 128, 1024), low),
        wo_sum=pltpu.VMEM((4, 128, 1024), low),
        gu_sum=pltpu.VMEM((2, 1024, 128), low),
        dn_sum=pltpu.VMEM((512, 256), low),
        wo_fin=pltpu.VMEM((4, 128, 256), low),
        q_in=pltpu.VMEM((4, 2, 128, 384), low),
        q_sum=pltpu.VMEM((2, 128, 384), low),
        small=pltpu.VMEM((8, 1024), wide),
        small_p=pltpu.VMEM((4, 8, 1024), wide),
        small_q=pltpu.VMEM((8, 1024), wide),
        g_parts=scatter_scratch(),
        o_parts=scatter_scratch(),
        gu_parts=plane_scratch(1024, 128),
        dn_parts=plane_scratch(256, 256),
        wo_parts=plane_scratch(2, 128, 256),
        x_sems=ring_scratch(2),
        y_sems=ring_scratch(2),
        c_sems=ring_scratch(2),
        wo_sems=ring_scratch(1),
        qs_s=dma(2), qs_r=dma(8), qp_s=dma(3), qp_r=dma(3),
        id_s=dma(8), id_r=dma(8), gu_s=dma(8), gu_r=dma(8), gup_s=dma(4, 4), gup_r=dma(4, 4), dnp_s=dma(4, 4), dnp_r=dma(4, 4),
        dn_s=dma(4), dn_r=dma(4), pl_s=dma(4), pl_r=dma(4),
        wos_s=dma(), wos_r=dma(), m_s=dma(8), m_r=dma(8),
        mg_s=dma(8), mg_r=dma(8), side_s=dma(), side_r=dma(),
        guz_s=dma(2, 8), guz_r=dma(2, 8), dnz_s=dma(4), dnz_r=dma(4),
        woz_s=dma(4), woz_r=dma(4), qg_s=dma(4, 2), qg_r=dma(4, 2),
        qz_s=dma(2), qz_r=dma(2), sp_s=dma(8), sp_r=dma(4),
        sz_s=dma(8), sz_r=dma(8),
    )
    flat, inner = jax.tree.flatten(scratch)
    got = pl.pallas_call(
        functools.partial(layer_kernel, tuple(ins), tuple(outs), inner),
        name="whole",
        out_shape=tuple(outs.values()),
        in_specs=[*[vmem()] * 11, *[smem()] * 2, *[hbm()] * 5],
        out_specs=[vmem(), *[hbm()] * 6],
        scratch_shapes=flat,
        compiler_params=pltpu.CompilerParams(
            collective_id=0, has_side_effects=True, vmem_limit_bytes=64 << 20
        ),
    )(*ins.values())
    return types.SimpleNamespace(**dict(zip(outs, got)))


def finish_kernel(
    out, tok_grad, gu, dn, wo, qkv, small,
    out2, tok2, gate2, up2, dn2, wo2, q2, k2, v2, g1, g2, same, cross,
):
    out2[...] = out[...]
    tok2[...] = tok_grad[...]
    for t in range(8):
        gate2[:, 128 * t : 128 * (t + 1)] = gu[0, t].astype(wide)
        up2[:, 128 * t : 128 * (t + 1)] = gu[1, t].astype(wide)
    for m in range(4):
        dn2[128 * m : 128 * (m + 1), :] = dn[m].astype(wide)
    total = wo[0].astype(wide)
    for m in range(1, 4):
        total = total + wo[m].astype(wide)
    wo2[...] = total
    for n, ref in enumerate((q2, k2, v2)):
        for i in range(2):
            ref[:, 128 * i : 128 * (i + 1)] = qkv[i, :, 128 * n : 128 * (n + 1)].astype(wide)
    total = small[0]
    for t in range(1, 8):
        total = total + small[t]
    g1[...] = total[0:1]
    g2[...] = total[1:2]
    same[...] = total[2:3, 0:128]
    cross[...] = total[2:3, 128:256]


def finish(got):
    outs = (
        shape(1, 128, 1024), shape(1, 128, 1024),
        shape(128, 1024, kind=wide), shape(128, 1024, kind=wide), shape(512, 256, kind=wide),
        shape(128, 256, kind=wide), shape(128, 256, kind=wide), shape(128, 256, kind=wide),
        shape(128, 256, kind=wide), shape(1, 1024, kind=wide), shape(1, 1024, kind=wide),
        shape(1, 128, kind=wide), shape(1, 128, kind=wide),
    )
    return pl.pallas_call(
        finish_kernel,
        name="finish",
        out_shape=outs,
        in_specs=[vmem()] * 7,
        out_specs=[vmem()] * len(outs),
    )(got.out, got.tok_grad, got.gu_rx, got.dn_rx, got.wo_rx, got.q_rx, got.small_z)


def rope_rates():
    rates = np.float32(10000.0) ** (-np.arange(32, dtype=np.float32) * np.float32(2.0 / 64))
    return np.tile(rates.astype(np.float32), 4)[None]


def fast_body(
    tokens, attn_gain, query_weight, key_weight, value_weight, out_weight, same_bias, cross_bias,
    ffn_gain, gate_weight, up_weight, down_weight, segment_ids, variate_ids, time_ids, observed,
    cotangent,
):
    got = layer(dict(
        tokens=tokens, attn_gain=attn_gain, ffn_gain=ffn_gain,
        wq=query_weight, wk=key_weight, wv=value_weight, segment=segment_ids, freq=rope_rates(),
        variate=variate_ids, moment=time_ids, observed=observed,
        same_bias=same_bias, cross_bias=cross_bias,
        wo_in=out_weight, wg_in=gate_weight, wu_in=up_weight, wd_in=down_weight, cot=cotangent,
    ))
    out, tok, gate, up, dn, wo, q, k, v, g1, g2, same, cross = finish(got)
    return (
        out, tok, g1[0], q, k, v, wo, same[0, 0:16], cross[0, 0:16], g2[0], gate, up, dn,
    )


def fits(mesh):
    return mesh.shape["dp"] == 4 and mesh.shape["seq"] == 8


def solution(mesh):
    in_specs = (
        P("dp", "seq", None),
        P(),
        P("seq", "dp"),
        P("seq", "dp"),
        P("seq", "dp"),
        P("seq", "dp"),
        P(),
        P(),
        P(),
        P("seq", "dp"),
        P("seq", "dp"),
        P("seq", "dp"),
        P("dp", "seq"),
        P("dp", "seq"),
        P("dp", "seq"),
        P("dp", "seq"),
        P("dp", "seq", None),
    )
    out_specs = (
        P("dp", "seq", None),
        P("dp", "seq", None),
        P(),
        P("seq", "dp"),
        P("seq", "dp"),
        P("seq", "dp"),
        P("seq", "dp"),
        P(),
        P(),
        P(),
        P("seq", "dp"),
        P("seq", "dp"),
        P("seq", "dp"),
    )
    part = fast_body if fits(mesh) else body
    return jax.shard_map(part, mesh=mesh, in_specs=in_specs, out_specs=out_specs, check_vma=False)
```

```python
import functools
import types

import jax
import jax.numpy as jnp
import numpy as np
from jax import lax
from jax.experimental import pallas as pl
from jax.experimental.pallas import tpu as pltpu
from jax.sharding import PartitionSpec as P

epsilon = 1e-06


def product(left_side, right_side):
    return jnp.dot(left_side, right_side, preferred_element_type=jnp.float32)


def contract_rows(left_side, right_side):
    return lax.dot_general(
        left_side, right_side, (((0,), (0,)), ((), ())), preferred_element_type=jnp.float32
    )


def contract_cols(left_side, right_side):
    return lax.dot_general(
        left_side, right_side, (((1,), (1,)), ((), ())), preferred_element_type=jnp.float32
    )


def angles_of(moments, head_width):
    half_width = head_width // 2
    powers = jnp.arange(half_width).astype(jnp.float32) * (2.0 / head_width)
    return moments.astype(jnp.float32)[:, None] * (10000.0 ** (-powers))[None, :]


def rotate(values, angles, head_count):
    row_count, model_width = values.shape
    shaped = values.reshape(row_count, head_count, model_width // head_count)
    half_width = model_width // head_count // 2
    first_half = shaped[..., :half_width]
    second = shaped[..., half_width:]
    cosine = jnp.cos(angles)[:, None, :]
    sine_part = jnp.sin(angles)[:, None, :]
    turned = jnp.concatenate(
        [first_half * cosine - second * sine_part, second * cosine + first_half * sine_part],
        axis=-1,
    )
    return turned.reshape(row_count, model_width)


def normalize(values, gain_row):
    factor = lax.rsqrt(jnp.mean(values * values, axis=-1, keepdims=True) + epsilon)
    normed = values * factor
    return (normed, factor, normed * gain_row)


def norm_back(incoming, normed, factor, gain_row):
    scaled = incoming * gain_row
    inner_sum = jnp.mean(scaled * normed, axis=-1, keepdims=True)
    return (factor * (scaled - normed * inner_sum), jnp.sum(incoming * normed, axis=0))


def make_tables(segment, variate, key_segment, key_variate, first_row):
    query_place = first_row + jnp.arange(segment.shape[0])
    key_place = jnp.arange(key_segment.shape[0])
    allowed = (segment.astype(jnp.float32)[:, None] == key_segment.astype(jnp.float32)[None, :]) | (
        query_place[:, None] == key_place[None, :]
    )
    same_kind = variate.astype(jnp.float32)[:, None] == key_variate.astype(jnp.float32)[None, :]
    return (allowed, same_kind)


def block_scores(
    block_index, query_low, keys_all, same_kind, same_bias, cross_bias, head_group, head_width
):
    block_width = head_group * head_width
    query_block = lax.dynamic_slice_in_dim(
        query_low, block_index * block_width, block_width, 1
    ).reshape(query_low.shape[0], head_group, head_width)
    key_block = lax.dynamic_slice_in_dim(
        keys_all, block_index * block_width, block_width, 1
    ).reshape(keys_all.shape[0], head_group, head_width)
    raw_scores = jnp.einsum(
        "thd,shd->hts", query_block, key_block, preferred_element_type=jnp.float32
    )
    same_part = lax.dynamic_slice_in_dim(same_bias, block_index * head_group, head_group)
    cross_part = lax.dynamic_slice_in_dim(cross_bias, block_index * head_group, head_group)
    offset = jnp.where(same_kind[None], same_part[:, None, None], cross_part[:, None, None])
    return (raw_scores * head_width ** (-0.5) + offset, query_block, key_block)


def body(
    tokens,
    attn_gain,
    query_weight,
    key_weight,
    value_weight,
    out_weight,
    same_bias,
    cross_bias,
    ffn_gain,
    gate_weight,
    up_weight,
    down_weight,
    segment_ids,
    variate_ids,
    time_ids,
    observed,
    cotangent,
):
    row_count = tokens.shape[1]
    model_width = tokens.shape[2]
    head_count = same_bias.shape[0]
    head_width = model_width // head_count
    head_group = max(1, 128 // head_width)
    block_width = head_group * head_width
    block_total = head_count // head_group
    scaling = head_width ** (-0.5)
    first_row = lax.axis_index("seq") * row_count
    gain_one = attn_gain.astype(jnp.bfloat16).astype(jnp.float32)
    gain_two = ffn_gain.astype(jnp.bfloat16).astype(jnp.float32)
    low_masters = (
        query_weight.astype(jnp.bfloat16),
        key_weight.astype(jnp.bfloat16),
        value_weight.astype(jnp.bfloat16),
        out_weight.astype(jnp.bfloat16),
        gate_weight.astype(jnp.bfloat16),
        up_weight.astype(jnp.bfloat16),
        down_weight.astype(jnp.bfloat16),
    )
    row_parts = (
        lax.all_gather(low_masters[0], "seq", axis=0, tiled=True),
        lax.all_gather(low_masters[1], "seq", axis=0, tiled=True),
        lax.all_gather(low_masters[2], "seq", axis=0, tiled=True),
        lax.all_gather(low_masters[3], "seq", axis=0, tiled=True),
        lax.all_gather(low_masters[4], "seq", axis=0, tiled=True),
        lax.all_gather(low_masters[5], "seq", axis=0, tiled=True),
        lax.all_gather(low_masters[6], "seq", axis=0, tiled=True),
    )
    gathered = (
        lax.all_gather(row_parts[0], "dp", axis=1, tiled=True),
        lax.all_gather(row_parts[1], "dp", axis=1, tiled=True),
        lax.all_gather(row_parts[2], "dp", axis=1, tiled=True),
        lax.all_gather(row_parts[3], "dp", axis=1, tiled=True),
        lax.all_gather(row_parts[4], "dp", axis=1, tiled=True),
        lax.all_gather(row_parts[5], "dp", axis=1, tiled=True),
        lax.all_gather(row_parts[6], "dp", axis=1, tiled=True),
    )
    w_query, w_key, w_value, w_out, w_gate, w_up, w_down = gathered
    inputs = tokens[0].astype(jnp.float32)
    segment = segment_ids[0]
    variate = variate_ids[0]
    seen_row = observed[0]
    angles = angles_of(time_ids[0], head_width)
    normed_one, factor_one, scaled_one = normalize(inputs, gain_one)
    first_low = scaled_one.astype(jnp.bfloat16)
    query_low = rotate(product(first_low, w_query), angles, head_count).astype(jnp.bfloat16)
    key_low = rotate(product(first_low, w_key), angles, head_count).astype(jnp.bfloat16)
    value_low = product(first_low, w_value).astype(jnp.bfloat16)
    key_segment = jnp.where(seen_row == 1, segment, -1).astype(jnp.bfloat16)
    key_variate = variate.astype(jnp.bfloat16)
    keys_all, values_all, segments_all, variates_all = (
        lax.all_gather(key_low, "seq", axis=0, tiled=True),
        lax.all_gather(value_low, "seq", axis=0, tiled=True),
        lax.all_gather(key_segment, "seq", axis=0, tiled=True),
        lax.all_gather(key_variate, "seq", axis=0, tiled=True),
    )
    length = keys_all.shape[0]
    allowed, same_kind = make_tables(segment, variate, segments_all, variates_all, first_row)

    def forward_block(block_index, state_now):
        mixed, summary = state_now
        scores, query_block, key_block = block_scores(
            block_index,
            query_low,
            keys_all,
            same_kind,
            same_bias,
            cross_bias,
            head_group,
            head_width,
        )
        row_top = jnp.max(jnp.where(allowed[None], scores, -jnp.inf), axis=-1, keepdims=True)
        exponent = jnp.exp(jnp.where(allowed[None], scores - row_top, -jnp.inf))
        row_total = jnp.sum(exponent, axis=-1, keepdims=True)
        prob_low = (exponent / row_total).astype(jnp.bfloat16)
        value_block = lax.dynamic_slice_in_dim(
            values_all, block_index * block_width, block_width, 1
        ).reshape(length, head_group, head_width)
        attended = jnp.einsum(
            "hts,shd->thd", prob_low, value_block, preferred_element_type=jnp.float32
        ).reshape(row_count, block_width)
        mixed = lax.dynamic_update_slice_in_dim(mixed, attended, block_index * block_width, 1)
        summary = lax.dynamic_update_slice_in_dim(
            summary, (row_top + jnp.log(row_total))[..., 0], block_index * head_group, 0
        )
        return (mixed, summary)

    mixed, summary = lax.fori_loop(
        0,
        block_total,
        forward_block,
        (
            jnp.zeros((row_count, model_width), jnp.float32),
            jnp.zeros((head_count, row_count), jnp.float32),
        ),
    )
    mixed_low = mixed.astype(jnp.bfloat16)
    middle = inputs + product(mixed_low, w_out)
    normed_two, factor_two, scaled_two = normalize(middle, gain_two)
    second_low = scaled_two.astype(jnp.bfloat16)
    gate_pre = product(second_low, w_gate)
    up_pre = product(second_low, w_up)
    sigma = jax.nn.sigmoid(gate_pre)
    activated = gate_pre * sigma
    hidden_low = (activated * up_pre).astype(jnp.bfloat16)
    result = middle + product(hidden_low, w_down)
    rows_again = (
        lax.all_gather(low_masters[0], "seq", axis=0, tiled=True),
        lax.all_gather(low_masters[1], "seq", axis=0, tiled=True),
        lax.all_gather(low_masters[2], "seq", axis=0, tiled=True),
        lax.all_gather(low_masters[3], "seq", axis=0, tiled=True),
        lax.all_gather(low_masters[4], "seq", axis=0, tiled=True),
        lax.all_gather(low_masters[5], "seq", axis=0, tiled=True),
        lax.all_gather(low_masters[6], "seq", axis=0, tiled=True),
    )
    regathered = (
        lax.all_gather(rows_again[0], "dp", axis=1, tiled=True),
        lax.all_gather(rows_again[1], "dp", axis=1, tiled=True),
        lax.all_gather(rows_again[2], "dp", axis=1, tiled=True),
        lax.all_gather(rows_again[3], "dp", axis=1, tiled=True),
        lax.all_gather(rows_again[4], "dp", axis=1, tiled=True),
        lax.all_gather(rows_again[5], "dp", axis=1, tiled=True),
        lax.all_gather(rows_again[6], "dp", axis=1, tiled=True),
    )
    w_query, w_key, w_value, w_out, w_gate, w_up, w_down = regathered
    cot_low = cotangent[0]
    hidden_grad = contract_cols(cot_low, w_down)
    down_grad = contract_rows(hidden_low, cot_low)
    gate_grad = (hidden_grad * up_pre * sigma * (1.0 + gate_pre * (1.0 - sigma))).astype(
        jnp.bfloat16
    )
    up_grad = (hidden_grad * activated).astype(jnp.bfloat16)
    gate_w_grad = contract_rows(second_low, gate_grad)
    up_w_grad = contract_rows(second_low, up_grad)
    second_grad = contract_cols(gate_grad, w_gate) + contract_cols(up_grad, w_up)
    middle_part, ffn_gain_grad = norm_back(second_grad, normed_two, factor_two, gain_two)
    middle_grad = cot_low.astype(jnp.float32) + middle_part
    middle_low = middle_grad.astype(jnp.bfloat16)
    out_w_grad = contract_rows(mixed_low, middle_low)
    mixed_grad = contract_cols(middle_low, w_out).astype(jnp.bfloat16)
    keys_back, values_back, segments_back, variates_back = (
        lax.all_gather(key_low, "seq", axis=0, tiled=True),
        lax.all_gather(value_low, "seq", axis=0, tiled=True),
        lax.all_gather(key_segment, "seq", axis=0, tiled=True),
        lax.all_gather(key_variate, "seq", axis=0, tiled=True),
    )
    allowed_back, same_back = make_tables(segment, variate, segments_back, variates_back, first_row)

    def query_side(block_index):
        scores, query_block, key_block = block_scores(
            block_index,
            query_low,
            keys_back,
            same_back,
            same_bias,
            cross_bias,
            head_group,
            head_width,
        )
        lse_block = lax.dynamic_slice_in_dim(summary, block_index * head_group, head_group, 0)
        probabilities = jnp.exp(
            jnp.where(allowed_back[None], scores - lse_block[:, :, None], -jnp.inf)
        )
        grad_block = lax.dynamic_slice_in_dim(
            mixed_grad, block_index * block_width, block_width, 1
        ).reshape(row_count, head_group, head_width)
        value_block = lax.dynamic_slice_in_dim(
            values_back, block_index * block_width, block_width, 1
        ).reshape(length, head_group, head_width)
        prob_grad = jnp.einsum(
            "thd,shd->hts", grad_block, value_block, preferred_element_type=jnp.float32
        )
        inner_sum = jnp.sum(probabilities * prob_grad, axis=-1, keepdims=True)
        score_low = (probabilities * (prob_grad - inner_sum)).astype(jnp.bfloat16)
        score_wide = score_low.astype(jnp.float32)
        same_part = jnp.sum(jnp.where(same_back[None], score_wide, 0.0), axis=(1, 2))
        cross_part = jnp.sum(jnp.where(same_back[None], 0.0, score_wide), axis=(1, 2))
        query_part = (
            jnp.einsum(
                "hts,shd->thd", score_low, key_block, preferred_element_type=jnp.float32
            ).reshape(row_count, block_width)
            * scaling
        )
        return (
            probabilities,
            score_low,
            query_block,
            grad_block,
            inner_sum[..., 0],
            same_part,
            cross_part,
            query_part,
        )

    def backward_block(block_index, state_now):
        query_grad, key_grad, value_grad, same_grad, cross_grad = state_now
        (
            probabilities,
            score_low,
            query_block,
            grad_block,
            inner_sum,
            same_part,
            cross_part,
            query_part,
        ) = query_side(block_index)
        key_part = (
            jnp.einsum(
                "hts,thd->shd", score_low, query_block, preferred_element_type=jnp.float32
            ).reshape(length, block_width)
            * scaling
        )
        value_part = jnp.einsum(
            "hts,thd->shd",
            probabilities.astype(jnp.bfloat16),
            grad_block,
            preferred_element_type=jnp.float32,
        ).reshape(length, block_width)
        query_grad = lax.dynamic_update_slice_in_dim(
            query_grad, query_part, block_index * block_width, 1
        )
        key_grad = lax.dynamic_update_slice_in_dim(key_grad, key_part, block_index * block_width, 1)
        value_grad = lax.dynamic_update_slice_in_dim(
            value_grad, value_part, block_index * block_width, 1
        )
        same_grad = lax.dynamic_update_slice_in_dim(
            same_grad, same_part, block_index * head_group, 0
        )
        cross_grad = lax.dynamic_update_slice_in_dim(
            cross_grad, cross_part, block_index * head_group, 0
        )
        return (query_grad, key_grad, value_grad, same_grad, cross_grad)

    start_state = (
        jnp.zeros((row_count, model_width), jnp.float32),
        jnp.zeros((length, model_width), jnp.float32),
        jnp.zeros((length, model_width), jnp.float32),
        jnp.zeros((head_count,), jnp.float32),
        jnp.zeros((head_count,), jnp.float32),
    )
    query_grad, key_grad, value_grad, same_grad, cross_grad = lax.fori_loop(
        0, block_total, backward_block, start_state
    )
    key_share, value_share = (
        lax.psum_scatter(
            key_grad.astype(jnp.bfloat16), "seq", scatter_dimension=0, tiled=True
        ).astype(jnp.float32),
        lax.psum_scatter(
            value_grad.astype(jnp.bfloat16), "seq", scatter_dimension=0, tiled=True
        ).astype(jnp.float32),
    )
    query_pre_grad = rotate(query_grad, -angles, head_count).astype(jnp.bfloat16)
    key_pre_grad = rotate(key_share, -angles, head_count).astype(jnp.bfloat16)
    value_pre_grad = value_share.astype(jnp.bfloat16)
    query_w_grad = contract_rows(first_low, query_pre_grad)
    key_w_grad = contract_rows(first_low, key_pre_grad)
    value_w_grad = contract_rows(first_low, value_pre_grad)
    first_grad = (
        contract_cols(query_pre_grad, w_query)
        + contract_cols(key_pre_grad, w_key)
        + contract_cols(value_pre_grad, w_value)
    )
    input_part, attn_gain_grad = norm_back(first_grad, normed_one, factor_one, gain_one)
    input_grad = (middle_grad + input_part).astype(jnp.bfloat16)
    col_shares = (
        lax.psum_scatter(
            query_w_grad.astype(jnp.bfloat16), "dp", scatter_dimension=1, tiled=True
        ).astype(jnp.float32),
        lax.psum_scatter(
            key_w_grad.astype(jnp.bfloat16), "dp", scatter_dimension=1, tiled=True
        ).astype(jnp.float32),
        lax.psum_scatter(
            value_w_grad.astype(jnp.bfloat16), "dp", scatter_dimension=1, tiled=True
        ).astype(jnp.float32),
        lax.psum_scatter(
            out_w_grad.astype(jnp.bfloat16), "dp", scatter_dimension=1, tiled=True
        ).astype(jnp.float32),
        lax.psum_scatter(
            gate_w_grad.astype(jnp.bfloat16), "dp", scatter_dimension=1, tiled=True
        ).astype(jnp.float32),
        lax.psum_scatter(
            up_w_grad.astype(jnp.bfloat16), "dp", scatter_dimension=1, tiled=True
        ).astype(jnp.float32),
        lax.psum_scatter(
            down_grad.astype(jnp.bfloat16), "dp", scatter_dimension=1, tiled=True
        ).astype(jnp.float32),
    )
    shares = (
        lax.psum_scatter(
            col_shares[0].astype(jnp.bfloat16), "seq", scatter_dimension=0, tiled=True
        ).astype(jnp.float32),
        lax.psum_scatter(
            col_shares[1].astype(jnp.bfloat16), "seq", scatter_dimension=0, tiled=True
        ).astype(jnp.float32),
        lax.psum_scatter(
            col_shares[2].astype(jnp.bfloat16), "seq", scatter_dimension=0, tiled=True
        ).astype(jnp.float32),
        lax.psum_scatter(
            col_shares[3].astype(jnp.bfloat16), "seq", scatter_dimension=0, tiled=True
        ).astype(jnp.float32),
        lax.psum_scatter(
            col_shares[4].astype(jnp.bfloat16), "seq", scatter_dimension=0, tiled=True
        ).astype(jnp.float32),
        lax.psum_scatter(
            col_shares[5].astype(jnp.bfloat16), "seq", scatter_dimension=0, tiled=True
        ).astype(jnp.float32),
        lax.psum_scatter(
            col_shares[6].astype(jnp.bfloat16), "seq", scatter_dimension=0, tiled=True
        ).astype(jnp.float32),
    )
    small_totals = lax.psum((same_grad, cross_grad, attn_gain_grad, ffn_gain_grad), ("dp", "seq"))
    return (
        result.astype(jnp.bfloat16)[None],
        input_grad[None],
        small_totals[2],
        shares[0],
        shares[1],
        shares[2],
        shares[3],
        small_totals[0],
        small_totals[1],
        small_totals[3],
        shares[4],
        shares[5],
        shares[6],
    )


MESH = pl.DeviceIdType.MESH
NEG = -1e30
low = jnp.bfloat16
wide = jnp.float32

def remote(src, dst, send_sem, recv_sem, d, s):
    return pltpu.make_async_remote_copy(
        src_ref=src,
        dst_ref=dst,
        send_sem=send_sem,
        recv_sem=recv_sem,
        device_id=(d, s),
        device_id_type=MESH,
    )


def arrived(dst, recv_sem, d, s):
    remote(dst, dst, recv_sem, recv_sem, d, s).wait_recv()


def sent(src, send_sem, d, s):
    remote(src, src, send_sem, send_sem, d, s).wait_send()


def pair_of(s):
    z = s // 2
    c = lax.rem(s, 2)
    return 2 * (2 * c + lax.rem(z, 2)) + z // 2


class Chain:
    def __init__(self, d, s, view, parts, up_sem, recv_sem, side_sem, side_recv):
        self.d, self.s, self.z, self.c = d, s, s // 2, lax.rem(s, 2)
        self.view, self.parts = view, parts
        self.up_sem, self.recv_sem = up_sem, recv_sem
        self.side_sem, self.side_recv = side_sem, side_recv

    def block(self, z):
        return self.view(2 * z + self.c)

    def part(self, z, h):
        n = 128 // self.parts
        return self.block(z).at[pl.ds(n * h, n)]

    def up(self, z, h):
        b = self.part(z, h)
        return remote(
            b, b, self.up_sem.at[(self.z - z) * self.parts + h],
            self.recv_sem.at[z * self.parts + h], self.d, self.s + 2,
        )

    def down(self, z, h):
        b = self.part(z, h)
        return remote(
            b, b, self.up_sem.at[(3 + z - self.z) * self.parts + h],
            self.recv_sem.at[z * self.parts + h], self.d, self.s - 2,
        )

    def side(self, z):
        b = self.block(z)
        return remote(b, b, self.side_sem.at[z], self.side_recv.at[z], self.d, self.s + 1 - 2 * self.c)

    def start_lane(self):
        for h in range(self.parts):

            @pl.when(self.z < 3)
            def _():
                self.up(self.z, h).start()

            @pl.when(self.z > 0)
            def _():
                self.down(self.z, h).start()

    def start(self):
        self.start_lane()
        self.side(self.z).start()

    def lane_step(self, k, share=False):
        lo, hi = self.z - k, self.z + k
        for h in range(self.parts):
            last = share and h == self.parts - 1

            @pl.when(lo >= 0)
            def _():
                arrived(self.part(lo, h), self.recv_sem.at[lo * self.parts + h], self.d, self.s)

                @pl.when(self.z < 3)
                def _():
                    self.up(lo, h).start()

                if last:
                    self.side(lo).start()

            @pl.when(hi <= 3)
            def _():
                arrived(self.part(hi, h), self.recv_sem.at[hi * self.parts + h], self.d, self.s)

                @pl.when(self.z > 0)
                def _():
                    self.down(hi, h).start()

                if last:
                    self.side(hi).start()

    def step(self, k):
        self.lane_step(k, True)

    def wait_side(self, z):
        arrived(self.view(2 * z + 1 - self.c), self.side_recv.at[z], self.d, self.s)

    def drain(self):
        own = self.block(self.z)
        for z in range(4):
            sent(own, self.side_sem.at[z], self.d, self.s)
        self.lane_drain()

    def lane_drain(self):
        for h in range(self.parts):
            own = self.part(self.z, h)
            for k in range(3):

                @pl.when((self.z < 3) & (self.z - k >= 0))
                def _():
                    sent(own, self.up_sem.at[k * self.parts + h], self.d, self.s)

                @pl.when((self.z > 0) & (self.z + k <= 3))
                def _():
                    sent(own, self.up_sem.at[(3 + k) * self.parts + h], self.d, self.s)

    def start_direct(self):
        own = self.block(self.z)
        for k in range(1, 4):
            t = lax.rem(self.z + k, 4)
            remote(
                own, own, self.up_sem.at[k], self.recv_sem.at[self.z], self.d, 2 * t + self.c
            ).start()
        self.side(self.z).start()

    def collect(self, z):
        arrived(self.block(z), self.recv_sem.at[z], self.d, self.s)
        self.side(z).start()

    def drain_direct(self):
        own = self.block(self.z)
        for z in range(4):
            sent(own, self.side_sem.at[z], self.d, self.s)
        for k in range(1, 4):
            sent(own, self.up_sem.at[k], self.d, self.s)


class Plane:
    def __init__(self, d, s, whole, half, send_sem, recv_sem):
        self.d, self.s = d, s
        self.dx = d + 1 - 2 * lax.rem(d, 2)
        self.dy = lax.rem(d + 2, 4)
        self.far = 3 - d
        self.whole, self.half = whole, half
        self.send_sem, self.recv_sem = send_sem, recv_sem

    def start(self):
        w = self.whole(self.d)
        remote(w, w, self.send_sem.at[0], self.recv_sem.at[0], self.dx, self.s).start()
        remote(w, w, self.send_sem.at[1], self.recv_sem.at[1], self.dy, self.s).start()

    def step(self):
        arrived(self.whole(self.dx), self.recv_sem.at[0], self.d, self.s)
        h = self.half(self.dx, 0)
        remote(h, h, self.send_sem.at[2], self.recv_sem.at[2], self.dy, self.s).start()
        arrived(self.whole(self.dy), self.recv_sem.at[1], self.d, self.s)
        h = self.half(self.dy, 1)
        remote(h, h, self.send_sem.at[3], self.recv_sem.at[3], self.dx, self.s).start()

    def finish(self):
        arrived(self.half(self.far, 0), self.recv_sem.at[2], self.d, self.s)
        arrived(self.half(self.far, 1), self.recv_sem.at[3], self.d, self.s)
        w = self.whole(self.d)
        sent(w, self.send_sem.at[0], self.d, self.s)
        sent(w, self.send_sem.at[1], self.d, self.s)
        h = self.half(self.d, 0)
        sent(h, self.send_sem.at[2], self.d, self.s)
        h = self.half(self.d, 1)
        sent(h, self.send_sem.at[3], self.d, self.s)


def lanes(i):
    return pl.ds(pl.multiple_of(i * 128, 128), 128)


def rows(i, n=128):
    return pl.ds(pl.multiple_of(i * n, n), n)


def dot(a, b):
    return jnp.dot(a, b, preferred_element_type=wide)


def dot_nt(a, b):
    return lax.dot_general(a, b, (((1,), (1,)), ((), ())), preferred_element_type=wide)


def dot_tn(a, b):
    return lax.dot_general(a, b, (((0,), (0,)), ((), ())), preferred_element_type=wide)


def head_lanes(h):
    place = lax.broadcasted_iota(jnp.int32, (1, 128), 1)
    return (place // 64) == h


def partner(x):
    place = lax.broadcasted_iota(jnp.int32, x.shape, 1)
    return jnp.where(lax.rem(place, 64) < 32, pltpu.roll(x, 96, 1), pltpu.roll(x, 32, 1))


class Scatter:
    def __init__(self, d, s, keep, own, side_out, side_in, out, got, relay, sems):
        self.d, self.s, self.z, self.c = d, s, s // 2, lax.rem(s, 2)
        self.keep, self.own, self.side_out, self.side_in = keep, own, side_out, side_in
        self.out, self.got, self.relay = out, got, relay
        self.side_s, self.side_r, self.send_s, self.recv = (sems.at[i] for i in range(4))

    def passes(self, z):
        return ((self.z == 1) & (z >= 2)) | ((self.z == 2) & (z <= 1))

    def give(self, j, z, value):
        first, second = value[:128], value[128:]
        even = self.c == 0
        self.side_out[z] = jnp.where(even, second, first).astype(low)
        remote(
            self.side_out.at[z], self.side_in.at[z], self.side_s.at[z], self.side_r.at[z],
            self.d, self.s + 1 - 2 * self.c,
        ).start()
        self.keep[j % 2] = jnp.where(even, first, second)

    def send(self, z, place, slot, chip):
        remote(
            self.out.at[z], place.at[slot], self.send_s.at[z],
            self.recv.at[slot if place is self.got else 2 + slot], self.d, 2 * chip + self.c,
        ).start()

    def pass_on(self, j, z):
        arrived(self.side_in.at[z], self.side_r.at[z], self.d, self.s)
        total = self.keep[j % 2] + self.side_in[z].astype(wide)
        end = (self.z == 0) | (self.z == 3)
        near = (z - self.z == 1) | (self.z - z == 1)

        @pl.when(z == self.z)
        def _():
            self.own[...] = total

        @pl.when(z != self.z)
        def _():
            self.out[z] = total.astype(low)

            @pl.when(near & jnp.logical_not(self.passes(z)))
            def _():
                self.send(z, self.got, 0, z)

            @pl.when(end & jnp.logical_not(near))
            def _():
                self.send(z, self.relay, lax.rem(z, 2), 1 + self.z // 3)

    def add_relay(self, z):
        @pl.when(self.passes(z))
        def _():
            slot = lax.rem(z, 2)
            arrived(self.relay.at[slot], self.recv.at[2 + slot], self.d, self.s)
            self.out[z] = (self.out[z].astype(wide) + self.relay[slot].astype(wide)).astype(low)
            self.send(z, self.got, 1, z)

    def total(self):
        value = self.own[...]
        for slot in range(2):
            arrived(self.got.at[slot], self.recv.at[slot], self.d, self.s)
            value = value + self.got[slot].astype(wide)
        return value

    def drain(self):
        for z in range(4):
            sent(self.side_out.at[z], self.side_s.at[z], self.d, self.s)

            @pl.when(z != self.z)
            def _():
                sent(self.out.at[z], self.send_s.at[z], self.d, self.s)


def scatter_scratch():
    blocks = pltpu.VMEM((4, 128, 1024), low)
    return dict(
        keep=pltpu.VMEM((2, 128, 1024), wide),
        own=pltpu.VMEM((128, 1024), wide),
        side_out=blocks,
        side_in=blocks,
        out=blocks,
        got=pltpu.VMEM((2, 128, 1024), low),
        relay=pltpu.VMEM((2, 128, 1024), low),
        sems=dma(4, 4),
    )


def ring_scratch(parts):
    return dict(
        up_sem=dma(6 * parts), recv_sem=dma(4 * parts), side_sem=dma(4), side_recv=dma(4)
    )


class PlaneScatter:
    def __init__(self, d, s, part, first_a, first_b, middle_out, second, send_sem, recv_sem):
        self.d, self.s = d, s
        self.dx = d + 1 - 2 * lax.rem(d, 2)
        self.dy = lax.rem(d + 2, 4)
        self.far = 3 - d
        self.part = part
        self.first = (first_a, first_b)
        self.middle_out, self.second = middle_out, second
        self.send_sem, self.recv_sem = send_sem, recv_sem

    def start(self):
        for n, near in enumerate((self.dx, self.dy)):
            for m, block in enumerate((self.far, near)):
                k = 2 * n + m
                remote(
                    self.part(block, n), self.first[n].at[m], self.send_sem.at[k], self.recv_sem.at[k],
                    near, self.s,
                ).start()

    def step(self):
        for n, other in enumerate((self.dy, self.dx)):
            arrived(self.first[n].at[0], self.recv_sem.at[2 * n], self.d, self.s)
            total = self.part(other, n)[...].astype(wide) + self.first[n][0].astype(wide)
            self.middle_out[n] = total.astype(low)
            remote(
                self.middle_out.at[n], self.second.at[n], self.send_sem.at[4 + n],
                self.recv_sem.at[4 + n], other, self.s,
            ).start()

    def total(self, n):
        arrived(self.first[n].at[1], self.recv_sem.at[2 * n + 1], self.d, self.s)
        arrived(self.second.at[n], self.recv_sem.at[4 + n], self.d, self.s)
        value = self.part(self.d, n)[...].astype(wide) + self.first[n][1].astype(wide)
        return value + self.second[n].astype(wide)

    def drain(self):
        for k in range(4):
            sent(self.first[0].at[0], self.send_sem.at[k], self.d, self.s)
        for k in range(2):
            sent(self.middle_out.at[0], self.send_sem.at[4 + k], self.d, self.s)


def plane_scratch(*dims):
    blocks = pltpu.VMEM((2, *dims), low)
    return dict(
        first_a=blocks, first_b=blocks, middle_out=blocks, second=blocks,
        send_sem=dma(6), recv_sem=dma(6),
    )


def owner_of(dd, i):
    return 2 * (lax.rem(dd, 2) + 2 * i) + dd // 2


def chip_order(z, j):
    table = ((0, 1, 2, 3), (1, 0, 2, 3), (2, 1, 3, 0), (3, 2, 1, 0))
    value = z * 0 + table[0][j]
    for n in range(1, 4):
        value = jnp.where(z == n, table[n][j], value)
    return value


def far_order(z, j):
    table = ((3, 2, 1, 0), (3, 2, 0, 1), (0, 1, 3, 2), (0, 1, 2, 3))
    value = z * 0 + table[0][j]
    for n in range(1, 4):
        value = jnp.where(z == n, table[n][j], value)
    return value


def pair_owner(p):
    dd, i = p // 2, p % 2
    return 2 * (dd % 2 + 2 * i) + dd // 2


def row_norm(value):
    return lax.rsqrt(jnp.mean(value * value, axis=-1, keepdims=True) + epsilon)


def layer_kernel(given, made, form, *refs):
    names = (*given, *made)
    held = jax.tree.unflatten(form, refs[len(names) :])
    r = types.SimpleNamespace(**dict(zip(names, refs)), **held)
    d = lax.axis_index("dp")
    s = lax.axis_index("seq")
    z = s // 2
    c = lax.rem(s, 2)
    dx = d + 1 - 2 * lax.rem(d, 2)
    dy = lax.rem(d + 2, 4)
    sibling = s + 1 - 2 * c
    home = 2 * c + lax.rem(z, 2)
    is_home = d == home
    pair = pair_of(s)
    cols_d = lanes(d)
    wide_of = lambda i: pl.ds(pl.multiple_of(i * 256, 256), 256)
    wide_d = wide_of(d)

    own_is_target = is_home & (lax.rem(s, 4) == d)
    barrier = pltpu.get_barrier_semaphore()
    for k in range(1, 8):
        pl.semaphore_signal(barrier, inc=1, device_id=(d, lax.rem(s + k, 8)), device_id_type=MESH)
    for k in range(1, 4):
        pl.semaphore_signal(barrier, inc=1, device_id=(lax.rem(d + k, 4), s), device_id_type=MESH)
    for i in range(2):
        giver = owner_of(d, i)

        @pl.when((giver != s) | (lax.rem(s, 4) != d))
        def _():
            pl.semaphore_signal(
                barrier, inc=1, device_id=(lax.rem(s, 4), giver), device_id_type=MESH
            )

    loads = [
        pltpu.make_async_copy(src, dst, r.load_s.at[n])
        for n, (src, dst) in enumerate((
            (r.wo_in, r.wo_f), (r.wg_in, r.gu_f.at[0]), (r.wu_in, r.gu_f.at[1]), (r.wd_in, r.dn_f),
            (r.cot.at[0], r.call.at[s]),
        ))
    ]
    for load in loads:
        load.start()

    for i in range(2):
        for n, w in enumerate((r.wq, r.wk, r.wv)):
            r.qkv_src[i, :, 128 * n : 128 * (n + 1)] = w[:, 128 * i : 128 * (i + 1)].astype(low)
    segment = r.segment[...]
    r.ids[0:1, :] = segment.astype(wide)
    r.ids[1:2, :] = jnp.where(r.observed[...] == 1, segment, -1).astype(wide)
    r.ids[2:3, :] = r.variate[...].astype(wide)
    r.ids[3:4, :] = r.moment[...].astype(wide)
    r.ids[4:8, :] = jnp.zeros((4, 128), wide)
    r.idr[s] = r.ids[...]
    gain_one = r.attn_gain[...].reshape(1, 1024).astype(low).astype(wide)
    gain_two = r.ffn_gain[...].reshape(1, 1024).astype(low).astype(wide)
    value = r.tokens[0].astype(wide)
    r.xall[s] = (value * row_norm(value) * gain_one).astype(low)

    @pl.when(own_is_target)
    def _():
        pl.semaphore_wait(barrier, 11)

    @pl.when(jnp.logical_not(own_is_target))
    def _():
        pl.semaphore_wait(barrier, 12)

    owner = [owner_of(d, i) for i in range(2)]
    for i in range(2):

        @pl.when(owner[i] != s)
        def _():
            remote(r.qkv_src.at[i], r.wqkv.at[rows(s)], r.qs_s.at[i], r.qs_r.at[s], d, owner[i]).start()

        @pl.when(owner[i] == s)
        def _():
            r.wqkv[rows(s), :] = r.qkv_src[i]

    for k in range(1, 8):
        remote(r.ids, r.idr.at[s], r.id_s.at[k], r.id_r.at[s], d, lax.rem(s + k, 8)).start()
    loads[0].wait()
    r.wo[s, :, wide_d] = r.wo_f[...].astype(low)
    wo_ring = Chain(d, s, lambda b: r.wo.at[b, :, wide_d], 1, **r.wo_sems)
    wo_ring.start_lane()
    x_ring = ring = Chain(d, s, lambda b: r.xall.at[b], 2, **r.x_sems)
    ring.start()

    for load in loads[1:]:
        load.wait()
    r.gu_src[...] = r.gu_f[...].astype(low)
    r.dn_src[...] = r.dn_f[...].astype(low)
    c_ring = Chain(d, s, lambda b: r.call.at[b], 2, **r.c_sems)

    for k in range(1, 8):
        t = lax.rem(s + k, 8)
        arrived(r.idr.at[t], r.id_r.at[t], d, s)
    for b in range(8):
        block = r.idr[b]
        for n in range(4):
            r.keyrow[n : n + 1, 128 * b : 128 * (b + 1)] = block[n : n + 1, :]
        r.idc[128 * b : 128 * (b + 1), :] = jnp.concatenate([block] * 16, axis=0).T
    wo_ring.lane_step(1)

    half_qkv = lambda n: r.wqkv.at[pl.ds(512 * n, 512)]

    @pl.when(is_home)
    def _():
        for k in range(1, 8):
            t = lax.rem(s + k, 8)
            arrived(r.wqkv.at[rows(t)], r.qs_r.at[t], d, s)
        remote(r.wqkv, r.wqkv, r.qp_s.at[0], r.qp_r.at[0], dx, s).start()
        remote(r.wqkv, r.wqkv, r.qp_s.at[1], r.qp_r.at[0], dy, s).start()

    wo_ring.lane_step(2)
    ring.step(1)
    wo_ring.lane_step(3)
    place = lax.broadcasted_iota(jnp.int32, (1, 128), 1)
    sign = jnp.where(lax.rem(place, 64) < 32, -1.0, 1.0)
    freq = r.freq[...]

    def trig(b, carry):
        angle = r.idc[rows(b), 3:4] * freq
        r.cosine[rows(b), :] = jnp.cos(angle)
        r.sine[rows(b), :] = jnp.sin(angle) * sign
        return carry

    lax.fori_loop(0, 8, trig, 0)
    ring.step(2)

    for k in range(1, 8):
        t = lax.rem(s + k, 8)
        remote(
            r.gu_src.at[:, :, lanes(t)], r.wgu.at[:, rows(s), cols_d], r.gu_s.at[k], r.gu_r.at[s], d, t
        ).start()
    r.wgu[:, rows(s), cols_d] = r.gu_src[:, :, lanes(s)]
    for m in range(4):
        t = c * 4 + m

        @pl.when(t != s)
        def _():
            remote(
                r.dn_src.at[pl.ds(128 * m, 128)], r.wd.at[rows(z), wide_d],
                r.dn_s.at[m], r.dn_r.at[z], d, t,
            ).start()

        @pl.when(t == s)
        def _():
            r.wd[rows(z), wide_d] = r.dn_src[pl.ds(128 * m, 128), :]

    @pl.when(home == dx)
    def _():
        arrived(r.wqkv, r.qp_r.at[0], d, s)
        remote(half_qkv(0), half_qkv(0), r.qp_s.at[2], r.qp_r.at[1], dy, s).start()

    @pl.when(home == dy)
    def _():
        arrived(r.wqkv, r.qp_r.at[0], d, s)
        remote(half_qkv(1), half_qkv(1), r.qp_s.at[2], r.qp_r.at[2], dx, s).start()

    def group(i):
        zs = chip_order(z, i)
        part = rows(zs, 256)
        gu_part = Plane(
            d, s, lambda i: r.wgu.at[:, part, lanes(i)], lambda i, n: r.wgu.at[n, part, lanes(i)],
            r.gup_s.at[zs], r.gup_r.at[zs],
        )
        dn_part = Plane(
            d, s, lambda i: r.wd.at[rows(zs), wide_of(i)],
            lambda i, n: r.wd.at[rows(2 * zs + n, 64), wide_of(i)],
            r.dnp_s.at[zs], r.dnp_r.at[zs],
        )
        return zs, gu_part, dn_part

    def group_start(i):
        zs, gu_part, dn_part = group(i)
        for m in range(2):
            t = 2 * zs + m

            @pl.when(t != s)
            def _():
                arrived(r.wgu.at[:, rows(t), cols_d], r.gu_r.at[t], d, s)

        gu_part.start()

        @pl.when(2 * zs + s // 4 != s)
        def _():
            arrived(r.wd.at[rows(zs), wide_d], r.dn_r.at[zs], d, s)

        dn_part.start()

    def group_step(i):
        zs, gu_part, dn_part = group(i)
        gu_part.step()
        dn_part.step()

    def group_finish(i):
        zs, gu_part, dn_part = group(i)
        gu_part.finish()
        dn_part.finish()

    wo_lane = r.wo.reshape(4, 2, 128, 1024)
    wo_plane = Plane(
        d, s, lambda i: wo_lane.at[:, c, :, wide_of(i)],
        lambda i, n: wo_lane.at[pl.ds(2 * n, 2), c, :, wide_of(i)],
        r.pl_s, r.pl_r,
    )
    wo_side = lambda: remote(
        wo_lane.at[:, c], wo_lane.at[:, c], r.wos_s, r.wos_r, d, sibling
    )
    wo_plane.start()
    ring.step(3)
    group_start(0)
    for zz in range(4):
        ring.wait_side(zz)

    @pl.when(home == 3 - d)
    def _():
        arrived(half_qkv(0), r.qp_r.at[1], d, s)
        arrived(half_qkv(1), r.qp_r.at[2], d, s)

    def project(i, carry):
        pick = rows(i, 256)
        pre = dot(r.xall[pl.ds(2 * i, 2)].reshape(256, 1024), r.wqkv[...])
        cs, sn = r.cosine[pick, :], r.sine[pick, :]
        qp, kp = pre[:, :128], pre[:, 128:256]
        r.q_all[pick, :] = (qp * cs + partner(qp) * sn).astype(low)
        r.k_all[pick, :] = (kp * cs + partner(kp) * sn).astype(low)
        r.v_all[pick, :] = pre[:, 256:].astype(low)
        return carry

    c_ring.start()
    lax.fori_loop(0, 4, project, 0)

    def tables(pick, first, count):
        seg_col, var_col = r.idc[pick, 0:1], r.idc[pick, 2:3]
        q_place = first + lax.broadcasted_iota(jnp.int32, (count, 1), 0)
        k_place = lax.broadcasted_iota(jnp.int32, (1, 1024), 1)
        allowed = (seg_col == r.keyrow[1:2, :]) | (q_place == k_place)
        return allowed, var_col == r.keyrow[2:3, :]

    def scores_of(qh, h, same):
        scores = dot_nt(qh, r.k_all[...]) * 0.125
        return scores + jnp.where(same, r.same_bias[2 * pair + h], r.cross_bias[2 * pair + h])

    def attend(b, carry):
        pick = rows(b)
        allowed, same = tables(pick, b * 128, 128)
        q_block = r.q_all[pick, :]
        attended, total_lse = None, None
        for h in range(2):
            mine = head_lanes(h)
            qh = jnp.where(mine, q_block, jnp.zeros_like(q_block))
            scores = jnp.where(allowed, scores_of(qh, h, same), NEG)
            top = jnp.max(scores, axis=-1, keepdims=True)
            e = jnp.exp(scores - top)
            total = jnp.sum(e, axis=-1, keepdims=True)
            part = dot((e * (1.0 / total)).astype(low), r.v_all[...])
            one = top + jnp.log(total)
            attended = part if h == 0 else jnp.where(mine, part, attended)
            total_lse = one if h == 0 else jnp.where(mine, one, total_lse)
        r.head_out[b] = attended.astype(low)
        r.lse[pick, :] = jnp.broadcast_to(total_lse, (128, 128))
        return carry

    def send_mixed(t):
        @pl.when(t != s)
        def _():
            remote(r.head_out.at[t], r.mixed.at[pair], r.m_s.at[t], r.m_r.at[s], d, t).start()

        @pl.when(t == s)
        def _():
            r.mixed[pair] = r.head_out[t]

    lax.fori_loop(0, 2, attend, 0)
    send_mixed(0)
    send_mixed(1)
    wo_plane.step()
    group_start(1)
    lax.fori_loop(2, 4, attend, 0)
    send_mixed(2)
    send_mixed(3)
    group_step(0)
    lax.fori_loop(4, 6, attend, 0)
    send_mixed(4)
    send_mixed(5)
    group_start(2)
    lax.fori_loop(6, 8, attend, 0)
    send_mixed(6)
    send_mixed(7)
    wo_plane.finish()
    wo_side().start()
    c_ring.step(1)
    group_step(1)
    group_start(3)
    for t in range(8):

        @pl.when(t != s)
        def _():
            arrived(r.mixed.at[pair_of(t)], r.m_r.at[t], d, s)

    arrived(wo_lane.at[:, 1 - c], r.wos_r, d, s)

    joined = jnp.concatenate([r.mixed[p] for p in range(8)], axis=1)
    middle = r.tokens[0].astype(wide) + dot(joined, r.wo[...].reshape(1024, 1024))
    r.sall[s] = (middle * row_norm(middle) * gain_two).astype(low)
    ring = Chain(d, s, lambda b: r.sall.at[b], 2, **r.y_sems)
    ring.start()
    r.mid[...] = middle
    group_step(2)
    ring.step(1)
    group_step(3)
    ring.step(2)
    c_ring.step(2)
    for i in range(4):
        group_finish(i)

    grads = Scatter(d, s, **r.g_parts)
    outs = Scatter(d, s, **r.o_parts)
    for j in range(4):
        zj = chip_order(z, j)
        if j == 3:
            ring.step(3)
        ring.wait_side(zj)
        pick = rows(zj, 256)
        block = r.sall[pl.ds(2 * zj, 2)].reshape(256, 1024)
        gate_pre = dot(block, r.wgu[0])
        up_pre = dot(block, r.wgu[1])
        r.pre[0, pick, :] = gate_pre
        r.pre[1, pick, :] = up_pre
        hidden = (gate_pre * jax.nn.sigmoid(gate_pre) * up_pre).astype(low)
        r.hid[pick, :] = hidden
    for j in range(4):
        zj = chip_order(z, j)
        if j > 2:
            c_ring.step(j)
        c_ring.wait_side(zj)
        pick = rows(zj, 256)
        hg = dot_nt(r.call[pl.ds(2 * zj, 2)].reshape(256, 1024), r.wd[...])
        gate_pre, up_pre = r.pre[0, pick, :], r.pre[1, pick, :]
        sigma = jax.nn.sigmoid(gate_pre)
        g_low = (hg * up_pre * sigma * (1.0 + gate_pre * (1.0 - sigma))).astype(low)
        u_low = (hg * (gate_pre * sigma)).astype(low)
        r.gg[pick, :] = g_low
        r.ug[pick, :] = u_low
        grads.give(j, zj, dot_nt(g_low, r.wgu[0]) + dot_nt(u_low, r.wgu[1]))
        if j > 0:
            grads.pass_on(j - 1, chip_order(z, j - 1))
        if j > 1:
            grads.add_relay(chip_order(z, j - 2))
    grads.pass_on(3, chip_order(z, 3))
    grads.add_relay(chip_order(z, 2))

    def weigh(i, carry):
        block = r.sall[:, :, wide_of(i)].reshape(1024, 256)
        r.gu_grad[0, rows(i, 256), :] = dot_tn(block, r.gg[...]).astype(low)
        r.gu_grad[1, rows(i, 256), :] = dot_tn(block, r.ug[...]).astype(low)
        return carry

    lax.fori_loop(0, 4, weigh, 0)
    grads.add_relay(chip_order(z, 3))
    gu = PlaneScatter(d, s, lambda i, n: r.gu_grad.at[n, :, lanes(i)], **r.gu_parts)
    dn = PlaneScatter(
        d, s, lambda i, n: r.dn_grad.at[pl.ds(256 * n, 256), wide_of(i)], **r.dn_parts
    )
    wo = PlaneScatter(
        d, s, lambda i, n: r.wo_sum.at[pl.ds(2 * n, 2), :, wide_of(i)], **r.wo_parts
    )
    gu.start()

    def weigh_down(i, carry):
        cols = wide_of(i)
        r.dn_grad[:, cols] = dot_tn(r.hid[...], r.call[:, :, cols].reshape(1024, 256)).astype(low)
        return carry

    lax.fori_loop(0, 4, weigh_down, 0)
    dn.start()

    middle = r.mid[...]
    factor = row_norm(middle)
    normed = middle * factor
    second_grad = grads.total()
    scaled = second_grad * gain_two
    inner = jnp.mean(scaled * normed, axis=-1, keepdims=True)
    r.small[...] = jnp.zeros_like(r.small)
    r.small[1:2, :] = jnp.sum(second_grad * normed, axis=0, keepdims=True)
    value = r.call[s].astype(wide) + factor * (scaled - normed * inner)
    r.mid_grad[...] = value
    v_low = value.astype(low)
    mg = dot_nt(v_low, r.wo[...].reshape(1024, 1024)).astype(low)
    for p in range(8):
        r.mg_src[p] = mg[:, 128 * p : 128 * (p + 1)]
        t = pair_owner(p)

        @pl.when(s != t)
        def _():
            remote(r.mg_src.at[p], r.mgrad.at[s], r.mg_s.at[p], r.mg_r.at[s], d, t).start()

        @pl.when(s == t)
        def _():
            r.mgrad[s] = r.mg_src[p]

    def weigh_out(i, carry):
        left = jnp.concatenate([r.mixed[2 * i], r.mixed[2 * i + 1]], axis=1)
        part = dot_tn(left, v_low).astype(low)
        r.wo_grad[i, 0] = part[:128]
        r.wo_grad[i, 1] = part[128:]
        return carry

    lax.fori_loop(0, 4, weigh_out, 0)
    side = remote(r.wo_grad.at[:, 1 - c], r.wo_in2, r.side_s, r.side_r, d, sibling)
    side.start()
    for j in range(4):
        zj = far_order(z, j)
        outs.give(j, zj, dot(r.hid[rows(zj, 256), :], r.wd[...]))
        if j > 0:
            outs.pass_on(j - 1, far_order(z, j - 1))
    outs.pass_on(3, z)
    r.dk[...] = jnp.zeros_like(r.dk)
    r.dv[...] = jnp.zeros_like(r.dv)
    r.bsum[...] = jnp.zeros_like(r.bsum)
    gu.step()
    side.wait_recv()
    for b in range(4):
        r.wo_sum[b] = (r.wo_grad[b, c].astype(wide) + r.wo_in2[b].astype(wide)).astype(low)
    wo.start()
    for k in range(1, 8):
        t = lax.rem(s + k, 8)
        arrived(r.mgrad.at[t], r.mg_r.at[t], d, s)

    def unturn(x, pick):
        return x * r.cosine[pick, :] - partner(x) * r.sine[pick, :]

    def attend_back(b):
        pick = rows(b, 256)
        allowed, same = tables(pick, b * 256, 256)
        q_block = r.q_all[pick, :]
        m_block = r.mgrad[pl.ds(2 * b, 2)].reshape(256, 128)
        dq = None
        for h in range(2):
            mine = head_lanes(h)
            qh = jnp.where(mine, q_block, jnp.zeros_like(q_block))
            mh = jnp.where(mine, m_block, jnp.zeros_like(m_block))
            scores = scores_of(qh, h, same) - r.lse[pick, 64 * h : 64 * h + 1]
            p = jnp.exp(jnp.where(allowed, scores, NEG))
            pg = dot_nt(mh, r.v_all[...])
            inner = jnp.sum(p * pg, axis=-1, keepdims=True)
            ds = (p * (pg - inner)).astype(low)
            ds_wide = ds.astype(wide)
            r.bsum[2 * h : 2 * h + 1, :] += jnp.sum(jnp.where(same, ds_wide, 0.0), axis=0, keepdims=True)
            r.bsum[2 * h + 1 : 2 * h + 2, :] += jnp.sum(jnp.where(same, 0.0, ds_wide), axis=0, keepdims=True)
            one = dot(ds, r.k_all[...]) * 0.125
            dq = one if h == 0 else jnp.where(mine, one, dq)
            r.dk[...] += dot_tn(ds, qh)
            r.dv[...] += dot_tn(p.astype(low), mh)
        r.gr[pick, 0:128] = unturn(dq, pick).astype(low)

    def keep(n, src, dst):
        return pltpu.make_async_copy(src, dst, r.own_s.at[n])

    def send_gu(n):
        r.gu_sum[n] = gu.total(n).astype(low)
        for k in range(1, 8):
            t = lax.rem(s + k, 8)
            remote(
                r.gu_sum.at[n, rows(t)], r.gu_rx.at[n, s], r.guz_s.at[n, k], r.guz_r.at[n, s], d, t
            ).start()
        keep(n, r.gu_sum.at[n, rows(s)], r.gu_rx.at[n, s]).start()

    def send_dn():
        for j in range(4):
            t = 2 * j + s // 4

            @pl.when(t != s)
            def _():
                remote(
                    r.dn_sum.at[pl.ds(128 * j, 128)], r.dn_rx.at[lax.rem(s, 4)], r.dnz_s.at[j],
                    r.dnz_r.at[lax.rem(s, 4)], d, t,
                ).start()

            @pl.when(t == s)
            def _():
                keep(2, r.dn_sum.at[pl.ds(128 * j, 128)], r.dn_rx.at[lax.rem(s, 4)]).start()

    attend_back(0)
    attend_back(1)
    dn.step()
    outs.add_relay(far_order(z, 0))
    attend_back(2)
    send_gu(0)
    send_gu(1)
    attend_back(3)
    outs.add_relay(far_order(z, 1))

    def turn(b, carry):
        pick = rows(b, 256)
        r.gr[pick, 128:256] = unturn(r.dk[pick, :] * 0.125, pick).astype(low)
        r.gr[pick, 256:384] = r.dv[pick, :].astype(low)
        return carry

    lax.fori_loop(0, 4, turn, 0)
    grads.drain()
    for j in range(4):
        zj = far_order(z, j)
        grads.give(j, zj, dot_nt(r.gr[rows(zj, 256), :], r.wqkv[...]))
        if j > 0:
            grads.pass_on(j - 1, far_order(z, j - 1))
    grads.pass_on(3, z)

    def weigh_qkv(i, carry):
        block = r.xall[:, :, wide_of(i)].reshape(1024, 256)
        value = dot_tn(block, r.gr[...])
        along = jnp.sum(value * r.wqkv[rows(i, 256), :].astype(wide), axis=1, keepdims=True)
        r.small[0:1, wide_of(i)] = jnp.broadcast_to(along, (256, 128)).T[0:1]
        value = value.astype(low)
        r.qkv_grad[2 * i] = value[:128]
        r.qkv_grad[2 * i + 1] = value[128:]
        return carry

    for n in range(2):
        r.dn_sum[pl.ds(256 * n, 256), :] = dn.total(n).astype(low)
    send_dn()
    lax.fori_loop(0, 4, weigh_qkv, 0)
    grads.add_relay(far_order(z, 0))
    r.small[0:1, :] = r.small[0:1, :] / gain_one
    place = lax.broadcasted_iota(jnp.int32, (1, 1024), 1)
    line = jnp.zeros((1, 1024), wide)
    for h in range(2):
        for n in range(2):
            k = 2 * h + n
            one = jnp.sum(r.bsum[k : k + 1, :], axis=1, keepdims=True)
            line = line + jnp.where(place == 128 * n + 2 * pair + h, one, 0.0)
    r.small[2:3, :] = line
    for k in range(1, 4):
        t = lax.rem(d + k, 4)
        remote(r.small, r.small_p.at[d], r.sp_s.at[k], r.sp_r.at[d], t, s).start()
    for k in range(1, 4):
        t = lax.rem(d + k, 4)
        for m in range(2):
            remote(
                r.qkv_grad.at[t + 4 * m], r.q_in.at[d, m], r.qg_s.at[t, m], r.qg_r.at[d, m], t, s
            ).start()
    wo.step()
    grads.add_relay(far_order(z, 1))
    for k in range(1, 4):
        t = lax.rem(d + k, 4)
        arrived(r.small_p.at[t], r.sp_r.at[t], d, s)
    r.small_p[d] = r.small[...]
    r.small_q[...] = r.small_p[0] + r.small_p[1] + r.small_p[2] + r.small_p[3]
    for k in range(1, 8):
        t = lax.rem(s + k, 8)
        remote(r.small_q, r.small_z.at[s], r.sz_s.at[k], r.sz_r.at[s], d, t).start()
    keep(5, r.small_q, r.small_z.at[s]).start()

    r.out_v[...] = (r.mid[...] + outs.total()).astype(low)
    keep(4, r.out_v, r.out.at[0]).start()
    for n in range(2):
        r.wo_fin[pl.ds(2 * n, 2)] = wo.total(n).astype(low)
    keep(6, r.wo_fin.at[z], r.wo_rx.at[z]).start()
    for k in range(1, 4):
        t = lax.rem(z + k, 4)
        remote(r.wo_fin.at[t], r.wo_rx.at[z], r.woz_s.at[t], r.woz_r.at[z], d, 2 * t + c).start()

    for m in range(2):
        value = r.qkv_grad[d + 4 * m].astype(wide)
        for k in range(1, 4):
            t = lax.rem(d + k, 4)
            arrived(r.q_in.at[t, m], r.qg_r.at[t, m], d, s)
            value = value + r.q_in[t, m].astype(wide)
        r.q_sum[m] = value.astype(low)
        target = d + 4 * m
        mine = (target == s) & is_home

        @pl.when(jnp.logical_not(mine))
        def _():
            remote(
                r.q_sum.at[m], r.q_rx.at[z // 2], r.qz_s.at[m], r.qz_r.at[z // 2], home, target
            ).start()

        @pl.when(mine)
        def _():
            keep(3, r.q_sum.at[m], r.q_rx.at[z // 2]).start()

    value = r.tokens[0].astype(wide)
    factor = row_norm(value)
    normed = value * factor
    first_grad = grads.total()
    scaled = first_grad * gain_one
    inner = jnp.mean(scaled * normed, axis=-1, keepdims=True)

    r.tok_grad[0] = (r.mid_grad[...] + factor * (scaled - normed * inner)).astype(low)

    for k in range(1, 8):
        t = lax.rem(s + k, 8)
        for n in range(2):
            arrived(r.gu_rx.at[n, t], r.guz_r.at[n, t], d, s)
    for m in range(4):

        @pl.when(4 * c + m != s)
        def _():
            arrived(r.dn_rx.at[m], r.dnz_r.at[m], d, s)

    for k in range(1, 4):
        t = lax.rem(z + k, 4)
        arrived(r.wo_rx.at[t], r.woz_r.at[t], d, s)
    for i in range(2):

        @pl.when((owner[i] != s) | (lax.rem(s, 4) != d))
        def _():
            arrived(r.q_rx.at[i], r.qz_r.at[i], d, s)

    for k in range(1, 8):
        t = lax.rem(s + k, 8)
        arrived(r.small_z.at[t], r.sz_r.at[t], d, s)

    keep(0, r.gu_sum.at[0, rows(0)], r.gu_rx.at[0, 0]).wait()
    keep(1, r.gu_sum.at[0, rows(0)], r.gu_rx.at[0, 0]).wait()
    keep(4, r.out_v, r.out.at[0]).wait()
    keep(5, r.small_q, r.small_z.at[0]).wait()
    keep(6, r.wo_fin.at[0], r.wo_rx.at[0]).wait()

    @pl.when(s // 4 == lax.rem(s, 2))
    def _():
        keep(2, r.dn_sum.at[pl.ds(0, 128)], r.dn_rx.at[0]).wait()

    @pl.when(own_is_target)
    def _():
        keep(3, r.q_sum.at[0], r.q_rx.at[0]).wait()

    x_ring.drain()
    c_ring.drain()
    ring.drain()
    wo_ring.lane_drain()
    wo_side().wait_send()
    for i in range(2):

        @pl.when(owner[i] != s)
        def _():
            sent(r.qkv_src.at[i], r.qs_s.at[i], d, s)

    for k in range(1, 8):
        sent(r.ids, r.id_s.at[k], d, s)
        sent(r.gu_src.at[:, :, pl.ds(0, 128)], r.gu_s.at[k], d, s)

    @pl.when(is_home)
    def _():
        sent(r.wqkv, r.qp_s.at[0], d, s)
        sent(r.wqkv, r.qp_s.at[1], d, s)

    @pl.when((home == dx) | (home == dy))
    def _():
        sent(half_qkv(0), r.qp_s.at[2], d, s)

    for m in range(4):

        @pl.when(c * 4 + m != s)
        def _():
            sent(r.dn_src.at[pl.ds(128 * m, 128)], r.dn_s.at[m], d, s)

    for t in range(8):

        @pl.when(t != s)
        def _():
            sent(r.head_out.at[t], r.m_s.at[t], d, s)

        @pl.when(s != pair_owner(t))
        def _():
            sent(r.mg_src.at[t], r.mg_s.at[t], d, s)

    side.wait_send()
    gu.drain()
    dn.drain()
    wo.drain()
    grads.drain()
    outs.drain()
    for k in range(1, 8):
        for n in range(2):
            sent(r.gu_sum.at[n, rows(0)], r.guz_s.at[n, k], d, s)
        sent(r.small_q, r.sz_s.at[k], d, s)
    for j in range(4):

        @pl.when(2 * j + s // 4 != s)
        def _():
            sent(r.dn_sum.at[pl.ds(0, 128)], r.dnz_s.at[j], d, s)

    for k in range(1, 4):
        t = lax.rem(z + k, 4)
        sent(r.wo_fin.at[t], r.woz_s.at[t], d, s)
        t = lax.rem(d + k, 4)
        for m in range(2):
            sent(r.q_sum.at[m], r.qg_s.at[t, m], d, s)
        sent(r.small, r.sp_s.at[k], d, s)
    for m in range(2):

        @pl.when(jnp.logical_not((d + 4 * m == s) & is_home))
        def _():
            sent(r.q_sum.at[m], r.qz_s.at[m], d, s)


def vmem():
    return pl.BlockSpec(memory_space=pltpu.VMEM)


def hbm():
    return pl.BlockSpec(memory_space=pl.ANY)


def smem():
    return pl.BlockSpec(memory_space=pltpu.SMEM)


def shape(*dims, kind=low):
    return jax.ShapeDtypeStruct(dims, kind)


def dma(*dims):
    return pltpu.SemaphoreType.DMA(dims)


def layer(ins):
    outs = dict(
        tok_grad=shape(1, 128, 1024),
        out=shape(1, 128, 1024),
        gu_rx=shape(2, 8, 128, 128),
        dn_rx=shape(4, 128, 256),
        wo_rx=shape(4, 128, 256),
        q_rx=shape(2, 128, 384),
        small_z=shape(8, 8, 1024, kind=wide),
    )
    scratch = dict(
        xall=pltpu.VMEM((8, 128, 1024), low),
        q_all=pltpu.VMEM((1024, 128), low),
        k_all=pltpu.VMEM((1024, 128), low),
        v_all=pltpu.VMEM((1024, 128), low),
        lse=pltpu.VMEM((1024, 128), wide),
        wqkv=pltpu.VMEM((1024, 384), low),
        wo=pltpu.VMEM((8, 128, 1024), low),
        wgu=pltpu.VMEM((2, 1024, 512), low),
        wd=pltpu.VMEM((512, 1024), low),
        call=pltpu.VMEM((8, 128, 1024), low),
        ids=pltpu.VMEM((8, 128), wide),
        idr=pltpu.VMEM((8, 8, 128), wide),
        idc=pltpu.VMEM((1024, 128), wide),
        keyrow=pltpu.VMEM((8, 1024), wide),
        cosine=pltpu.VMEM((1024, 128), wide),
        sine=pltpu.VMEM((1024, 128), wide),
        mixed=pltpu.VMEM((8, 128, 128), low),
        wo_f=pltpu.VMEM((128, 256), wide),
        gu_f=pltpu.VMEM((2, 128, 1024), wide),
        dn_f=pltpu.VMEM((512, 256), wide),
        load_s=dma(5),
        own_s=dma(11),
        out_v=pltpu.VMEM((128, 1024), low),
        qkv_src=pltpu.VMEM((2, 128, 384), low),
        gu_src=pltpu.VMEM((2, 128, 1024), low),
        dn_src=pltpu.VMEM((512, 256), low),
        head_out=pltpu.VMEM((8, 128, 128), low),
        sall=pltpu.VMEM((8, 128, 1024), low),
        pre=pltpu.VMEM((2, 1024, 512), wide),
        gg=pltpu.VMEM((1024, 512), low),
        ug=pltpu.VMEM((1024, 512), low),
        hid=pltpu.VMEM((1024, 512), low),
        mid=pltpu.VMEM((128, 1024), wide),
        mid_grad=pltpu.VMEM((128, 1024), wide),
        mg_src=pltpu.VMEM((8, 128, 128), low),
        mgrad=pltpu.VMEM((8, 128, 128), low),
        gu_grad=pltpu.VMEM((2, 1024, 512), low),
        dn_grad=pltpu.VMEM((512, 1024), low),
        wo_grad=pltpu.VMEM((4, 2, 128, 1024), low),
        dk=pltpu.VMEM((1024, 128), wide),
        dv=pltpu.VMEM((1024, 128), wide),
        gr=pltpu.VMEM((1024, 384), low),
        bsum=pltpu.VMEM((8, 1024), wide),
        qkv_grad=pltpu.VMEM((8, 128, 384), low),
        wo_in2=pltpu.VMEM((4, 128, 1024), low),
        wo_sum=pltpu.VMEM((4, 128, 1024), low),
        gu_sum=pltpu.VMEM((2, 1024, 128), low),
        dn_sum=pltpu.VMEM((512, 256), low),
        wo_fin=pltpu.VMEM((4, 128, 256), low),
        q_in=pltpu.VMEM((4, 2, 128, 384), low),
        q_sum=pltpu.VMEM((2, 128, 384), low),
        small=pltpu.VMEM((8, 1024), wide),
        small_p=pltpu.VMEM((4, 8, 1024), wide),
        small_q=pltpu.VMEM((8, 1024), wide),
        g_parts=scatter_scratch(),
        o_parts=scatter_scratch(),
        gu_parts=plane_scratch(1024, 128),
        dn_parts=plane_scratch(256, 256),
        wo_parts=plane_scratch(2, 128, 256),
        x_sems=ring_scratch(2),
        y_sems=ring_scratch(2),
        c_sems=ring_scratch(2),
        wo_sems=ring_scratch(1),
        qs_s=dma(2), qs_r=dma(8), qp_s=dma(3), qp_r=dma(3),
        id_s=dma(8), id_r=dma(8), gu_s=dma(8), gu_r=dma(8), gup_s=dma(4, 4), gup_r=dma(4, 4), dnp_s=dma(4, 4), dnp_r=dma(4, 4),
        dn_s=dma(4), dn_r=dma(4), pl_s=dma(4), pl_r=dma(4),
        wos_s=dma(), wos_r=dma(), m_s=dma(8), m_r=dma(8),
        mg_s=dma(8), mg_r=dma(8), side_s=dma(), side_r=dma(),
        guz_s=dma(2, 8), guz_r=dma(2, 8), dnz_s=dma(4), dnz_r=dma(4),
        woz_s=dma(4), woz_r=dma(4), qg_s=dma(4, 2), qg_r=dma(4, 2),
        qz_s=dma(2), qz_r=dma(2), sp_s=dma(8), sp_r=dma(4),
        sz_s=dma(8), sz_r=dma(8),
    )
    flat, inner = jax.tree.flatten(scratch)
    got = pl.pallas_call(
        functools.partial(layer_kernel, tuple(ins), tuple(outs), inner),
        name="whole",
        out_shape=tuple(outs.values()),
        in_specs=[*[vmem()] * 11, *[smem()] * 2, *[hbm()] * 5],
        out_specs=[vmem(), *[hbm()] * 6],
        scratch_shapes=flat,
        compiler_params=pltpu.CompilerParams(
            collective_id=0, has_side_effects=True, vmem_limit_bytes=64 << 20
        ),
    )(*ins.values())
    return types.SimpleNamespace(**dict(zip(outs, got)))


def finish_kernel(
    out, tok_grad, gu, dn, wo, qkv, small,
    out2, tok2, gate2, up2, dn2, wo2, q2, k2, v2, g1, g2, same, cross,
):
    out2[...] = out[...]
    tok2[...] = tok_grad[...]
    for t in range(8):
        gate2[:, 128 * t : 128 * (t + 1)] = gu[0, t].astype(wide)
        up2[:, 128 * t : 128 * (t + 1)] = gu[1, t].astype(wide)
    for m in range(4):
        dn2[128 * m : 128 * (m + 1), :] = dn[m].astype(wide)
    total = wo[0].astype(wide)
    for m in range(1, 4):
        total = total + wo[m].astype(wide)
    wo2[...] = total
    for n, ref in enumerate((q2, k2, v2)):
        for i in range(2):
            ref[:, 128 * i : 128 * (i + 1)] = qkv[i, :, 128 * n : 128 * (n + 1)].astype(wide)
    total = small[0]
    for t in range(1, 8):
        total = total + small[t]
    g1[...] = total[0:1]
    g2[...] = total[1:2]
    same[...] = total[2:3, 0:128]
    cross[...] = total[2:3, 128:256]


def finish(got):
    outs = (
        shape(1, 128, 1024), shape(1, 128, 1024),
        shape(128, 1024, kind=wide), shape(128, 1024, kind=wide), shape(512, 256, kind=wide),
        shape(128, 256, kind=wide), shape(128, 256, kind=wide), shape(128, 256, kind=wide),
        shape(128, 256, kind=wide), shape(1, 1024, kind=wide), shape(1, 1024, kind=wide),
        shape(1, 128, kind=wide), shape(1, 128, kind=wide),
    )
    return pl.pallas_call(
        finish_kernel,
        name="finish",
        out_shape=outs,
        in_specs=[vmem()] * 7,
        out_specs=[vmem()] * len(outs),
    )(got.out, got.tok_grad, got.gu_rx, got.dn_rx, got.wo_rx, got.q_rx, got.small_z)


def rope_rates():
    rates = np.float32(10000.0) ** (-np.arange(32, dtype=np.float32) * np.float32(2.0 / 64))
    return np.tile(rates.astype(np.float32), 4)[None]


def fast_body(
    tokens, attn_gain, query_weight, key_weight, value_weight, out_weight, same_bias, cross_bias,
    ffn_gain, gate_weight, up_weight, down_weight, segment_ids, variate_ids, time_ids, observed,
    cotangent,
):
    got = layer(dict(
        tokens=tokens, attn_gain=attn_gain, ffn_gain=ffn_gain,
        wq=query_weight, wk=key_weight, wv=value_weight, segment=segment_ids, freq=rope_rates(),
        variate=variate_ids, moment=time_ids, observed=observed,
        same_bias=same_bias, cross_bias=cross_bias,
        wo_in=out_weight, wg_in=gate_weight, wu_in=up_weight, wd_in=down_weight, cot=cotangent,
    ))
    out, tok, gate, up, dn, wo, q, k, v, g1, g2, same, cross = finish(got)
    return (
        out, tok, g1[0], q, k, v, wo, same[0, 0:16], cross[0, 0:16], g2[0], gate, up, dn,
    )


def fits(mesh):
    return mesh.shape["dp"] == 4 and mesh.shape["seq"] == 8


def solution(mesh):
    in_specs = (
        P("dp", "seq", None),
        P(),
        P("seq", "dp"),
        P("seq", "dp"),
        P("seq", "dp"),
        P("seq", "dp"),
        P(),
        P(),
        P(),
        P("seq", "dp"),
        P("seq", "dp"),
        P("seq", "dp"),
        P("dp", "seq"),
        P("dp", "seq"),
        P("dp", "seq"),
        P("dp", "seq"),
        P("dp", "seq", None),
    )
    out_specs = (
        P("dp", "seq", None),
        P("dp", "seq", None),
        P(),
        P("seq", "dp"),
        P("seq", "dp"),
        P("seq", "dp"),
        P("seq", "dp"),
        P(),
        P(),
        P(),
        P("seq", "dp"),
        P("seq", "dp"),
        P("seq", "dp"),
    )
    part = fast_body if fits(mesh) else body
    return jax.shard_map(part, mesh=mesh, in_specs=in_specs, out_specs=out_specs, check_vma=False)
```
